32 devices in a mesh: head: 8 (over z, y), fsdp: 4 (over x, core).
Axes of the slice: x: 2, y: 2, z: 4, core: 2. Of those that a mesh axis runs over, the one named last changes fastest.
Arguments:
- hidden: bfloat16 [4, 1024, 2048], P('fsdp', 'head'), may hold values from -6 to 6
- w_qkv: bfloat16 [2048, 6144], P(('head', 'fsdp')), may hold values from -0.125 to 0.125
- w_out: bfloat16 [2048, 2048], P(('head', 'fsdp')), may hold values from -0.75 to 0.75
- w_router: bfloat16 [2048, 16], P(('head', 'fsdp')), may hold values from -0.0625 to 0.0625
- g_attn: bfloat16 [2048], P(('head', 'fsdp')), may hold values from 0.099609375 to 1.8984375
- g_ffn: bfloat16 [2048], P(('head', 'fsdp')), may hold values from 0.099609375 to 1.8984375
- g_q: bfloat16 [2048], P(('head', 'fsdp')), may hold values from 0.69921875 to 2
- g_k: bfloat16 [2048], P(('head', 'fsdp')), may hold values from 0.69921875 to 2
- w_gate: bfloat16 [16, 2048, 1024], P('head', 'fsdp'), may hold values from -0.125 to 0.125
- w_up: bfloat16 [16, 2048, 1024], P('head', 'fsdp'), may hold values from -0.125 to 0.125
- w_down: bfloat16 [16, 1024, 2048], P('head', 'fsdp'), may hold values from -0.75 to 0.75
- lengths: int32 [4], P('fsdp'), may hold values from 256 to 1024, as said below
- routes: int32 [4, 1024, 8], P('fsdp', 'head'), may hold values from 0 to 15, all different within a row; in each aligned block of 128 rows (0 to 127, 128 to 255, ..., all dimensions but the last counted through in order) at most 96 rows name the same one
- route_codes: int32 [4, 1024, 8], P('fsdp', 'head'), may hold values from -384 to 383
- cotangent: bfloat16 [4, 1024, 2048], P('fsdp', 'head'), may hold values from -6 to 6
Outputs:
- out: bfloat16 [4, 1024, 2048], P('fsdp', 'head')
- d_hidden: float32 [4, 1024, 2048], P('fsdp', 'head')
- d_w_qkv: float32 [2048, 6144], P(('head', 'fsdp'))
- d_w_out: float32 [2048, 2048], P(('head', 'fsdp'))
- d_w_router: float32 [2048, 16], P(('head', 'fsdp'))
- d_g_attn: float32 [2048], P(('head', 'fsdp'))
- d_g_ffn: float32 [2048], P(('head', 'fsdp'))
- d_g_q: float32 [2048], P(('head', 'fsdp'))
- d_g_k: float32 [2048], P(('head', 'fsdp'))
- d_w_gate: float32 [16, 2048, 1024], P('head', 'fsdp')
- d_w_up: float32 [16, 2048, 1024], P('head', 'fsdp')
- d_w_down: float32 [16, 1024, 2048], P('head', 'fsdp')
The draws below stay inside these ranges and needn't reach their ends.
Inputs may be any that keep to these rules, and one draw needn't show every extreme that they name: `lengths`: keys at positions at or after a sequence's length are masked. Some sequence has 1024 valid slots, some 1024 // 4. Each token names 8 different experts. In the 128 tokens of one device no expert is named by more than 96 routes, and some expert reaches 96.
All inputs are finite; a program needn't handle non-finite values.
Results may differ from the reference program's by a relative error of at most 0.018.
Values may be sent and summed in bfloat16 or wider, within the bound.
A program may use at most 256 MiB of HBM per device.

```python
import math
import jax
import jax.numpy as jnp
import numpy as np
from jax import lax

D = 2048
HEADS = 16
HD = 128
FF = 1024
TOP = 8
TOK_DEV = 128
EXPERTS = 16
SEQ_LEN = 1024
SEQS = 4
CAP = 96


def draw_lengths(key, part):
    first_key = jax.random.fold_in(key, 11)
    second_key = jax.random.fold_in(key, 12)
    shortest = SEQ_LEN // 4
    drawn = jax.random.randint(first_key, (SEQS,), shortest, SEQ_LEN + 1)
    order = jax.random.permutation(second_key, SEQS)
    drawn = drawn.at[order[0]].set(SEQ_LEN)
    drawn = drawn.at[order[1]].set(shortest)
    return drawn.astype(jnp.int32)


def touch_ends(array, key, low, largest):
    spot = [jax.random.randint(jax.random.fold_in(key, axis), (), 0, length) for axis, length in enumerate(array.shape)]
    main_axis = array.shape.index(max(array.shape))
    beside = spot[:main_axis] + [(spot[main_axis] + 1) % array.shape[main_axis]] + spot[main_axis + 1:]
    return array.at[tuple(spot)].set(low).at[tuple(beside)].set(largest)


def with_spikes(values, key, source, target, blocks, factor):
    def block_of(position):
        return (jnp.arange(values.shape[position]) // (values.shape[position] // blocks)).reshape((-1,) + (1,) * (values.ndim - 1 - position))

    first = jax.random.permutation(key, blocks)[block_of(target)]
    far = (block_of(target) + blocks // 2) % blocks
    return jnp.where((block_of(source) == first) | (block_of(source) == far), factor * values, values)


def block_levels(rng, shape, pieces, low, high):
    factor_of = 1.0
    for position, blocks in pieces:
        heights = jax.random.uniform(jax.random.fold_in(jax.random.fold_in(rng, 6), position), (blocks,), jnp.float32, low / len(pieces), high / len(pieces))
        factor_of = factor_of * jnp.repeat(jnp.exp(heights), shape[position] // blocks).reshape((-1,) + (1,) * (len(shape) - 1 - position))
    return factor_of


def shared_out(key, own, number, rows, count, top, reach, skew):
    sequence = jax.random.permutation(key, count)
    crowded, usual = shares(count, rows * top, reach, skew, True), shares(count, rows * top, reach, skew, False)
    places = jnp.arange(count)

    def named(sizes, turn):
        used = int((sizes > 0).sum())
        fixed = max(1, used // 4)
        passed = fixed + (places - fixed + turn * (used - fixed)) % max(1, count - fixed)
        return jnp.zeros((count,), jnp.int32).at[sequence[jnp.where(places < fixed, places, passed)]].set(jnp.asarray(sizes, jnp.int32))

    sizes = jnp.where(number % 4 == 0, named(crowded, number // 4), named(usual, number - number // 4 - 1))
    mixed = jax.random.permutation(jax.random.fold_in(own, 3), count)
    source_of, sink = mixed[0:count // 2 * 2:2], mixed[1:count // 2 * 2:2]
    room = jnp.minimum(sizes[source_of] - 1, reach - sizes[sink]) // 2
    room = jnp.where((source_of == sequence[0]) | (sink == sequence[0]) | (sizes[sink] == 0), 0, jnp.maximum(room, 0))
    passed = jax.random.randint(jax.random.fold_in(own, 4), (count // 2,), 0, 1 << 20) % (room + 1)
    sizes = sizes.at[source_of].add(-passed).at[sink].add(passed)
    items = jnp.searchsorted(jnp.cumsum(sizes), jnp.arange(rows * top), side="right").astype(jnp.int32)
    table = items.reshape(top, rows).T
    table = table[jax.random.permutation(jax.random.fold_in(own, 1), rows)]
    turn = jax.random.randint(jax.random.fold_in(own, 2), (rows, 1), 0, top)
    return jnp.take_along_axis(table, (jnp.arange(top)[None, :] + turn) % top, axis=1)


def shares(count, total, reach, slope, full):
    loads = [(1 << 20) // math.isqrt(standing ** slope) + 1 for standing in range(1, count + 1)]
    largest = reach if full else min(reach, max(-(-total // count), total * loads[0] // sum(loads)))
    least = 1 if total - largest >= count - 1 else 0
    holding, rest = [largest] + [least] * (count - 1), total - largest - least * (count - 1)
    while rest > 0:
        candidates = [i for i in range(1, count) if holding[i] < largest] or [i for i in range(1, count) if holding[i] < reach]
        whole, remaining = sum([loads[i] for i in candidates]), rest
        for i in candidates:
            more = min(reach - holding[i], max(1, remaining * loads[i] // whole), rest)
            holding[i] = holding[i] + more
            rest = rest - more
    return np.array(holding)


def normal_values(key, dims, deviation, limit, cuts=(), kind=jnp.bfloat16):
    level = block_levels(key, dims, cuts, -0.22, 0.18) if cuts else 1.0
    array = jax.random.normal(key, dims, jnp.float32) * deviation * level
    return jnp.minimum(jnp.maximum(array, -limit), limit).astype(kind)


def gaussian_with(key, shape, scale, reach, split, heavy, kind=jnp.bfloat16):
    values = scale * jax.random.normal(key, shape, jnp.float32)
    if split:
        values = values * block_levels(key, shape, split, -0.22, 0.18)
    return jnp.clip(with_spikes(values, jax.random.fold_in(key, 3), *heavy), -reach, reach).astype(kind)


def setup_inputs(seed: int = 0) -> dict:
    streams_of = jax.random.split(jax.random.key(seed), 16)
    hidden = gaussian_with(streams_of[0], (SEQS, SEQ_LEN, D), 1.0, 6.0, ((0, 4), (1, 8)), (1, 2, 8, 2.0))
    w_qkv = normal_values(streams_of[1], (D, 3 * D), D ** -0.5, 0.125, ((0, 32),))
    w_out = normal_values(streams_of[2], (D, D), (D // 32) ** -0.5, 0.75, ((0, 32),))
    w_router = normal_values(streams_of[3], (D, EXPERTS), (4 * D) ** -0.5, 0.0625, ((0, 32),))
    g_attn = jnp.clip(1.0 + 0.18 * jax.random.normal(streams_of[4], (D,), jnp.float32), 0.099609375, 1.8984375).astype(jnp.bfloat16)
    g_ffn = jnp.clip(1.0 + 0.18 * jax.random.normal(streams_of[5], (D,), jnp.float32), 0.099609375, 1.8984375).astype(jnp.bfloat16)
    g_q = jnp.clip(jnp.exp(math.log(2.0) - 1.0509388 * jax.random.uniform(streams_of[6], (D,), jnp.float32) ** block_levels(streams_of[6], (D,), ((0, 32),), -0.2, 0.2)), 0.69921875, 2.0).astype(jnp.bfloat16)
    g_k = jnp.clip(jnp.exp(math.log(2.0) - 1.0509388 * jax.random.uniform(streams_of[7], (D,), jnp.float32) ** block_levels(streams_of[7], (D,), ((0, 32),), -0.2, 0.2)), 0.69921875, 2.0).astype(jnp.bfloat16)
    w_gate = normal_values(streams_of[8], (EXPERTS, D, FF), D ** -0.5, 0.125, ((0, 8), (1, 4)))
    w_up = normal_values(streams_of[9], (EXPERTS, D, FF), D ** -0.5, 0.125, ((0, 8), (1, 4)))
    w_down = normal_values(streams_of[10], (EXPERTS, FF, D), (FF // 16) ** -0.5, 0.75, ((0, 8), (1, 4)))
    lengths = draw_lengths(jax.random.fold_in(streams_of[15], 71), 0)
    routes_keys = jax.random.split(jax.random.fold_in(streams_of[12], 1), SEQS * SEQ_LEN // TOK_DEV)
    routes_turns = jax.random.permutation(jax.random.fold_in(streams_of[12], 3), SEQS * SEQ_LEN // TOK_DEV)
    routes = jax.vmap(lambda own, number: shared_out(jax.random.fold_in(streams_of[12], 2), own, number, TOK_DEV, EXPERTS, TOP, CAP, 1))(routes_keys, routes_turns).reshape((SEQS, SEQ_LEN, TOP))
    route_codes = touch_ends(jax.random.randint(streams_of[13], (SEQS, SEQ_LEN, TOP), -384, 384), jax.random.fold_in(streams_of[13], 1), -384, 383).astype(jnp.int32)
    cotangent = normal_values(streams_of[14], (SEQS, SEQ_LEN, D), 1.0, 6.0, ((0, 4), (1, 8)))
    return dict(hidden=hidden, w_qkv=w_qkv, w_out=w_out, w_router=w_router, g_attn=g_attn, g_ffn=g_ffn, g_q=g_q, g_k=g_k, w_gate=w_gate, w_up=w_up, w_down=w_down, lengths=lengths, routes=routes, route_codes=route_codes, cotangent=cotangent)


EPS = 1e-06
ROPE_BASE = 10000.0
HIGH = lax.Precision.HIGHEST
NEGATIVE = -1e+30

@jax.custom_vjp
def low(v):
    return lax.optimization_barrier(v.astype(jnp.bfloat16)).astype(jnp.float32)

@jax.custom_vjp
def low_back(v):
    return v

def low_keep(v):
    return (low(v), None)

def low_pass(kept, grad):
    return (grad,)

def back_keep(v):
    return (v, None)

def back_low(kept, grad):
    return (low(grad),)
low.defvjp(low_keep, low_pass)
low_back.defvjp(back_keep, back_low)

def normed(values, gain):
    return values * lax.rsqrt(lax.optimization_barrier(jnp.mean(values * values, axis=-1, keepdims=True)) + EPS) * gain

def rotary(values, positions):
    half_dim = HD // 2
    frequency = ROPE_BASE ** (-2.0 * jnp.arange(half_dim, dtype=jnp.float32) / HD)
    angles = positions.astype(jnp.float32)[:, None] * frequency[None, :]
    cosine = jnp.cos(angles)[:, None, :]
    sine = jnp.sin(angles)[:, None, :]
    shaped = values.reshape(values.shape[:-1] + (HEADS, HD))
    first = shaped[..., :half_dim]
    second = shaped[..., half_dim:]
    turned = jnp.concatenate([first * cosine - second * sine, second * cosine + first * sine], axis=-1)
    return turned.reshape(values.shape)

def attend_sequence(packed):
    queries, keys, values, length = packed
    query_heads = queries.reshape(SEQ_LEN, HEADS, HD)
    key_heads = keys.reshape(SEQ_LEN, HEADS, HD)
    value_heads = values.reshape(SEQ_LEN, HEADS, HD)
    valid = jnp.arange(SEQ_LEN, dtype=jnp.int32) < length
    scale = 1.0 / math.sqrt(HD)
    qblock = min(512, SEQ_LEN)

    def block_fn(query_block):
        scores = low_back(jnp.einsum('qhd,khd->hqk', query_block, key_heads, precision=HIGH) * scale)
        scores = jnp.where(valid[None, None, :], scores, NEGATIVE)
        row_peak = lax.optimization_barrier(jnp.max(scores, axis=-1, keepdims=True))
        exponent = jnp.exp(scores - row_peak)
        probabilities = low(exponent / lax.optimization_barrier(jnp.sum(exponent, axis=-1, keepdims=True)))
        return jnp.einsum('hqk,khd->qhd', probabilities, value_heads, precision=HIGH)
    result = lax.map(jax.checkpoint(block_fn), query_heads.reshape(SEQ_LEN // qblock, qblock, HEADS, HD))
    return result.reshape(SEQ_LEN, HEADS * HD)

def experts_apply(ffn_input, route_ids, route_offsets, w_router, w_gate, w_up, w_down):
    token_count = ffn_input.shape[0]
    logits = jnp.dot(ffn_input, w_router, precision=HIGH)
    chosen = jnp.take_along_axis(logits, route_ids, axis=1) + route_offsets.astype(jnp.float32) / 1024.0
    chosen_peak = lax.optimization_barrier(jnp.max(chosen, axis=1, keepdims=True))
    chosen_exp = jnp.exp(chosen - chosen_peak)
    gates = chosen_exp / lax.optimization_barrier(jnp.sum(chosen_exp, axis=1, keepdims=True))
    block_count = token_count // TOK_DEV
    flat_routes = route_ids.reshape(block_count, TOK_DEV * TOP)
    counts = (flat_routes[:, :, None] == jnp.arange(EXPERTS, dtype=jnp.int32)[None, None, :]).astype(jnp.int32)
    ranks = jnp.cumsum(counts, axis=1) - 1
    slots = lax.optimization_barrier(jnp.sum(counts * ranks, axis=2))
    depth = block_count * CAP
    places = (flat_routes * depth + jnp.arange(block_count, dtype=jnp.int32)[:, None] * CAP + slots).reshape(-1)
    owners = jnp.repeat(jnp.arange(token_count, dtype=jnp.int32), TOP)
    routed = low_back(ffn_input[owners])
    buffer = jnp.zeros((EXPERTS * depth, D), jnp.float32).at[places].set(routed)

    def expert_fn(packed):
        inputs, gate_weight, up_weight, down_weight = packed
        gate_pre = low_back(jnp.dot(inputs, gate_weight, precision=HIGH))
        up_pre = low_back(jnp.dot(inputs, up_weight, precision=HIGH))
        activated = low(jax.nn.silu(gate_pre) * up_pre)
        return low_back(low(jnp.dot(activated, down_weight, precision=HIGH)))
    produced = lax.map(jax.checkpoint(expert_fn), (buffer.reshape(EXPERTS, depth, D), w_gate, w_up, w_down))
    picked = produced.reshape(EXPERTS * depth, D)[places].reshape(token_count, TOP, D)
    return lax.optimization_barrier(jnp.sum(gates[:, :, None] * picked, axis=1))

def layer(hidden, w_qkv, w_out, w_router, g_attn, g_ffn, g_q, g_k, w_gate, w_up, w_down, lengths, routes, route_codes):
    attn_input = low(normed(hidden, g_attn)).reshape(-1, D)
    projected = low_back(jnp.dot(attn_input, w_qkv, precision=HIGH)).reshape(SEQS, SEQ_LEN, 3 * D)
    positions = jnp.arange(SEQ_LEN, dtype=jnp.int32)
    queries = low_back(low(rotary(normed(projected[..., :D], g_q), positions)))
    keys = low_back(low(rotary(normed(projected[..., D:2 * D], g_k), positions)))
    values = low_back(low(projected[..., 2 * D:]))
    attended = lax.map(attend_sequence, (queries, keys, values, lengths))
    attended = low_back(low(attended)).reshape(-1, D)
    attn_out = low_back(jnp.dot(attended, w_out, precision=HIGH))
    residual = hidden.reshape(-1, D) + attn_out
    ffn_input = low(normed(residual, g_ffn))
    mixed = experts_apply(ffn_input, routes.reshape(-1, TOP), route_codes.reshape(-1, TOP), w_router, w_gate, w_up, w_down)
    return (residual + mixed).reshape(SEQS, SEQ_LEN, D)

def reference(hidden, w_qkv, w_out, w_router, g_attn, g_ffn, g_q, g_k, w_gate, w_up, w_down, lengths, routes, route_codes, cotangent):

    def forward(p_hidden, p_qkv, p_out, p_router, p_attn, p_ffn, p_query, p_key, p_gate, p_up, p_down):
        return layer(p_hidden, p_qkv, p_out, p_router, p_attn, p_ffn, p_query, p_key, p_gate, p_up, p_down, lengths, routes, route_codes)
    result, backward = jax.vjp(forward, hidden.astype(jnp.float32), w_qkv.astype(jnp.float32), w_out.astype(jnp.float32), w_router.astype(jnp.float32), g_attn.astype(jnp.float32), g_ffn.astype(jnp.float32), g_q.astype(jnp.float32), g_k.astype(jnp.float32), w_gate.astype(jnp.float32), w_up.astype(jnp.float32), w_down.astype(jnp.float32))
    grads = backward(cotangent.astype(jnp.float32))
    return (result.astype(jnp.bfloat16), grads[0], grads[1], grads[2], grads[3], grads[4], grads[5], grads[6], grads[7], grads[8], grads[9], grads[10])
```

```python
import math

import jax
import jax.numpy as jnp
from jax import lax
from jax.sharding import PartitionSpec as P

HEADS = 16
HD = 128
FF = 1024
TOP = 8
EXP_DEV = 2

EPS = 1e-06
ROPE_BASE = 10000.0
NEGATIVE = -1e30
BF = jnp.bfloat16
F32 = jnp.float32


def ring_head(n, k):
    k %= n
    return 2 * k if k < n // 2 else 2 * n - 1 - 2 * k


def ring_links(n):
    right = [(ring_head(n, k), ring_head(n, k + 1)) for k in range(n)]
    return right, [(b, a) for a, b in right]


def ring_place():
    n = lax.axis_size("head")
    me = lax.axis_index("head")
    odd = me % 2
    return (1 - odd) * (me // 2) + odd * (n - 1 - me // 2)


def head_at(offset):
    n = lax.axis_size("head")
    k = (ring_place() + offset + n) % n
    down = k // (n // 2)
    return (1 - down) * 2 * k + down * (2 * n - 1 - 2 * k)


def gather_ring(block):
    n = lax.axis_size("head")
    right, left = ring_links(n)
    half = n // 2
    rows = block.shape[0] // 2
    out = jnp.zeros((n,) + block.shape, block.dtype)

    def put(out, piece, offset):
        return lax.dynamic_update_slice_in_dim(out, piece[None], head_at(offset), 0)

    out = put(out, block, 0)
    r = l = block
    for step in range(1, half):
        r = lax.ppermute(r, "head", right)
        l = lax.ppermute(l, "head", left)
        out = put(out, r, -step)
        out = put(out, l, step)
    a = lax.ppermute(r[:rows], "head", right)
    b = lax.ppermute(l[rows:], "head", left)
    return put(out, jnp.concatenate([a, b], 0), half)


def scatter_ring(parts):
    n = lax.axis_size("head")
    right, left = ring_links(n)
    half = n // 2
    rows = parts.shape[1] // 2

    def piece(offset):
        return lax.dynamic_index_in_dim(parts, head_at(offset), 0, keepdims=False)

    far = piece(half)
    r = lax.ppermute(far[:rows], "head", right)
    l = lax.ppermute(far[rows:], "head", left)
    for step in range(half - 1, 0, -1):
        br = piece(step).astype(F32)
        bl = piece(-step).astype(F32)
        if step == half - 1:
            br = jnp.concatenate([br[:rows] + r.astype(F32), br[rows:]], 0)
            bl = jnp.concatenate([bl[:rows], bl[rows:] + l.astype(F32)], 0)
        else:
            br = br + r.astype(F32)
            bl = bl + l.astype(F32)
        r = lax.ppermute(br.astype(BF), "head", right)
        l = lax.ppermute(bl.astype(BF), "head", left)
    return piece(0).astype(F32) + r.astype(F32) + l.astype(F32)


def rotate(values, cosine, sine):
    half = HD // 2
    shaped = values.reshape(values.shape[0], -1, HD)
    first = shaped[..., :half]
    second = shaped[..., half:]
    turned = jnp.concatenate(
        [first * cosine - second * sine, second * cosine + first * sine], axis=-1
    )
    return turned.reshape(values.shape)


def dot(a, b, dims=((1,), (0,))):
    return lax.dot_general(a, b, (dims, ((), ())), preferred_element_type=F32)


NT = ((1,), (1,))
TN = ((0,), (0,))


def body(
    hidden,
    w_qkv,
    w_out,
    w_router,
    g_attn,
    g_ffn,
    g_q,
    g_k,
    w_gate,
    w_up,
    w_down,
    lengths,
    routes,
    route_codes,
    cotangent,
):
    n = lax.axis_size("head")
    m = lax.axis_size("fsdp")
    me = lax.axis_index("head")
    rows = hidden.shape[1]
    width = hidden.shape[2]
    seq = rows * n
    lh = HEADS // n
    dh = lh * HD
    experts = EXP_DEV * n
    shard = w_qkv.shape[0]
    scale = 1.0 / math.sqrt(HD)
    both = ("head", "fsdp")

    small = jnp.concatenate(
        [w_router, g_attn[:, None], g_ffn[:, None], g_q[:, None], g_k[:, None]], axis=1
    )
    small = lax.all_gather(small, both, axis=0, tiled=True)
    router = small[:, :experts]
    gain_attn = small[:, experts].astype(F32)
    gain_ffn = small[:, experts + 1].astype(F32)
    gains_q = lax.dynamic_slice_in_dim(small[:, experts + 2], me * dh, dh, 0).astype(F32)
    gains_k = lax.dynamic_slice_in_dim(small[:, experts + 3], me * dh, dh, 0).astype(F32)

    cols = w_qkv.reshape(shard, 3, n, dh).transpose(2, 0, 1, 3).reshape(n, shard, 3 * dh)
    cols = lax.all_to_all(cols, "head", split_axis=0, concat_axis=0, tiled=True)
    qkv = lax.all_gather(cols, "fsdp", axis=1, tiled=True).reshape(width, 3 * dh)

    tokens_all = gather_ring(hidden[0]).reshape(seq, width)
    info = gather_ring(jnp.concatenate([routes[0], route_codes[0]], axis=1)).reshape(seq, 2 * TOP)
    full_out = lax.all_gather(w_out, both, axis=0, tiled=True)
    full_gate = lax.all_gather(w_gate, "fsdp", axis=1, tiled=True)
    full_up = lax.all_gather(w_up, "fsdp", axis=1, tiled=True)
    full_down = lax.all_gather(w_down, "fsdp", axis=1, tiled=True)

    def own(values):
        return lax.dynamic_slice_in_dim(values, me * rows, rows, 0)

    def inverse_rms(values):
        return lax.rsqrt(jnp.mean(values * values, axis=-1, keepdims=True) + EPS)

    wide = tokens_all.astype(F32)
    attn_input = (wide * inverse_rms(wide) * gain_attn).astype(BF)
    projected = dot(attn_input, qkv)
    proj_q = projected[:, :dh]
    proj_k = projected[:, dh : 2 * dh]
    squares = jnp.stack([jnp.sum(proj_q * proj_q, axis=1), jnp.sum(proj_k * proj_k, axis=1)])
    squares = lax.psum(squares, "head") / width
    inv_q = lax.rsqrt(squares[0] + EPS)[:, None]
    inv_k = lax.rsqrt(squares[1] + EPS)[:, None]

    frequency = ROPE_BASE ** (-2.0 * jnp.arange(HD // 2, dtype=F32) / HD)
    angles = jnp.arange(seq, dtype=F32)[:, None] * frequency[None, :]
    cosine = jnp.cos(angles)[:, None, :]
    sine = jnp.sin(angles)[:, None, :]
    queries = rotate(proj_q * inv_q * gains_q, cosine, sine).astype(BF)
    keys = rotate(proj_k * inv_k * gains_k, cosine, sine).astype(BF)
    values = projected[:, 2 * dh :].astype(BF)
    valid = jnp.arange(seq, dtype=jnp.int32) < lengths[0]

    def probs_of(q, k):
        scores = jnp.where(valid[None, :], dot(q, k, NT) * scale, NEGATIVE)
        exponent = jnp.exp(scores - jnp.max(scores, axis=-1, keepdims=True))
        return exponent / jnp.sum(exponent, axis=-1, keepdims=True)

    attended = []
    for head in range(lh):
        part = slice(head * HD, (head + 1) * HD)
        probabilities = probs_of(queries[:, part], keys[:, part]).astype(BF)
        attended.append(dot(probabilities, values[:, part]).astype(BF))
    attended = jnp.concatenate(attended, axis=1)

    attended_all = gather_ring(attended).transpose(1, 0, 2).reshape(seq, width)
    residual = wide + dot(attended_all, full_out)
    inv_ffn = inverse_rms(residual)
    ffn_input = (residual * inv_ffn * gain_ffn).astype(BF)

    logits = dot(ffn_input, router)
    matches = info[:, :TOP, None] == jnp.arange(experts, dtype=jnp.int32)[None, None, :]
    chosen = (
        jnp.sum(jnp.where(matches, logits[:, None, :], 0.0), axis=-1)
        + info[:, TOP:].astype(F32) / 1024.0
    )
    chosen = jnp.exp(chosen - jnp.max(chosen, axis=1, keepdims=True))
    gates = chosen / jnp.sum(chosen, axis=1, keepdims=True)
    spread = jnp.sum(jnp.where(matches, gates[:, :, None], 0.0), axis=1)
    mine = lax.dynamic_slice_in_dim(spread, me * EXP_DEV, EXP_DEV, 1)

    cot_all = gather_ring(cotangent[0]).reshape(seq, width)
    mixed = jnp.zeros((seq, width), F32)
    grad_in = jnp.zeros((seq, width), F32)
    gate_dots, gate_grads, up_grads, down_grads = [], [], [], []
    for e in range(EXP_DEV):
        gate = mine[:, e : e + 1]
        gate_pre = dot(ffn_input, full_gate[e])
        up_pre = dot(ffn_input, full_up[e])
        sig = jax.nn.sigmoid(gate_pre)
        silu = gate_pre * sig
        act = (silu * up_pre).astype(BF)
        produced = dot(act, full_down[e]).astype(BF).astype(F32)
        mixed = mixed + gate * produced
        cot_f = cot_all.astype(F32)
        gate_dots.append(jnp.sum(produced * cot_f, axis=1))
        grad_out = (gate * cot_f).astype(BF)
        grad_act = dot(grad_out, full_down[e], NT)
        grad_gate_pre = (grad_act * up_pre * sig * (1.0 + gate_pre * (1.0 - sig))).astype(BF)
        grad_up_pre = (grad_act * silu).astype(BF)
        down_grads.append(dot(act, grad_out, TN).astype(BF))
        gate_grads.append(dot(ffn_input, grad_gate_pre, TN).astype(BF))
        up_grads.append(dot(ffn_input, grad_up_pre, TN).astype(BF))
        grad_in = grad_in + dot(grad_gate_pre, full_gate[e], NT) + dot(grad_up_pre, full_up[e], NT)

    grad_ffn = scatter_ring(grad_in.astype(BF).reshape(n, rows, width))
    summed = scatter_ring(mixed.astype(BF).reshape(n, rows, width))

    def over_fsdp(grads):
        return lax.psum_scatter(
            jnp.stack(grads), "fsdp", scatter_dimension=1, tiled=True
        ).astype(F32)

    grad_w_gate = over_fsdp(gate_grads)
    grad_w_up = over_fsdp(up_grads)
    grad_w_down = over_fsdp(down_grads)

    dots = jnp.stack(gate_dots).reshape(EXP_DEV, n, rows).transpose(1, 0, 2)
    dots = lax.all_to_all(dots, "head", split_axis=0, concat_axis=0, tiled=True)
    dots = dots.reshape(experts, rows).T
    own_spread = own(spread)
    own_residual = own(residual)
    out_rows = own_residual + summed
    grad_rows = cotangent[0].astype(F32)
    grad_logits = own_spread * (dots - jnp.sum(own_spread * dots, axis=1, keepdims=True))
    high = lax.Precision.HIGHEST
    grad_ffn = grad_ffn + jnp.dot(grad_logits, router.astype(F32).T, precision=high)
    grad_router = jnp.dot(own(ffn_input).astype(F32).T, grad_logits, precision=high)

    def norm_back(values, gain, grad):
        inv = inverse_rms(values)
        unit = values * inv
        scaled = grad * gain
        back = inv * (scaled - unit * jnp.mean(scaled * unit, axis=-1, keepdims=True))
        return back, jnp.sum(grad * unit, axis=0)

    back, grad_gain_ffn = norm_back(own_residual, gain_ffn, grad_ffn)
    grad_residual = grad_rows + back
    grad_attn_out = grad_residual.astype(BF)
    grad_attended = dot(grad_attn_out, full_out, NT).astype(BF)
    grad_heads = lax.all_to_all(
        grad_attended.reshape(rows, n, dh), "head", split_axis=1, concat_axis=0, tiled=True
    ).reshape(seq, dh)

    grad_q, grad_k, grad_v = [], [], []
    for head in range(lh):
        part = slice(head * HD, (head + 1) * HD)
        probabilities = probs_of(queries[:, part], keys[:, part])
        grad_probs = dot(grad_heads[:, part], values[:, part], NT)
        inner = jnp.sum(probabilities * grad_probs, axis=-1, keepdims=True)
        grad_scores = (probabilities * (grad_probs - inner)).astype(BF)
        grad_q.append((dot(grad_scores, keys[:, part]) * scale).astype(BF))
        grad_k.append((dot(grad_scores, queries[:, part], TN) * scale).astype(BF))
        grad_v.append(dot(probabilities.astype(BF), grad_heads[:, part], TN).astype(BF))
    turned_q = rotate(jnp.concatenate(grad_q, axis=1).astype(F32), cosine, -sine)
    turned_k = rotate(jnp.concatenate(grad_k, axis=1).astype(F32), cosine, -sine)
    unit_q = proj_q * inv_q
    unit_k = proj_k * inv_k
    means = jnp.stack(
        [jnp.sum(turned_q * gains_q * unit_q, axis=1), jnp.sum(turned_k * gains_k * unit_k, axis=1)]
    )
    means = lax.psum(means, "head") / width
    grad_projected = jnp.concatenate(
        [
            (inv_q * (turned_q * gains_q - unit_q * means[0][:, None])).astype(BF),
            (inv_k * (turned_k * gains_k - unit_k * means[1][:, None])).astype(BF),
            jnp.concatenate(grad_v, axis=1),
        ],
        axis=1,
    )
    grad_gain_q = jnp.sum(turned_q * unit_q, axis=0)
    grad_gain_k = jnp.sum(turned_k * unit_k, axis=0)

    grad_attn_in = dot(grad_projected, qkv, NT).astype(BF)
    grad_attn_in = scatter_ring(grad_attn_in.reshape(n, rows, width))
    grad_qkv = dot(attn_input, grad_projected, TN).astype(BF).reshape(n, m * shard, 3 * dh)
    grad_qkv = lax.psum_scatter(grad_qkv, "fsdp", scatter_dimension=1, tiled=True)
    grad_qkv = lax.all_to_all(grad_qkv, "head", split_axis=0, concat_axis=0, tiled=True)
    grad_qkv = grad_qkv.reshape(n, shard, 3, dh).transpose(1, 2, 0, 3).reshape(shard, 3 * width)

    grad_all = gather_ring(grad_attn_out).reshape(seq, width)
    grad_out_w = dot(attended, grad_all, TN)
    grad_out_w = lax.psum_scatter(grad_out_w, "fsdp", scatter_dimension=0, tiled=True)

    back, grad_gain_attn = norm_back(hidden[0].astype(F32), gain_attn, grad_attn_in)
    grad_hidden = grad_residual + back

    def at_mine(piece):
        return lax.dynamic_update_slice_in_dim(jnp.zeros((width,), F32), piece, me * dh, 0)[:, None]

    pack = jnp.concatenate(
        [
            grad_router,
            grad_gain_attn[:, None],
            grad_gain_ffn[:, None],
            at_mine(grad_gain_q),
            at_mine(grad_gain_k),
        ],
        axis=1,
    ).reshape(n * m, shard * (experts + 4))
    pack = lax.all_to_all(pack, both, split_axis=0, concat_axis=0, tiled=True)
    pack = jnp.sum(pack, axis=0).reshape(shard, experts + 4)
    return (
        out_rows.astype(BF)[None],
        grad_hidden[None],
        grad_qkv.astype(F32),
        grad_out_w,
        pack[:, :experts],
        pack[:, experts],
        pack[:, experts + 1],
        pack[:, experts + 2],
        pack[:, experts + 3],
        grad_w_gate,
        grad_w_up,
        grad_w_down,
    )


def solution(mesh):
    both = ("head", "fsdp")
    return jax.shard_map(
        body,
        mesh=mesh,
        in_specs=(
            P("fsdp", "head", None),
            P(both, None),
            P(both, None),
            P(both, None),
            P(both),
            P(both),
            P(both),
            P(both),
            P("head", "fsdp", None),
            P("head", "fsdp", None),
            P("head", "fsdp", None),
            P("fsdp"),
            P("fsdp", "head", None),
            P("fsdp", "head", None),
            P("fsdp", "head", None),
        ),
        out_specs=(
            P("fsdp", "head", None),
            P("fsdp", "head", None),
            P(both, None),
            P(both, None),
            P(both, None),
            P(both),
            P(both),
            P(both),
            P(both),
            P("head", "fsdp", None),
            P("head", "fsdp", None),
            P("head", "fsdp", None),
        ),
        check_vma=False,
    )
```

```python
import functools
import math

import jax
import jax.numpy as jnp
from jax import lax
from jax.experimental import pallas as pl
from jax.experimental.pallas import tpu as pltpu
from jax.sharding import PartitionSpec as P

HEADS = 16
HD = 128
FF = 1024
TOP = 8
EXP_DEV = 2

EPS = 1e-06
ROPE_BASE = 10000.0
NEGATIVE = -1e30
BF = jnp.bfloat16
F32 = jnp.float32
NN = ((1,), (0,))
NT = ((1,), (1,))
TN = ((0,), (0,))
ANY = pl.BlockSpec(memory_space=pl.ANY)
WHOLE = pl.BlockSpec(memory_space=pltpu.VMEM)
DMA = pltpu.SemaphoreType.DMA


def dot(a, b, dims=NN):
    return lax.dot_general(a, b, (dims, ((), ())), preferred_element_type=F32)


def cost(us):
    return pl.CostEstimate(flops=0, bytes_accessed=int(us * 3.6e6), transcendentals=0)


def ring_place():
    n = lax.axis_size("head")
    me = lax.axis_index("head")
    odd = me % 2
    return (1 - odd) * (me // 2) + odd * (n - 1 - me // 2)


def head_at(offset):
    n = lax.axis_size("head")
    k = (ring_place() + (offset + n)) % n
    down = k // (n // 2)
    return (1 - down) * 2 * k + down * (2 * n - 1 - 2 * k)


def remote(src, dst, send, recv, device):
    return pltpu.make_async_remote_copy(
        src_ref=src,
        dst_ref=dst,
        send_sem=send,
        recv_sem=recv,
        device_id=device,
        device_id_type=pl.DeviceIdType.MESH,
    )


def greet(devices):
    barrier = pltpu.get_barrier_semaphore()
    for device in devices:
        pl.semaphore_signal(
            barrier, inc=1, device_id=device, device_id_type=pl.DeviceIdType.MESH
        )
    pl.semaphore_wait(barrier, len(devices))


def other_heads():
    n = lax.axis_size("head")
    me = lax.axis_index("head")
    return [{"head": (me + d) % n} for d in range(1, n)]


def other_parts():
    m = lax.axis_size("fsdp")
    f = lax.axis_index("fsdp")
    return [{"fsdp": (f + d) % m} for d in range(1, m)]


class Ring:
    def __init__(self, own, place, send, recv, n):
        self.own, self.place, self.send, self.recv = own, place, send, recv
        self.half = n // 2

    def exists(self, way, step, c):
        return step < self.half or c == way

    def message(self, way, step, c):
        owner = head_at((1 - step) if way == 0 else (step - 1))
        return remote(
            self.own(c) if step == 1 else self.place(owner, c),
            self.place(owner, c),
            self.send.at[way, step - 1, c],
            self.recv.at[way, step - 1, c],
            {"head": head_at(1 if way == 0 else -1)},
        )

    def start(self):
        for c in range(2):
            for way in range(2):
                if self.exists(way, 1, c):
                    self.message(way, 1, c).start()

    def step(self, step):
        for c in range(2):
            for way in range(2):
                if self.exists(way, step, c):
                    self.message(way, step, c).wait_recv()
                    if step < self.half and self.exists(way, step + 1, c):
                        self.message(way, step + 1, c).start()

    def finish(self):
        for step in range(1, self.half + 1):
            for c in range(2):
                for way in range(2):
                    if self.exists(way, step, c):
                        self.message(way, step, c).wait_send()


def ring_sems(n):
    return [DMA((2, n // 2, 2)), DMA((2, n // 2, 2))]


class Carry:
    def __init__(self, pairs, across, refs):
        count = len(pairs) + len(across)
        self.pairs, self.across = len(pairs), len(across)
        self.ins, self.outs = refs[:count], refs[count : 2 * count]

    def begin(self, send, recv):
        m = lax.axis_size("fsdp")
        f = lax.axis_index("fsdp")
        nx = m // 2
        x, core = f // 2, f % 2
        self.copies = []
        for j in range(self.pairs + self.across):
            if j < self.pairs:
                self.copies.append(
                    remote(
                        self.ins[j], self.outs[j], send.at[j, 0], recv.at[j, 0],
                        {"fsdp": x * 2 + 1 - core},
                    )
                )
                continue
            for i in range(1, nx):
                self.copies.append(
                    remote(
                        self.ins[j].at[i - 1], self.outs[j].at[i - 1],
                        send.at[j, i - 1], recv.at[j, i - 1],
                        {"fsdp": ((x + i) % nx) * 2 + core},
                    )
                )
        for c in self.copies:
            c.start()

    def end(self):
        for c in self.copies:
            c.wait()


def carry_sems(arrays, m):
    shape = (max(len(arrays), 1), max(m // 2 - 1, 1))
    return [DMA(shape), DMA(shape)]


def shapes_of(arrays):
    return [jax.ShapeDtypeStruct(a.shape, a.dtype) for a in arrays]


def entry_kernel(n, m, x_ref, w_ref, wo_ref, gain_ref, hid_ref, qkv_ref, wpair_ref, gall_ref,
                 send, recv, copies, w_send, w_recv, f_send, f_recv,
                 g_send, g_recv, a_send, a_recv, o_send, o_recv):
    me = lax.axis_index("head")
    f = lax.axis_index("fsdp")
    rows = x_ref.shape[0] // 2
    dh = qkv_ref.shape[3] // 3
    width = w_ref.shape[1] // 3
    nx = m // 2
    greet(other_heads() + other_parts())

    ring = Ring(
        lambda c: x_ref.at[pl.ds(c * rows, rows)],
        lambda h, c: hid_ref.at[h, pl.ds(c * rows, rows)],
        send, recv, n,
    )
    ring.start()

    x, core = f // 2, f % 2

    def part(i, side):
        return ((x + i) % nx) * 2 + side

    outs = [
        remote(
            wo_ref, wpair_ref.at[x], o_send.at[i - 1], o_recv.at[i - 1],
            {"fsdp": part(nx - i, core)},
        )
        for i in range(1, nx)
    ]
    for c in outs:
        c.start()
    locals_ = [
        pltpu.make_async_copy(wo_ref, wpair_ref.at[x], copies.at[5]),
        pltpu.make_async_copy(gain_ref, gall_ref.at[me, f], copies.at[0]),
        pltpu.make_async_copy(x_ref, hid_ref.at[me], copies.at[1]),
    ] + [
        pltpu.make_async_copy(
            w_ref.at[:, pl.ds(pl.multiple_of(j * width + me * dh, 128), dh)],
            qkv_ref.at[me, f, :, pl.ds(j * dh, dh)],
            copies.at[2 + j],
        )
        for j in range(3)
    ]
    for c in locals_:
        c.start()
    to_parts = [
        remote(gain_ref, gall_ref.at[me, f], g_send.at[d], g_recv.at[d], dev)
        for d, dev in enumerate(other_parts())
    ]
    for c in to_parts:
        c.start()
    columns = []
    for d, dev in enumerate(other_heads()):
        for j in range(3):
            columns.append(
                remote(
                    w_ref.at[:, pl.ds(pl.multiple_of(j * width + dev["head"] * dh, 128), dh)],
                    qkv_ref.at[me, f, :, pl.ds(j * dh, dh)],
                    w_send.at[d, j],
                    w_recv.at[d, j],
                    dev,
                )
            )
    for c in columns:
        c.start()
    for c in locals_:
        c.wait()
    for c in to_parts:
        c.wait_recv()
    gains = [
        remote(gall_ref.at[me], gall_ref.at[me], a_send.at[d], a_recv.at[d], dev)
        for d, dev in enumerate(other_heads())
    ]
    for c in gains:
        c.start()
    ring.step(1)
    for c in columns:
        c.wait_recv()
    across = [
        remote(
            qkv_ref.at[:, f], qkv_ref.at[:, f], f_send.at[i], f_recv.at[i],
            {"fsdp": part(nx - i, core)},
        )
        for i in range(1, nx)
    ]
    for c in across:
        c.start()
    ring.step(2)

    def beside(i):
        return remote(
            qkv_ref.at[:, part(i, core)], qkv_ref.at[:, part(i, core)],
            f_send.at[nx + i], f_recv.at[nx + i], {"fsdp": part(0, 1 - core)},
        )

    beside(0).start()
    for step in range(3, n // 2 + 1):
        ring.step(step)
    for i, c in enumerate(across):
        c.wait_recv()
        beside(i + 1).start()
    for i in range(nx):
        beside(i).wait_recv()
    for c in gains + outs:
        c.wait_recv()
    ring.finish()
    for c in outs + to_parts + columns + gains + across:
        c.wait_send()
    for i in range(nx):
        beside(i).wait_send()


def entry(x, w, w_out, gains, n, m):
    rows, width = x.shape
    shard = w.shape[0]
    dh = w.shape[1] // 3 // n
    return pl.pallas_call(
        functools.partial(entry_kernel, n, m),
        out_shape=[
            jax.ShapeDtypeStruct((n, rows, width), BF),
            jax.ShapeDtypeStruct((n, m, shard, 3 * dh), BF),
            jax.ShapeDtypeStruct((m // 2,) + w_out.shape, BF),
            jax.ShapeDtypeStruct((n, m) + gains.shape, F32),
        ],
        in_specs=[ANY] * 4,
        out_specs=[ANY] * 4,
        scratch_shapes=ring_sems(n)
        + [DMA((6,)), DMA((n - 1, 3)), DMA((n - 1, 3)), DMA((m,)), DMA((m,)), DMA((m - 1,)), DMA((m - 1,)), DMA((n - 1,)), DMA((n - 1,)), DMA((m // 2,)), DMA((m // 2,))],
        compiler_params=pltpu.CompilerParams(collective_id=0, has_side_effects=True),
        cost_estimate=cost(50),
    )(x, w, w_out, gains)


def gather_kernel(n, pairs, across, more, x_ref, extra, *refs):
    count = len(pairs) + len(across)
    second, refs = refs[: len(more)], refs[len(more) :]
    carry = Carry(pairs, across, refs[:count] + refs[count + 2 : 2 * count + 2])
    out_ref, extra_out = refs[count : count + 2]
    refs = refs[2 * count + 2 :]
    seconds, refs = refs[: len(more)], refs[len(more) :]
    send, recv, copies, e_send, e_recv, c_send, c_recv = refs[:7]
    rows = x_ref.shape[0] // 2
    me = lax.axis_index("head")
    greet(other_heads() + (other_parts() if count else []))
    ring = Ring(
        lambda c: x_ref.at[pl.ds(c * rows, rows)],
        lambda h, c: out_ref.at[h, pl.ds(c * rows, rows)],
        send, recv, n,
    )
    ring.start()
    carry.begin(c_send, c_recv)
    moves = [
        pltpu.make_async_copy(x_ref, out_ref.at[me], copies.at[0]),
        pltpu.make_async_copy(extra.at[me], extra_out.at[me], copies.at[1]),
    ] + [
        remote(extra.at[dev["head"]], extra_out.at[me], e_send.at[d], e_recv.at[d], dev)
        for d, dev in enumerate(other_heads())
    ]
    for c in moves:
        c.start()
    for step in range(1, n // 2):
        ring.step(step)
    others = [
        Ring(
            lambda c, a=a: a.at[pl.ds(c * rows, rows)],
            lambda h, c, b=b: b.at[h, pl.ds(c * rows, rows)],
            refs[7 + 3 * i], refs[8 + 3 * i], n,
        )
        for i, (a, b) in enumerate(zip(second, seconds))
    ]
    for i, other in enumerate(others):
        other.start()
        moves.append(pltpu.make_async_copy(second[i], seconds[i].at[me], refs[9 + 3 * i].at[0]))
        moves[-1].start()
    ring.step(n // 2)
    for other in others:
        for step in range(1, n // 2 + 1):
            other.step(step)
    for c in moves:
        c.wait()
    for r in [ring] + others:
        r.finish()
    carry.end()


def gather(x, extra, n, m, identity, across=(), more=()):
    return pl.pallas_call(
        functools.partial(gather_kernel, n, (), across, more),
        out_shape=[
            jax.ShapeDtypeStruct((n,) + x.shape, x.dtype),
            jax.ShapeDtypeStruct(extra.shape, extra.dtype),
        ]
        + shapes_of(across)
        + [jax.ShapeDtypeStruct((n,) + a.shape, a.dtype) for a in more],
        in_specs=[ANY] * (2 + len(across) + len(more)),
        out_specs=[ANY] * (2 + len(across) + len(more)),
        scratch_shapes=ring_sems(n)
        + [DMA((2,)), DMA((n - 1,)), DMA((n - 1,))]
        + carry_sems(across, m)
        + (ring_sems(n) + [DMA((1,))]) * len(more),
        compiler_params=pltpu.CompilerParams(collective_id=identity, has_side_effects=True),
        cost_estimate=cost(42),
    )(x, extra, *more, *across)


def ring_sum_kernel(n, k, pairs, across, *refs):
    count = len(pairs) + len(across)
    parts, extra, refs = refs[:k], refs[k], refs[k + 1 :]
    carry = Carry(pairs, across, refs[:count] + refs[count + 2 : 2 * count + 2])
    out_ref, extra_out = refs[count : count + 2]
    own, sbuf, rbuf, loads, send, recv, copy, e_send, e_recv, c_send, c_recv = refs[2 * count + 2 :]
    half = n // 2
    me = lax.axis_index("head")
    rows = out_ref.shape[0] // 2
    order = [half] + [s * w for s in range(half - 1, 0, -1) for w in (1, -1)] + [0]
    slot = {o: i for i, o in enumerate(order)}
    fetch = {
        (o, i): pltpu.make_async_copy(
            parts[i].at[head_at(o)], own.at[slot[o], i], loads.at[slot[o], i]
        )
        for o in order
        for i in range(k)
    }
    for o in order:
        for i in range(k):
            fetch[o, i].start()
    greet(other_heads() + (other_parts() if count else []))
    carry.begin(c_send, c_recv)
    mine = pltpu.make_async_copy(extra.at[me], extra_out.at[me], copy.at[0])
    mine.start()
    direct = [
        remote(extra.at[dev["head"]], extra_out.at[me], e_send.at[d], e_recv.at[d], dev)
        for d, dev in enumerate(other_heads())
    ]
    for c in direct:
        c.start()
    ready = set()

    def piece(o, c):
        if o not in ready:
            for i in range(k):
                fetch[o, i].wait()
            ready.add(o)
        total = own[slot[o], 0, pl.ds(c * rows, rows)].astype(F32)
        for i in range(1, k):
            total = total + own[slot[o], i, pl.ds(c * rows, rows)].astype(F32)
        return total

    def message(way, t, c):
        return remote(
            sbuf.at[way, t - 1, c], rbuf.at[way, t - 1, c],
            send.at[way, t - 1, c], recv.at[way, t - 1, c],
            {"head": head_at(1 if way == 0 else -1)},
        )

    def offset(way, o):
        return o if way == 0 or o == half else -o

    started = []

    def ship(way, t, c, value):
        sbuf[way, t - 1, c] = value.astype(BF)
        message(way, t, c).start()
        started.append((way, t, c))

    for way in range(2):
        ship(way, 1, way, piece(half, way))
    for way in range(2):
        ship(way, 2, 1 - way, piece(offset(way, half - 1), 1 - way))
    for t in range(1, half):
        for c in range(2):
            for way in range(2):
                if t == 1 and c != way:
                    continue
                message(way, t, c).wait_recv()
                ship(
                    way, t + 1, c,
                    piece(offset(way, half - t), c) + rbuf[way, t - 1, c].astype(F32),
                )
    for c in range(2):
        for way in range(2):
            message(way, half, c).wait_recv()
        out_ref[pl.ds(c * rows, rows)] = (
            piece(0, c) + rbuf[0, half - 1, c].astype(F32) + rbuf[1, half - 1, c].astype(F32)
        )
    for way, t, c in started:
        message(way, t, c).wait_send()
    mine.wait()
    for c in direct:
        c.wait()
    carry.end()


def ring_sum(parts, extra, n, m, identity, pairs=(), across=()):
    k = len(parts)
    rows, width = parts[0].shape[1:]
    half = n // 2
    return pl.pallas_call(
        functools.partial(ring_sum_kernel, n, k, pairs, across),
        out_shape=[
            jax.ShapeDtypeStruct((rows, width), F32),
            jax.ShapeDtypeStruct(extra.shape, F32),
        ]
        + shapes_of(pairs + across),
        in_specs=[ANY] * (k + 1 + len(pairs + across)),
        out_specs=[WHOLE, ANY] + [ANY] * len(pairs + across),
        scratch_shapes=[
            pltpu.VMEM((n, k, rows, width), BF),
            pltpu.VMEM((2, half, 2, rows // 2, width), BF),
            pltpu.VMEM((2, half, 2, rows // 2, width), BF),
            DMA((n, k)),
        ]
        + ring_sems(n)
        + [DMA((1,)), DMA((n - 1,)), DMA((n - 1,))]
        + carry_sems(pairs + across, m),
        compiler_params=pltpu.CompilerParams(
            collective_id=identity, has_side_effects=True, vmem_limit_bytes=50 << 20
        ),
        cost_estimate=cost(45),
    )(*parts, extra, *pairs, *across)


def exchange_kernel(n, modes, *refs):
    count = len(modes)
    ins, outs = refs[:count], refs[count : 2 * count]
    send, recv, copies = refs[2 * count :]
    me = lax.axis_index("head")

    def entry_of(ref, i, columns):
        if not columns:
            return ref.at[i]
        wide = ref.shape[1] // n
        return ref.at[:, pl.ds(pl.multiple_of(i * wide, 128), wide)]

    greet(other_heads())
    moves, mine = [], []
    for i, mode in enumerate(modes):
        to = entry_of(outs[i], me, mode == "to_columns")
        for d, dev in enumerate(other_heads()):
            source = entry_of(ins[i], dev["head"], mode == "from_columns")
            moves.append(remote(source, to, send.at[i, d], recv.at[i, d], dev))
        source = entry_of(ins[i], me, mode == "from_columns")
        mine.append(pltpu.make_async_copy(source, to, copies.at[i]))
    for c in moves + mine:
        c.start()
    for c in moves + mine:
        c.wait()


def exchange(arrays, modes, n, identity):
    count = len(arrays)

    def shape(a, mode):
        if mode == "to_columns":
            return (a.shape[1], n * a.shape[2])
        if mode == "from_columns":
            return (n, a.shape[0], a.shape[1] // n)
        return a.shape

    return pl.pallas_call(
        functools.partial(exchange_kernel, n, modes),
        out_shape=[
            jax.ShapeDtypeStruct(shape(a, mode), a.dtype) for a, mode in zip(arrays, modes)
        ],
        in_specs=[ANY] * count,
        out_specs=[ANY] * count,
        scratch_shapes=[DMA((count, n - 1)), DMA((count, n - 1)), DMA((count,))],
        compiler_params=pltpu.CompilerParams(collective_id=identity, has_side_effects=True),
        cost_estimate=cost(15),
    )(*arrays)


def total_kernel(n, x_ref, out_ref, buf, send, recv):
    me = lax.axis_index("head")
    greet(other_heads())
    moves = [
        remote(x_ref, buf.at[me], send.at[d], recv.at[d], dev)
        for d, dev in enumerate(other_heads())
    ]
    for c in moves:
        c.start()
    buf[me] = x_ref[...]
    for c in moves:
        c.wait()
    total = buf[0]
    for i in range(1, n):
        total = total + buf[i]
    out_ref[...] = total


def total(x, n, identity):
    return pl.pallas_call(
        functools.partial(total_kernel, n),
        out_shape=jax.ShapeDtypeStruct(x.shape, F32),
        in_specs=[WHOLE],
        out_specs=WHOLE,
        scratch_shapes=[pltpu.VMEM((n,) + x.shape, F32), DMA((n - 1,)), DMA((n - 1,))],
        compiler_params=pltpu.CompilerParams(collective_id=identity, has_side_effects=True),
        cost_estimate=cost(6),
    )(x)


def probs_of(len_ref, q, k):
    scores = dot(q, k, NT) * (1.0 / math.sqrt(HD))
    at = lax.broadcasted_iota(jnp.int32, scores.shape, 1)
    scores = jnp.where(at < len_ref[0], scores, NEGATIVE)
    exponent = jnp.exp(scores - jnp.max(scores, axis=-1, keepdims=True))
    return exponent / jnp.sum(exponent, axis=-1, keepdims=True)


QB = 256
HIGH = lax.Precision.HIGHEST


def spread_rows(sums, i):
    pick = lax.broadcasted_iota(jnp.int32, sums.shape, 0) == i
    return lax.dot_general(
        sums, pick.astype(F32), (TN, ((), ())), precision=HIGH, preferred_element_type=F32
    )


def row_sums(values):
    ones = jnp.ones((8, values.shape[1]), F32)
    return lax.dot_general(
        ones, values, (NT, ((), ())), precision=HIGH, preferred_element_type=F32
    )[:1]


def turn(values, cosine, sine):
    return values * cosine + pltpu.roll(values, HD // 2, 1) * sine


def middle_kernel(n, m, len_ref, hid_ref, qkv_ref, wpair_ref, ga_ref, gq_ref, gk_ref, cos_ref, sin_ref,
                  ain_ref, proj_ref, sums_ref, q_ref, k_ref, v_ref, att_ref, tok_ref, wout_ref,
                  hid, qkv, ain, buf, own,
                  h_sem, w_sem, a_sem, s_send, s_recv, send, recv, o_sem, c_send, c_recv,
                  t_send, t_recv, t_sem):
    me = lax.axis_index("head")
    f = lax.axis_index("fsdp")
    nx = m // 2
    x, core = f // 2, f % 2
    rows, width = hid.shape[1:]
    dh = q_ref.shape[1]
    seq = n * rows
    loads = [pltpu.make_async_copy(hid_ref.at[i], hid.at[i], h_sem.at[i]) for i in range(n)]
    load_w = pltpu.make_async_copy(qkv_ref, qkv, w_sem.at[0])
    load_w.start()
    for c in loads:
        c.start()
    greet(other_heads() + [{"fsdp": x * 2 + 1 - core}])

    halves = nx // 2
    wring = Ring(
        lambda c: wpair_ref.at[pl.ds(c * halves, halves)],
        lambda h, c: wout_ref.at[h, pl.ds(c * halves, halves), core],
        send, recv, n,
    )
    wring.start()
    mine = pltpu.make_async_copy(wpair_ref, wout_ref.at[me, :, core], o_sem.at[0])
    mine.start()

    def beside(offset, slot):
        ref = wout_ref.at[head_at(offset), :, core]
        return remote(ref, ref, c_send.at[slot], c_recv.at[slot], {"fsdp": x * 2 + 1 - core})

    def advance(step):
        wring.step(step)
        if step < n // 2:
            beside(step, 2 * step - 1).start()
            beside(-step, 2 * step).start()
        else:
            beside(step, n - 1).start()

    stores = []
    load_w.wait()
    for i in range(n):
        at = pl.ds(i * rows, rows)
        loads[i].wait()
        wide = hid[i].astype(F32)
        inv = lax.rsqrt(jnp.mean(wide * wide, axis=-1, keepdims=True) + EPS)
        ain[i] = (wide * inv * ga_ref[...]).astype(BF)
        stores.append(pltpu.make_async_copy(ain.at[i], ain_ref.at[i], a_sem.at[i]))
        stores[-1].start()
        projected = dot(ain[i], qkv[...])
        proj_ref[at, :] = projected[:, : 2 * dh]
        v_ref[at, :] = projected[:, 2 * dh :].astype(BF)
        proj_q = projected[:, :dh]
        proj_k = projected[:, dh : 2 * dh]
        own[pl.ds(i, 1), :] = row_sums(proj_q * proj_q)
        own[pl.ds(n + i, 1), :] = row_sums(proj_k * proj_k)
        if i == 0:
            mine.wait()
            beside(0, 0).start()
        if i == n // 2:
            advance(1)
    moves = [
        remote(own, buf.at[me], s_send.at[d], s_recv.at[d], dev)
        for d, dev in enumerate(other_heads())
    ]
    for c in moves:
        c.start()
    buf[me] = own[...]
    for c in moves:
        c.wait()
    total_of = buf[0]
    for i in range(1, n):
        total_of = total_of + buf[i]
    sums_ref[...] = total_of
    inv_all = lax.rsqrt(total_of / width + EPS)
    advance(2)
    for i in range(n):
        at = pl.ds(i * rows, rows)
        inv_q = spread_rows(inv_all[:n], i)
        inv_k = spread_rows(inv_all[n:], i)
        cosine = cos_ref[at, :]
        sine = sin_ref[at, :]
        for head in range(dh // HD):
            lanes = pl.ds(head * HD, HD)
            k_lanes = pl.ds(dh + head * HD, HD)
            q_ref[at, lanes] = turn(
                proj_ref[at, lanes] * inv_q * gq_ref[:, lanes], cosine, sine
            ).astype(BF)
            k_ref[at, lanes] = turn(
                proj_ref[at, k_lanes] * inv_k * gk_ref[:, lanes], cosine, sine
            ).astype(BF)
    sends = []
    for j in range(seq // QB):
        at = pl.ds(j * QB, QB)
        for head in range(dh // HD):
            lanes = pl.ds(head * HD, HD)
            probs = probs_of(len_ref, q_ref[at, lanes], k_ref[:, lanes])
            att_ref[at, lanes] = dot(probs.astype(BF), v_ref[:, lanes]).astype(BF)
        if j + 3 <= n // 2:
            advance(j + 3)
    to = tok_ref.at[:, pl.ds(pl.multiple_of(me * dh, 128), dh)]
    for d, dev in enumerate(other_heads()):
        source = att_ref.at[pl.ds(pl.multiple_of(dev["head"] * rows, rows), rows)]
        sends.append(remote(source, to, t_send.at[d], t_recv.at[d], dev))
    sends.append(
        pltpu.make_async_copy(
            att_ref.at[pl.ds(pl.multiple_of(me * rows, rows), rows)], to, t_sem.at[0]
        )
    )
    for c in sends:
        c.start()
    for step in range(seq // QB + 3, n // 2 + 1):
        advance(step)
    for c in sends + stores:
        c.wait()
    for slot in range(n):
        beside(0, slot).wait_recv()
    beside(0, 0).wait_send()
    for step in range(1, n // 2):
        beside(step, 2 * step - 1).wait_send()
        beside(-step, 2 * step).wait_send()
    beside(n // 2, n - 1).wait_send()
    wring.finish()


def middle(lengths, hid, qkv, wpair, gain_attn, gain_q, gain_k, cosine, sine, n, m):
    rows, width = hid.shape[1:]
    seq = n * rows
    dh = gain_q.shape[1]
    heads = jax.ShapeDtypeStruct((seq, dh), BF)
    shard = wpair.shape[1]
    return pl.pallas_call(
        functools.partial(middle_kernel, n, m),
        out_shape=[
            jax.ShapeDtypeStruct((n, rows, width), BF),
            jax.ShapeDtypeStruct((seq, 2 * dh), F32),
            jax.ShapeDtypeStruct((2 * n, rows), F32),
            heads, heads, heads, heads,
            jax.ShapeDtypeStruct((rows, width), BF),
            jax.ShapeDtypeStruct((n, m // 2, 2, shard, width), BF),
        ],
        in_specs=[pl.BlockSpec(memory_space=pltpu.SMEM)] + [ANY] * 3 + [WHOLE] * 5,
        out_specs=[ANY] + [WHOLE] * 6 + [ANY] * 2,
        scratch_shapes=[
            pltpu.VMEM((n, rows, width), BF),
            pltpu.VMEM((width, 3 * dh), BF),
            pltpu.VMEM((n, rows, width), BF),
            pltpu.VMEM((n, 2 * n, rows), F32),
            pltpu.VMEM((2 * n, rows), F32),
            DMA((n,)), DMA((1,)), DMA((n,)), DMA((n - 1,)), DMA((n - 1,)),
        ]
        + ring_sems(n)
        + [DMA((1,)), DMA((n,)), DMA((n,)), DMA((n - 1,)), DMA((n - 1,)), DMA((1,))],
        compiler_params=pltpu.CompilerParams(
            collective_id=2, has_side_effects=True, vmem_limit_bytes=56 << 20
        ),
        cost_estimate=cost(50),
    )(lengths, hid, qkv, wpair, gain_attn, gain_q, gain_k, cosine, sine)


def attend_back_kernel(len_ref, q_ref, k_ref, v_ref, g_ref, dq_ref, dk_ref, dv_ref, dk, dv):
    scale = 1.0 / math.sqrt(HD)

    @pl.when(pl.program_id(1) == 0)
    def _():
        dk[...] = jnp.zeros_like(dk)
        dv[...] = jnp.zeros_like(dv)

    probs = probs_of(len_ref, q_ref[...], k_ref[...])
    grad_probs = dot(g_ref[...], v_ref[...], NT)
    inner = jnp.sum(probs * grad_probs, axis=-1, keepdims=True)
    grad_scores = (probs * (grad_probs - inner)).astype(BF)
    dq_ref[...] = (dot(grad_scores, k_ref[...]) * scale).astype(BF)
    dk[...] += dot(grad_scores, q_ref[...], TN)
    dv[...] += dot(probs.astype(BF), g_ref[...], TN)

    @pl.when(pl.program_id(1) == pl.num_programs(1) - 1)
    def _():
        dk_ref[...] = (dk[...] * scale).astype(BF)
        dv_ref[...] = dv[...].astype(BF)


def attend_back(lengths, q, k, v, grad):
    seq, wide = q.shape
    block = pl.BlockSpec((QB, HD), lambda h, i: (i, h))
    whole = pl.BlockSpec((seq, HD), lambda h, i: (0, h))
    return pl.pallas_call(
        attend_back_kernel,
        out_shape=[jax.ShapeDtypeStruct((seq, wide), BF)] * 3,
        grid=(wide // HD, seq // QB),
        in_specs=[pl.BlockSpec(memory_space=pltpu.SMEM), block, whole, whole, block],
        out_specs=[block, whole, whole],
        scratch_shapes=[pltpu.VMEM((seq, HD), F32)] * 2,
        compiler_params=pltpu.CompilerParams(vmem_limit_bytes=50 << 20),
        cost_estimate=cost(15),
    )(lengths, q, k, v, grad)


def expert_kernel(m, *refs):
    x_ref, xt_ref, cot_ref, gate_ref = refs[:4]
    gate_w, up_w, down_w = refs[4 : 4 + m], refs[4 + m : 4 + 2 * m], refs[4 + 2 * m : 4 + 3 * m]
    dots_ref, mix_ref, gin_ref, same_ref, other_ref = refs[4 + 3 * m : 9 + 3 * m]
    (x, xt, cot, gate_v, up_v, down_v, act, gact, ggp, gup, dgate, dup, ddown, mix, gin,
     in_sem, w_sem, d_sem, dw_sem, dd_sem, o_sem) = refs[9 + 3 * m :]
    f = lax.axis_index("fsdp")
    nx = m // 2
    xi, core = f // 2, f % 2
    seq, width = x.shape
    ff = gate_v.shape[1]
    tile = ff // m
    block = width // m
    source = [
        ((xi + i) % nx) * 2 + (core + side) % 2 for side in range(2) for i in range(nx)
    ]

    def rows_of(r, size):
        return pl.ds(pl.multiple_of(source[r] * size, size), size)

    loads = {
        "x": [pltpu.make_async_copy(x_ref, x, in_sem.at[0])],
        "cot": [pltpu.make_async_copy(cot_ref, cot, in_sem.at[1])],
        "xt": [pltpu.make_async_copy(xt_ref, xt, in_sem.at[2])],
        "down": [
            pltpu.make_async_copy(down_w[r], down_v.at[rows_of(r, tile)], d_sem.at[r])
            for r in range(m)
        ],
    }
    for t in range(m):
        cols = pl.ds(t * tile, tile)
        loads[t] = [
            pltpu.make_async_copy(
                w[r].at[:, cols], v.at[rows_of(r, block), cols], w_sem.at[i, r, t]
            )
            for i, (w, v) in enumerate(((gate_w, gate_v), (up_w, up_v)))
            for r in range(m)
        ]
    for key in ["x", 0, "cot", "down", "xt"] + list(range(1, m)):
        for c in loads[key]:
            c.start()

    def arrived(*keys):
        for key in keys:
            for c in loads[key]:
                c.wait()

    rb = min(512, seq)
    stores = []
    arrived("x")
    for t in range(m):
        cols = pl.ds(t * tile, tile)
        arrived(t)
        if t == 0:
            arrived("cot", "down")

        @pl.loop(0, seq // rb)
        def _(i, cols=cols, t=t):
            at = pl.ds(pl.multiple_of(i * rb, rb), rb)
            gate_pre = dot(x[at, :], gate_v[:, cols])
            up_pre = dot(x[at, :], up_v[:, cols])
            back = dot(cot[at, :], down_v[cols, :], NT)
            gate = gate_ref[at, :]
            sig = 1.0 / (1.0 + jnp.exp(-gate_pre))
            silu = gate_pre * sig
            value = silu * up_pre
            dots = jnp.sum(value * back, axis=1, keepdims=True)
            if t == 0:
                dots_ref[at, :] = dots
            else:
                dots_ref[at, :] += dots
            grad_act = gate * back
            gact[at, cols] = (gate * value).astype(BF)
            ggp[at, cols] = (grad_act * up_pre * sig * (1.0 + gate_pre * (1.0 - sig))).astype(BF)
            gup[at, cols] = (grad_act * silu).astype(BF)

        if t == 0:
            arrived("xt")

        @pl.loop(0, m)
        def _(r, cols=cols):
            at = pl.ds(pl.multiple_of(r * block, block), block)
            dgate[at, cols] = dot(xt[at, :], ggp[:, cols]).astype(BF)
            dup[at, cols] = dot(xt[at, :], gup[:, cols]).astype(BF)

        for i, v in enumerate((dgate, dup)):
            for r in range(m):
                to = (same_ref if r < nx else other_ref).at[r % nx, i, :, cols]
                stores.append(
                    pltpu.make_async_copy(v.at[rows_of(r, block), cols], to, dw_sem.at[i, r, t])
                )
                stores[-1].start()

        @pl.loop(0, width // 512)
        def _(r, cols=cols):
            at = pl.ds(pl.multiple_of(r * 512, 512), 512)
            ddown[cols, at] = dot(gact[:, cols], cot[:, at], TN).astype(BF)

    for r in range(m):
        for side in range(2):
            to = (same_ref if r < nx else other_ref).at[r % nx, 2, pl.ds(side * tile, tile)]
            stores.append(
                pltpu.make_async_copy(
                    ddown.at[rows_of(r, tile), pl.ds(side * ff, ff)], to, dd_sem.at[r, side]
                )
            )
            stores[-1].start()

    for r in range(width // 512):
        at = pl.ds(r * 512, 512)

        @pl.loop(0, seq // rb)
        def _(i, at=at):
            here = pl.ds(pl.multiple_of(i * rb, rb), rb)
            mix[here, at] = dot(gact[here, :], down_v[:, at]).astype(BF)
            gin[here, at] = (
                dot(ggp[here, :], gate_v[at, :], NT) + dot(gup[here, :], up_v[at, :], NT)
            ).astype(BF)

        for i, (v, to) in enumerate(((mix, mix_ref), (gin, gin_ref))):
            stores.append(pltpu.make_async_copy(v.at[:, at], to.at[:, at], o_sem.at[i, r]))
            stores[-1].start()
    for c in stores:
        c.wait()


def expert(x, xt, cot, gate, gates_w, ups_w, downs_w):
    m = len(gates_w)
    nx = m // 2
    seq, width = x.shape
    block, ff = gates_w[0].shape

    def vm(*shape):
        return pltpu.VMEM(shape, BF)

    grads = jax.ShapeDtypeStruct((nx, 3, block, ff), BF)
    rows = jax.ShapeDtypeStruct((seq, width), BF)
    return pl.pallas_call(
        functools.partial(expert_kernel, m),
        out_shape=[jax.ShapeDtypeStruct((seq, 1), F32), rows, rows, grads, grads],
        in_specs=[ANY, ANY, ANY, WHOLE] + [ANY] * (3 * m),
        out_specs=[WHOLE] + [ANY] * 4,
        scratch_shapes=[
            vm(seq, width), vm(width, seq), vm(seq, width),
            vm(width, ff), vm(width, ff), vm(ff, width),
            vm(8, 128), vm(seq, ff), vm(seq, ff), vm(seq, ff),
            vm(width, ff), vm(width, ff), vm(ff, width),
            vm(seq, width), vm(seq, width),
            DMA((3,)), DMA((2, m, m)), DMA((m,)), DMA((2, m, m)), DMA((m, 2)), DMA((2, width // 512)),
        ],
        compiler_params=pltpu.CompilerParams(vmem_limit_bytes=60 << 20),
        cost_estimate=pl.CostEstimate(
            flops=18 * seq * width * ff, bytes_accessed=48 << 20, transcendentals=0
        ),
    )(x, xt, cot, gate, *gates_w, *ups_w, *downs_w)


def rotate(values, cosine, sine):
    half = HD // 2
    shaped = values.reshape(values.shape[0], -1, HD)
    other = jnp.concatenate([shaped[..., half:], shaped[..., :half]], axis=-1)
    return (shaped * cosine[:, None, :] + other * sine[:, None, :]).reshape(values.shape)


def fsdp_links(m, shift, flip):
    nx = m // 2
    return [
        (((f // 2 + shift) % nx) * 2 + (f + flip) % 2, f) for f in range(m)
    ]


def weight_pieces(w, m):
    pieces = [w] + [lax.ppermute(w, "fsdp", fsdp_links(m, i, 0)) for i in range(1, m // 2)]
    return pieces + [lax.ppermute(p, "fsdp", fsdp_links(m, 0, 1)) for p in pieces]


def joined(same, got):
    return same.astype(F32) + got.astype(F32)


def body(
    hidden,
    w_qkv,
    w_out,
    w_router,
    g_attn,
    g_ffn,
    g_q,
    g_k,
    w_gate,
    w_up,
    w_down,
    lengths,
    routes,
    route_codes,
    cotangent,
):
    n = lax.axis_size("head")
    m = lax.axis_size("fsdp")
    me = lax.axis_index("head")
    rows = hidden.shape[1]
    width = hidden.shape[2]
    seq = rows * n
    lh = HEADS // n
    dh = lh * HD
    experts = EXP_DEV * n
    shard = w_qkv.shape[0]
    both = ("head", "fsdp")

    small = jnp.concatenate(
        [w_router, g_attn[:, None], g_ffn[:, None], g_q[:, None], g_k[:, None]], axis=1
    ).astype(F32)
    spots = -(-(experts + 4) * shard // 1024) * 8
    small = jnp.pad(small.reshape(-1), (0, spots * 128 - (experts + 4) * shard)).reshape(spots, 128)

    tokens_all, qkv, wpair, small = entry(hidden[0], w_qkv, w_out, small, n, m)
    late = lax.optimization_barrier((w_gate, w_up, w_down, small))
    pieces = [[weight_pieces(w[e], m) for w in late[:3]] for e in range(EXP_DEV)]
    small = late[3]
    qkv = qkv.reshape(width, 3 * dh)
    small = small.reshape(n, m, spots * 128)[:, :, : (experts + 4) * shard]
    small = small.reshape(width, experts + 4)
    router = small[:, :experts].astype(BF)
    gain_attn = small[:, experts]
    gain_ffn = small[:, experts + 1]
    gains_q = lax.dynamic_slice_in_dim(small[:, experts + 2], me * dh, dh, 0)
    gains_k = lax.dynamic_slice_in_dim(small[:, experts + 3], me * dh, dh, 0)

    def inverse_rms(values):
        return lax.rsqrt(jnp.mean(values * values, axis=-1, keepdims=True) + EPS)

    frequency = ROPE_BASE ** (-2.0 * jnp.arange(HD // 2, dtype=F32) / HD)
    angles = jnp.arange(seq, dtype=F32)[:, None] * frequency[None, :]
    cosine = jnp.tile(jnp.cos(angles), (1, 2))
    sine = jnp.sin(angles)
    sine = jnp.concatenate([-sine, sine], axis=1)
    attn_input, proj, squares, queries, keys, values, attended, attended_tok, full_out = middle(
        lengths, tokens_all, qkv, wpair, gain_attn[None], gains_q[None], gains_k[None],
        cosine, sine, n, m,
    )
    attn_input = attn_input.reshape(seq, width)
    full_out = full_out.reshape(width, width)
    squares = squares.reshape(2, seq) / width
    inv_q = lax.rsqrt(squares[0] + EPS)[:, None]
    inv_k = lax.rsqrt(squares[1] + EPS)[:, None]
    proj_q = proj[:, :dh]
    proj_k = proj[:, dh:]
    residual = hidden[0].astype(F32) + dot(attended_tok, full_out)
    own_input = (residual * inverse_rms(residual) * gain_ffn).astype(BF)

    logits = dot(own_input, router)
    matches = routes[0][:, :, None] == jnp.arange(experts, dtype=jnp.int32)[None, None, :]
    chosen = (
        jnp.sum(jnp.where(matches, logits[:, None, :], 0.0), axis=-1)
        + route_codes[0].astype(F32) / 1024.0
    )
    chosen = jnp.exp(chosen - jnp.max(chosen, axis=1, keepdims=True))
    gates = chosen / jnp.sum(chosen, axis=1, keepdims=True)
    spread = jnp.sum(jnp.where(matches, gates[:, :, None], 0.0), axis=1)

    ffn_input, mine, cot_all = gather(
        own_input, spread.T.reshape(n, EXP_DEV, rows), n, m, 1, (), (cotangent[0],)
    )
    cot_all = cot_all.reshape(seq, width)
    ffn_input = ffn_input.reshape(seq, width)
    mine = mine.transpose(0, 2, 1).reshape(seq, EXP_DEV)
    turned = ffn_input.T
    span = min(seq, 1024)
    dots, mixes, grads_in, weight_grads = [], [], [], []
    for e in range(EXP_DEV):
        chunks = [
            expert(
                ffn_input[s : s + span], turned[:, s : s + span], cot_all[s : s + span],
                mine[s : s + span, e : e + 1], *pieces[e],
            )
            for s in range(0, seq, span)
        ]
        dot_e, mix_e, gin_e, *wg = [
            c[0] if len(c) == 1 else c for c in zip(*chunks)
        ]
        if len(chunks) > 1:
            dot_e, mix_e, gin_e = (jnp.concatenate(v, 0) for v in (dot_e, mix_e, gin_e))
            wg = [sum(v[1:], v[0]) for v in wg]
        dots.append(dot_e)
        mixes.append(mix_e)
        grads_in.append(gin_e.reshape(n, rows, width))
        weight_grads.append(wg)
    (same0, other0), (same1, other1) = weight_grads
    got0 = lax.ppermute(other0, "fsdp", fsdp_links(m, 0, 1))
    got0, *grads_in = lax.optimization_barrier((got0, *grads_in))
    away0 = [joined(same0[1:, p], got0[1:, p]).astype(BF) for p in (slice(0, 2), slice(2, 3))]
    dots = jnp.stack([d.reshape(n, rows) for d in dots], axis=1)
    grad_ffn, dots, got1, sums0 = ring_sum(
        grads_in, dots, n, m, 4, (other1,), (away0[0],)
    )
    away1 = [joined(same1[1:, p], got1[1:, p]).astype(BF) for p in (slice(0, 2), slice(2, 3))]
    summed, _ = ring_sum(
        [v.reshape(n, rows, width) for v in mixes], jnp.zeros((n, 8, 128), F32), n, m, 8
    )

    dots = dots.reshape(experts, rows).T
    grad_rows = cotangent[0].astype(F32)
    grad_logits = spread * (dots - jnp.sum(spread * dots, axis=1, keepdims=True))
    high = lax.Precision.HIGHEST
    grad_ffn = grad_ffn + jnp.dot(grad_logits, router.astype(F32).T, precision=high)
    grad_router = jnp.dot(own_input.astype(F32).T, grad_logits, precision=high)

    def norm_back(values, gain, grad):
        inv = inverse_rms(values)
        unit = values * inv
        scaled = grad * gain
        back = inv * (scaled - unit * jnp.mean(scaled * unit, axis=-1, keepdims=True))
        return back, jnp.sum(grad * unit, axis=0)

    back, grad_gain_ffn = norm_back(residual, gain_ffn, grad_ffn)
    grad_residual = grad_rows + back
    grad_attn_out = grad_residual.astype(BF)
    grad_attended = dot(grad_attn_out, full_out, NT).astype(BF)
    grad_all, grad_heads, sums0d, sums1d = gather(
        grad_attn_out, grad_attended.reshape(rows, n, dh).transpose(1, 0, 2), n, m, 5,
        (away0[1], away1[1]),
    )
    grad_heads = grad_heads.reshape(seq, dh)
    grad_q, grad_k, grad_v = attend_back(lengths, queries, keys, values, grad_heads)
    turned_q = rotate(grad_q.astype(F32), cosine, -sine)
    turned_k = rotate(grad_k.astype(F32), cosine, -sine)
    unit_q = proj_q * inv_q
    unit_k = proj_k * inv_k
    means = jnp.stack(
        [jnp.sum(turned_q * gains_q * unit_q, axis=1), jnp.sum(turned_k * gains_k * unit_k, axis=1)]
    )
    means = total(means.reshape(-1, 128), n, 3).reshape(2, seq) / width
    grad_projected = jnp.concatenate(
        [
            (inv_q * (turned_q * gains_q - unit_q * means[0][:, None])).astype(BF),
            (inv_k * (turned_k * gains_k - unit_k * means[1][:, None])).astype(BF),
            grad_v,
        ],
        axis=1,
    )
    grad_gain_q = jnp.sum(turned_q * unit_q, axis=0)
    grad_gain_k = jnp.sum(turned_k * unit_k, axis=0)

    grad_out_w = dot(attended, grad_all.reshape(seq, width), TN).astype(BF)
    grad_out_w = lax.psum_scatter(grad_out_w, "fsdp", scatter_dimension=0, tiled=True).astype(F32)
    weights = dot(attn_input, grad_projected, TN).astype(BF).reshape(n, m * shard, 3 * dh)
    weights = lax.psum_scatter(weights, "fsdp", scatter_dimension=1, tiled=True)
    grad_attn_in = dot(grad_projected, qkv, NT).astype(BF)
    out_rows = residual + summed
    grad_attn_in, _, sums1 = ring_sum(
        [grad_attn_in.reshape(n, rows, width)], jnp.zeros((n, 8, 128), F32), n, m, 6,
        (), (away1[0],),
    )
    def settle(same, got, wide, tall):
        wide = joined(same[0, :2], got[0, :2]) + jnp.sum(wide.astype(F32), axis=0)
        tall = joined(same[0, 2], got[0, 2]) + jnp.sum(tall[:, 0].astype(F32), axis=0)
        half = tall.shape[0] // 2
        return wide[0], wide[1], jnp.concatenate([tall[:half], tall[half:]], axis=1)

    grad_w_gate, grad_w_up, grad_w_down = (
        jnp.stack(pair)
        for pair in zip(settle(same0, got0, sums0, sums0d), settle(same1, got1, sums1, sums1d))
    )
    weights = lax.all_to_all(weights, "head", split_axis=0, concat_axis=0, tiled=True)
    grad_qkv = weights.reshape(n, shard, 3, dh).transpose(1, 2, 0, 3).astype(F32)
    grad_qkv = grad_qkv.reshape(shard, 3 * width)

    back, grad_gain_attn = norm_back(hidden[0].astype(F32), gain_attn, grad_attn_in)
    grad_hidden = grad_residual + back

    def at_mine(piece):
        return lax.dynamic_update_slice_in_dim(jnp.zeros((width,), F32), piece, me * dh, 0)[:, None]

    pack = jnp.concatenate(
        [
            grad_router,
            grad_gain_attn[:, None],
            grad_gain_ffn[:, None],
            at_mine(grad_gain_q),
            at_mine(grad_gain_k),
        ],
        axis=1,
    ).reshape(n * m, shard * (experts + 4))
    pack = lax.all_to_all(pack, both, split_axis=0, concat_axis=0, tiled=True)
    pack = jnp.sum(pack, axis=0).reshape(shard, experts + 4)
    return (
        out_rows.astype(BF)[None],
        grad_hidden[None],
        grad_qkv,
        grad_out_w,
        pack[:, :experts],
        pack[:, experts],
        pack[:, experts + 1],
        pack[:, experts + 2],
        pack[:, experts + 3],
        grad_w_gate,
        grad_w_up,
        grad_w_down,
    )


def solution(mesh):
    both = ("head", "fsdp")
    return jax.shard_map(
        body,
        mesh=mesh,
        in_specs=(
            P("fsdp", "head", None),
            P(both, None),
            P(both, None),
            P(both, None),
            P(both),
            P(both),
            P(both),
            P(both),
            P("head", "fsdp", None),
            P("head", "fsdp", None),
            P("head", "fsdp", None),
            P("fsdp"),
            P("fsdp", "head", None),
            P("fsdp", "head", None),
            P("fsdp", "head", None),
        ),
        out_specs=(
            P("fsdp", "head", None),
            P("fsdp", "head", None),
            P(both, None),
            P(both, None),
            P(both, None),
            P(both),
            P(both),
            P(both),
            P(both),
            P("head", "fsdp", None),
            P("head", "fsdp", None),
            P("head", "fsdp", None),
        ),
        check_vma=False,
    )
```

```python
import functools
import math

import jax
import jax.numpy as jnp
from jax import lax
from jax.experimental import pallas as pl
from jax.experimental.pallas import tpu as pltpu
from jax.sharding import PartitionSpec as P

HEADS = 16
HD = 128
FF = 1024
TOP = 8
EXP_DEV = 2

EPS = 1e-06
ROPE_BASE = 10000.0
NEGATIVE = -1e30
BF = jnp.bfloat16
F32 = jnp.float32
NN = ((1,), (0,))
NT = ((1,), (1,))
TN = ((0,), (0,))
ANY = pl.BlockSpec(memory_space=pl.ANY)
WHOLE = pl.BlockSpec(memory_space=pltpu.VMEM)
DMA = pltpu.SemaphoreType.DMA


def dot(a, b, dims=NN):
    return lax.dot_general(a, b, (dims, ((), ())), preferred_element_type=F32)


def cost(us):
    return pl.CostEstimate(flops=0, bytes_accessed=int(us * 3.6e6), transcendentals=0)


def ring_place():
    n = lax.axis_size("head")
    me = lax.axis_index("head")
    odd = me % 2
    return (1 - odd) * (me // 2) + odd * (n - 1 - me // 2)


def head_at(offset):
    n = lax.axis_size("head")
    k = (ring_place() + (offset + n)) % n
    down = k // (n // 2)
    return (1 - down) * 2 * k + down * (2 * n - 1 - 2 * k)


def remote(src, dst, send, recv, device):
    return pltpu.make_async_remote_copy(
        src_ref=src,
        dst_ref=dst,
        send_sem=send,
        recv_sem=recv,
        device_id=device,
        device_id_type=pl.DeviceIdType.MESH,
    )


def greet(devices):
    barrier = pltpu.get_barrier_semaphore()
    for device in devices:
        pl.semaphore_signal(
            barrier, inc=1, device_id=device, device_id_type=pl.DeviceIdType.MESH
        )
    pl.semaphore_wait(barrier, len(devices))


def other_heads():
    n = lax.axis_size("head")
    me = lax.axis_index("head")
    return [{"head": (me + d) % n} for d in range(1, n)]


def other_parts():
    m = lax.axis_size("fsdp")
    f = lax.axis_index("fsdp")
    return [{"fsdp": (f + d) % m} for d in range(1, m)]


class Ring:
    def __init__(self, own, place, send, recv, n):
        self.own, self.place, self.send, self.recv = own, place, send, recv
        self.half = n // 2

    def exists(self, way, step, c):
        return step < self.half or c == way

    def message(self, way, step, c):
        owner = head_at((1 - step) if way == 0 else (step - 1))
        return remote(
            self.own(c) if step == 1 else self.place(owner, c),
            self.place(owner, c),
            self.send.at[way, step - 1, c],
            self.recv.at[way, step - 1, c],
            {"head": head_at(1 if way == 0 else -1)},
        )

    def start(self):
        for c in range(2):
            for way in range(2):
                if self.exists(way, 1, c):
                    self.message(way, 1, c).start()

    def step(self, step):
        for c in range(2):
            for way in range(2):
                if self.exists(way, step, c):
                    self.message(way, step, c).wait_recv()
                    if step < self.half and self.exists(way, step + 1, c):
                        self.message(way, step + 1, c).start()

    def finish(self):
        for step in range(1, self.half + 1):
            for c in range(2):
                for way in range(2):
                    if self.exists(way, step, c):
                        self.message(way, step, c).wait_send()


def ring_sems(n):
    return [DMA((2, n // 2, 2)), DMA((2, n // 2, 2))]


class Carry:
    def __init__(self, kinds, ins, outs, send, recv):
        self.jobs = list(zip(kinds, ins, outs))
        self.send, self.recv = send, recv

    def copies(self, j):
        m = lax.axis_size("fsdp")
        f = lax.axis_index("fsdp")
        nx = m // 2
        x, core = f // 2, f % 2
        kind, src, dst = self.jobs[j]
        if kind == "pair":
            other = {"fsdp": x * 2 + 1 - core}
            return [remote(src, dst, self.send.at[j, 0], self.recv.at[j, 0], other)]
        return [
            remote(
                src if kind == "share" else src.at[i - 1], dst.at[i - 1],
                self.send.at[j, i - 1], self.recv.at[j, i - 1],
                {"fsdp": ((x + i) % nx) * 2 + core},
            )
            for i in range(1, nx)
        ]

    def begin(self, some=None):
        for j in range(len(self.jobs)) if some is None else some:
            for c in self.copies(j):
                c.start()

    def arrived(self, j):
        for c in self.copies(j):
            c.wait_recv()

    def end(self, seen=()):
        for j in range(len(self.jobs)):
            for c in self.copies(j):
                if j not in seen:
                    c.wait_recv()
                c.wait_send()


def carry_sems(kinds, m):
    shape = (max(len(kinds), 1), max(m // 2 - 1, 1))
    return [DMA(shape), DMA(shape)]


def carry_shapes(kinds, arrays, m):
    return [
        jax.ShapeDtypeStruct((m // 2 - 1,) * (kind == "share") + a.shape, a.dtype)
        for kind, a in zip(kinds, arrays)
    ]


def gather_kernel(n, kinds, more, x_ref, extra, *refs):
    count = len(kinds)
    second, refs = refs[: len(more)], refs[len(more) :]
    carry = Carry(kinds, refs[:count], refs[count + 2 : 2 * count + 2], *refs[-2:])
    out_ref, extra_out = refs[count : count + 2]
    refs = refs[2 * count + 2 :]
    seconds, refs = refs[: len(more)], refs[len(more) :]
    send, recv, copies, e_send, e_recv = refs[:5]
    rows = x_ref.shape[0] // 2
    me = lax.axis_index("head")
    greet(other_heads() + (other_parts() if count else []))
    ring = Ring(
        lambda c: x_ref.at[pl.ds(c * rows, rows)],
        lambda h, c: out_ref.at[h, pl.ds(c * rows, rows)],
        send, recv, n,
    )
    ring.start()
    carry.begin()
    moves = [
        pltpu.make_async_copy(x_ref, out_ref.at[me], copies.at[0]),
        pltpu.make_async_copy(extra.at[me], extra_out.at[me], copies.at[1]),
    ] + [
        remote(extra.at[dev["head"]], extra_out.at[me], e_send.at[d], e_recv.at[d], dev)
        for d, dev in enumerate(other_heads())
    ]
    for c in moves:
        c.start()
    for step in range(1, n // 2):
        ring.step(step)
    others = [
        Ring(
            lambda c, a=a: a.at[pl.ds(c * rows, rows)],
            lambda h, c, b=b: b.at[h, pl.ds(c * rows, rows)],
            refs[5 + 3 * i], refs[6 + 3 * i], n,
        )
        for i, (a, b) in enumerate(zip(second, seconds))
    ]
    for i, other in enumerate(others):
        other.start()
        moves.append(pltpu.make_async_copy(second[i], seconds[i].at[me], refs[7 + 3 * i].at[0]))
        moves[-1].start()
    ring.step(n // 2)
    for other in others:
        for step in range(1, n // 2 + 1):
            other.step(step)
    for c in moves:
        c.wait()
    for r in [ring] + others:
        r.finish()
    carry.end()


def gather(x, extra, n, m, identity, kinds=(), arrays=(), more=()):
    return pl.pallas_call(
        functools.partial(gather_kernel, n, kinds, more),
        out_shape=[
            jax.ShapeDtypeStruct((n,) + x.shape, x.dtype),
            jax.ShapeDtypeStruct(extra.shape, extra.dtype),
        ]
        + carry_shapes(kinds, arrays, m)
        + [jax.ShapeDtypeStruct((n,) + a.shape, a.dtype) for a in more],
        in_specs=[WHOLE] * (2 + len(more)) + [ANY] * len(kinds),
        out_specs=[ANY] * (2 + len(kinds) + len(more)),
        scratch_shapes=ring_sems(n)
        + [DMA((2,)), DMA((n - 1,)), DMA((n - 1,))]
        + (ring_sems(n) + [DMA((1,))]) * len(more)
        + carry_sems(kinds, m),
        compiler_params=pltpu.CompilerParams(collective_id=identity, has_side_effects=True),
        cost_estimate=cost(42),
    )(x, extra, *more, *arrays)


class RingSum:
    def __init__(self, n, parts, out_ref, own, sbuf, rbuf, loads, send, recv):
        self.n, self.half, self.parts, self.out_ref = n, n // 2, parts, out_ref
        self.own, self.sbuf, self.rbuf, self.loads = own, sbuf, rbuf, loads
        self.send, self.recv = send, recv
        self.rows = out_ref.shape[0] // 2
        self.order = (
            [self.half] + [s * w for s in range(self.half - 1, 0, -1) for w in (1, -1)] + [0]
        )
        self.ready, self.started = set(), []

    def fetch(self, o):
        i = self.order.index(o)
        return pltpu.make_async_copy(self.parts.at[head_at(o)], self.own.at[i], self.loads.at[i])

    def load(self):
        for o in self.order:
            self.fetch(o).start()

    def piece(self, o, c):
        if o not in self.ready:
            self.fetch(o).wait()
            self.ready.add(o)
        return self.own[self.order.index(o), pl.ds(c * self.rows, self.rows)].astype(F32)

    def buffer(self, way, t, c):
        first = 1 if c == way else 2
        return self.sbuf.at[way, t - 1] if t == first else self.rbuf.at[way, t - 2, c]

    def message(self, way, t, c):
        return remote(
            self.buffer(way, t, c), self.rbuf.at[way, t - 1, c],
            self.send.at[way, t - 1, c], self.recv.at[way, t - 1, c],
            {"head": head_at(1 if way == 0 else -1)},
        )

    def offset(self, way, o):
        return o if way == 0 or o == self.half else -o

    def ship(self, way, t, c, value):
        self.buffer(way, t, c)[...] = value.astype(BF)
        self.message(way, t, c).start()
        self.started.append((way, t, c))

    def start(self):
        for way in range(2):
            self.ship(way, 1, way, self.piece(self.half, way))
        for way in range(2):
            self.ship(way, 2, 1 - way, self.piece(self.offset(way, self.half - 1), 1 - way))

    def step(self, t):
        if t < self.half:
            for c in range(2):
                for way in range(2):
                    if t == 1 and c != way:
                        continue
                    self.message(way, t, c).wait_recv()
                    self.ship(
                        way, t + 1, c,
                        self.piece(self.offset(way, self.half - t), c)
                        + self.rbuf[way, t - 1, c].astype(F32),
                    )
            return
        last = self.half - 1
        for c in range(2):
            for way in range(2):
                self.message(way, self.half, c).wait_recv()
            self.out_ref[pl.ds(c * self.rows, self.rows)] = (
                self.piece(0, c)
                + self.rbuf[0, last, c].astype(F32)
                + self.rbuf[1, last, c].astype(F32)
            )

    def finish(self):
        for way, t, c in self.started:
            self.message(way, t, c).wait_send()


def ring_sum_scratch(n, rows, width):
    return [
        pltpu.VMEM((n, rows, width), BF),
        pltpu.VMEM((2, 2, rows // 2, width), BF),
        pltpu.VMEM((2, n // 2, 2, rows // 2, width), BF),
        DMA((n,)),
    ] + ring_sems(n)


def probs_of(len_ref, q, k):
    scores = dot(q, k, NT) * (1.0 / math.sqrt(HD))
    at = lax.broadcasted_iota(jnp.int32, scores.shape, 1)
    scores = jnp.where(at < len_ref[0], scores, NEGATIVE)
    exponent = jnp.exp(scores - jnp.max(scores, axis=-1, keepdims=True))
    return exponent / jnp.sum(exponent, axis=-1, keepdims=True)


QB = 256


def as_column(row):
    return jnp.broadcast_to(row, (row.shape[1], row.shape[1])).T


def as_row(column):
    return jnp.broadcast_to(column, (column.shape[0], column.shape[0])).T[:1]


def turn(values, cosine, sine):
    return values * cosine + pltpu.roll(values, HD // 2, 1) * sine


def opening_kernel(n, m, kinds, *refs):
    k = len(kinds)
    len_ref, x_ref, w_ref, wo_ref, gain_ref, cos_ref, sin_ref = refs[:7]
    (ain_ref, qkv_ref, proj_ref, sums_ref, q_ref, k_ref, v_ref, att_ref, tok_ref, wout_ref,
     gall_ref) = refs[7 + k : 18 + k]
    (hid, qkv, wpair, gall, ain, buf, own, out_sem, copies, s_send, s_recv,
     w_send, w_recv, f_send, f_recv, g_send, g_recv, a_send, a_recv, o_send, o_recv,
     c_send, c_recv, t_send, t_recv, t_sem, h_send, h_recv, r_send, r_recv) = refs[18 + 2 * k : -2]
    carry = Carry(kinds, refs[7 : 7 + k], refs[18 + k : 18 + 2 * k], *refs[-2:])
    me = lax.axis_index("head")
    f = lax.axis_index("fsdp")
    nx = m // 2
    x, core = f // 2, f % 2
    rows, width = x_ref.shape
    dh = q_ref.shape[1]
    seq = n * rows
    part_rows = rows // 2

    def part(i, side):
        return ((x + i) % nx) * 2 + side

    pair = {"fsdp": part(0, 1 - core)}
    greet(other_heads() + other_parts())

    ring = Ring(
        lambda c: x_ref.at[pl.ds(c * part_rows, part_rows)],
        lambda h, c: hid.at[h, pl.ds(c * part_rows, part_rows)],
        h_send, h_recv, n,
    )
    to_parts = [
        remote(gain_ref, gall.at[me, f], g_send.at[d], g_recv.at[d], dev)
        for d, dev in enumerate(other_parts())
    ]
    outs = [
        remote(
            wo_ref, wpair.at[x], o_send.at[i - 1], o_recv.at[i - 1], {"fsdp": part(nx - i, core)}
        )
        for i in range(1, nx)
    ]
    columns = [
        remote(
            w_ref.at[:, pl.ds(pl.multiple_of(j * width + dev["head"] * dh, 128), dh)],
            qkv.at[me, f, :, pl.ds(j * dh, dh)],
            w_send.at[d, j],
            w_recv.at[d, j],
            dev,
        )
        for d, dev in enumerate(other_heads())
        for j in range(3)
    ]
    for c in to_parts + outs:
        c.start()
    carry.begin([0])
    ring.start()
    for c in columns:
        c.start()
    gall[me, f] = gain_ref[...]
    wpair[x] = wo_ref[...]
    hid[me] = x_ref[...]
    for j in range(3):
        qkv[me, f, :, pl.ds(j * dh, dh)] = w_ref[
            :, pl.ds(pl.multiple_of(j * width + me * dh, 128), dh)
        ]
    for c in to_parts:
        c.wait_recv()
    gains = [
        remote(gall.at[me], gall.at[me], a_send.at[d], a_recv.at[d], dev)
        for d, dev in enumerate(other_heads())
    ]
    for c in gains:
        c.start()
    for c in gains:
        c.wait_recv()

    def gain_row(k):
        return jnp.concatenate(
            [
                sum(gall[h, i * fs + j, k : k + 1, :] for j in range(fs))
                for h in range(n)
                for i in range(m // fs)
            ],
            axis=1,
        )

    fs = 128 // w_ref.shape[0]
    gain_attn = gain_row(0)
    stores = []

    def store(src, dst, sem):
        stores.append(pltpu.make_async_copy(src, dst, sem))
        stores[-1].start()

    def normalise(i, slot):
        wide = hid[i].astype(F32)
        inv = lax.rsqrt(jnp.mean(wide * wide, axis=-1, keepdims=True) + EPS)
        ain[i] = (wide * inv * gain_attn).astype(BF)
        store(ain.at[i], ain_ref.at[i], out_sem.at[slot])

    normalise(me, 0)
    for c in columns:
        c.wait_recv()
    across = [
        remote(qkv.at[:, f], qkv.at[:, f], f_send.at[i], f_recv.at[i], {"fsdp": part(nx - i, core)})
        for i in range(1, nx)
    ]
    for c in across:
        c.start()
    carry.begin(range(1, len(carry.jobs)))

    def beside(i):
        there = qkv.at[:, part(i, core)]
        return remote(there, there, f_send.at[nx + i], f_recv.at[nx + i], pair)

    beside(0).start()
    for step in range(1, n // 2):
        ring.step(step)
        normalise(head_at(step), 2 * step - 1)
        normalise(head_at(-step), 2 * step)

    halves = nx // 2
    for c in outs:
        c.wait_recv()
    wring = Ring(
        lambda c: wpair.at[pl.ds(c * halves, halves)],
        lambda h, c: wout_ref.at[h, pl.ds(c * halves, halves), core],
        r_send, r_recv, n,
    )
    wring.start()
    mine = pltpu.make_async_copy(wpair, wout_ref.at[me, :, core], copies.at[0])
    mine.start()

    def over(offset, slot):
        there = wout_ref.at[head_at(offset), :, core]
        return remote(there, there, c_send.at[slot], c_recv.at[slot], pair)

    def advance(step):
        wring.step(step)
        if step < n // 2:
            over(step, 2 * step - 1).start()
            over(-step, 2 * step).start()
        else:
            over(step, n - 1).start()

    ring.step(n // 2)
    normalise(head_at(n // 2), n - 1)
    for i, c in enumerate(across):
        c.wait_recv()
        beside(i + 1).start()
    mine.wait()
    over(0, 0).start()
    for i in range(nx):
        beside(i).wait_recv()
    store(qkv, qkv_ref, copies.at[1])
    weight = qkv.reshape(width, 3 * dh)
    for g in range(n // 2):
        at = pl.ds(g * 2 * rows, 2 * rows)
        projected = dot(ain[2 * g : 2 * g + 2].reshape(2 * rows, width), weight[...])
        proj_ref[at, :] = projected[:, : 2 * dh]
        v_ref[at, :] = projected[:, 2 * dh :].astype(BF)
        for k in range(2):
            squares = projected[:, k * dh : (k + 1) * dh]
            squares = jnp.sum(squares * squares, axis=1, keepdims=True)
            for j in range(2):
                own[pl.ds(k * n + 2 * g + j, 1), :] = as_row(squares[j * rows : (j + 1) * rows])
    moves = [
        remote(own, buf.at[me], s_send.at[d], s_recv.at[d], dev)
        for d, dev in enumerate(other_heads())
    ]
    for c in moves:
        c.start()
    buf[me] = own[...]
    gain_q, gain_k = (
        jnp.concatenate(
            [
                sum(gall[me, i * fs + j, k : k + 1, :] for j in range(fs))
                for i in range(m // fs)
            ],
            axis=1,
        )
        for k in (2, 3)
    )
    gall_ref[...] = gall[...]
    for c in moves:
        c.wait()
    total_of = buf[0]
    for i in range(1, n):
        total_of = total_of + buf[i]
    sums_ref[...] = total_of
    inv_all = lax.rsqrt(total_of / width + EPS)
    advance(1)
    for i in range(n):
        at = pl.ds(i * rows, rows)
        inv_q = as_column(inv_all[i : i + 1])
        inv_k = as_column(inv_all[n + i : n + i + 1])
        cosine = cos_ref[at, :]
        sine = sin_ref[at, :]
        for head in range(dh // HD):
            lanes = pl.ds(head * HD, HD)
            k_lanes = pl.ds(dh + head * HD, HD)
            span = slice(head * HD, (head + 1) * HD)
            q_ref[at, lanes] = turn(
                proj_ref[at, lanes] * inv_q * gain_q[:, span], cosine, sine
            ).astype(BF)
            k_ref[at, lanes] = turn(
                proj_ref[at, k_lanes] * inv_k * gain_k[:, span], cosine, sine
            ).astype(BF)
    to = tok_ref.at[:, pl.ds(pl.multiple_of(me * dh, 128), dh)]

    def leave(h):
        return remote(att_ref.at[pl.ds(h * rows, rows)], to, t_send.at[h], t_recv.at[me], {"head": h})

    def arrive(h):
        return remote(
            att_ref.at[pl.ds(h * rows, rows)], tok_ref.at[:, pl.ds(h * dh, dh)],
            t_send.at[h], t_recv.at[h], {"head": h},
        )

    def stay(h):
        return pltpu.make_async_copy(att_ref.at[pl.ds(h * rows, rows)], to, t_sem.at[h])

    for j in range(seq // QB):
        at = pl.ds(j * QB, QB)
        for head in range(dh // HD):
            lanes = pl.ds(head * HD, HD)
            probs = probs_of(len_ref, q_ref[at, lanes], k_ref[:, lanes])
            att_ref[at, lanes] = dot(probs.astype(BF), v_ref[:, lanes]).astype(BF)
        for h in range(j * QB // rows, (j + 1) * QB // rows):

            @pl.when(me != h)
            def _(h=h):
                leave(h).start()

            @pl.when(me == h)
            def _(h=h):
                stay(h).start()

        if j == 1:
            advance(2)
    for step in range(3, n // 2 + 1):
        advance(step)
    for h in range(n):

        @pl.when(me != h)
        def _(h=h):
            leave(h).wait_send()
            arrive(h).wait_recv()

        @pl.when(me == h)
        def _(h=h):
            stay(h).wait()

    for c in stores:
        c.wait()
    for slot in range(n):
        over(0, slot).wait_recv()
    over(0, 0).wait_send()
    for step in range(1, n // 2):
        over(step, 2 * step - 1).wait_send()
        over(-step, 2 * step).wait_send()
    over(n // 2, n - 1).wait_send()
    for c in to_parts + outs + columns + gains + across:
        c.wait_send()
    for i in range(nx):
        beside(i).wait_send()
    ring.finish()
    wring.finish()
    carry.end()


def opening(lengths, x, w, w_out, gains, cosine, sine, n, m, kinds, arrays):
    rows, width = x.shape
    seq = n * rows
    shard = w.shape[0]
    dh = w.shape[1] // 3 // n
    heads = jax.ShapeDtypeStruct((seq, dh), BF)
    count = len(kinds)
    return pl.pallas_call(
        functools.partial(opening_kernel, n, m, kinds),
        out_shape=[
            jax.ShapeDtypeStruct((n, rows, width), BF),
            jax.ShapeDtypeStruct((n, m, shard, 3 * dh), BF),
            jax.ShapeDtypeStruct((seq, 2 * dh), F32),
            jax.ShapeDtypeStruct((2 * n, rows), F32),
            heads, heads, heads, heads,
            jax.ShapeDtypeStruct((rows, width), BF),
            jax.ShapeDtypeStruct((n, m // 2, 2, shard, width), BF),
            jax.ShapeDtypeStruct((n, m) + gains.shape, F32),
        ]
        + carry_shapes(kinds, arrays, m),
        in_specs=[pl.BlockSpec(memory_space=pltpu.SMEM)] + [WHOLE] * 6 + [ANY] * count,
        out_specs=[ANY] * 2 + [WHOLE] * 6 + [ANY] * 2 + [WHOLE] + [ANY] * count,
        scratch_shapes=[
            pltpu.VMEM((n, rows, width), BF),
            pltpu.VMEM((n, m, shard, 3 * dh), BF),
            pltpu.VMEM((m // 2, shard, width), BF),
            pltpu.VMEM((n, m) + gains.shape, F32),
            pltpu.VMEM((n, rows, width), BF),
            pltpu.VMEM((n, 2 * n, rows), F32),
            pltpu.VMEM((2 * n, rows), F32),
            DMA((n,)), DMA((2,)), DMA((n - 1,)), DMA((n - 1,)),
            DMA((n - 1, 3)), DMA((n - 1, 3)), DMA((m,)), DMA((m,)), DMA((m - 1,)), DMA((m - 1,)),
            DMA((n - 1,)), DMA((n - 1,)), DMA((m // 2,)), DMA((m // 2,)),
            DMA((n,)), DMA((n,)), DMA((n,)), DMA((n,)), DMA((n,)),
        ]
        + ring_sems(n)
        + ring_sems(n)
        + carry_sems(kinds, m),
        compiler_params=pltpu.CompilerParams(
            collective_id=0, has_side_effects=True, vmem_limit_bytes=56 << 20
        ),
        cost_estimate=cost(100),
    )(lengths, x, w, w_out, gains, cosine, sine, *arrays)


def weave(chunks, polls):
    whole = sum(w for w, _ in chunks)
    done, k = 0.0, 0
    for weight, run in chunks:
        run()
        done += weight
        while k < len(polls) - 1 and done * len(polls) >= (k + 1) * whole:
            polls[k]()
            k += 1
    for poll in polls[k:]:
        poll()


def span_of(seq):
    return seq if seq <= 512 else 256


def source_order(m):
    f = lax.axis_index("fsdp")
    nx = m // 2
    x, core = f // 2, f % 2
    return [((x + i) % nx) * 2 + (core + side) % 2 for side in range(2) for i in range(nx)]


def piece_of(kept, r, nx):
    side, i = divmod(r, nx)
    return kept[2 * side] if i == 0 else kept[2 * side + 1].at[nx - 1 - i]


class Weights:
    def __init__(self, m, kept, bufs, sems):
        self.m, self.kept, self.bufs, self.sems = m, kept, bufs, sems

    def copies(self, key):
        m, nx = self.m, self.m // 2
        order = source_order(m)
        gate, up, down = self.bufs
        g_sem, d_sem = self.sems
        block, tile = gate.shape[0] // m, down.shape[0] // m
        rows = lambda r, size: pl.ds(pl.multiple_of(order[r] * size, size), size)
        if key == "down":
            return [
                pltpu.make_async_copy(
                    piece_of(self.kept[2], r, nx), down.at[rows(r, tile)], d_sem.at[r]
                )
                for r in range(m)
            ]
        cols = pl.ds(key * tile, tile)
        return [
            pltpu.make_async_copy(
                piece_of(self.kept[i], r, nx).at[:, cols], v.at[rows(r, block), cols],
                g_sem.at[i, r, key],
            )
            for i, v in enumerate((gate, up))
            for r in range(m)
        ]

    def start(self, key):
        for c in self.copies(key):
            c.start()

    def wait(self, key):
        for c in self.copies(key):
            c.wait()


def forward_chunk(e, t, x, cot, gates_ref, at, weights, acts, dots_ref, first):
    gate_v, up_v, down_v = weights.bufs
    tile = down_v.shape[0] // weights.m
    cols = pl.ds(t * tile, tile)
    weights.wait(t)
    if t == 0:
        weights.wait("down")
    gate_pre = dot(x[...], gate_v[:, cols])
    up_pre = dot(x[...], up_v[:, cols])
    back = dot(cot[...], down_v[cols, :], NT)
    gate = gates_ref[at, e : e + 1]
    sig = 1.0 / (1.0 + jnp.exp(-gate_pre))
    silu = gate_pre * sig
    value = silu * up_pre
    dots = jnp.sum(value * back, axis=1, keepdims=True)
    if first:
        dots_ref[at, e : e + 1] = dots
    else:
        dots_ref[at, e : e + 1] += dots
    grad_act = gate * back
    acts[e, 0, :, cols] = (gate * value).astype(BF)
    acts[e, 1, :, cols] = (grad_act * up_pre * sig * (1.0 + gate_pre * (1.0 - sig))).astype(BF)
    acts[e, 2, :, cols] = (grad_act * silu).astype(BF)


def experts_steps(m, x_ref, cot_ref, gates_ref, weights, x, cot, acts, stage,
                  dots_ref, acts_ref, gin_ref, mix_ref, in_sem, a_sem, o_sem, polls, between, more=()):
    seq, width = x_ref.shape
    span = x.shape[0]
    spans = seq // span
    chunks = []
    stores = []

    def copy(store):
        store.start()
        stores.append(store)

    for q in range(spans):
        at = pl.ds(q * span, span)
        load_x = pltpu.make_async_copy(x_ref.at[at], x, in_sem.at[0])
        load_cot = pltpu.make_async_copy(cot_ref.at[at], cot, in_sem.at[1])

        def load(q=q, load_x=load_x, load_cot=load_cot):
            if q:
                while stores:
                    stores.pop().wait()
                load_x.start()
                load_cot.start()
            load_x.wait()
            load_cot.wait()

        if q == 0:
            load_x.start()
            for w in weights:
                if w is weights[0]:
                    w.start(0)
                    load_cot.start()
                    w.start("down")
                    for t in range(1, m):
                        w.start(t)
            between(0)
        chunks.append((0.1, load))
        for e in range(EXP_DEV):
            for t in range(m):

                def run(e=e, t=t, q=q, at=at):
                    if q == 0 and e == 0 and t == m // 2:
                        between(1)
                    if q:
                        weights[e].wait = lambda key: None
                    forward_chunk(
                        e, t, x, cot, gates_ref, at, weights[e], acts, dots_ref, t == 0
                    )

                chunks.append((1.6 * 4 / m, run))

            def keep(e=e, at=at):
                copy(pltpu.make_async_copy(acts.at[e], acts_ref.at[e, :, at], a_sem.at[e]))

            chunks.append((0.0, keep))
        for r in range(width // 512):

            def run(r=r, at=at):
                lanes = pl.ds(r * 512, 512)
                mixed, grads = None, None
                for e in range(EXP_DEV):
                    gate_v, up_v, down_v = weights[e].bufs
                    a = dot(acts[e, 0], down_v[:, lanes])
                    b = dot(acts[e, 1], gate_v[lanes, :], NT) + dot(acts[e, 2], up_v[lanes, :], NT)
                    mixed = a if mixed is None else mixed + a
                    grads = b if grads is None else grads + b
                stage[0, :, lanes] = grads.astype(BF)
                stage[1, :, lanes] = mixed.astype(BF)
                for i, to in enumerate((gin_ref, mix_ref)):
                    copy(
                        pltpu.make_async_copy(
                            stage.at[i, :, lanes], to.at[at, lanes], o_sem.at[i, r]
                        )
                    )

            chunks.append((3.2, run))
    weave(chunks + list(more), polls)
    for c in stores:
        c.wait()


def experts_scratch(m, seq, width, ff):
    span = span_of(seq)
    return [
        pltpu.VMEM((EXP_DEV, width, ff), BF),
        pltpu.VMEM((EXP_DEV, width, ff), BF),
        pltpu.VMEM((EXP_DEV, ff, width), BF),
        DMA((EXP_DEV, 2, m, m)),
        DMA((EXP_DEV, m)),
        pltpu.VMEM((span, width), BF),
        pltpu.VMEM((span, width), BF),
        pltpu.VMEM((EXP_DEV, 3, span, ff), BF),
        pltpu.VMEM((2, span, width), BF),
        DMA((2,)), DMA((EXP_DEV,)), DMA((2, width // 512)),
    ]


def weights_of(e, m, kept, gate_v, up_v, down_v, g_sem, d_sem):
    return Weights(
        m, kept, (gate_v.at[e], up_v.at[e], down_v.at[e]), (g_sem.at[e], d_sem.at[e])
    )


def experts_a_kernel(n, m, *refs):
    x_ref, cot_ref, gates_ref = refs[:3]
    w0, fresh, (xb_own, cotb_own) = refs[3:15], refs[15:25], refs[25:27]
    dots_ref, acts_ref, gin_ref, mix_ref, xb_ref, cotb_ref, up1c, down1c = refs[27:35]
    scratch, rest = refs[35:47], refs[47:]
    gate_v, up_v, down_v, g_sem, d_sem = scratch[:5]
    send0, recv0, send1, recv1, l_sem, c_send, c_recv = rest
    half = xb_own.shape[0] // 2
    me = lax.axis_index("head")
    g1, u1, d1 = fresh[:4], fresh[4:7] + (up1c,), fresh[7:10] + (down1c,)
    weights = [
        weights_of(0, m, (w0[:4], w0[4:8], w0[8:12]), gate_v, up_v, down_v, g_sem, d_sem),
        weights_of(1, m, (g1, u1, d1), gate_v, up_v, down_v, g_sem, d_sem),
    ]
    carry = Carry(("pair",) * 2, (fresh[5], fresh[8]), (up1c, down1c), c_send, c_recv)

    def ring_of(own, out, send, recv):
        return Ring(
            lambda c: own.at[pl.ds(c * half, half)],
            lambda h, c: out.at[h, pl.ds(c * half, half)],
            send, recv, n,
        )

    rings = [ring_of(xb_own, xb_ref, send0, recv0), ring_of(cotb_own, cotb_ref, send1, recv1)]
    mine = [
        pltpu.make_async_copy(xb_own, xb_ref.at[me], l_sem.at[0]),
        pltpu.make_async_copy(cotb_own, cotb_ref.at[me], l_sem.at[1]),
    ]

    def between(stage):
        if stage == 0:
            greet([{"head": head_at(1)}, {"head": head_at(-1)}] + other_parts())
            for ring in rings:
                ring.start()
            carry.begin()
            for c in mine:
                c.start()
        else:
            for j in range(2):
                carry.arrived(j)
            for key in [0, "down"] + list(range(1, m)):
                weights[1].start(key)

    def poll(step):
        for ring in rings:
            ring.step(step)

    experts_steps(
        m, x_ref, cot_ref, gates_ref, weights, *scratch[5:9], dots_ref, acts_ref, gin_ref, mix_ref,
        *scratch[9:12], [functools.partial(poll, s) for s in range(1, n // 2 + 1)], between,
    )
    for c in mine:
        c.wait()
    for ring in rings:
        ring.finish()
    carry.end(seen=(0, 1))


def row_outputs(x, ff):
    seq, width = x.shape
    return [
        jax.ShapeDtypeStruct((seq, EXP_DEV), F32),
        jax.ShapeDtypeStruct((EXP_DEV, 3, seq, ff), BF),
        jax.ShapeDtypeStruct((seq, width), BF),
        jax.ShapeDtypeStruct((seq, width), BF),
    ]


def big(us, identity):
    return dict(
        compiler_params=pltpu.CompilerParams(
            collective_id=identity, has_side_effects=True, vmem_limit_bytes=60 << 20
        ),
        cost_estimate=cost(us),
    )


def experts_a(x, cot, gates, weights0, fresh, x_b, cot_b, n, m):
    seq, width = x.shape
    ff = fresh[0].shape[1]
    w0 = [a for kept in weights0 for a in kept]
    out = jax.ShapeDtypeStruct((n,) + x_b.shape, BF)
    return pl.pallas_call(
        functools.partial(experts_a_kernel, n, m),
        out_shape=row_outputs(x, ff)
        + [out, out]
        + [jax.ShapeDtypeStruct(fresh[i].shape, BF) for i in (5, 8)],
        in_specs=[ANY, ANY, WHOLE] + [ANY] * 22 + [WHOLE] * 2,
        out_specs=[WHOLE] + [ANY] * 7,
        scratch_shapes=experts_scratch(m, seq, width, ff)
        + ring_sems(n)
        + ring_sems(n)
        + [DMA((2,))]
        + carry_sems(("pair",) * 2, m),
        **big(45, 4),
    )(x, cot, gates, *w0, *fresh, x_b, cot_b)


class Leave:
    def __init__(self, m, same, got, local, send, recv):
        self.m, self.same, self.got = m, same, got
        self.local, self.send, self.recv = local, send, recv
        self.stores, self.away = [], []

    def put(self, r, src, index, spot):
        nx = self.m // 2
        f = lax.axis_index("fsdp")
        if r < nx:
            self.stores.append(
                pltpu.make_async_copy(src, self.same.at[(r,) + index], self.local.at[r, spot])
            )
            self.stores[-1].start()
        else:
            self.away.append(
                remote(
                    src, self.got.at[(r - nx,) + index], self.send.at[r, spot],
                    self.recv.at[r, spot], {"fsdp": (f // 2) * 2 + 1 - f % 2},
                )
            )
            self.away[-1].start()

    def wide(self, i, v):
        order = source_order(self.m)
        block = v.shape[0] // self.m
        for r in range(self.m):
            at = pl.ds(pl.multiple_of(order[r] * block, block), block)
            self.put(r, v.at[at], (i,), i)

    def tall(self, v):
        order = source_order(self.m)
        tile, ff = v.shape[0] // self.m, v.shape[0]
        for r in range(self.m):
            at = pl.ds(pl.multiple_of(order[r] * tile, tile), tile)
            for side in range(2):
                self.put(
                    r, v.at[at, pl.ds(side * ff, ff)], (2, pl.ds(side * tile, tile)), 2 + side
                )

    def finish(self):
        for c in self.stores:
            c.wait()
        for c in self.away:
            c.wait()


def leave_sems(m):
    return [DMA((m, 4)), DMA((m, 4)), DMA((m, 4))]


def experts_b_kernel(n, m, early, *refs):
    x_ref, cot_ref, gates_ref = refs[:3]
    w, (gin_a, mix_a, xa_ref, cota_ref, acts_a) = refs[3:27], refs[27:32]
    dots_ref, acts_ref, gin_ref, mix_ref, grad_ref, sum_ref = refs[32:38]
    refs = refs[38:]
    if early:
        (same, got), refs = refs[:2], refs[2:]
    scratch, rest = refs[:12], refs[12:]
    gate_v, up_v, down_v, g_sem, d_sem, x, cot, acts = scratch[:8]
    weights = [
        weights_of(
            e, m, tuple(w[12 * e + 4 * i : 12 * e + 4 * i + 4] for i in range(3)),
            gate_v, up_v, down_v, g_sem, d_sem,
        )
        for e in range(EXP_DEV)
    ]
    rings = [
        RingSum(n, gin_a, grad_ref, *rest[:6]),
        RingSum(n, mix_a, sum_ref, *rest[6:12]),
    ]

    def between(stage):
        if stage == 0:
            for ring in rings:
                ring.load()
            for key in [0, "down"] + list(range(1, m)):
                weights[1].start(key)
            f = lax.axis_index("fsdp")
            pair = [{"fsdp": (f // 2) * 2 + 1 - f % 2}] if early else []
            greet([{"head": head_at(1)}, {"head": head_at(-1)}] + pair)
            for ring in rings:
                ring.start()

    def poll(step):
        for ring in rings:
            ring.step(step)

    more = []
    if early:
        part = x.shape[0]
        leave = Leave(m, same, got, *rest[12:15])
        l_sem = rest[15]
        dgate, dup, ddown = gate_v.at[0], up_v.at[0], down_v.at[0]
        x_a, cot_a = down_v.at[1, pl.ds(0, part)], down_v.at[1, pl.ds(part, part)]
        kept = [gate_v.at[1, pl.ds(k * part, part)] for k in range(3)]
        loads = [
            pltpu.make_async_copy(xa_ref, x_a, l_sem.at[0]),
            pltpu.make_async_copy(cota_ref, cot_a, l_sem.at[1]),
        ] + [
            pltpu.make_async_copy(acts_a.at[0, k], kept[k], l_sem.at[2 + k]) for k in range(3)
        ]

        def begin():
            for c in loads:
                c.start()
            for c in loads:
                c.wait()

        more.append((0.5, begin))
        for b in range(x.shape[1] // 512):

            def run(b=b):
                at = pl.ds(b * 512, 512)
                turned, turned_a = x[:, at].T, x_a[:, at].T
                dgate[at, :] = (dot(turned, acts[0, 1]) + dot(turned_a, kept[1][...])).astype(BF)
                dup[at, :] = (dot(turned, acts[0, 2]) + dot(turned_a, kept[2][...])).astype(BF)

            more.append((2.4, run))
        more.append((0.0, lambda: (leave.wide(0, dgate), leave.wide(1, dup))))
        for t in range(gate_v.shape[2] // 256):

            def run(t=t):
                at = pl.ds(t * 256, 256)
                ddown[at, :] = (
                    dot(acts[0, 0, :, at].T, cot[...]) + dot(kept[0][:, at].T, cot_a[...])
                ).astype(BF)

            more.append((1.2, run))
        more.append((0.0, lambda: leave.tall(ddown)))
    experts_steps(
        m, x_ref, cot_ref, gates_ref, weights, *scratch[5:9], dots_ref, acts_ref, gin_ref, mix_ref,
        *scratch[9:12], [functools.partial(poll, s) for s in range(1, n // 2 + 1)], between, more,
    )
    for ring in rings:
        ring.finish()
    if early:
        leave.finish()


def experts_b(x, cot, gates, weights, gin_a, mix_a, x_a, cot_a, acts_a, n, m):
    seq, width = x.shape
    ff = weights[0][0].shape[1]
    early = seq <= 512
    flat = [a for kept in weights for a in kept]
    rows = seq // n
    own = jax.ShapeDtypeStruct((rows, width), F32)
    parts = [a.reshape(n, rows, width) for a in (gin_a, mix_a)]
    grads = [jax.ShapeDtypeStruct((m // 2, 3, width // m, ff), BF)] * (2 * early)
    return pl.pallas_call(
        functools.partial(experts_b_kernel, n, m, early),
        out_shape=row_outputs(x, ff) + [own, own] + grads,
        in_specs=[ANY, ANY, WHOLE] + [ANY] * 29,
        out_specs=[WHOLE, ANY, ANY, ANY, WHOLE, WHOLE] + [ANY] * len(grads),
        scratch_shapes=experts_scratch(m, seq, width, ff)
        + ring_sum_scratch(n, rows, width)
        + ring_sum_scratch(n, rows, width)
        + (leave_sems(m) + [DMA((5,))]) * early,
        **big(60, 7),
    )(x, cot, gates, *flat, *parts, x_a, cot_a, acts_a)


def experts_d_kernel(n, m, experts, kinds, *refs):
    xs, cots, all_acts = refs[0:6:3], refs[1:6:3], refs[2:6:3]
    gin_b, mix_b, extra = refs[6:9]
    k, g = len(kinds), 2 * len(experts)
    outs, (grad_ref, sum_ref, extra_out) = refs[9 + k : 9 + k + g], refs[9 + k + g : 12 + k + g]
    carry = Carry(kinds, refs[9 : 9 + k], refs[12 + k + g : 12 + 2 * k + g], *refs[-2:])
    (x, cot, acts, dgate, dup, ddown, x_sem, a_sem, copy, e_send, e_recv) = refs[
        12 + 2 * k + g : 23 + 2 * k + g
    ]
    rest = refs[23 + 2 * k + g : -2]
    me = lax.axis_index("head")
    rows, width = x.shape
    part = rows // 2
    ff = acts.shape[2]
    rings = [
        RingSum(n, gin_b, grad_ref, *rest[:6]),
        RingSum(n, mix_b, sum_ref, *rest[6:12]),
    ]
    loads = [
        pltpu.make_async_copy(src[i], dst.at[pl.ds(i * part, part)], x_sem.at[k, i])
        for k, (src, dst) in enumerate(((xs, x), (cots, cot)))
        for i in range(2)
    ]

    def act_loads(e):
        return [
            pltpu.make_async_copy(
                all_acts[i].at[e], acts.at[:, pl.ds(i * part, part)], a_sem.at[i]
            )
            for i in range(2)
        ]

    for c in loads + act_loads(experts[0]):
        c.start()
    for ring in rings:
        ring.load()
    greet(other_heads() + other_parts())
    carry.begin()
    for ring in rings:
        ring.start()
    direct = [pltpu.make_async_copy(extra.at[me], extra_out.at[me], copy.at[0])] + [
        remote(extra.at[dev["head"]], extra_out.at[me], e_send.at[d], e_recv.at[d], dev)
        for d, dev in enumerate(other_heads())
    ]
    for c in direct:
        c.start()
    chunks, leaves = [], []
    for j, e in enumerate(experts):
        leave = Leave(m, outs[2 * j], outs[2 * j + 1], *rest[12 + 3 * j : 15 + 3 * j])

        def begin(j=j, e=e):
            if j:
                leaves[j - 1].finish()
                for c in act_loads(e):
                    c.start()
            for c in (loads if j == 0 else []) + act_loads(e):
                c.wait()

        leaves.append(leave)
        chunks.append((0.1, begin))
        for b in range(width // 512):

            def run(b=b):
                at = pl.ds(b * 512, 512)
                turned = x[:, at].T
                dgate[at, :] = dot(turned, acts[1]).astype(BF)
                dup[at, :] = dot(turned, acts[2]).astype(BF)

            chunks.append((2.2, run))
        chunks.append(
            (0.0, lambda leave=leave: (leave.wide(0, dgate), leave.wide(1, dup)))
        )
        for t in range(ff // 256):

            def run(t=t):
                at = pl.ds(t * 256, 256)
                ddown[at, :] = dot(acts[0, :, at].T, cot[...]).astype(BF)

            chunks.append((1.1, run))
        chunks.append((0.0, lambda leave=leave: leave.tall(ddown)))

    def poll(step):
        for ring in rings:
            ring.step(step)

    weave(chunks, [functools.partial(poll, t) for t in range(1, n // 2 + 1)])
    for ring in rings:
        ring.finish()
    for c in direct:
        c.wait()
    leaves[-1].finish()
    carry.end()


def experts_d(first, second, gin_b, mix_b, dots, n, m, experts, kinds, arrays):
    seq = first[2].shape[2]
    ff = first[2].shape[3]
    rows, width = first[0].shape[1:]
    grads = jax.ShapeDtypeStruct((m // 2, 3, width // m, ff), BF)
    own = jax.ShapeDtypeStruct((rows, width), F32)
    k, g = len(kinds), 2 * len(experts)

    def flat(parts):
        return [parts[0].reshape(seq, width), parts[1].reshape(seq, width), parts[2]]

    out = pl.pallas_call(
        functools.partial(experts_d_kernel, n, m, experts, kinds),
        out_shape=[grads] * g
        + [own, own, jax.ShapeDtypeStruct(dots.shape, F32)]
        + carry_shapes(kinds, arrays, m),
        in_specs=[ANY] * 8 + [WHOLE] + [ANY] * k,
        out_specs=[ANY] * g + [WHOLE, WHOLE, ANY] + [ANY] * k,
        scratch_shapes=[
            pltpu.VMEM((2 * seq, width), BF),
            pltpu.VMEM((2 * seq, width), BF),
            pltpu.VMEM((3, 2 * seq, ff), BF),
            pltpu.VMEM((width, ff), BF),
            pltpu.VMEM((width, ff), BF),
            pltpu.VMEM((ff, width), BF),
            DMA((2, 2)), DMA((2,)), DMA((1,)), DMA((n - 1,)), DMA((n - 1,)),
        ]
        + ring_sum_scratch(n, rows, width)
        + ring_sum_scratch(n, rows, width)
        + leave_sems(m) * len(experts)
        + carry_sems(kinds, m),
        **big(45, 8),
    )(
        *flat(first), *flat(second), gin_b.reshape(n, rows, width), mix_b.reshape(n, rows, width),
        dots, *arrays,
    )
    return [tuple(out[2 * j : 2 * j + 2]) for j in range(g // 2)], *out[g : g + 3], out[g + 3 :]


class RingSumHere(RingSum):
    def __init__(self, n, parts, out_ref, sbuf, rbuf, send, recv):
        super().__init__(n, parts, out_ref, None, sbuf, rbuf, None, send, recv)

    def piece(self, o, c):
        return self.parts[head_at(o), pl.ds(c * self.rows, self.rows)].astype(F32)


def closing_kernel(n, m, kinds, early, *refs):
    k = len(kinds)
    (len_ref, gatt_ref, gao_ref, q_ref, k_ref, v_ref, att_ref, proj_ref, sums_ref, gains_ref,
     cos_ref, sin_ref, ain_ref, qkv_ref) = refs[:14]
    (gin_ref, dqkv_ref, dout_ref, dgains_ref) = refs[14 + k : 18 + k]
    (gheads, gao, ain, qkv, gin, dproj, scaled, dk, dv, own, buf,
     dqkv, gq, xs, xr, fin, dout, go, xso, xro, sbuf, rbuf,
     l_sem, a_send, a_recv, s_send, s_recv, p_send, p_recv, x_send, x_recv, t_send, t_recv, t_sem,
     g_send, g_recv, r_send, r_recv) = refs[18 + 2 * k : -2]
    carry = Carry(kinds, refs[14 : 14 + k], refs[18 + k : 18 + 2 * k], *refs[-2:])
    me = lax.axis_index("head")
    f = lax.axis_index("fsdp")
    nx = m // 2
    x, core = f // 2, f % 2
    rows, width = gao_ref.shape
    half_rows = rows // 2
    seq, dh = q_ref.shape
    scale = 1.0 / math.sqrt(HD)
    order = source_order(m)
    loads = [
        pltpu.make_async_copy(ain_ref, ain, l_sem.at[0]),
        pltpu.make_async_copy(qkv_ref, qkv, l_sem.at[1]),
    ]
    for c in loads:
        c.start()
    greet(other_heads() + other_parts())

    here = gheads.at[pl.ds(pl.multiple_of(me * rows, rows), rows)]
    sends = [
        remote(
            gatt_ref.at[:, pl.ds(pl.multiple_of(dev["head"] * dh, 128), dh)], here,
            a_send.at[d], a_recv.at[d], dev,
        )
        for d, dev in enumerate(other_heads())
    ]
    for c in sends:
        c.start()
    carry.begin(range(early))
    gring = Ring(
        lambda c: gao_ref.at[pl.ds(c * half_rows, half_rows)],
        lambda h, c: gao.at[h, pl.ds(c * half_rows, half_rows)],
        g_send, g_recv, n,
    )
    gring.start()
    here[...] = gatt_ref[:, pl.ds(pl.multiple_of(me * dh, 128), dh)]
    gao[me] = gao_ref[...]
    for c in sends:
        c.wait_recv()

    for head in range(dh // HD):
        lanes = pl.ds(head * HD, HD)
        for j in range(seq // QB):
            at = pl.ds(j * QB, QB)
            probs = probs_of(len_ref, q_ref[at, lanes], k_ref[:, lanes])
            grad_probs = dot(gheads[at, lanes], v_ref[:, lanes], NT)
            inner = jnp.sum(probs * grad_probs, axis=-1, keepdims=True)
            grad_scores = (probs * (grad_probs - inner)).astype(BF)
            dproj[at, lanes] = (dot(grad_scores, k_ref[:, lanes]) * scale).astype(BF)
            add_k = dot(grad_scores, q_ref[at, lanes], TN)
            add_v = dot(probs.astype(BF), gheads[at, lanes], TN)
            if j == 0:
                dk[...] = add_k
                dv[...] = add_v
            else:
                dk[...] += add_k
                dv[...] += add_v
        dproj[:, pl.ds(dh + head * HD, HD)] = (dk[...] * scale).astype(BF)
        dproj[:, pl.ds(2 * dh + head * HD, HD)] = dv[...].astype(BF)
        gring.step(head + 1)
    for step in range(dh // HD + 1, 3):
        gring.step(step)

    inv_all = lax.rsqrt(sums_ref[...] / width + EPS)
    dgains = [jnp.zeros((1, HD), F32) for _ in range(2 * dh // HD)]
    for i in range(n):
        at = pl.ds(i * rows, rows)
        cosine = cos_ref[at, :]
        sine = -sin_ref[at, :]
        for kind in range(2):
            inv = as_column(inv_all[kind * n + i : kind * n + i + 1])
            sums = jnp.zeros((rows, 1), F32)
            for head in range(dh // HD):
                spot = kind * (dh // HD) + head
                lanes = pl.ds(kind * dh + head * HD, HD)
                turned = turn(dproj[at, lanes].astype(F32), cosine, sine)
                unit = proj_ref[at, lanes] * inv
                dgains[spot] = dgains[spot] + jnp.sum(turned * unit, axis=0, keepdims=True)
                grad = turned * gains_ref[kind : kind + 1, head * HD : (head + 1) * HD]
                scaled[at, lanes] = grad
                sums = sums + jnp.sum(grad * unit, axis=1, keepdims=True)
            own[pl.ds(kind * n + i, 1), :] = as_row(sums)
    for spot, value in enumerate(dgains):
        dgains_ref[pl.ds(spot, 1), :] = value
    moves = [
        remote(own, buf.at[me], s_send.at[d], s_recv.at[d], dev)
        for d, dev in enumerate(other_heads())
    ]
    for c in moves:
        c.start()
    buf[me] = own[...]
    for c in moves:
        c.wait()
    total_of = buf[0]
    for i in range(1, n):
        total_of = total_of + buf[i]
    means = total_of / width
    for i in range(n):
        at = pl.ds(i * rows, rows)
        for kind in range(2):
            inv = as_column(inv_all[kind * n + i : kind * n + i + 1])
            mean = as_column(means[kind * n + i : kind * n + i + 1])
            for head in range(dh // HD):
                lanes = pl.ds(kind * dh + head * HD, HD)
                unit = proj_ref[at, lanes] * inv
                dproj[at, lanes] = (inv * (scaled[at, lanes] - unit * mean)).astype(BF)

    for c in loads:
        c.wait()
    weight = qkv.reshape(width, 3 * dh)
    for g in range(n // 2):
        back = dot(dproj[pl.ds(g * 2 * rows, 2 * rows), :], weight[...], NT).astype(BF)
        gin[2 * g : 2 * g + 2] = back.reshape(2, rows, width)
    gring.step(3)
    ring = RingSumHere(n, gin, gin_ref, sbuf, rbuf, r_send, r_recv)
    ring.start()

    flat = dqkv.reshape(width, 3 * dh)
    for b in range(width // 512):
        at = pl.ds(b * 512, 512)
        turned = ain.reshape(seq, width)[:, at].T
        flat[at, :] = dot(turned, dproj[...]).astype(BF)
    pair = {"fsdp": x * 2 + 1 - core}
    pairs = [
        remote(dqkv.at[:, order[nx + i]], gq.at[i], p_send.at[i], p_recv.at[i], pair)
        for i in range(nx)
    ]
    for c in pairs:
        c.start()
    for step in range(4, n // 2 + 1):
        gring.step(step)
    for b in range(width // 512):
        at = pl.ds(b * 512, 512)
        value = dot(att_ref[...], gao.reshape(seq, width)[:, at], TN)
        dout[:, :, at] = value.astype(BF).reshape(dout.shape[:2] + (512,))
    pairs_out = [
        remote(dout.at[order[nx + i]], go.at[i], p_send.at[nx + i], p_recv.at[nx + i], pair)
        for i in range(nx)
    ]
    for c in pairs_out:
        c.start()
    ring.step(1)
    for c in pairs + pairs_out:
        c.wait_recv()
    across = []
    for i in range(1, nx):
        there = {"fsdp": ((x + i) % nx) * 2 + core}
        xs[i - 1] = (dqkv[:, order[i]].astype(F32) + gq[i].astype(F32)).astype(BF)
        xso[i - 1] = (dout[order[i]].astype(F32) + go[i].astype(F32)).astype(BF)
        across.append(remote(xs.at[i - 1], xr.at[i - 1], x_send.at[0, i - 1], x_recv.at[0, i - 1], there))
        across.append(remote(xso.at[i - 1], xro.at[i - 1], x_send.at[1, i - 1], x_recv.at[1, i - 1], there))
    for c in across:
        c.start()
    carry.begin(range(early, len(carry.jobs)))
    for step in range(2, n // 2):
        ring.step(step)
    for c in across:
        c.wait_recv()
    value = dqkv[:, order[0]].astype(F32) + gq[0].astype(F32)
    value_out = dout[order[0]].astype(F32) + go[0].astype(F32)
    for i in range(1, nx):
        value = value + xr[i - 1].astype(F32)
        value_out = value_out + xro[i - 1].astype(F32)
    fin[...] = value.astype(BF)
    dout_ref[...] = value_out
    to = dqkv_ref.at[me]
    last = [
        remote(fin.at[dev["head"]], to, t_send.at[d], t_recv.at[d], dev)
        for d, dev in enumerate(other_heads())
    ]
    for c in last:
        c.start()
    mine = pltpu.make_async_copy(fin.at[me], to, t_sem.at[0])
    mine.start()
    ring.step(n // 2)
    for c in last:
        c.wait()
    mine.wait()
    for c in sends + pairs + pairs_out + across:
        c.wait_send()
    gring.finish()
    ring.finish()
    carry.end()


def closing(lengths, gatt, gao, q, k, v, att, proj, sums, gains, cosine, sine, ain, qkv, n, m, kinds,
            arrays, early):
    rows, width = gao.shape
    seq, dh = q.shape
    nx = m // 2
    shard = qkv.shape[2]
    count = len(kinds)

    def vm(*shape, dtype=BF):
        return pltpu.VMEM(shape, dtype)

    return pl.pallas_call(
        functools.partial(closing_kernel, n, m, kinds, early),
        out_shape=[
            jax.ShapeDtypeStruct((rows, width), F32),
            jax.ShapeDtypeStruct((n, shard, 3 * dh), BF),
            jax.ShapeDtypeStruct((shard, width), F32),
            jax.ShapeDtypeStruct((2 * dh // HD, HD), F32),
        ]
        + carry_shapes(kinds, arrays, m),
        in_specs=[pl.BlockSpec(memory_space=pltpu.SMEM)] + [WHOLE] * 11 + [ANY] * (2 + count),
        out_specs=[WHOLE, ANY, WHOLE, WHOLE] + [ANY] * count,
        scratch_shapes=[
            vm(seq, dh), vm(n, rows, width), vm(n, rows, width), vm(n, m, shard, 3 * dh),
            vm(n, rows, width), vm(seq, 3 * dh), vm(seq, 2 * dh, dtype=F32),
            vm(seq, HD, dtype=F32), vm(seq, HD, dtype=F32),
            vm(2 * n, rows, dtype=F32), vm(n, 2 * n, rows, dtype=F32),
            vm(n, m, shard, 3 * dh), vm(nx, n, shard, 3 * dh),
            vm(nx - 1, n, shard, 3 * dh), vm(nx - 1, n, shard, 3 * dh), vm(n, shard, 3 * dh),
            vm(m, shard, width), vm(nx, shard, width),
            vm(nx - 1, shard, width), vm(nx - 1, shard, width),
            vm(2, 2, rows // 2, width), vm(2, n // 2, 2, rows // 2, width),
            DMA((2,)), DMA((n - 1,)), DMA((n - 1,)), DMA((n - 1,)), DMA((n - 1,)),
            DMA((m,)), DMA((m,)), DMA((2, nx - 1)), DMA((2, nx - 1)),
            DMA((n - 1,)), DMA((n - 1,)), DMA((1,)),
        ]
        + ring_sems(n)
        + ring_sems(n)
        + carry_sems(kinds, m),
        **big(110, 5),
    )(lengths, gatt, gao, q, k, v, att, proj, sums, gains, cosine, sine, ain, qkv, *arrays)


def joined(same, got):
    return same.astype(F32) + got.astype(F32)


def body(
    hidden,
    w_qkv,
    w_out,
    w_router,
    g_attn,
    g_ffn,
    g_q,
    g_k,
    w_gate,
    w_up,
    w_down,
    lengths,
    routes,
    route_codes,
    cotangent,
):
    n = lax.axis_size("head")
    m = lax.axis_size("fsdp")
    me = lax.axis_index("head")
    rows = hidden.shape[1]
    width = hidden.shape[2]
    seq = rows * n
    lh = HEADS // n
    dh = lh * HD
    experts = EXP_DEV * n
    shard = w_qkv.shape[0]
    both = ("head", "fsdp")

    sides = 128 // shard
    lane = jnp.arange(128, dtype=jnp.int32) // shard == lax.axis_index("fsdp") % sides

    def placed(gain):
        return jnp.where(lane, jnp.tile(gain.astype(F32), sides), 0.0)

    small = jnp.stack([placed(g) for g in (g_attn, g_ffn, g_q, g_k)])
    small = jnp.concatenate(
        [small, jnp.zeros((4, 128), F32), w_router.astype(F32).reshape(-1, 128)]
    )
    block = w_gate.shape[1]
    gate_w, up_w, down_w = ([w[e] for e in range(EXP_DEV)] for w in (w_gate, w_up, w_down))
    def inverse_rms(values):
        return lax.rsqrt(jnp.mean(values * values, axis=-1, keepdims=True) + EPS)

    frequency = ROPE_BASE ** (-2.0 * jnp.arange(HD // 2, dtype=F32) / HD)
    angles = jnp.arange(seq, dtype=F32)[:, None] * frequency[None, :]
    cosine = jnp.tile(jnp.cos(angles), (1, 2))
    sine = jnp.sin(angles)
    sine = jnp.concatenate([-sine, sine], axis=1)
    (attn_input, qkv, proj, sums, queries, keys, values, attended, attended_tok, full_out, small,
     gate0x, up0x, down0x, gate1x) = opening(
        lengths, hidden[0], w_qkv, w_out, small, cosine, sine, n, m, ("share",) * 4,
        (gate_w[0], up_w[0], down_w[0], gate_w[1]),
    )
    router = small[:, :, 8:].reshape(width, experts).astype(BF)
    lanes = small[:, :, :4].reshape(n, m // sides, sides, 4, 128).sum(axis=2)
    gain_attn, gain_ffn, gain_q, gain_k = lanes.transpose(2, 0, 1, 3).reshape(4, width)
    gains_q = lax.dynamic_slice_in_dim(gain_q, me * dh, dh, 0)
    gains_k = lax.dynamic_slice_in_dim(gain_k, me * dh, dh, 0)
    full_out = full_out.reshape(width, width)
    residual = hidden[0].astype(F32) + dot(attended_tok, full_out)
    own_input = (residual * inverse_rms(residual) * gain_ffn).astype(BF)

    logits = dot(own_input, router)
    matches = routes[0][:, :, None] == jnp.arange(experts, dtype=jnp.int32)[None, None, :]
    chosen = (
        jnp.sum(jnp.where(matches, logits[:, None, :], 0.0), axis=-1)
        + route_codes[0].astype(F32) / 1024.0
    )
    chosen = jnp.exp(chosen - jnp.max(chosen, axis=1, keepdims=True))
    gates = chosen / jnp.sum(chosen, axis=1, keepdims=True)
    spread = jnp.sum(jnp.where(matches, gates[:, :, None], 0.0), axis=1)

    half = rows // 2
    gate_sets = spread.T.reshape(n, EXP_DEV, rows)
    out_e0 = [gate_w[0], gate0x, up_w[0], up0x, down_w[0], down0x]
    out_e1 = [gate_w[1], gate1x, up_w[1], down_w[1]]
    x_a, mine, up1x, down1x, *got, cot_a = gather(
        own_input[:half], gate_sets, n, m, 1, ("share",) * 2 + ("pair",) * 10,
        (up_w[1], down_w[1], *out_e0, *out_e1), (cotangent[0, :half],),
    )
    weights0 = [(out_e0[i], out_e0[i + 1], got[i], got[i + 1]) for i in (0, 2, 4)]
    mine = mine.transpose(0, 2, 1)
    span = n * half

    def rows_of(part):
        return part.reshape(span, width)

    gates_a = mine[:, :half].reshape(span, EXP_DEV)
    gates_b = mine[:, half:].reshape(span, EXP_DEV)
    fresh = [gate_w[1], gate1x, got[6], got[7], up_w[1], up1x, got[8], down_w[1], down1x, got[9]]
    dots_a, acts_a, gin_a, mix_a, x_b, cot_b, up1c, down1c = experts_a(
        rows_of(x_a), rows_of(cot_a), gates_a, weights0, fresh, own_input[half:],
        cotangent[0, half:], n, m,
    )
    weights1 = [
        (gate_w[1], gate1x, got[6], got[7]),
        (up_w[1], up1x, got[8], up1c),
        (down_w[1], down1x, got[9], down1c),
    ]
    dots_b, acts_b, gin_b, mix_b, grad_ffn_a, summed_a, *grads0 = experts_b(
        rows_of(x_b), rows_of(cot_b), gates_b, weights0 + weights1, gin_a, mix_a,
        rows_of(x_a), rows_of(cot_a), acts_a, n, m,
    )
    dots = jnp.concatenate(
        [d.reshape(n, half, EXP_DEV).transpose(0, 2, 1) for d in (dots_a, dots_b)], axis=2
    )

    def outgoing(same, got, *spans):
        return [joined(same[1:, a:b], got[1:, a:b]).astype(BF) for a, b in spans]

    early = len(grads0) > 0
    away0 = outgoing(*grads0, (0, 2), (2, 3)) if early else []
    grads, grad_ffn_b, summed_b, dots, sums0 = experts_d(
        (x_a, cot_a, acts_a), (x_b, cot_b, acts_b), gin_b, mix_b, dots, n, m,
        (1,) if early else (0, 1), ("across",) * early, away0[:1],
    )
    grads = [tuple(grads0)] * early + grads
    grad_ffn = jnp.concatenate([grad_ffn_a, grad_ffn_b], axis=0)
    summed = jnp.concatenate([summed_a, summed_b], axis=0)
    if not early:
        away0 = outgoing(*grads[0], (0, 2), (2, 3))
    away1 = outgoing(*grads[1], (0, 1), (1, 2), (2, 3))

    dots = dots.reshape(experts, rows).T
    grad_rows = cotangent[0].astype(F32)
    grad_logits = spread * (dots - jnp.sum(spread * dots, axis=1, keepdims=True))
    high = lax.Precision.HIGHEST
    grad_ffn = grad_ffn + jnp.dot(grad_logits, router.astype(F32).T, precision=high)
    grad_router = jnp.dot(own_input.astype(F32).T, grad_logits, precision=high)

    def norm_back(values, gain, grad):
        inv = inverse_rms(values)
        unit = values * inv
        scaled = grad * gain
        back = inv * (scaled - unit * jnp.mean(scaled * unit, axis=-1, keepdims=True))
        return back, jnp.sum(grad * unit, axis=0)

    back, grad_gain_ffn = norm_back(residual, gain_ffn, grad_ffn)
    grad_residual = grad_rows + back
    grad_attn_out = grad_residual.astype(BF)
    grad_attended = dot(grad_attn_out, full_out, NT).astype(BF)
    riders = away0[early:] + away1
    first = 2 if early else 1
    grad_attn_in, grad_qkv, grad_out_w, grad_gains, *arrived = closing(
        lengths, grad_attended, grad_attn_out, queries, keys, values, attended, proj, sums,
        jnp.stack([gains_q, gains_k]), cosine, sine, attn_input, qkv, n, m,
        ("across",) * len(riders), riders, first,
    )
    sums0 = list(sums0) + arrived[: len(away0) - early]
    sums1 = arrived[len(away0) - early :]
    grad_gain_q, grad_gain_k = grad_gains.reshape(2, dh)
    out_rows = residual + summed

    def settled(i, tall=False):
        result = []
        for (same, got), sums in zip(grads, (sums0, sums1)):
            k = i
            for part in sums:
                if k < part.shape[1]:
                    break
                k -= part.shape[1]
            value = joined(same[0, i], got[0, i])
            for j in range(part.shape[0]):
                value = value + part[j, k].astype(F32)
            if tall:
                half = value.shape[0] // 2
                value = jnp.concatenate([value[:half], value[half:]], axis=1)
            result.append(value)
        return jnp.stack(result)

    grad_w_gate, grad_w_up, grad_w_down = settled(0), settled(1), settled(2, True)
    grad_qkv = grad_qkv.reshape(n, shard, 3, dh).transpose(1, 2, 0, 3).astype(F32)
    grad_qkv = grad_qkv.reshape(shard, 3 * width)

    back, grad_gain_attn = norm_back(hidden[0].astype(F32), gain_attn, grad_attn_in)
    grad_hidden = grad_residual + back

    def at_mine(piece):
        return lax.dynamic_update_slice_in_dim(jnp.zeros((width,), F32), piece, me * dh, 0)[:, None]

    pack = jnp.concatenate(
        [
            grad_router,
            grad_gain_attn[:, None],
            grad_gain_ffn[:, None],
            at_mine(grad_gain_q),
            at_mine(grad_gain_k),
        ],
        axis=1,
    ).reshape(n * m, shard * (experts + 4))
    pack = lax.all_to_all(pack, both, split_axis=0, concat_axis=0, tiled=True)
    pack = jnp.sum(pack, axis=0).reshape(shard, experts + 4)
    return (
        out_rows.astype(BF)[None],
        grad_hidden[None],
        grad_qkv,
        grad_out_w,
        pack[:, :experts],
        pack[:, experts],
        pack[:, experts + 1],
        pack[:, experts + 2],
        pack[:, experts + 3],
        grad_w_gate,
        grad_w_up,
        grad_w_down,
    )


def solution(mesh):
    both = ("head", "fsdp")
    return jax.shard_map(
        body,
        mesh=mesh,
        in_specs=(
            P("fsdp", "head", None),
            P(both, None),
            P(both, None),
            P(both, None),
            P(both),
            P(both),
            P(both),
            P(both),
            P("head", "fsdp", None),
            P("head", "fsdp", None),
            P("head", "fsdp", None),
            P("fsdp"),
            P("fsdp", "head", None),
            P("fsdp", "head", None),
            P("fsdp", "head", None),
        ),
        out_specs=(
            P("fsdp", "head", None),
            P("fsdp", "head", None),
            P(both, None),
            P(both, None),
            P(both, None),
            P(both),
            P(both),
            P(both),
            P(both),
            P("head", "fsdp", None),
            P("head", "fsdp", None),
            P("head", "fsdp", None),
        ),
        check_vma=False,
    )
```

```python
import functools
import math

import jax
import jax.numpy as jnp
import numpy as np
from jax import lax
from jax.experimental import pallas as pl
from jax.experimental.pallas import tpu as pltpu
from jax.sharding import PartitionSpec as P

HEADS = 16
HD = 128
FF = 1024
TOP = 8
EXP_DEV = 2

EPS = 1e-06
ROPE_BASE = 10000.0
NEGATIVE = -1e30
BF = jnp.bfloat16
F32 = jnp.float32
NN = ((1,), (0,))
NT = ((1,), (1,))
TN = ((0,), (0,))
ANY = pl.BlockSpec(memory_space=pl.ANY)
WHOLE = pl.BlockSpec(memory_space=pltpu.VMEM)
DMA = pltpu.SemaphoreType.DMA


def dot(a, b, dims=NN):
    return lax.dot_general(a, b, (dims, ((), ())), preferred_element_type=F32)


def cost(us):
    return pl.CostEstimate(flops=0, bytes_accessed=int(us * 3.6e6), transcendentals=0)


def ring_place():
    n = lax.axis_size("head")
    me = lax.axis_index("head")
    odd = me % 2
    return (1 - odd) * (me // 2) + odd * (n - 1 - me // 2)


def head_at(offset):
    n = lax.axis_size("head")
    k = (ring_place() + (offset + n)) % n
    down = k // (n // 2)
    return (1 - down) * 2 * k + down * (2 * n - 1 - 2 * k)


def remote(src, dst, send, recv, device):
    return pltpu.make_async_remote_copy(
        src_ref=src,
        dst_ref=dst,
        send_sem=send,
        recv_sem=recv,
        device_id=device,
        device_id_type=pl.DeviceIdType.MESH,
    )


def greet(devices):
    barrier = pltpu.get_barrier_semaphore()
    for device in devices:
        pl.semaphore_signal(
            barrier, inc=1, device_id=device, device_id_type=pl.DeviceIdType.MESH
        )
    pl.semaphore_wait(barrier, len(devices))


def other_heads():
    n = lax.axis_size("head")
    me = lax.axis_index("head")
    return [{"head": (me + d) % n} for d in range(1, n)]


def other_parts():
    m = lax.axis_size("fsdp")
    f = lax.axis_index("fsdp")
    return [{"fsdp": (f + d) % m} for d in range(1, m)]


class Ring:
    def __init__(self, own, place, send, recv, n):
        self.own, self.place, self.send, self.recv = own, place, send, recv
        self.half = n // 2

    def exists(self, way, step, c):
        return step < self.half or c == way

    def message(self, way, step, c):
        owner = head_at((1 - step) if way == 0 else (step - 1))
        return remote(
            self.own(c) if step == 1 else self.place(owner, c),
            self.place(owner, c),
            self.send.at[way, step - 1, c],
            self.recv.at[way, step - 1, c],
            {"head": head_at(1 if way == 0 else -1)},
        )

    def start(self):
        for c in range(2):
            for way in range(2):
                if self.exists(way, 1, c):
                    self.message(way, 1, c).start()

    def step(self, step):
        for c in range(2):
            for way in range(2):
                if self.exists(way, step, c):
                    self.message(way, step, c).wait_recv()
                    if step < self.half and self.exists(way, step + 1, c):
                        self.message(way, step + 1, c).start()

    def finish(self):
        for step in range(1, self.half + 1):
            for c in range(2):
                for way in range(2):
                    if self.exists(way, step, c):
                        self.message(way, step, c).wait_send()


def ring_sems(n):
    return [DMA((2, n // 2, 2)), DMA((2, n // 2, 2))]


class Carry:
    def __init__(self, kinds, ins, outs, send, recv, *joins):
        self.jobs, k = [], 0
        stages = list(joins)
        for kind, dst in zip(kinds, outs):
            name = kind if isinstance(kind, str) else kind[0]
            if name == "join":
                self.jobs.append((name, stages.pop(0), dst, kind[1:], ins[k : k + 2]))
                k += 2
                continue
            src = ins[k] if isinstance(kind, str) else ins[k].at[kind[1]]
            self.jobs.append((name, src, dst, None, None))
            k += 1
        self.tmp, self.j_sem = stages if stages else (None, None)
        self.fetched = None
        self.send, self.recv = send, recv

    def copies(self, j):
        m = lax.axis_size("fsdp")
        f = lax.axis_index("fsdp")
        nx = m // 2
        x, core = f // 2, f % 2
        name, src, dst = self.jobs[j][:3]
        if name == "pair":
            other = {"fsdp": x * 2 + 1 - core}
            return [remote(src, dst, self.send.at[j, 0], self.recv.at[j, 0], other)]
        return [
            remote(
                src if name == "share" else src.at[i - 1], dst.at[i - 1],
                self.send.at[j, i - 1], self.recv.at[j, i - 1],
                {"fsdp": ((x + i) % nx) * 2 + core},
            )
            for i in range(1, nx)
        ]

    def fetch(self, j):
        _, stage, _, (a, b), arrays = self.jobs[j]
        tmp = self.tmp.at[:, pl.ds(0, b - a)]
        self.fetched = [
            pltpu.make_async_copy(
                arrays[i].at[pl.ds(1, stage.shape[0]), pl.ds(a, b - a)], (stage, tmp)[i],
                self.j_sem.at[i],
            )
            for i in range(2)
        ]
        for c in self.fetched:
            c.start()

    def first(self):
        if self.jobs and self.jobs[0][0] == "join":
            self.fetch(0)

    def join(self, j):
        _, stage, _, (a, b), _ = self.jobs[j]
        if self.fetched is None:
            self.fetch(j)
        for c in self.fetched:
            c.wait()
        self.fetched = None
        for i in range(stage.shape[0]):
            for k in range(b - a):

                @pl.loop(0, stage.shape[2] // 64)
                def _(r, i=i, k=k):
                    at = pl.ds(pl.multiple_of(r * 64, 64), 64)
                    stage[i, k, at] = (
                        stage[i, k, at].astype(F32) + self.tmp[i, k, at].astype(F32)
                    ).astype(BF)

    def begin(self, some=None):
        for j in range(len(self.jobs)) if some is None else some:
            if self.jobs[j][0] == "join":
                self.join(j)
            for c in self.copies(j):
                c.start()

    def arrived(self, j):
        for c in self.copies(j):
            c.wait_recv()

    def end(self, seen=()):
        for j in range(len(self.jobs)):
            for c in self.copies(j):
                if j not in seen:
                    c.wait_recv()
                c.wait_send()


def carry_plan(kinds, arrays, m):
    shapes, stages, k = [], [], 0
    for kind in kinds:
        if kind[0] == "join":
            a, b = kind[1:]
            shape = (m // 2 - 1, b - a) + arrays[k].shape[2:]
            stages.append(shape)
            k += 2
        else:
            name = kind if isinstance(kind, str) else kind[0]
            shape = arrays[k].shape if isinstance(kind, str) else arrays[k].shape[1:]
            shape = (m // 2 - 1,) * (name == "share") + shape
            k += 1
        shapes.append(jax.ShapeDtypeStruct(shape, BF))
    sems = (max(len(kinds), 1), max(m // 2 - 1, 1))
    scratch = [DMA(sems), DMA(sems)] + [pltpu.VMEM(shape, BF) for shape in stages]
    if stages:
        widest = max(stages, key=lambda shape: shape[1])
        scratch += [pltpu.VMEM(widest, BF), DMA((2,))]
    return k, shapes, scratch


def carried(kinds):
    joins = sum(kind[0] == "join" for kind in kinds)
    return len(kinds) + joins, 2 + joins + 2 * (joins > 0)


def gather_kernel(n, kinds, more, x_ref, extra, *refs):
    count, scratch = carried(kinds)
    second, refs = refs[: len(more)], refs[len(more) :]
    carry = Carry(
        kinds, refs[:count], refs[count + 2 : count + 2 + len(kinds)], *refs[-scratch:]
    )
    out_ref, extra_out = refs[count : count + 2]
    refs = refs[count + 2 + len(kinds) :]
    seconds, refs = refs[: len(more)], refs[len(more) :]
    send, recv, copies, e_send, e_recv = refs[:5]
    rows = x_ref.shape[0] // 2
    me = lax.axis_index("head")
    greet(other_heads() + other_parts())
    ring = Ring(
        lambda c: x_ref.at[pl.ds(c * rows, rows)],
        lambda h, c: out_ref.at[h, pl.ds(c * rows, rows)],
        send, recv, n,
    )
    ring.start()
    carry.begin()
    moves = [
        pltpu.make_async_copy(x_ref, out_ref.at[me], copies.at[0]),
        pltpu.make_async_copy(extra.at[me], extra_out.at[me], copies.at[1]),
    ] + [
        remote(extra.at[dev["head"]], extra_out.at[me], e_send.at[d], e_recv.at[d], dev)
        for d, dev in enumerate(other_heads())
    ]
    for c in moves:
        c.start()
    for step in range(1, n // 2):
        ring.step(step)
    others = [
        Ring(
            lambda c, a=a: a.at[pl.ds(c * rows, rows)],
            lambda h, c, b=b: b.at[h, pl.ds(c * rows, rows)],
            refs[5 + 3 * i], refs[6 + 3 * i], n,
        )
        for i, (a, b) in enumerate(zip(second, seconds))
    ]
    for i, other in enumerate(others):
        other.start()
        moves.append(pltpu.make_async_copy(second[i], seconds[i].at[me], refs[7 + 3 * i].at[0]))
        moves[-1].start()
    ring.step(n // 2)
    for other in others:
        for step in range(1, n // 2 + 1):
            other.step(step)
    for c in moves:
        c.wait()
    for r in [ring] + others:
        r.finish()
    carry.end()


def gather(x, extra, n, m, identity, kinds=(), arrays=(), more=()):
    count, shapes, scratch = carry_plan(kinds, arrays, m)
    return pl.pallas_call(
        functools.partial(gather_kernel, n, kinds, more),
        out_shape=[
            jax.ShapeDtypeStruct((n,) + x.shape, x.dtype),
            jax.ShapeDtypeStruct(extra.shape, extra.dtype),
        ]
        + shapes
        + [jax.ShapeDtypeStruct((n,) + a.shape, a.dtype) for a in more],
        in_specs=[WHOLE] * (2 + len(more)) + [ANY] * count,
        out_specs=[ANY] * (2 + len(kinds) + len(more)),
        scratch_shapes=ring_sems(n)
        + [DMA((2,)), DMA((n - 1,)), DMA((n - 1,))]
        + (ring_sems(n) + [DMA((1,))]) * len(more)
        + scratch,
        compiler_params=pltpu.CompilerParams(collective_id=identity, has_side_effects=True),
        cost_estimate=cost(42),
    )(x, extra, *more, *arrays)


class RingSum:
    def __init__(self, n, parts, out_ref, own, sbuf, rbuf, loads, send, recv):
        self.n, self.half, self.parts, self.out_ref = n, n // 2, parts, out_ref
        self.own, self.sbuf, self.rbuf, self.loads = own, sbuf, rbuf, loads
        self.send, self.recv = send, recv
        self.rows = out_ref.shape[0] // 2
        self.order = (
            [self.half] + [s * w for s in range(self.half - 1, 0, -1) for w in (1, -1)] + [0]
        )
        self.ready, self.started = set(), []

    def fetch(self, o):
        i = self.order.index(o)
        return pltpu.make_async_copy(self.parts.at[head_at(o)], self.own.at[i], self.loads.at[i])

    def load(self):
        for o in self.order:
            self.fetch(o).start()

    def piece(self, o, c):
        if o not in self.ready:
            self.fetch(o).wait()
            self.ready.add(o)
        return self.own[self.order.index(o), pl.ds(c * self.rows, self.rows)].astype(F32)

    def buffer(self, way, t, c):
        first = 1 if c == way else 2
        return self.sbuf.at[way, t - 1] if t == first else self.rbuf.at[way, t - 2, c]

    def message(self, way, t, c):
        return remote(
            self.buffer(way, t, c), self.rbuf.at[way, t - 1, c],
            self.send.at[way, t - 1, c], self.recv.at[way, t - 1, c],
            {"head": head_at(1 if way == 0 else -1)},
        )

    def offset(self, way, o):
        return o if way == 0 or o == self.half else -o

    def ship(self, way, t, c, value):
        self.buffer(way, t, c)[...] = value.astype(BF)
        self.message(way, t, c).start()
        self.started.append((way, t, c))

    def start(self):
        for way in range(2):
            self.ship(way, 1, way, self.piece(self.half, way))
        for way in range(2):
            self.ship(way, 2, 1 - way, self.piece(self.offset(way, self.half - 1), 1 - way))

    def step(self, t):
        if t < self.half:
            for c in range(2):
                for way in range(2):
                    if t == 1 and c != way:
                        continue
                    self.message(way, t, c).wait_recv()
                    self.ship(
                        way, t + 1, c,
                        self.piece(self.offset(way, self.half - t), c)
                        + self.rbuf[way, t - 1, c].astype(F32),
                    )
            return
        last = self.half - 1
        for c in range(2):
            for way in range(2):
                self.message(way, self.half, c).wait_recv()
            self.out_ref[pl.ds(c * self.rows, self.rows)] = (
                self.piece(0, c)
                + self.rbuf[0, last, c].astype(F32)
                + self.rbuf[1, last, c].astype(F32)
            )

    def finish(self):
        for way, t, c in self.started:
            self.message(way, t, c).wait_send()


def ring_sum_scratch(n, rows, width):
    return [
        pltpu.VMEM((n, rows, width), BF),
        pltpu.VMEM((2, 2, rows // 2, width), BF),
        pltpu.VMEM((2, n // 2, 2, rows // 2, width), BF),
        DMA((n,)),
    ] + ring_sems(n)


def probs_of(len_ref, q, k):
    scores = dot(q, k, NT) * (1.0 / math.sqrt(HD))
    at = lax.broadcasted_iota(jnp.int32, scores.shape, 1)
    scores = jnp.where(at < len_ref[0], scores, NEGATIVE)
    exponent = jnp.exp(scores - jnp.max(scores, axis=-1, keepdims=True))
    return exponent / jnp.sum(exponent, axis=-1, keepdims=True)


def query_block(seq):
    return 256 if seq <= 1024 else 128


def as_column(row):
    return jnp.broadcast_to(row, (row.shape[1], row.shape[1])).T


def as_row(column):
    return jnp.broadcast_to(column, (column.shape[0], column.shape[0])).T[:1]


def turn(values, cosine, sine):
    return values * cosine + pltpu.roll(values, HD // 2, 1) * sine


def opening_kernel(n, m, kinds, *refs):
    k, _ = carried(kinds)
    len_ref, x_ref, w_ref, wo_ref, gain_ref, cos_ref, sin_ref = refs[:7]
    (ain_ref, qkv_ref, proj_ref, sums_ref, q_ref, k_ref, v_ref, att_ref, tok_ref, wout_ref,
     gall_ref) = refs[7 + k : 18 + k]
    (hid, qkv, wpair, gall, ain, buf, own, out_sem, copies, s_send, s_recv,
     w_send, w_recv, f_send, f_recv, g_send, g_recv, a_send, a_recv, o_send, o_recv,
     c_send, c_recv, t_send, t_recv, t_sem, h_send, h_recv, r_send, r_recv) = refs[18 + 2 * k : -2]
    carry = Carry(kinds, refs[7 : 7 + k], refs[18 + k : 18 + 2 * k], *refs[-2:])
    me = lax.axis_index("head")
    f = lax.axis_index("fsdp")
    nx = m // 2
    x, core = f // 2, f % 2
    rows, width = x_ref.shape
    dh = q_ref.shape[1]
    seq = n * rows
    qb = query_block(seq)
    part_rows = rows // 2

    def part(i, side):
        return ((x + i) % nx) * 2 + side

    pair = {"fsdp": part(0, 1 - core)}
    greet(other_heads() + other_parts())

    ring = Ring(
        lambda c: x_ref.at[pl.ds(c * part_rows, part_rows)],
        lambda h, c: hid.at[h, pl.ds(c * part_rows, part_rows)],
        h_send, h_recv, n,
    )
    to_parts = [
        remote(gain_ref, gall.at[me, f], g_send.at[d], g_recv.at[d], dev)
        for d, dev in enumerate(other_parts())
    ]
    outs = [
        remote(
            wo_ref, wpair.at[x], o_send.at[i - 1], o_recv.at[i - 1], {"fsdp": part(nx - i, core)}
        )
        for i in range(1, nx)
    ]
    columns = [
        remote(
            w_ref.at[:, pl.ds(pl.multiple_of(j * width + dev["head"] * dh, 128), dh)],
            qkv.at[me, f, :, pl.ds(j * dh, dh)],
            w_send.at[d, j],
            w_recv.at[d, j],
            dev,
        )
        for d, dev in enumerate(other_heads())
        for j in range(3)
    ]
    for c in to_parts + outs:
        c.start()
    carry.begin([0])
    ring.start()
    for c in columns:
        c.start()
    gall[me, f] = gain_ref[...]
    wpair[x] = wo_ref[...]
    hid[me] = x_ref[...]
    for j in range(3):
        qkv[me, f, :, pl.ds(j * dh, dh)] = w_ref[
            :, pl.ds(pl.multiple_of(j * width + me * dh, 128), dh)
        ]
    for c in to_parts:
        c.wait_recv()
    gains = [
        remote(gall.at[me], gall.at[me], a_send.at[d], a_recv.at[d], dev)
        for d, dev in enumerate(other_heads())
    ]
    for c in gains:
        c.start()
    for c in gains:
        c.wait_recv()

    def gain_row(k):
        return jnp.concatenate(
            [
                sum(gall[h, i * fs + j, k : k + 1, :] for j in range(fs))
                for h in range(n)
                for i in range(m // fs)
            ],
            axis=1,
        )

    fs = 128 // w_ref.shape[0]
    gain_attn = gain_row(0)
    stores = []

    def store(src, dst, sem):
        stores.append(pltpu.make_async_copy(src, dst, sem))
        stores[-1].start()

    def normalise(i, slot):
        wide = hid[i].astype(F32)
        inv = lax.rsqrt(jnp.mean(wide * wide, axis=-1, keepdims=True) + EPS)
        ain[i] = (wide * inv * gain_attn).astype(BF)
        store(ain.at[i], ain_ref.at[i], out_sem.at[slot])

    normalise(me, 0)
    for c in columns:
        c.wait_recv()
    across = [
        remote(qkv.at[:, f], qkv.at[:, f], f_send.at[i], f_recv.at[i], {"fsdp": part(nx - i, core)})
        for i in range(1, nx)
    ]
    for c in across:
        c.start()
    carry.begin(range(1, len(carry.jobs)))

    def beside(i):
        there = qkv.at[:, part(i, core)]
        return remote(there, there, f_send.at[nx + i], f_recv.at[nx + i], pair)

    beside(0).start()
    for step in range(1, n // 2):
        ring.step(step)
        normalise(head_at(step), 2 * step - 1)
        normalise(head_at(-step), 2 * step)

    halves = nx // 2
    for c in outs:
        c.wait_recv()
    wring = Ring(
        lambda c: wpair.at[pl.ds(c * halves, halves)],
        lambda h, c: wout_ref.at[h, pl.ds(c * halves, halves), core],
        r_send, r_recv, n,
    )
    wring.start()
    mine = pltpu.make_async_copy(wpair, wout_ref.at[me, :, core], copies.at[0])
    mine.start()

    def over(offset, slot):
        there = wout_ref.at[head_at(offset), :, core]
        return remote(there, there, c_send.at[slot], c_recv.at[slot], pair)

    def advance(step):
        wring.step(step)
        if step < n // 2:
            over(step, 2 * step - 1).start()
            over(-step, 2 * step).start()
        else:
            over(step, n - 1).start()

    ring.step(n // 2)
    normalise(head_at(n // 2), n - 1)
    for i, c in enumerate(across):
        c.wait_recv()
        beside(i + 1).start()
    mine.wait()
    over(0, 0).start()
    for i in range(nx):
        beside(i).wait_recv()
    store(qkv, qkv_ref, copies.at[1])
    weight = qkv.reshape(width, 3 * dh)
    for g in range(n // 2):
        at = pl.ds(g * 2 * rows, 2 * rows)
        projected = dot(ain[2 * g : 2 * g + 2].reshape(2 * rows, width), weight[...])
        proj_ref[at, :] = projected[:, : 2 * dh]
        v_ref[at, :] = projected[:, 2 * dh :].astype(BF)
        for k in range(2):
            squares = projected[:, k * dh : (k + 1) * dh]
            squares = jnp.sum(squares * squares, axis=1, keepdims=True)
            for j in range(2):
                own[pl.ds(k * n + 2 * g + j, 1), :] = as_row(squares[j * rows : (j + 1) * rows])
    moves = [
        remote(own, buf.at[me], s_send.at[d], s_recv.at[d], dev)
        for d, dev in enumerate(other_heads())
    ]
    for c in moves:
        c.start()
    buf[me] = own[...]
    gain_q, gain_k = (
        jnp.concatenate(
            [
                sum(gall[me, i * fs + j, k : k + 1, :] for j in range(fs))
                for i in range(m // fs)
            ],
            axis=1,
        )
        for k in (2, 3)
    )
    gall_ref[...] = gall[...]
    for c in moves:
        c.wait()
    total_of = buf[0]
    for i in range(1, n):
        total_of = total_of + buf[i]
    sums_ref[...] = total_of
    inv_all = lax.rsqrt(total_of / width + EPS)
    advance(1)
    for i in range(n):
        at = pl.ds(i * rows, rows)
        inv_q = as_column(inv_all[i : i + 1])
        inv_k = as_column(inv_all[n + i : n + i + 1])
        cosine = cos_ref[at, :]
        sine = sin_ref[at, :]
        for head in range(dh // HD):
            lanes = pl.ds(head * HD, HD)
            k_lanes = pl.ds(dh + head * HD, HD)
            span = slice(head * HD, (head + 1) * HD)
            q_ref[at, lanes] = turn(
                proj_ref[at, lanes] * inv_q * gain_q[:, span], cosine, sine
            ).astype(BF)
            k_ref[at, lanes] = turn(
                proj_ref[at, k_lanes] * inv_k * gain_k[:, span], cosine, sine
            ).astype(BF)
    to = tok_ref.at[:, pl.ds(pl.multiple_of(me * dh, 128), dh)]

    def leave(h):
        return remote(att_ref.at[pl.ds(h * rows, rows)], to, t_send.at[h], t_recv.at[me], {"head": h})

    def arrive(h):
        return remote(
            att_ref.at[pl.ds(h * rows, rows)], tok_ref.at[:, pl.ds(h * dh, dh)],
            t_send.at[h], t_recv.at[h], {"head": h},
        )

    def stay(h):
        return pltpu.make_async_copy(att_ref.at[pl.ds(h * rows, rows)], to, t_sem.at[h])

    for j in range(seq // qb):
        at = pl.ds(j * qb, qb)
        for head in range(dh // HD):
            lanes = pl.ds(head * HD, HD)
            probs = probs_of(len_ref, q_ref[at, lanes], k_ref[:, lanes])
            att_ref[at, lanes] = dot(probs.astype(BF), v_ref[:, lanes]).astype(BF)
        for h in range(j * qb // rows, (j + 1) * qb // rows):

            @pl.when(me != h)
            def _(h=h):
                leave(h).start()

            @pl.when(me == h)
            def _(h=h):
                stay(h).start()

        if j == 1:
            advance(2)
    for step in range(3, n // 2 + 1):
        advance(step)
    for h in range(n):

        @pl.when(me != h)
        def _(h=h):
            leave(h).wait_send()
            arrive(h).wait_recv()

        @pl.when(me == h)
        def _(h=h):
            stay(h).wait()

    for c in stores:
        c.wait()
    for slot in range(n):
        over(0, slot).wait_recv()
    over(0, 0).wait_send()
    for step in range(1, n // 2):
        over(step, 2 * step - 1).wait_send()
        over(-step, 2 * step).wait_send()
    over(n // 2, n - 1).wait_send()
    for c in to_parts + outs + columns + gains + across:
        c.wait_send()
    for i in range(nx):
        beside(i).wait_send()
    ring.finish()
    wring.finish()
    carry.end()


def opening(lengths, x, w, w_out, gains, cosine, sine, n, m, kinds, arrays):
    rows, width = x.shape
    seq = n * rows
    shard = w.shape[0]
    dh = w.shape[1] // 3 // n
    heads = jax.ShapeDtypeStruct((seq, dh), BF)
    count, shapes, scratch = carry_plan(kinds, arrays, m)
    return pl.pallas_call(
        functools.partial(opening_kernel, n, m, kinds),
        out_shape=[
            jax.ShapeDtypeStruct((n, rows, width), BF),
            jax.ShapeDtypeStruct((n, m, shard, 3 * dh), BF),
            jax.ShapeDtypeStruct((seq, 2 * dh), F32),
            jax.ShapeDtypeStruct((2 * n, rows), F32),
            heads, heads, heads, heads,
            jax.ShapeDtypeStruct((rows, width), BF),
            jax.ShapeDtypeStruct((n, m // 2, 2, shard, width), BF),
            jax.ShapeDtypeStruct((n, m) + gains.shape, F32),
        ]
        + shapes,
        in_specs=[pl.BlockSpec(memory_space=pltpu.SMEM)] + [WHOLE] * 6 + [ANY] * count,
        out_specs=[ANY] * 2 + [WHOLE] * 6 + [ANY] * 2 + [WHOLE] + [ANY] * count,
        scratch_shapes=[
            pltpu.VMEM((n, rows, width), BF),
            pltpu.VMEM((n, m, shard, 3 * dh), BF),
            pltpu.VMEM((m // 2, shard, width), BF),
            pltpu.VMEM((n, m) + gains.shape, F32),
            pltpu.VMEM((n, rows, width), BF),
            pltpu.VMEM((n, 2 * n, rows), F32),
            pltpu.VMEM((2 * n, rows), F32),
            DMA((n,)), DMA((2,)), DMA((n - 1,)), DMA((n - 1,)),
            DMA((n - 1, 3)), DMA((n - 1, 3)), DMA((m,)), DMA((m,)), DMA((m - 1,)), DMA((m - 1,)),
            DMA((n - 1,)), DMA((n - 1,)), DMA((m // 2,)), DMA((m // 2,)),
            DMA((n,)), DMA((n,)), DMA((n,)), DMA((n,)), DMA((n,)),
        ]
        + ring_sems(n)
        + ring_sems(n)
        + scratch,
        compiler_params=pltpu.CompilerParams(
            collective_id=0, has_side_effects=True, vmem_limit_bytes=56 << 20
        ),
        cost_estimate=cost(100),
    )(lengths, x, w, w_out, gains, cosine, sine, *arrays)


def weave(chunks, polls):
    whole = sum(w for w, _ in chunks)
    done, k = 0.0, 0
    for weight, run in chunks:
        run()
        done += weight
        while k < len(polls) - 1 and done * len(polls) >= (k + 1) * whole:
            polls[k]()
            k += 1
    for poll in polls[k:]:
        poll()


def span_of(seq):
    return seq if seq <= 512 else 256


def source_order(m):
    f = lax.axis_index("fsdp")
    nx = m // 2
    x, core = f // 2, f % 2
    return [((x + i) % nx) * 2 + (core + side) % 2 for side in range(2) for i in range(nx)]


def piece_of(kept, r, nx):
    side, i = divmod(r, nx)
    return kept[2 * side] if i == 0 else kept[2 * side + 1].at[nx - 1 - i]


class Weights:
    def __init__(self, m, kept, bufs, sems):
        self.m, self.kept, self.bufs, self.sems = m, kept, bufs, sems

    def copies(self, key):
        m, nx = self.m, self.m // 2
        order = source_order(m)
        gate, up, down = self.bufs
        g_sem, d_sem = self.sems
        block, tile = gate.shape[0] // m, down.shape[0] // m
        rows = lambda r, size: pl.ds(pl.multiple_of(order[r] * size, size), size)
        if key == "down":
            return [
                pltpu.make_async_copy(
                    piece_of(self.kept[2], r, nx), down.at[rows(r, tile)], d_sem.at[r]
                )
                for r in range(m)
            ]
        cols = pl.ds(key * tile, tile)
        return [
            pltpu.make_async_copy(
                piece_of(self.kept[i], r, nx).at[:, cols], v.at[rows(r, block), cols],
                g_sem.at[i, r, key],
            )
            for i, v in enumerate((gate, up))
            for r in range(m)
        ]

    def start(self, key):
        for c in self.copies(key):
            c.start()

    def wait(self, key):
        for c in self.copies(key):
            c.wait()


def front_chunk(t, x, weights, pre):
    gate_v, up_v, down_v = weights.bufs
    tile = down_v.shape[0] // weights.m
    cols = pl.ds(t * tile, tile)
    weights.wait(t)
    pre[0, :, cols] = dot(x[...], gate_v[:, cols])
    pre[1, :, cols] = dot(x[...], up_v[:, cols])


def forward_chunk(e, t, x, cot, gates_ref, at, weights, acts, dots_ref, first, pre=None):
    gate_v, up_v, down_v = weights.bufs
    tile = down_v.shape[0] // weights.m
    cols = pl.ds(t * tile, tile)
    if t == 0:
        weights.wait("down")
    if pre is None:
        weights.wait(t)
        gate_pre = dot(x[...], gate_v[:, cols])
        up_pre = dot(x[...], up_v[:, cols])
    else:
        gate_pre = pre[0, :, cols]
        up_pre = pre[1, :, cols]
    back = dot(cot[...], down_v[cols, :], NT)
    gate = gates_ref[at, e : e + 1]
    sig = 1.0 / (1.0 + jnp.exp(-gate_pre))
    silu = gate_pre * sig
    value = silu * up_pre
    dots = jnp.sum(value * back, axis=1, keepdims=True)
    if first:
        dots_ref[at, e : e + 1] = dots
    else:
        dots_ref[at, e : e + 1] += dots
    grad_act = gate * back
    acts[e, 0, :, cols] = (gate * value).astype(BF)
    acts[e, 1, :, cols] = (grad_act * up_pre * sig * (1.0 + gate_pre * (1.0 - sig))).astype(BF)
    acts[e, 2, :, cols] = (grad_act * silu).astype(BF)


def experts_steps(m, x_ref, cot_ref, gates_ref, weights, x, cot, acts, stage, pre,
                  dots_ref, acts_ref, gin_ref, mix_ref, in_sem, a_sem, o_sem, polls, between, more=()):
    seq, width = x_ref.shape
    span = x.shape[0]
    spans = seq // span
    chunks = []
    stores = []

    def copy(store):
        store.start()
        stores.append(store)

    for q in range(spans):
        at = pl.ds(q * span, span)
        load_x = pltpu.make_async_copy(x_ref.at[at], x, in_sem.at[0])
        load_cot = pltpu.make_async_copy(cot_ref.at[at], cot, in_sem.at[1])

        def load(q=q, load_x=load_x, load_cot=load_cot):
            if q:
                while stores:
                    stores.pop().wait()
                load_x.start()
                load_cot.start()
            load_x.wait()
            load_cot.wait()

        if q == 0:
            load_x.start()
            for w in weights:
                if w is weights[0]:
                    w.start(0)
                    load_cot.start()
                    w.start("down")
                    for t in range(1, m):
                        w.start(t)
            between(0)
        chunks.append((0.1, load))
        for e in range(EXP_DEV):
            late = e == EXP_DEV - 1

            def front(t, e=e, q=q):
                if q == 0 and t == m - 1:
                    between(2)
                if q:
                    weights[e].wait = lambda key: None
                front_chunk(t, x, weights[e], pre)

            if late:
                for t in range(m):
                    chunks.append((1.1 * 4 / m, functools.partial(front, t)))
            for t in range(m):

                def run(e=e, t=t, q=q, at=at, late=late):
                    if q == 0 and not late and t == m // 2:
                        between(1)
                    if q == 0 and late and t == 0:
                        between(3)
                    if q:
                        weights[e].wait = lambda key: None
                    forward_chunk(
                        e, t, x, cot, gates_ref, at, weights[e], acts, dots_ref, t == 0,
                        pre if late else None,
                    )

                chunks.append(((0.6 if late else 1.6) * 4 / m, run))

            def keep(e=e, at=at):
                copy(pltpu.make_async_copy(acts.at[e], acts_ref.at[e, :, at], a_sem.at[e]))

            chunks.append((0.0, keep))
        for r in range(width // 512):

            def run(r=r, at=at):
                lanes = pl.ds(r * 512, 512)
                mixed, grads = None, None
                for e in range(EXP_DEV):
                    gate_v, up_v, down_v = weights[e].bufs
                    a = dot(acts[e, 0], down_v[:, lanes])
                    b = dot(acts[e, 1], gate_v[lanes, :], NT) + dot(acts[e, 2], up_v[lanes, :], NT)
                    mixed = a if mixed is None else mixed + a
                    grads = b if grads is None else grads + b
                stage[0, :, lanes] = grads.astype(BF)
                stage[1, :, lanes] = mixed.astype(BF)
                for i, to in enumerate((gin_ref, mix_ref)):
                    copy(
                        pltpu.make_async_copy(
                            stage.at[i, :, lanes], to.at[at, lanes], o_sem.at[i, r]
                        )
                    )

            chunks.append((3.2, run))
    weave(chunks + list(more), polls)
    for c in stores:
        c.wait()


def experts_scratch(m, seq, width, ff):
    span = span_of(seq)
    return [
        pltpu.VMEM((EXP_DEV, width, ff), BF),
        pltpu.VMEM((EXP_DEV, width, ff), BF),
        pltpu.VMEM((EXP_DEV, ff, width), BF),
        DMA((EXP_DEV, 2, m, m)),
        DMA((EXP_DEV, m)),
        pltpu.VMEM((span, width), BF),
        pltpu.VMEM((span, width), BF),
        pltpu.VMEM((EXP_DEV, 3, span, ff), BF),
        pltpu.VMEM((2, span, width), BF),
        pltpu.VMEM((2, span, ff), F32),
        DMA((2,)), DMA((EXP_DEV,)), DMA((2, width // 512)),
    ]


def weights_of(e, m, kept, gate_v, up_v, down_v, g_sem, d_sem):
    return Weights(
        m, kept, (gate_v.at[e], up_v.at[e], down_v.at[e]), (g_sem.at[e], d_sem.at[e])
    )


LATE = (("share", 1), "pair", "pair", "pair")


def experts_a_kernel(n, m, *refs):
    x_ref, cot_ref, gates_ref = refs[:3]
    wg, wu, wd = refs[3:6]
    w0, fresh, (xb_own, cotb_own) = refs[6:15], refs[15:20], refs[20:22]
    dots_ref, acts_ref, gin_ref, mix_ref, xb_ref, cotb_ref, down1x, gate1c, up1c, down1c = refs[22:32]
    scratch, rest = refs[32:45], refs[45:]
    gate_v, up_v, down_v, g_sem, d_sem = scratch[:5]
    send0, recv0, send1, recv1, l_sem, c_send, c_recv = rest
    half = xb_own.shape[0] // 2
    me = lax.axis_index("head")
    gate1x, gate1o, up1x, up1o, down1o = fresh
    g1 = (wg.at[1], gate1x, gate1o, gate1c)
    u1 = (wu.at[1], up1x, up1o, up1c)
    d1 = (wd.at[1], down1x, down1o, down1c)
    kept0 = [(w.at[0],) + tuple(w0[3 * i : 3 * i + 3]) for i, w in enumerate((wg, wu, wd))]
    weights = [
        weights_of(0, m, kept0, gate_v, up_v, down_v, g_sem, d_sem),
        weights_of(1, m, (g1, u1, d1), gate_v, up_v, down_v, g_sem, d_sem),
    ]
    carry = Carry(
        LATE, (wd, gate1x, up1x, down1x), (down1x, gate1c, up1c, down1c), c_send, c_recv
    )

    def ring_of(own, out, send, recv):
        return Ring(
            lambda c: own.at[pl.ds(c * half, half)],
            lambda h, c: out.at[h, pl.ds(c * half, half)],
            send, recv, n,
        )

    rings = [ring_of(xb_own, xb_ref, send0, recv0), ring_of(cotb_own, cotb_ref, send1, recv1)]
    mine = [
        pltpu.make_async_copy(xb_own, xb_ref.at[me], l_sem.at[0]),
        pltpu.make_async_copy(cotb_own, cotb_ref.at[me], l_sem.at[1]),
    ]

    def between(stage):
        if stage == 0:
            greet([{"head": head_at(1)}, {"head": head_at(-1)}] + other_parts())
            for ring in rings:
                ring.start()
            carry.begin(range(3))
            for c in mine:
                c.start()
        elif stage == 1:
            for j in (1, 2):
                carry.arrived(j)
            for key in range(m):
                weights[1].start(key)
        elif stage == 2:
            carry.arrived(0)
            carry.begin([3])
        else:
            carry.arrived(3)
            weights[1].start("down")

    def poll(step):
        for ring in rings:
            ring.step(step)

    experts_steps(
        m, x_ref, cot_ref, gates_ref, weights, *scratch[5:10], dots_ref, acts_ref, gin_ref, mix_ref,
        *scratch[10:13], [functools.partial(poll, s) for s in range(1, n // 2 + 1)], between,
    )
    for c in mine:
        c.wait()
    for ring in rings:
        ring.finish()
    carry.end(seen=range(4))


def row_outputs(x, ff):
    seq, width = x.shape
    return [
        jax.ShapeDtypeStruct((seq, EXP_DEV), F32),
        jax.ShapeDtypeStruct((EXP_DEV, 3, seq, ff), BF),
        jax.ShapeDtypeStruct((seq, width), BF),
        jax.ShapeDtypeStruct((seq, width), BF),
    ]


def big(us, identity):
    return dict(
        compiler_params=pltpu.CompilerParams(
            collective_id=identity, has_side_effects=True, vmem_limit_bytes=60 << 20
        ),
        cost_estimate=cost(us),
    )


def experts_a(x, cot, gates, weights, weights0, fresh, x_b, cot_b, n, m):
    seq, width = x.shape
    ff = fresh[0].shape[-1]
    w0 = [a for kept in weights0 for a in kept]
    out = jax.ShapeDtypeStruct((n,) + x_b.shape, BF)
    gate1x, up1x = fresh[0], fresh[2]
    moved = (weights[2], gate1x, up1x)
    late = [jax.ShapeDtypeStruct((m // 2 - 1,) + weights[2].shape[1:], BF)]
    late += [jax.ShapeDtypeStruct(a.shape, BF) for a in moved[1:]] + late
    return pl.pallas_call(
        functools.partial(experts_a_kernel, n, m),
        out_shape=row_outputs(x, ff) + [out, out] + late,
        in_specs=[ANY, ANY, WHOLE] + [ANY] * 17 + [WHOLE] * 2,
        out_specs=[WHOLE] + [ANY] * 9,
        scratch_shapes=experts_scratch(m, seq, width, ff)
        + ring_sems(n)
        + ring_sems(n)
        + [DMA((2,))]
        + [DMA((4, max(m // 2 - 1, 1)))] * 2,
        **big(45, 4),
    )(x, cot, gates, *weights, *w0, *fresh, x_b, cot_b)


class Leave:
    def __init__(self, m, same, got, local, send, recv):
        self.m, self.same, self.got = m, same, got
        self.local, self.send, self.recv = local, send, recv
        self.stores, self.away = [], []

    def put(self, r, src, index, spot):
        nx = self.m // 2
        f = lax.axis_index("fsdp")
        if r < nx:
            self.stores.append(
                pltpu.make_async_copy(src, self.same.at[(r,) + index], self.local.at[r, spot])
            )
            self.stores[-1].start()
        else:
            self.away.append(
                remote(
                    src, self.got.at[(r - nx,) + index], self.send.at[r, spot],
                    self.recv.at[r, spot], {"fsdp": (f // 2) * 2 + 1 - f % 2},
                )
            )
            self.away[-1].start()

    def wide(self, i, v):
        order = source_order(self.m)
        block = v.shape[0] // self.m
        for r in range(self.m):
            at = pl.ds(pl.multiple_of(order[r] * block, block), block)
            self.put(r, v.at[at], (i,), i)

    def tall(self, v):
        order = source_order(self.m)
        tile, ff = v.shape[0] // self.m, v.shape[0]
        for r in range(self.m):
            at = pl.ds(pl.multiple_of(order[r] * tile, tile), tile)
            for side in range(2):
                self.put(
                    r, v.at[at, pl.ds(side * ff, ff)], (2, pl.ds(side * tile, tile)), 2 + side
                )

    def finish(self):
        for c in self.stores:
            c.wait()
        for c in self.away:
            c.wait()


def leave_sems(m):
    return [DMA((m, 4)), DMA((m, 4)), DMA((m, 4))]


def experts_b_kernel(n, m, early, *refs):
    x_ref, cot_ref, gates_ref = refs[:3]
    own, w, (gin_a, mix_a, xa_ref, cota_ref, acts_a) = refs[3:6], refs[6:24], refs[24:29]
    dots_ref, acts_ref, gin_ref, mix_ref, grad_ref, sum_ref = refs[29:35]
    refs = refs[35:]
    if early:
        (same, got), refs = refs[:2], refs[2:]
    scratch, rest = refs[:13], refs[13:]
    gate_v, up_v, down_v, g_sem, d_sem, x, cot, acts = scratch[:8]
    weights = [
        weights_of(
            e, m,
            [
                (own[i].at[e],) + tuple(w[9 * e + 3 * i : 9 * e + 3 * i + 3]) for i in range(3)
            ],
            gate_v, up_v, down_v, g_sem, d_sem,
        )
        for e in range(EXP_DEV)
    ]
    rings = [
        RingSum(n, gin_a, grad_ref, *rest[:6]),
        RingSum(n, mix_a, sum_ref, *rest[6:12]),
    ]

    def between(stage):
        if stage == 0:
            for ring in rings:
                ring.load()
            for key in [0, "down"] + list(range(1, m)):
                weights[1].start(key)
            f = lax.axis_index("fsdp")
            pair = [{"fsdp": (f // 2) * 2 + 1 - f % 2}] if early else []
            greet([{"head": head_at(1)}, {"head": head_at(-1)}] + pair)
            for ring in rings:
                ring.start()

    def poll(step):
        for ring in rings:
            ring.step(step)

    more = []
    if early:
        part = x.shape[0]
        leave = Leave(m, same, got, *rest[12:15])
        l_sem = rest[15]
        dgate, dup, ddown = gate_v.at[0], up_v.at[0], down_v.at[0]
        x_a, cot_a = down_v.at[1, pl.ds(0, part)], down_v.at[1, pl.ds(part, part)]
        kept = [gate_v.at[1, pl.ds(k * part, part)] for k in range(3)]
        loads = [
            pltpu.make_async_copy(xa_ref, x_a, l_sem.at[0]),
            pltpu.make_async_copy(cota_ref, cot_a, l_sem.at[1]),
        ] + [
            pltpu.make_async_copy(acts_a.at[0, k], kept[k], l_sem.at[2 + k]) for k in range(3)
        ]

        def begin():
            for c in loads:
                c.start()
            for c in loads:
                c.wait()

        more.append((0.5, begin))
        for b in range(x.shape[1] // 512):

            def run(b=b):
                at = pl.ds(b * 512, 512)
                turned, turned_a = x[:, at].T, x_a[:, at].T
                dgate[at, :] = (dot(turned, acts[0, 1]) + dot(turned_a, kept[1][...])).astype(BF)
                dup[at, :] = (dot(turned, acts[0, 2]) + dot(turned_a, kept[2][...])).astype(BF)

            more.append((2.4, run))
        more.append((0.0, lambda: (leave.wide(0, dgate), leave.wide(1, dup))))
        for t in range(gate_v.shape[2] // 256):

            def run(t=t):
                at = pl.ds(t * 256, 256)
                ddown[at, :] = (
                    dot(acts[0, 0, :, at].T, cot[...]) + dot(kept[0][:, at].T, cot_a[...])
                ).astype(BF)

            more.append((1.2, run))
        more.append((0.0, lambda: leave.tall(ddown)))
    experts_steps(
        m, x_ref, cot_ref, gates_ref, weights, *scratch[5:10], dots_ref, acts_ref, gin_ref, mix_ref,
        *scratch[10:13], [functools.partial(poll, s) for s in range(1, n // 2 + 1)], between, more,
    )
    for ring in rings:
        ring.finish()
    if early:
        leave.finish()


def experts_b(x, cot, gates, own_w, weights, gin_a, mix_a, x_a, cot_a, acts_a, n, m):
    seq, width = x.shape
    ff = own_w[0].shape[2]
    early = seq <= 512
    flat = [a for kept in weights for a in kept]
    rows = seq // n
    own = jax.ShapeDtypeStruct((rows, width), F32)
    parts = [a.reshape(n, rows, width) for a in (gin_a, mix_a)]
    grads = [jax.ShapeDtypeStruct((m // 2, 3, width // m, ff), BF)] * (2 * early)
    return pl.pallas_call(
        functools.partial(experts_b_kernel, n, m, early),
        out_shape=row_outputs(x, ff) + [own, own] + grads,
        in_specs=[ANY, ANY, WHOLE] + [ANY] * 26,
        out_specs=[WHOLE, ANY, ANY, ANY, WHOLE, WHOLE] + [ANY] * len(grads),
        scratch_shapes=experts_scratch(m, seq, width, ff)
        + ring_sum_scratch(n, rows, width)
        + ring_sum_scratch(n, rows, width)
        + (leave_sems(m) + [DMA((5,))]) * early,
        **big(60, 7),
    )(x, cot, gates, *own_w, *flat, *parts, x_a, cot_a, acts_a)


def experts_d_kernel(n, m, experts, kinds, *refs):
    xs, cots, all_acts = refs[0:6:3], refs[1:6:3], refs[2:6:3]
    gin_b, mix_b, extra = refs[6:9]
    (k, back), kk, g = carried(kinds), len(kinds), 2 * len(experts)
    outs, (grad_ref, sum_ref, extra_out) = refs[9 + k : 9 + k + g], refs[9 + k + g : 12 + k + g]
    carry = Carry(kinds, refs[9 : 9 + k], refs[12 + k + g : 12 + k + kk + g], *refs[-back:])
    (x, cot, acts, dgate, dup, ddown, x_sem, a_sem, copy, e_send, e_recv) = refs[
        12 + k + kk + g : 23 + k + kk + g
    ]
    rest = refs[23 + k + kk + g : -back]
    me = lax.axis_index("head")
    rows, width = x.shape
    part = rows // 2
    ff = acts.shape[2]
    rings = [
        RingSum(n, gin_b, grad_ref, *rest[:6]),
        RingSum(n, mix_b, sum_ref, *rest[6:12]),
    ]
    loads = [
        pltpu.make_async_copy(src[i], dst.at[pl.ds(i * part, part)], x_sem.at[k, i])
        for k, (src, dst) in enumerate(((xs, x), (cots, cot)))
        for i in range(2)
    ]

    def act_loads(e):
        return [
            pltpu.make_async_copy(
                all_acts[i].at[e], acts.at[:, pl.ds(i * part, part)], a_sem.at[i]
            )
            for i in range(2)
        ]

    carry.first()
    for ring in rings:
        ring.load()
    for c in loads + act_loads(experts[0]):
        c.start()
    greet(other_heads() + other_parts())
    carry.begin()
    for ring in rings:
        ring.start()
    direct = [pltpu.make_async_copy(extra.at[me], extra_out.at[me], copy.at[0])] + [
        remote(extra.at[dev["head"]], extra_out.at[me], e_send.at[d], e_recv.at[d], dev)
        for d, dev in enumerate(other_heads())
    ]
    for c in direct:
        c.start()
    chunks, leaves = [], []
    for j, e in enumerate(experts):
        leave = Leave(m, outs[2 * j], outs[2 * j + 1], *rest[12 + 3 * j : 15 + 3 * j])

        def begin(j=j, e=e):
            if j:
                leaves[j - 1].finish()
                for c in act_loads(e):
                    c.start()
            for c in (loads if j == 0 else []) + act_loads(e):
                c.wait()

        leaves.append(leave)
        chunks.append((0.1, begin))
        for b in range(width // 512):

            def run(b=b):
                at = pl.ds(b * 512, 512)
                turned = x[:, at].T
                dgate[at, :] = dot(turned, acts[1]).astype(BF)
                dup[at, :] = dot(turned, acts[2]).astype(BF)

            chunks.append((2.2, run))
        chunks.append(
            (0.0, lambda leave=leave: (leave.wide(0, dgate), leave.wide(1, dup)))
        )
        for t in range(ff // 256):

            def run(t=t):
                at = pl.ds(t * 256, 256)
                ddown[at, :] = dot(acts[0, :, at].T, cot[...]).astype(BF)

            chunks.append((1.1, run))
        chunks.append((0.0, lambda leave=leave: leave.tall(ddown)))

    def poll(step):
        for ring in rings:
            ring.step(step)

    weave(chunks, [functools.partial(poll, t) for t in range(1, n // 2 + 1)])
    for ring in rings:
        ring.finish()
    for c in direct:
        c.wait()
    leaves[-1].finish()
    carry.end()


def experts_d(first, second, gin_b, mix_b, dots, n, m, experts, kinds, arrays):
    seq = first[2].shape[2]
    ff = first[2].shape[3]
    rows, width = first[0].shape[1:]
    grads = jax.ShapeDtypeStruct((m // 2, 3, width // m, ff), BF)
    own = jax.ShapeDtypeStruct((rows, width), F32)
    (k, shapes, scratch), g = carry_plan(kinds, arrays, m), 2 * len(experts)

    def flat(parts):
        return [parts[0].reshape(seq, width), parts[1].reshape(seq, width), parts[2]]

    out = pl.pallas_call(
        functools.partial(experts_d_kernel, n, m, experts, kinds),
        out_shape=[grads] * g
        + [own, own, jax.ShapeDtypeStruct(dots.shape, F32)]
        + shapes,
        in_specs=[ANY] * 8 + [WHOLE] + [ANY] * k,
        out_specs=[ANY] * g + [WHOLE, WHOLE, ANY] + [ANY] * len(kinds),
        scratch_shapes=[
            pltpu.VMEM((2 * seq, width), BF),
            pltpu.VMEM((2 * seq, width), BF),
            pltpu.VMEM((3, 2 * seq, ff), BF),
            pltpu.VMEM((width, ff), BF),
            pltpu.VMEM((width, ff), BF),
            pltpu.VMEM((ff, width), BF),
            DMA((2, 2)), DMA((2,)), DMA((1,)), DMA((n - 1,)), DMA((n - 1,)),
        ]
        + ring_sum_scratch(n, rows, width)
        + ring_sum_scratch(n, rows, width)
        + leave_sems(m) * len(experts)
        + scratch,
        **big(45, 8),
    )(
        *flat(first), *flat(second), gin_b.reshape(n, rows, width), mix_b.reshape(n, rows, width),
        dots, *arrays,
    )
    return [tuple(out[2 * j : 2 * j + 2]) for j in range(g // 2)], *out[g : g + 3], out[g + 3 :]


class RingSumHere(RingSum):
    def __init__(self, n, parts, out_ref, sbuf, rbuf, send, recv):
        super().__init__(n, parts, out_ref, None, sbuf, rbuf, None, send, recv)

    def piece(self, o, c):
        return self.parts[head_at(o), pl.ds(c * self.rows, self.rows)].astype(F32)


def closing_kernel(n, m, kinds, early, *refs):
    (k, back), kk = carried(kinds), len(kinds)
    (len_ref, gatt_ref, gao_ref, q_ref, k_ref, v_ref, att_ref, proj_ref, sums_ref, gains_ref,
     cos_ref, sin_ref, ain_ref, qkv_ref) = refs[:14]
    (gin_ref, dqkv_ref, dout_ref, dgains_ref) = refs[14 + k : 18 + k]
    (gheads, gao, ain, qkv, gin, dproj, scaled, dk, dv, own, buf,
     dqkv, gq, xs, xr, fin, dout, go, xso, xro, sbuf, rbuf,
     l_sem, a_send, a_recv, s_send, s_recv, p_send, p_recv, x_send, x_recv, t_send, t_recv, t_sem,
     g_send, g_recv, r_send, r_recv) = refs[18 + k + kk : -back]
    carry = Carry(kinds, refs[14 : 14 + k], refs[18 + k : 18 + k + kk], *refs[-back:])
    me = lax.axis_index("head")
    f = lax.axis_index("fsdp")
    nx = m // 2
    x, core = f // 2, f % 2
    rows, width = gao_ref.shape
    half_rows = rows // 2
    seq, dh = q_ref.shape
    qb = query_block(seq)
    scale = 1.0 / math.sqrt(HD)
    order = source_order(m)
    carry.first()
    loads = [
        pltpu.make_async_copy(ain_ref, ain, l_sem.at[0]),
        pltpu.make_async_copy(qkv_ref, qkv, l_sem.at[1]),
    ]
    for c in loads:
        c.start()
    greet(other_heads() + other_parts())

    here = gheads.at[pl.ds(pl.multiple_of(me * rows, rows), rows)]
    sends = [
        remote(
            gatt_ref.at[:, pl.ds(pl.multiple_of(dev["head"] * dh, 128), dh)], here,
            a_send.at[d], a_recv.at[d], dev,
        )
        for d, dev in enumerate(other_heads())
    ]
    for c in sends:
        c.start()
    gring = Ring(
        lambda c: gao_ref.at[pl.ds(c * half_rows, half_rows)],
        lambda h, c: gao.at[h, pl.ds(c * half_rows, half_rows)],
        g_send, g_recv, n,
    )
    gring.start()
    carry.begin(range(early))
    here[...] = gatt_ref[:, pl.ds(pl.multiple_of(me * dh, 128), dh)]
    gao[me] = gao_ref[...]
    for c in sends:
        c.wait_recv()

    for head in range(dh // HD):
        lanes = pl.ds(head * HD, HD)
        for j in range(seq // qb):
            at = pl.ds(j * qb, qb)
            probs = probs_of(len_ref, q_ref[at, lanes], k_ref[:, lanes])
            grad_probs = dot(gheads[at, lanes], v_ref[:, lanes], NT)
            inner = jnp.sum(probs * grad_probs, axis=-1, keepdims=True)
            grad_scores = (probs * (grad_probs - inner)).astype(BF)
            dproj[at, lanes] = (dot(grad_scores, k_ref[:, lanes]) * scale).astype(BF)
            add_k = dot(grad_scores, q_ref[at, lanes], TN)
            add_v = dot(probs.astype(BF), gheads[at, lanes], TN)
            if j == 0:
                dk[...] = add_k
                dv[...] = add_v
            else:
                dk[...] += add_k
                dv[...] += add_v
        dproj[:, pl.ds(dh + head * HD, HD)] = (dk[...] * scale).astype(BF)
        dproj[:, pl.ds(2 * dh + head * HD, HD)] = dv[...].astype(BF)
        gring.step(head + 1)
    for step in range(dh // HD + 1, 3):
        gring.step(step)

    inv_all = lax.rsqrt(sums_ref[...] / width + EPS)
    dgains = [jnp.zeros((1, HD), F32) for _ in range(2 * dh // HD)]
    for i in range(n):
        at = pl.ds(i * rows, rows)
        cosine = cos_ref[at, :]
        sine = -sin_ref[at, :]
        for kind in range(2):
            inv = as_column(inv_all[kind * n + i : kind * n + i + 1])
            sums = jnp.zeros((rows, 1), F32)
            for head in range(dh // HD):
                spot = kind * (dh // HD) + head
                lanes = pl.ds(kind * dh + head * HD, HD)
                turned = turn(dproj[at, lanes].astype(F32), cosine, sine)
                unit = proj_ref[at, lanes] * inv
                dgains[spot] = dgains[spot] + jnp.sum(turned * unit, axis=0, keepdims=True)
                grad = turned * gains_ref[kind : kind + 1, head * HD : (head + 1) * HD]
                scaled[at, lanes] = grad
                sums = sums + jnp.sum(grad * unit, axis=1, keepdims=True)
            own[pl.ds(kind * n + i, 1), :] = as_row(sums)
    for spot, value in enumerate(dgains):
        dgains_ref[pl.ds(spot, 1), :] = value
    moves = [
        remote(own, buf.at[me], s_send.at[d], s_recv.at[d], dev)
        for d, dev in enumerate(other_heads())
    ]
    for c in moves:
        c.start()
    buf[me] = own[...]
    for c in moves:
        c.wait()
    total_of = buf[0]
    for i in range(1, n):
        total_of = total_of + buf[i]
    means = total_of / width
    for i in range(n):
        at = pl.ds(i * rows, rows)
        for kind in range(2):
            inv = as_column(inv_all[kind * n + i : kind * n + i + 1])
            mean = as_column(means[kind * n + i : kind * n + i + 1])
            for head in range(dh // HD):
                lanes = pl.ds(kind * dh + head * HD, HD)
                unit = proj_ref[at, lanes] * inv
                dproj[at, lanes] = (inv * (scaled[at, lanes] - unit * mean)).astype(BF)

    for c in loads:
        c.wait()
    weight = qkv.reshape(width, 3 * dh)
    for g in range(n // 2):
        part = dot(dproj[pl.ds(g * 2 * rows, 2 * rows), :], weight[...], NT).astype(BF)
        gin[2 * g : 2 * g + 2] = part.reshape(2, rows, width)
    gring.step(3)
    ring = RingSumHere(n, gin, gin_ref, sbuf, rbuf, r_send, r_recv)
    ring.start()

    flat = dqkv.reshape(width, 3 * dh)
    for b in range(width // 512):
        at = pl.ds(b * 512, 512)
        turned = ain.reshape(seq, width)[:, at].T
        flat[at, :] = dot(turned, dproj[...]).astype(BF)
    pair = {"fsdp": x * 2 + 1 - core}
    pairs = [
        remote(dqkv.at[:, order[nx + i]], gq.at[i], p_send.at[i], p_recv.at[i], pair)
        for i in range(nx)
    ]
    for c in pairs:
        c.start()
    for step in range(4, n // 2 + 1):
        gring.step(step)
    for b in range(width // 512):
        at = pl.ds(b * 512, 512)
        value = dot(att_ref[...], gao.reshape(seq, width)[:, at], TN)
        dout[:, :, at] = value.astype(BF).reshape(dout.shape[:2] + (512,))
    pairs_out = [
        remote(dout.at[order[nx + i]], go.at[i], p_send.at[nx + i], p_recv.at[nx + i], pair)
        for i in range(nx)
    ]
    for c in pairs_out:
        c.start()
    ring.step(1)
    for c in pairs + pairs_out:
        c.wait_recv()
    across = []
    for i in range(1, nx):
        there = {"fsdp": ((x + i) % nx) * 2 + core}
        xs[i - 1] = (dqkv[:, order[i]].astype(F32) + gq[i].astype(F32)).astype(BF)
        xso[i - 1] = (dout[order[i]].astype(F32) + go[i].astype(F32)).astype(BF)
        across.append(remote(xs.at[i - 1], xr.at[i - 1], x_send.at[0, i - 1], x_recv.at[0, i - 1], there))
        across.append(remote(xso.at[i - 1], xro.at[i - 1], x_send.at[1, i - 1], x_recv.at[1, i - 1], there))
    for c in across:
        c.start()
    carry.begin(range(early, len(carry.jobs)))
    for step in range(2, n // 2):
        ring.step(step)
    for c in across:
        c.wait_recv()
    value = dqkv[:, order[0]].astype(F32) + gq[0].astype(F32)
    value_out = dout[order[0]].astype(F32) + go[0].astype(F32)
    for i in range(1, nx):
        value = value + xr[i - 1].astype(F32)
        value_out = value_out + xro[i - 1].astype(F32)
    fin[...] = value.astype(BF)
    dout_ref[...] = value_out
    to = [
        dqkv_ref.at[:, pl.ds(pl.multiple_of(j * width + me * dh, 128), dh)] for j in range(3)
    ]
    last = [
        remote(
            fin.at[dev["head"], :, pl.ds(j * dh, dh)], to[j], t_send.at[d, j], t_recv.at[d, j], dev
        )
        for d, dev in enumerate(other_heads())
        for j in range(3)
    ] + [
        pltpu.make_async_copy(fin.at[me, :, pl.ds(j * dh, dh)], to[j], t_sem.at[j])
        for j in range(3)
    ]
    for c in last:
        c.start()
    ring.step(n // 2)
    for c in last:
        c.wait()
    for c in sends + pairs + pairs_out + across:
        c.wait_send()
    gring.finish()
    ring.finish()
    carry.end()


def closing(lengths, gatt, gao, q, k, v, att, proj, sums, gains, cosine, sine, ain, qkv, n, m, kinds,
            arrays, early):
    rows, width = gao.shape
    seq, dh = q.shape
    nx = m // 2
    shard = qkv.shape[2]
    count, shapes, scratch = carry_plan(kinds, arrays, m)

    def vm(*shape, dtype=BF):
        return pltpu.VMEM(shape, dtype)

    return pl.pallas_call(
        functools.partial(closing_kernel, n, m, kinds, early),
        out_shape=[
            jax.ShapeDtypeStruct((rows, width), F32),
            jax.ShapeDtypeStruct((shard, 3 * width), BF),
            jax.ShapeDtypeStruct((shard, width), F32),
            jax.ShapeDtypeStruct((2 * dh // HD, HD), F32),
        ]
        + shapes,
        in_specs=[pl.BlockSpec(memory_space=pltpu.SMEM)] + [WHOLE] * 11 + [ANY] * (2 + count),
        out_specs=[WHOLE, ANY, WHOLE, WHOLE] + [ANY] * len(kinds),
        scratch_shapes=[
            vm(seq, dh), vm(n, rows, width), vm(n, rows, width), vm(n, m, shard, 3 * dh),
            vm(n, rows, width), vm(seq, 3 * dh), vm(seq, 2 * dh, dtype=F32),
            vm(seq, HD, dtype=F32), vm(seq, HD, dtype=F32),
            vm(2 * n, rows, dtype=F32), vm(n, 2 * n, rows, dtype=F32),
            vm(n, m, shard, 3 * dh), vm(nx, n, shard, 3 * dh),
            vm(nx - 1, n, shard, 3 * dh), vm(nx - 1, n, shard, 3 * dh), vm(n, shard, 3 * dh),
            vm(m, shard, width), vm(nx, shard, width),
            vm(nx - 1, shard, width), vm(nx - 1, shard, width),
            vm(2, 2, rows // 2, width), vm(2, n // 2, 2, rows // 2, width),
            DMA((2,)), DMA((n - 1,)), DMA((n - 1,)), DMA((n - 1,)), DMA((n - 1,)),
            DMA((m,)), DMA((m,)), DMA((2, nx - 1)), DMA((2, nx - 1)),
            DMA((n - 1, 3)), DMA((n - 1, 3)), DMA((3,)),
        ]
        + ring_sems(n)
        + ring_sems(n)
        + scratch,
        **big(110, 5),
    )(lengths, gatt, gao, q, k, v, att, proj, sums, gains, cosine, sine, ain, qkv, *arrays)


def settle_kernel(jobs, *refs):
    count = sum(len(sources) for sources, _ in jobs)
    outs = refs[count : count + 3]
    ins, result, l_sem, o_sem = refs[count + 3 :]
    steps, k = [], 0
    for sources, (which, e, columns) in jobs:
        arrays = refs[k : k + len(sources)]
        k += len(sources)
        rows = sources[0][1]
        for part in range(1 if columns else 2):
            size = rows if columns else rows // 2
            steps.append((arrays, sources, part * size, size, which, e, columns))

    def loads(i):
        arrays, sources, start, size = steps[i][:4]
        return [
            pltpu.make_async_copy(
                ref.at[index + (pl.ds(base + start, size),)], ins.at[i % 2, j, pl.ds(0, size)],
                l_sem.at[i % 2, j],
            )
            for j, (ref, (index, _, base)) in enumerate(zip(arrays, sources))
        ]

    def store(i):
        _, _, start, size, which, e, columns = steps[i]
        wide = result.shape[2]
        to = outs[which].at[e]
        to = to.at[:, pl.ds(columns[0], wide)] if columns else to.at[pl.ds(start, size)]
        return pltpu.make_async_copy(result.at[i % 2, pl.ds(0, size)], to, o_sem.at[i % 2])

    for c in loads(0):
        c.start()
    for i, (arrays, _, _, size, *_) in enumerate(steps):
        if i + 1 < len(steps):
            for c in loads(i + 1):
                c.start()
        for c in loads(i):
            c.wait()
        if i >= 2:
            store(i - 2).wait()
        value = ins[i % 2, 0, :size].astype(F32)
        for j in range(1, len(arrays)):
            value = value + ins[i % 2, j, :size].astype(F32)
        result[i % 2, :size] = value
        store(i).start()
    for i in range(max(len(steps) - 2, 0), len(steps)):
        store(i).wait()


def settle(grads, sums, m):
    block, ff = grads[0][0].shape[2:]
    tile = block // 2
    jobs, arrays = [], []
    for e, (same, got) in enumerate(grads):
        for which in range(3):
            k, holder = which, None
            for part in sums[e]:
                if k < part.shape[1]:
                    holder = part
                    break
                k -= part.shape[1]
            for half in range(1 if which < 2 else 2):
                rows, base = (block, 0) if which < 2 else (tile, half * tile)
                sources = [((0, which), rows, base)] * 2
                sources += [((i, k), rows, base) for i in range(m // 2 - 1)]
                arrays += [same, got] + [holder] * (m // 2 - 1)
                columns = None if which < 2 else (half * ff,)
                jobs.append((tuple(sources), (which, e, columns)))
    return pl.pallas_call(
        functools.partial(settle_kernel, tuple(jobs)),
        out_shape=[jax.ShapeDtypeStruct((EXP_DEV, block, ff), F32)] * 2
        + [jax.ShapeDtypeStruct((EXP_DEV, tile, 2 * ff), F32)],
        in_specs=[ANY] * len(arrays),
        out_specs=[ANY] * 3,
        scratch_shapes=[
            pltpu.VMEM((2, m // 2 + 1, tile, ff), BF),
            pltpu.VMEM((2, tile, ff), F32),
            DMA((2, m // 2 + 1)), DMA((2,)),
        ],
        compiler_params=pltpu.CompilerParams(vmem_limit_bytes=40 << 20),
        cost_estimate=cost(10),
    )(*arrays)


def joined(same, got):
    return same.astype(F32) + got.astype(F32)


def body(
    hidden,
    w_qkv,
    w_out,
    w_router,
    g_attn,
    g_ffn,
    g_q,
    g_k,
    w_gate,
    w_up,
    w_down,
    lengths,
    routes,
    route_codes,
    cotangent,
):
    n = lax.axis_size("head")
    m = lax.axis_size("fsdp")
    me = lax.axis_index("head")
    rows = hidden.shape[1]
    width = hidden.shape[2]
    seq = rows * n
    lh = HEADS // n
    dh = lh * HD
    experts = EXP_DEV * n
    shard = w_qkv.shape[0]
    both = ("head", "fsdp")

    sides = 128 // shard
    lane = jnp.arange(128, dtype=jnp.int32) // shard == lax.axis_index("fsdp") % sides
    small = jnp.tile(jnp.stack([g_attn, g_ffn, g_q, g_k]), (2, sides)).astype(F32)
    small = jnp.concatenate(
        [jnp.where(lane[None, :], small, 0.0), w_router.astype(F32).reshape(-1, 128)]
    )
    def inverse_rms(values):
        return lax.rsqrt(jnp.mean(values * values, axis=-1, keepdims=True) + EPS)

    angles = np.arange(seq)[:, None] * ROPE_BASE ** (-2.0 * np.arange(HD // 2) / HD)
    cosine = np.tile(np.cos(angles), (1, 2)).astype(np.float32)
    sine = np.concatenate([-np.sin(angles), np.sin(angles)], axis=1).astype(np.float32)
    (attn_input, qkv, proj, sums, queries, keys, values, attended, attended_tok, full_out, small,
     gate0x, up0x, down0x) = opening(
        lengths, hidden[0], w_qkv, w_out, small, cosine, sine, n, m, (("share", 0),) * 3,
        (w_gate, w_up, w_down),
    )
    router = small[:, :, 8:].reshape(width, experts).astype(BF)
    lanes = small[:, :, :4].reshape(n, m // sides, sides, 4, 128).sum(axis=2)
    gain_attn, gain_ffn, gain_q, gain_k = lanes.transpose(2, 0, 1, 3).reshape(4, width)
    gains_q = lax.dynamic_slice_in_dim(gain_q, me * dh, dh, 0)
    gains_k = lax.dynamic_slice_in_dim(gain_k, me * dh, dh, 0)
    full_out = full_out.reshape(width, width)
    residual = hidden[0].astype(F32) + dot(attended_tok, full_out)
    own_input = (residual * inverse_rms(residual) * gain_ffn).astype(BF)

    logits = dot(own_input, router)
    matches = routes[0][:, :, None] == jnp.arange(experts, dtype=jnp.int32)[None, None, :]
    chosen = (
        jnp.sum(jnp.where(matches, logits[:, None, :], 0.0), axis=-1)
        + route_codes[0].astype(F32) / 1024.0
    )
    chosen = jnp.exp(chosen - jnp.max(chosen, axis=1, keepdims=True))
    gates = chosen / jnp.sum(chosen, axis=1, keepdims=True)
    spread = jnp.sum(jnp.where(matches, gates[:, :, None], 0.0), axis=1)

    half = rows // 2
    gate_sets = spread.T.reshape(n, EXP_DEV, rows)
    own_w = (w_gate, w_up, w_down)
    over_x = (gate0x, up0x, down0x)
    x_a, mine, gate1x, up1x, *got, cot_a = gather(
        own_input[:half], gate_sets, n, m, 1,
        (("share", 1),) * 2 + (("pair", 0),) * 3 + ("pair",) * 3 + (("pair", 1),) * 3,
        (w_gate, w_up, *own_w, *over_x, *own_w), (cotangent[0, :half],),
    )
    weights0 = [(over_x[i], got[i], got[3 + i]) for i in range(3)]
    mine = mine.transpose(0, 2, 1)
    span = n * half

    def rows_of(part):
        return part.reshape(span, width)

    gates_a = mine[:, :half].reshape(span, EXP_DEV)
    gates_b = mine[:, half:].reshape(span, EXP_DEV)
    fresh = [gate1x, got[6], up1x, got[7], got[8]]
    dots_a, acts_a, gin_a, mix_a, x_b, cot_b, down1x, gate1c, up1c, down1c = experts_a(
        rows_of(x_a), rows_of(cot_a), gates_a, own_w, weights0, fresh, own_input[half:],
        cotangent[0, half:], n, m,
    )
    weights1 = [(gate1x, got[6], gate1c), (up1x, got[7], up1c), (down1x, got[8], down1c)]
    dots_b, acts_b, gin_b, mix_b, grad_ffn_a, summed_a, *grads0 = experts_b(
        rows_of(x_b), rows_of(cot_b), gates_b, own_w, weights0 + weights1, gin_a, mix_a,
        rows_of(x_a), rows_of(cot_a), acts_a, n, m,
    )
    dots = jnp.concatenate(
        [d.reshape(n, half, EXP_DEV).transpose(0, 2, 1) for d in (dots_a, dots_b)], axis=2
    )

    early = len(grads0) > 0
    grads, grad_ffn_b, summed_b, dots, sums0 = experts_d(
        (x_a, cot_a, acts_a), (x_b, cot_b, acts_b), gin_b, mix_b, dots, n, m,
        (1,) if early else (0, 1), (("join", 0, 2),) * early, tuple(grads0),
    )
    grads = [tuple(grads0)] * early + grads
    grad_ffn = jnp.concatenate([grad_ffn_a, grad_ffn_b], axis=0)
    summed = jnp.concatenate([summed_a, summed_b], axis=0)
    dots = dots.reshape(experts, rows).T
    grad_rows = cotangent[0].astype(F32)
    grad_logits = spread * (dots - jnp.sum(spread * dots, axis=1, keepdims=True))
    high = lax.Precision.HIGHEST
    grad_ffn = grad_ffn + jnp.dot(grad_logits, router.astype(F32).T, precision=high)
    grad_router = jnp.dot(own_input.astype(F32).T, grad_logits, precision=high)

    def norm_back(values, gain, grad):
        inv = inverse_rms(values)
        unit = values * inv
        scaled = grad * gain
        back = inv * (scaled - unit * jnp.mean(scaled * unit, axis=-1, keepdims=True))
        return back, jnp.sum(grad * unit, axis=0)

    back, grad_gain_ffn = norm_back(residual, gain_ffn, grad_ffn)
    grad_residual = grad_rows + back
    grad_attn_out = grad_residual.astype(BF)
    grad_attended = dot(grad_attn_out, full_out, NT).astype(BF)
    spans = [(span, 0) for span in (((2, 3),) if early else ((0, 2), (2, 3)))]
    spans += [(span, 1) for span in ((0, 1), (1, 2), (2, 3))]
    if early:
        kinds = tuple(("join",) + span for span, _ in spans)
        riders = [a for _, e in spans for a in grads[e]]
    else:
        kinds = ("across",) * len(spans)
        riders = [
            joined(*(part[1:, a:b] for part in grads[e])).astype(BF) for (a, b), e in spans
        ]
    grad_attn_in, grad_qkv, grad_out_w, grad_gains, *arrived = closing(
        lengths, grad_attended, grad_attn_out, queries, keys, values, attended, proj, sums,
        jnp.stack([gains_q, gains_k]), cosine, sine, attn_input, qkv, n, m,
        kinds, riders, 3,
    )
    sums0 = list(sums0) + arrived[:-3]
    sums1 = arrived[-3:]
    grad_gain_q, grad_gain_k = grad_gains.reshape(2, dh)
    out_rows = residual + summed

    grad_w_gate, grad_w_up, grad_w_down = settle(grads, (sums0, sums1), m)
    grad_qkv = grad_qkv.astype(F32)

    back, grad_gain_attn = norm_back(hidden[0].astype(F32), gain_attn, grad_attn_in)
    grad_hidden = grad_residual + back

    def at_mine(piece):
        return lax.dynamic_update_slice_in_dim(jnp.zeros((width,), F32), piece, me * dh, 0)

    pack = jnp.concatenate(
        [grad_router.reshape(n * m, shard * experts)]
        + [
            g.reshape(n * m, shard)
            for g in (grad_gain_attn, grad_gain_ffn, at_mine(grad_gain_q), at_mine(grad_gain_k))
        ],
        axis=1,
    )
    pack = lax.all_to_all(pack, both, split_axis=0, concat_axis=0, tiled=True)
    pack = jnp.sum(pack, axis=0)
    small_grads = pack[shard * experts :].reshape(4, shard)
    return (
        out_rows.astype(BF)[None],
        grad_hidden[None],
        grad_qkv,
        grad_out_w,
        pack[: shard * experts].reshape(shard, experts),
        small_grads[0],
        small_grads[1],
        small_grads[2],
        small_grads[3],
        grad_w_gate,
        grad_w_up,
        grad_w_down,
    )


def solution(mesh):
    both = ("head", "fsdp")
    return jax.shard_map(
        body,
        mesh=mesh,
        in_specs=(
            P("fsdp", "head", None),
            P(both, None),
            P(both, None),
            P(both, None),
            P(both),
            P(both),
            P(both),
            P(both),
            P("head", "fsdp", None),
            P("head", "fsdp", None),
            P("head", "fsdp", None),
            P("fsdp"),
            P("fsdp", "head", None),
            P("fsdp", "head", None),
            P("fsdp", "head", None),
        ),
        out_specs=(
            P("fsdp", "head", None),
            P("fsdp", "head", None),
            P(both, None),
            P(both, None),
            P(both, None),
            P(both),
            P(both),
            P(both),
            P(both),
            P("head", "fsdp", None),
            P("head", "fsdp", None),
            P("head", "fsdp", None),
        ),
        check_vma=False,
    )
```

```python
import functools
import math

import jax
import jax.numpy as jnp
import numpy as np
from jax import lax
from jax.experimental import pallas as pl
from jax.experimental.pallas import tpu as pltpu
from jax.sharding import PartitionSpec as P

HEADS = 16
HD = 128
FF = 1024
TOP = 8
EXP_DEV = 2

EPS = 1e-06
ROPE_BASE = 10000.0
NEGATIVE = -1e30
BF = jnp.bfloat16
F32 = jnp.float32
NN = ((1,), (0,))
NT = ((1,), (1,))
TN = ((0,), (0,))
ANY = pl.BlockSpec(memory_space=pl.ANY)
WHOLE = pl.BlockSpec(memory_space=pltpu.VMEM)
DMA = pltpu.SemaphoreType.DMA


def dot(a, b, dims=NN):
    return lax.dot_general(a, b, (dims, ((), ())), preferred_element_type=F32)


def cost(us):
    return pl.CostEstimate(flops=0, bytes_accessed=int(us * 3.6e6), transcendentals=0)


def ring_place():
    n = lax.axis_size("head")
    me = lax.axis_index("head")
    odd = me % 2
    return (1 - odd) * (me // 2) + odd * (n - 1 - me // 2)


def head_at(offset):
    n = lax.axis_size("head")
    k = (ring_place() + (offset + n)) % n
    down = k // (n // 2)
    return (1 - down) * 2 * k + down * (2 * n - 1 - 2 * k)


def remote(src, dst, send, recv, device):
    return pltpu.make_async_remote_copy(
        src_ref=src,
        dst_ref=dst,
        send_sem=send,
        recv_sem=recv,
        device_id=device,
        device_id_type=pl.DeviceIdType.MESH,
    )


def greet(devices):
    barrier = pltpu.get_barrier_semaphore()
    for device in devices:
        pl.semaphore_signal(
            barrier, inc=1, device_id=device, device_id_type=pl.DeviceIdType.MESH
        )
    pl.semaphore_wait(barrier, len(devices))


def other_heads():
    n = lax.axis_size("head")
    me = lax.axis_index("head")
    return [{"head": (me + d) % n} for d in range(1, n)]


def other_parts():
    m = lax.axis_size("fsdp")
    f = lax.axis_index("fsdp")
    return [{"fsdp": (f + d) % m} for d in range(1, m)]


class Ring:
    def __init__(self, own, place, send, recv, n):
        self.own, self.place, self.send, self.recv = own, place, send, recv
        self.half = n // 2

    def exists(self, way, step, c):
        return step < self.half or c == way

    def message(self, way, step, c):
        owner = head_at((1 - step) if way == 0 else (step - 1))
        return remote(
            self.own(c) if step == 1 else self.place(owner, c),
            self.place(owner, c),
            self.send.at[way, step - 1, c],
            self.recv.at[way, step - 1, c],
            {"head": head_at(1 if way == 0 else -1)},
        )

    def start(self):
        for c in range(2):
            for way in range(2):
                if self.exists(way, 1, c):
                    self.message(way, 1, c).start()

    def step(self, step):
        for c in range(2):
            for way in range(2):
                if self.exists(way, step, c):
                    self.message(way, step, c).wait_recv()
                    if step < self.half and self.exists(way, step + 1, c):
                        self.message(way, step + 1, c).start()

    def finish(self):
        for step in range(1, self.half + 1):
            for c in range(2):
                for way in range(2):
                    if self.exists(way, step, c):
                        self.message(way, step, c).wait_send()


def ring_sems(n):
    return [DMA((2, n // 2, 2)), DMA((2, n // 2, 2))]


class Carry:
    def __init__(self, kinds, ins, outs, send, recv, *joins):
        self.jobs, k = [], 0
        stages = list(joins)
        for kind, dst in zip(kinds, outs):
            name = kind if isinstance(kind, str) else kind[0]
            if name == "join":
                self.jobs.append((name, stages.pop(0), dst, kind[1:], ins[k : k + 2]))
                k += 2
                continue
            src = ins[k] if isinstance(kind, str) else ins[k].at[kind[1]]
            self.jobs.append((name, src, dst, None, None))
            k += 1
        self.tmp, self.j_sem = stages if stages else (None, None)
        self.fetched = None
        self.send, self.recv = send, recv

    def copies(self, j):
        m = lax.axis_size("fsdp")
        f = lax.axis_index("fsdp")
        nx = m // 2
        x, core = f // 2, f % 2
        name, src, dst = self.jobs[j][:3]
        if name == "pair":
            other = {"fsdp": x * 2 + 1 - core}
            return [remote(src, dst, self.send.at[j, 0], self.recv.at[j, 0], other)]
        return [
            remote(
                src if name == "share" else src.at[i - 1], dst.at[i - 1],
                self.send.at[j, i - 1], self.recv.at[j, i - 1],
                {"fsdp": ((x + i) % nx) * 2 + core},
            )
            for i in range(1, nx)
        ]

    def fetch(self, j):
        _, stage, _, (a, b), arrays = self.jobs[j]
        tmp = self.tmp.at[:, pl.ds(0, b - a)]
        self.fetched = [
            pltpu.make_async_copy(
                arrays[i].at[pl.ds(1, stage.shape[0]), pl.ds(a, b - a)], (stage, tmp)[i],
                self.j_sem.at[i],
            )
            for i in range(2)
        ]
        for c in self.fetched:
            c.start()

    def first(self):
        if self.jobs and self.jobs[0][0] == "join":
            self.fetch(0)

    def join(self, j):
        _, stage, _, (a, b), _ = self.jobs[j]
        if self.fetched is None:
            self.fetch(j)
        for c in self.fetched:
            c.wait()
        self.fetched = None
        for i in range(stage.shape[0]):
            for k in range(b - a):

                @pl.loop(0, stage.shape[2] // 64)
                def _(r, i=i, k=k):
                    at = pl.ds(pl.multiple_of(r * 64, 64), 64)
                    stage[i, k, at] = (
                        stage[i, k, at].astype(F32) + self.tmp[i, k, at].astype(F32)
                    ).astype(BF)

    def begin(self, some=None):
        for j in range(len(self.jobs)) if some is None else some:
            if self.jobs[j][0] == "join":
                self.join(j)
            for c in self.copies(j):
                c.start()

    def arrived(self, j):
        for c in self.copies(j):
            c.wait_recv()

    def end(self, seen=()):
        for j in range(len(self.jobs)):
            for c in self.copies(j):
                if j not in seen:
                    c.wait_recv()
                c.wait_send()


def carry_plan(kinds, arrays, m):
    shapes, stages, k = [], [], 0
    for kind in kinds:
        if kind[0] == "join":
            a, b = kind[1:]
            shape = (m // 2 - 1, b - a) + arrays[k].shape[2:]
            stages.append(shape)
            k += 2
        else:
            name = kind if isinstance(kind, str) else kind[0]
            shape = arrays[k].shape if isinstance(kind, str) else arrays[k].shape[1:]
            shape = (m // 2 - 1,) * (name == "share") + shape
            k += 1
        shapes.append(jax.ShapeDtypeStruct(shape, BF))
    sems = (max(len(kinds), 1), max(m // 2 - 1, 1))
    scratch = [DMA(sems), DMA(sems)] + [pltpu.VMEM(shape, BF) for shape in stages]
    if stages:
        widest = max(stages, key=lambda shape: shape[1])
        scratch += [pltpu.VMEM(widest, BF), DMA((2,))]
    return k, shapes, scratch


def carried(kinds):
    joins = sum(kind[0] == "join" for kind in kinds)
    return len(kinds) + joins, 2 + joins + 2 * (joins > 0)


def routing_kernel(n, m, experts, kinds, *refs):
    k, back = carried(kinds)
    (hid_ref, tok_ref, wout_ref, gain_ref, router_ref, routes_ref, codes_ref, cot_ref) = refs[:8]
    res_ref, own_ref, spread_ref, xa_ref, cota_ref, mine_ref = refs[8 + k : 14 + k]
    (wout, sets, w_sem, copies, x_send, x_recv, t_send, t_recv, e_send, e_recv) = refs[
        14 + k + len(kinds) : -back
    ]
    carry = Carry(kinds, refs[8 : 8 + k], refs[14 + k : 14 + k + len(kinds)], *refs[-back:])
    me = lax.axis_index("head")
    rows, width = hid_ref.shape
    half = rows // 2
    part = half // 2
    lanes = width // 4
    loads = [
        pltpu.make_async_copy(
            wout_ref.at[:, pl.ds(i * lanes, lanes)], wout.at[:, pl.ds(i * lanes, lanes)],
            w_sem.at[i],
        )
        for i in range(4)
    ]
    for c in loads:
        c.start()
    greet(other_heads() + other_parts())

    def ring_of(own, out, send, recv):
        return Ring(
            lambda c: own.at[pl.ds(c * part, part)],
            lambda h, c: out.at[h, pl.ds(c * part, part)],
            send, recv, n,
        )

    ring_cot = ring_of(cot_ref, cota_ref, t_send, t_recv)
    ring_x = ring_of(own_ref, xa_ref, x_send, x_recv)
    ring_cot.start()
    carry.begin()
    moves = [pltpu.make_async_copy(cot_ref.at[pl.ds(0, half)], cota_ref.at[me], copies.at[0])]
    moves[0].start()
    for i in range(4):
        at = pl.ds(i * lanes, lanes)
        loads[i].wait()
        res_ref[:, at] = hid_ref[:, at].astype(F32) + dot(tok_ref[...], wout[:, at])
    residual = res_ref[...]
    inv = lax.rsqrt(jnp.mean(residual * residual, axis=-1, keepdims=True) + EPS)
    own_ref[...] = (residual * inv * gain_ref[...]).astype(BF)
    ring_cot.step(1)
    ring_x.start()
    moves.append(pltpu.make_async_copy(own_ref.at[pl.ds(0, half)], xa_ref.at[me], copies.at[1]))
    moves[1].start()

    logits = dot(own_ref[...], router_ref[...])
    expert = lax.broadcasted_iota(jnp.int32, logits.shape, 1)
    matches, chosen = [], []
    for j in range(TOP):
        matches.append(expert == routes_ref[:, j : j + 1])
        picked = jnp.sum(jnp.where(matches[j], logits, 0.0), axis=1, keepdims=True)
        chosen.append(picked + codes_ref[:, j : j + 1].astype(F32) / 1024.0)
    peak = functools.reduce(jnp.maximum, chosen)
    chosen = [jnp.exp(c - peak) for c in chosen]
    whole = functools.reduce(lambda a, b: a + b, chosen)
    spread = jnp.zeros_like(logits)
    for j in range(TOP):
        spread = spread + jnp.where(matches[j], chosen[j] / whole, 0.0)
    spread_ref[...] = spread
    turned = spread.T
    for h in range(n):
        sets[h] = turned[h * EXP_DEV : (h + 1) * EXP_DEV]
    moves.append(pltpu.make_async_copy(sets.at[me], mine_ref.at[me], copies.at[2]))
    moves += [
        remote(sets.at[dev["head"]], mine_ref.at[me], e_send.at[d], e_recv.at[d], dev)
        for d, dev in enumerate(other_heads())
    ]
    for c in moves[2:]:
        c.start()
    for step in range(2, n // 2 + 1):
        ring_cot.step(step)
        ring_x.step(step - 1)
    ring_x.step(n // 2)
    for c in moves:
        c.wait()
    ring_cot.finish()
    ring_x.finish()
    carry.end()


def routing(hid, tok, w_out, gain, router, routes, codes, cot, n, m, experts, kinds, arrays):
    rows, width = hid.shape
    count, shapes, scratch = carry_plan(kinds, arrays, m)
    halves = jax.ShapeDtypeStruct((n, rows // 2, width), BF)
    return pl.pallas_call(
        functools.partial(routing_kernel, n, m, experts, kinds),
        out_shape=[
            jax.ShapeDtypeStruct((rows, width), F32),
            jax.ShapeDtypeStruct((rows, width), BF),
            jax.ShapeDtypeStruct((rows, 128), F32),
            halves, halves,
            jax.ShapeDtypeStruct((n, EXP_DEV, rows), F32),
        ]
        + shapes,
        in_specs=[WHOLE, WHOLE, ANY] + [WHOLE] * 5 + [ANY] * count,
        out_specs=[WHOLE] * 3 + [ANY] * (3 + len(kinds)),
        scratch_shapes=[
            pltpu.VMEM((width, width), BF),
            pltpu.VMEM((n, EXP_DEV, rows), F32),
            DMA((4,)), DMA((3,)),
        ]
        + ring_sems(n)
        + ring_sems(n)
        + [DMA((n - 1,)), DMA((n - 1,))]
        + scratch,
        compiler_params=pltpu.CompilerParams(
            collective_id=1, has_side_effects=True, vmem_limit_bytes=60 << 20
        ),
        cost_estimate=cost(55),
    )(hid, tok, w_out, gain, router, routes, codes, cot, *arrays)


class RingSum:
    def __init__(self, n, parts, out_ref, own, sbuf, rbuf, loads, send, recv):
        self.n, self.half, self.parts, self.out_ref = n, n // 2, parts, out_ref
        self.own, self.sbuf, self.rbuf, self.loads = own, sbuf, rbuf, loads
        self.send, self.recv = send, recv
        self.rows = out_ref.shape[0] // 2
        self.order = (
            [self.half] + [s * w for s in range(self.half - 1, 0, -1) for w in (1, -1)] + [0]
        )
        self.ready, self.started = set(), []

    def fetch(self, o):
        i = self.order.index(o)
        return pltpu.make_async_copy(self.parts.at[head_at(o)], self.own.at[i], self.loads.at[i])

    def load(self):
        for o in self.order:
            self.fetch(o).start()

    def piece(self, o, c):
        if o not in self.ready:
            self.fetch(o).wait()
            self.ready.add(o)
        return self.own[self.order.index(o), pl.ds(c * self.rows, self.rows)].astype(F32)

    def buffer(self, way, t, c):
        first = 1 if c == way else 2
        return self.sbuf.at[way, t - 1] if t == first else self.rbuf.at[way, t - 2, c]

    def message(self, way, t, c):
        return remote(
            self.buffer(way, t, c), self.rbuf.at[way, t - 1, c],
            self.send.at[way, t - 1, c], self.recv.at[way, t - 1, c],
            {"head": head_at(1 if way == 0 else -1)},
        )

    def offset(self, way, o):
        return o if way == 0 or o == self.half else -o

    def ship(self, way, t, c, value):
        self.buffer(way, t, c)[...] = value.astype(BF)
        self.message(way, t, c).start()
        self.started.append((way, t, c))

    def start(self):
        for way in range(2):
            self.ship(way, 1, way, self.piece(self.half, way))
        for way in range(2):
            self.ship(way, 2, 1 - way, self.piece(self.offset(way, self.half - 1), 1 - way))

    def step(self, t):
        if t < self.half:
            for c in range(2):
                for way in range(2):
                    if t == 1 and c != way:
                        continue
                    self.message(way, t, c).wait_recv()
                    self.ship(
                        way, t + 1, c,
                        self.piece(self.offset(way, self.half - t), c)
                        + self.rbuf[way, t - 1, c].astype(F32),
                    )
            return
        last = self.half - 1
        for c in range(2):
            for way in range(2):
                self.message(way, self.half, c).wait_recv()
            self.out_ref[pl.ds(c * self.rows, self.rows)] = (
                self.piece(0, c)
                + self.rbuf[0, last, c].astype(F32)
                + self.rbuf[1, last, c].astype(F32)
            )

    def finish(self):
        for way, t, c in self.started:
            self.message(way, t, c).wait_send()


def ring_sum_scratch(n, rows, width):
    return [
        pltpu.VMEM((n, rows, width), BF),
        pltpu.VMEM((2, 2, rows // 2, width), BF),
        pltpu.VMEM((2, n // 2, 2, rows // 2, width), BF),
        DMA((n,)),
    ] + ring_sems(n)


def probs_of(len_ref, q, k):
    scores = dot(q, k, NT) * (1.0 / math.sqrt(HD))
    at = lax.broadcasted_iota(jnp.int32, scores.shape, 1)
    scores = jnp.where(at < len_ref[0], scores, NEGATIVE)
    exponent = jnp.exp(scores - jnp.max(scores, axis=-1, keepdims=True))
    return exponent / jnp.sum(exponent, axis=-1, keepdims=True)


def query_block(seq):
    return 256 if seq <= 1024 else 128


def as_column(row):
    return jnp.broadcast_to(row, (row.shape[1], row.shape[1])).T


def as_row(column):
    return jnp.broadcast_to(column, (column.shape[0], column.shape[0])).T[:1]


def turn(values, cosine, sine):
    return values * cosine + pltpu.roll(values, HD // 2, 1) * sine


def opening_kernel(n, m, kinds, *refs):
    k, _ = carried(kinds)
    len_ref, x_ref, w_ref, wo_ref, gain_ref, cos_ref, sin_ref = refs[:7]
    (ain_ref, qkv_ref, proj_ref, sums_ref, q_ref, k_ref, v_ref, att_ref, tok_ref, wout_ref,
     gall_ref, wide_ref, narrow_ref) = refs[7 + k : 20 + k]
    (hid, qkv, wpair, gall, ain, buf, own, out_sem, copies, s_send, s_recv,
     w_send, w_recv, f_send, f_recv, g_send, g_recv, a_send, a_recv, o_send, o_recv,
     c_send, c_recv, t_send, t_recv, t_sem, h_send, h_recv, r_send, r_recv) = refs[20 + 2 * k : -2]
    carry = Carry(kinds, refs[7 : 7 + k], refs[20 + k : 20 + 2 * k], *refs[-2:])
    me = lax.axis_index("head")
    f = lax.axis_index("fsdp")
    nx = m // 2
    x, core = f // 2, f % 2
    rows, width = x_ref.shape
    dh = q_ref.shape[1]
    seq = n * rows
    qb = query_block(seq)
    part_rows = rows // 2

    def part(i, side):
        return ((x + i) % nx) * 2 + side

    pair = {"fsdp": part(0, 1 - core)}
    greet(other_heads() + other_parts())

    ring = Ring(
        lambda c: x_ref.at[pl.ds(c * part_rows, part_rows)],
        lambda h, c: hid.at[h, pl.ds(c * part_rows, part_rows)],
        h_send, h_recv, n,
    )
    to_parts = [
        remote(gain_ref, gall.at[me, f], g_send.at[d], g_recv.at[d], dev)
        for d, dev in enumerate(other_parts())
    ]
    outs = [
        remote(
            wo_ref, wpair.at[x], o_send.at[i - 1], o_recv.at[i - 1], {"fsdp": part(nx - i, core)}
        )
        for i in range(1, nx)
    ]
    columns = [
        remote(
            w_ref.at[:, pl.ds(pl.multiple_of(j * width + dev["head"] * dh, 128), dh)],
            qkv.at[me, f, :, pl.ds(j * dh, dh)],
            w_send.at[d, j],
            w_recv.at[d, j],
            dev,
        )
        for d, dev in enumerate(other_heads())
        for j in range(3)
    ]
    for c in to_parts + outs:
        c.start()
    carry.begin([0])
    ring.start()
    for c in columns:
        c.start()
    gall[me, f] = gain_ref[...]
    wpair[x] = wo_ref[...]
    hid[me] = x_ref[...]
    for j in range(3):
        qkv[me, f, :, pl.ds(j * dh, dh)] = w_ref[
            :, pl.ds(pl.multiple_of(j * width + me * dh, 128), dh)
        ]
    for c in to_parts:
        c.wait_recv()
    gains = [
        remote(gall.at[me], gall.at[me], a_send.at[d], a_recv.at[d], dev)
        for d, dev in enumerate(other_heads())
    ]
    for c in gains:
        c.start()
    for c in gains:
        c.wait_recv()

    def gain_row(k):
        return jnp.concatenate(
            [
                sum(gall[h, i * fs + j, k : k + 1, :] for j in range(fs))
                for h in range(n)
                for i in range(m // fs)
            ],
            axis=1,
        )

    fs = 128 // w_ref.shape[0]
    gain_attn = gain_row(0)
    stores = []

    def store(src, dst, sem):
        stores.append(pltpu.make_async_copy(src, dst, sem))
        stores[-1].start()

    def normalise(i, slot):
        wide = hid[i].astype(F32)
        inv = lax.rsqrt(jnp.mean(wide * wide, axis=-1, keepdims=True) + EPS)
        ain[i] = (wide * inv * gain_attn).astype(BF)
        store(ain.at[i], ain_ref.at[i], out_sem.at[slot])

    normalise(me, 0)
    for c in columns:
        c.wait_recv()
    across = [
        remote(qkv.at[:, f], qkv.at[:, f], f_send.at[i], f_recv.at[i], {"fsdp": part(nx - i, core)})
        for i in range(1, nx)
    ]
    for c in across:
        c.start()
    carry.begin(range(1, len(carry.jobs)))

    def beside(i):
        there = qkv.at[:, part(i, core)]
        return remote(there, there, f_send.at[nx + i], f_recv.at[nx + i], pair)

    beside(0).start()
    for step in range(1, n // 2):
        ring.step(step)
        normalise(head_at(step), 2 * step - 1)
        normalise(head_at(-step), 2 * step)

    halves = nx // 2
    for c in outs:
        c.wait_recv()
    wring = Ring(
        lambda c: wpair.at[pl.ds(c * halves, halves)],
        lambda h, c: wout_ref.at[h, pl.ds(c * halves, halves), core],
        r_send, r_recv, n,
    )
    wring.start()
    mine = pltpu.make_async_copy(wpair, wout_ref.at[me, :, core], copies.at[0])
    mine.start()

    def over(offset, slot):
        there = wout_ref.at[head_at(offset), :, core]
        return remote(there, there, c_send.at[slot], c_recv.at[slot], pair)

    def advance(step):
        wring.step(step)
        if step < n // 2:
            over(step, 2 * step - 1).start()
            over(-step, 2 * step).start()
        else:
            over(step, n - 1).start()

    ring.step(n // 2)
    normalise(head_at(n // 2), n - 1)
    for i, c in enumerate(across):
        c.wait_recv()
        beside(i + 1).start()
    mine.wait()
    over(0, 0).start()
    for i in range(nx):
        beside(i).wait_recv()
    store(qkv, qkv_ref, copies.at[1])
    weight = qkv.reshape(width, 3 * dh)
    for g in range(n // 2):
        at = pl.ds(g * 2 * rows, 2 * rows)
        projected = dot(ain[2 * g : 2 * g + 2].reshape(2 * rows, width), weight[...])
        proj_ref[at, :] = projected[:, : 2 * dh]
        v_ref[at, :] = projected[:, 2 * dh :].astype(BF)
        for k in range(2):
            squares = projected[:, k * dh : (k + 1) * dh]
            squares = jnp.sum(squares * squares, axis=1, keepdims=True)
            for j in range(2):
                own[pl.ds(k * n + 2 * g + j, 1), :] = as_row(squares[j * rows : (j + 1) * rows])
    moves = [
        remote(own, buf.at[me], s_send.at[d], s_recv.at[d], dev)
        for d, dev in enumerate(other_heads())
    ]
    for c in moves:
        c.start()
    buf[me] = own[...]
    gain_q, gain_k = (
        jnp.concatenate(
            [
                sum(gall[me, i * fs + j, k : k + 1, :] for j in range(fs))
                for i in range(m // fs)
            ],
            axis=1,
        )
        for k in (2, 3)
    )
    gall_ref[...] = gall[...]
    wide_ref[0:1] = gain_attn
    wide_ref[1:2] = gain_row(1)
    narrow_ref[0:1] = gain_q
    narrow_ref[1:2] = gain_k
    for c in moves:
        c.wait()
    total_of = buf[0]
    for i in range(1, n):
        total_of = total_of + buf[i]
    sums_ref[...] = total_of
    inv_all = lax.rsqrt(total_of / width + EPS)
    advance(1)
    for i in range(n):
        at = pl.ds(i * rows, rows)
        inv_q = as_column(inv_all[i : i + 1])
        inv_k = as_column(inv_all[n + i : n + i + 1])
        cosine = cos_ref[at, :]
        sine = sin_ref[at, :]
        for head in range(dh // HD):
            lanes = pl.ds(head * HD, HD)
            k_lanes = pl.ds(dh + head * HD, HD)
            span = slice(head * HD, (head + 1) * HD)
            q_ref[at, lanes] = turn(
                proj_ref[at, lanes] * inv_q * gain_q[:, span], cosine, sine
            ).astype(BF)
            k_ref[at, lanes] = turn(
                proj_ref[at, k_lanes] * inv_k * gain_k[:, span], cosine, sine
            ).astype(BF)
    to = tok_ref.at[:, pl.ds(pl.multiple_of(me * dh, 128), dh)]

    def leave(h):
        return remote(att_ref.at[pl.ds(h * rows, rows)], to, t_send.at[h], t_recv.at[me], {"head": h})

    def arrive(h):
        return remote(
            att_ref.at[pl.ds(h * rows, rows)], tok_ref.at[:, pl.ds(h * dh, dh)],
            t_send.at[h], t_recv.at[h], {"head": h},
        )

    def stay(h):
        return pltpu.make_async_copy(att_ref.at[pl.ds(h * rows, rows)], to, t_sem.at[h])

    for j in range(seq // qb):
        at = pl.ds(j * qb, qb)
        for head in range(dh // HD):
            lanes = pl.ds(head * HD, HD)
            probs = probs_of(len_ref, q_ref[at, lanes], k_ref[:, lanes])
            att_ref[at, lanes] = dot(probs.astype(BF), v_ref[:, lanes]).astype(BF)
        for h in range(j * qb // rows, (j + 1) * qb // rows):

            @pl.when(me != h)
            def _(h=h):
                leave(h).start()

            @pl.when(me == h)
            def _(h=h):
                stay(h).start()

        if j == 1:
            advance(2)
    for step in range(3, n // 2 + 1):
        advance(step)
    for h in range(n):

        @pl.when(me != h)
        def _(h=h):
            leave(h).wait_send()
            arrive(h).wait_recv()

        @pl.when(me == h)
        def _(h=h):
            stay(h).wait()

    for c in stores:
        c.wait()
    for slot in range(n):
        over(0, slot).wait_recv()
    over(0, 0).wait_send()
    for step in range(1, n // 2):
        over(step, 2 * step - 1).wait_send()
        over(-step, 2 * step).wait_send()
    over(n // 2, n - 1).wait_send()
    for c in to_parts + outs + columns + gains + across:
        c.wait_send()
    for i in range(nx):
        beside(i).wait_send()
    ring.finish()
    wring.finish()
    carry.end()


def opening(lengths, x, w, w_out, gains, cosine, sine, n, m, kinds, arrays):
    rows, width = x.shape
    seq = n * rows
    shard = w.shape[0]
    dh = w.shape[1] // 3 // n
    heads = jax.ShapeDtypeStruct((seq, dh), BF)
    count, shapes, scratch = carry_plan(kinds, arrays, m)
    return pl.pallas_call(
        functools.partial(opening_kernel, n, m, kinds),
        out_shape=[
            jax.ShapeDtypeStruct((n, rows, width), BF),
            jax.ShapeDtypeStruct((n, m, shard, 3 * dh), BF),
            jax.ShapeDtypeStruct((seq, 2 * dh), F32),
            jax.ShapeDtypeStruct((2 * n, rows), F32),
            heads, heads, heads, heads,
            jax.ShapeDtypeStruct((rows, width), BF),
            jax.ShapeDtypeStruct((n, m // 2, 2, shard, width), BF),
            jax.ShapeDtypeStruct((n, m) + gains.shape, F32),
            jax.ShapeDtypeStruct((2, width), F32),
            jax.ShapeDtypeStruct((2, dh), F32),
        ]
        + shapes,
        in_specs=[pl.BlockSpec(memory_space=pltpu.SMEM)] + [WHOLE] * 6 + [ANY] * count,
        out_specs=[ANY] * 2 + [WHOLE] * 6 + [ANY] * 2 + [WHOLE] * 3 + [ANY] * count,
        scratch_shapes=[
            pltpu.VMEM((n, rows, width), BF),
            pltpu.VMEM((n, m, shard, 3 * dh), BF),
            pltpu.VMEM((m // 2, shard, width), BF),
            pltpu.VMEM((n, m) + gains.shape, F32),
            pltpu.VMEM((n, rows, width), BF),
            pltpu.VMEM((n, 2 * n, rows), F32),
            pltpu.VMEM((2 * n, rows), F32),
            DMA((n,)), DMA((2,)), DMA((n - 1,)), DMA((n - 1,)),
            DMA((n - 1, 3)), DMA((n - 1, 3)), DMA((m,)), DMA((m,)), DMA((m - 1,)), DMA((m - 1,)),
            DMA((n - 1,)), DMA((n - 1,)), DMA((m // 2,)), DMA((m // 2,)),
            DMA((n,)), DMA((n,)), DMA((n,)), DMA((n,)), DMA((n,)),
        ]
        + ring_sems(n)
        + ring_sems(n)
        + scratch,
        compiler_params=pltpu.CompilerParams(
            collective_id=0, has_side_effects=True, vmem_limit_bytes=60 << 20
        ),
        cost_estimate=cost(100),
    )(lengths, x, w, w_out, gains, cosine, sine, *arrays)


def weave(chunks, polls):
    whole = sum(w for w, _ in chunks)
    done, k = 0.0, 0
    for weight, run in chunks:
        run()
        done += weight
        while k < len(polls) - 1 and done * len(polls) >= (k + 1) * whole:
            polls[k]()
            k += 1
    for poll in polls[k:]:
        poll()


def span_of(seq):
    return seq if seq <= 512 else 256


def source_order(m):
    f = lax.axis_index("fsdp")
    nx = m // 2
    x, core = f // 2, f % 2
    return [((x + i) % nx) * 2 + (core + side) % 2 for side in range(2) for i in range(nx)]


def piece_of(kept, r, nx):
    side, i = divmod(r, nx)
    return kept[2 * side] if i == 0 else kept[2 * side + 1].at[nx - 1 - i]


class Weights:
    def __init__(self, m, kept, bufs, sems):
        self.m, self.kept, self.bufs, self.sems = m, kept, bufs, sems

    def copies(self, key):
        m, nx = self.m, self.m // 2
        order = source_order(m)
        gate, up, down = self.bufs
        g_sem, d_sem = self.sems
        block, tile = gate.shape[0] // m, down.shape[0] // m
        rows = lambda r, size: pl.ds(pl.multiple_of(order[r] * size, size), size)
        if key == "down":
            return [
                pltpu.make_async_copy(
                    piece_of(self.kept[2], r, nx), down.at[rows(r, tile)], d_sem.at[r]
                )
                for r in range(m)
            ]
        cols = pl.ds(key * tile, tile)
        return [
            pltpu.make_async_copy(
                piece_of(self.kept[i], r, nx).at[:, cols], v.at[rows(r, block), cols],
                g_sem.at[i, r, key],
            )
            for i, v in enumerate((gate, up))
            for r in range(m)
        ]

    def start(self, key):
        for c in self.copies(key):
            c.start()

    def wait(self, key):
        for c in self.copies(key):
            c.wait()


def front_chunk(t, x, weights, pre):
    gate_v, up_v, down_v = weights.bufs
    tile = down_v.shape[0] // weights.m
    cols = pl.ds(t * tile, tile)
    weights.wait(t)
    pre[0, :, cols] = dot(x[...], gate_v[:, cols])
    pre[1, :, cols] = dot(x[...], up_v[:, cols])


def forward_chunk(e, t, x, cot, gates_ref, at, weights, acts, dots_ref, first, pre=None):
    gate_v, up_v, down_v = weights.bufs
    tile = down_v.shape[0] // weights.m
    cols = pl.ds(t * tile, tile)
    if t == 0:
        weights.wait("down")
    if pre is None:
        weights.wait(t)
        gate_pre = dot(x[...], gate_v[:, cols])
        up_pre = dot(x[...], up_v[:, cols])
    else:
        gate_pre = pre[0, :, cols]
        up_pre = pre[1, :, cols]
    back = dot(cot[...], down_v[cols, :], NT)
    gate = gates_ref[at, e : e + 1]
    sig = 1.0 / (1.0 + jnp.exp(-gate_pre))
    silu = gate_pre * sig
    value = silu * up_pre
    dots = jnp.sum(value * back, axis=1, keepdims=True)
    if first:
        dots_ref[at, e : e + 1] = dots
    else:
        dots_ref[at, e : e + 1] += dots
    grad_act = gate * back
    acts[e, 0, :, cols] = (gate * value).astype(BF)
    acts[e, 1, :, cols] = (grad_act * up_pre * sig * (1.0 + gate_pre * (1.0 - sig))).astype(BF)
    acts[e, 2, :, cols] = (grad_act * silu).astype(BF)


def experts_steps(m, x_ref, cot_ref, gates_ref, weights, x, cot, acts, stage, pre,
                  dots_ref, acts_ref, gin_ref, mix_ref, in_sem, a_sem, o_sem, polls, between, more=()):
    seq, width = x_ref.shape
    span = x.shape[0]
    spans = seq // span
    chunks = []
    stores = []

    def copy(store):
        store.start()
        stores.append(store)

    for q in range(spans):
        at = pl.ds(q * span, span)
        load_x = pltpu.make_async_copy(x_ref.at[at], x, in_sem.at[0])
        load_cot = pltpu.make_async_copy(cot_ref.at[at], cot, in_sem.at[1])

        def load(q=q, load_x=load_x, load_cot=load_cot):
            if q:
                while stores:
                    stores.pop().wait()
                load_x.start()
                load_cot.start()
            load_x.wait()
            load_cot.wait()

        if q == 0:
            load_x.start()
            for w in weights:
                if w is weights[0]:
                    w.start(0)
                    load_cot.start()
                    w.start("down")
                    for t in range(1, m):
                        w.start(t)
            between(0)
        chunks.append((0.1, load))
        for e in range(EXP_DEV):
            late = e == EXP_DEV - 1

            def front(t, e=e, q=q):
                if q == 0 and t == m - 1:
                    between(2)
                if q:
                    weights[e].wait = lambda key: None
                front_chunk(t, x, weights[e], pre)

            if late:
                for t in range(m):
                    chunks.append((1.1 * 4 / m, functools.partial(front, t)))
            for t in range(m):

                def run(e=e, t=t, q=q, at=at, late=late):
                    if q == 0 and not late and t == m // 2:
                        between(1)
                    if q == 0 and late and t == 0:
                        between(3)
                    if q:
                        weights[e].wait = lambda key: None
                    forward_chunk(
                        e, t, x, cot, gates_ref, at, weights[e], acts, dots_ref, t == 0,
                        pre if late else None,
                    )

                chunks.append(((0.6 if late else 1.6) * 4 / m, run))

            def keep(e=e, at=at):
                copy(pltpu.make_async_copy(acts.at[e], acts_ref.at[e, :, at], a_sem.at[e]))

            chunks.append((0.0, keep))
        for r in range(width // 512):

            def run(r=r, at=at):
                lanes = pl.ds(r * 512, 512)
                mixed, grads = None, None
                for e in range(EXP_DEV):
                    gate_v, up_v, down_v = weights[e].bufs
                    a = dot(acts[e, 0], down_v[:, lanes])
                    b = dot(acts[e, 1], gate_v[lanes, :], NT) + dot(acts[e, 2], up_v[lanes, :], NT)
                    mixed = a if mixed is None else mixed + a
                    grads = b if grads is None else grads + b
                stage[0, :, lanes] = grads.astype(BF)
                stage[1, :, lanes] = mixed.astype(BF)
                for i, to in enumerate((gin_ref, mix_ref)):
                    copy(
                        pltpu.make_async_copy(
                            stage.at[i, :, lanes], to.at[at, lanes], o_sem.at[i, r]
                        )
                    )

            chunks.append((3.2, run))
    weave(chunks + list(more), polls)
    for c in stores:
        c.wait()


def experts_scratch(m, seq, width, ff):
    span = span_of(seq)
    return [
        pltpu.VMEM((EXP_DEV, width, ff), BF),
        pltpu.VMEM((EXP_DEV, width, ff), BF),
        pltpu.VMEM((EXP_DEV, ff, width), BF),
        DMA((EXP_DEV, 2, m, m)),
        DMA((EXP_DEV, m)),
        pltpu.VMEM((span, width), BF),
        pltpu.VMEM((span, width), BF),
        pltpu.VMEM((EXP_DEV, 3, span, ff), BF),
        pltpu.VMEM((2, span, width), BF),
        pltpu.VMEM((2, span, ff), F32),
        DMA((2,)), DMA((EXP_DEV,)), DMA((2, width // 512)),
    ]


def weights_of(e, m, kept, gate_v, up_v, down_v, g_sem, d_sem):
    return Weights(
        m, kept, (gate_v.at[e], up_v.at[e], down_v.at[e]), (g_sem.at[e], d_sem.at[e])
    )


LATE = (("share", 1), "pair", "pair", "pair")


def experts_a_kernel(n, m, *refs):
    x_ref, cot_ref, gates_ref = refs[:3]
    wg, wu, wd = refs[3:6]
    w0, fresh, (xb_own, cotb_own) = refs[6:15], refs[15:20], refs[20:22]
    dots_ref, acts_ref, gin_ref, mix_ref, xb_ref, cotb_ref, down1x, gate1c, up1c, down1c = refs[22:32]
    scratch, rest = refs[32:45], refs[45:]
    gate_v, up_v, down_v, g_sem, d_sem = scratch[:5]
    send0, recv0, send1, recv1, l_sem, c_send, c_recv = rest
    half = xb_own.shape[0] // 2
    me = lax.axis_index("head")
    gate1x, gate1o, up1x, up1o, down1o = fresh
    g1 = (wg.at[1], gate1x, gate1o, gate1c)
    u1 = (wu.at[1], up1x, up1o, up1c)
    d1 = (wd.at[1], down1x, down1o, down1c)
    kept0 = [(w.at[0],) + tuple(w0[3 * i : 3 * i + 3]) for i, w in enumerate((wg, wu, wd))]
    weights = [
        weights_of(0, m, kept0, gate_v, up_v, down_v, g_sem, d_sem),
        weights_of(1, m, (g1, u1, d1), gate_v, up_v, down_v, g_sem, d_sem),
    ]
    carry = Carry(
        LATE, (wd, gate1x, up1x, down1x), (down1x, gate1c, up1c, down1c), c_send, c_recv
    )

    def ring_of(own, out, send, recv):
        return Ring(
            lambda c: own.at[pl.ds(c * half, half)],
            lambda h, c: out.at[h, pl.ds(c * half, half)],
            send, recv, n,
        )

    rings = [ring_of(xb_own, xb_ref, send0, recv0), ring_of(cotb_own, cotb_ref, send1, recv1)]
    mine = [
        pltpu.make_async_copy(xb_own, xb_ref.at[me], l_sem.at[0]),
        pltpu.make_async_copy(cotb_own, cotb_ref.at[me], l_sem.at[1]),
    ]

    def between(stage):
        if stage == 0:
            greet([{"head": head_at(1)}, {"head": head_at(-1)}] + other_parts())
            for ring in rings:
                ring.start()
            carry.begin(range(3))
            for c in mine:
                c.start()
        elif stage == 1:
            for j in (1, 2):
                carry.arrived(j)
            for key in range(m):
                weights[1].start(key)
        elif stage == 2:
            carry.arrived(0)
            carry.begin([3])
        else:
            carry.arrived(3)
            weights[1].start("down")

    def poll(step):
        for ring in rings:
            ring.step(step)

    experts_steps(
        m, x_ref, cot_ref, gates_ref, weights, *scratch[5:10], dots_ref, acts_ref, gin_ref, mix_ref,
        *scratch[10:13], [functools.partial(poll, s) for s in range(1, n // 2 + 1)], between,
    )
    for c in mine:
        c.wait()
    for ring in rings:
        ring.finish()
    carry.end(seen=range(4))


def row_outputs(x, ff):
    seq, width = x.shape
    return [
        jax.ShapeDtypeStruct((seq, EXP_DEV), F32),
        jax.ShapeDtypeStruct((EXP_DEV, 3, seq, ff), BF),
        jax.ShapeDtypeStruct((seq, width), BF),
        jax.ShapeDtypeStruct((seq, width), BF),
    ]


def big(us, identity):
    return dict(
        compiler_params=pltpu.CompilerParams(
            collective_id=identity, has_side_effects=True, vmem_limit_bytes=60 << 20
        ),
        cost_estimate=cost(us),
    )


def experts_a(x, cot, gates, weights, weights0, fresh, x_b, cot_b, n, m):
    seq, width = x.shape
    ff = fresh[0].shape[-1]
    w0 = [a for kept in weights0 for a in kept]
    out = jax.ShapeDtypeStruct((n,) + x_b.shape, BF)
    gate1x, up1x = fresh[0], fresh[2]
    moved = (weights[2], gate1x, up1x)
    late = [jax.ShapeDtypeStruct((m // 2 - 1,) + weights[2].shape[1:], BF)]
    late += [jax.ShapeDtypeStruct(a.shape, BF) for a in moved[1:]] + late
    return pl.pallas_call(
        functools.partial(experts_a_kernel, n, m),
        out_shape=row_outputs(x, ff) + [out, out] + late,
        in_specs=[ANY, ANY, WHOLE] + [ANY] * 17 + [WHOLE] * 2,
        out_specs=[WHOLE] + [ANY] * 9,
        scratch_shapes=experts_scratch(m, seq, width, ff)
        + ring_sems(n)
        + ring_sems(n)
        + [DMA((2,))]
        + [DMA((4, max(m // 2 - 1, 1)))] * 2,
        **big(45, 4),
    )(x, cot, gates, *weights, *w0, *fresh, x_b, cot_b)


class Leave:
    def __init__(self, m, same, got, local, send, recv):
        self.m, self.same, self.got = m, same, got
        self.local, self.send, self.recv = local, send, recv
        self.stores, self.away = [], []

    def put(self, r, src, index, spot):
        nx = self.m // 2
        f = lax.axis_index("fsdp")
        if r < nx:
            self.stores.append(
                pltpu.make_async_copy(src, self.same.at[(r,) + index], self.local.at[r, spot])
            )
            self.stores[-1].start()
        else:
            self.away.append(
                remote(
                    src, self.got.at[(r - nx,) + index], self.send.at[r, spot],
                    self.recv.at[r, spot], {"fsdp": (f // 2) * 2 + 1 - f % 2},
                )
            )
            self.away[-1].start()

    def wide(self, i, v):
        order = source_order(self.m)
        block = v.shape[0] // self.m
        for r in range(self.m):
            at = pl.ds(pl.multiple_of(order[r] * block, block), block)
            self.put(r, v.at[at], (i,), i)

    def tall(self, v):
        order = source_order(self.m)
        tile, ff = v.shape[0] // self.m, v.shape[0]
        for r in range(self.m):
            at = pl.ds(pl.multiple_of(order[r] * tile, tile), tile)
            for side in range(2):
                self.put(
                    r, v.at[at, pl.ds(side * ff, ff)], (2, pl.ds(side * tile, tile)), 2 + side
                )

    def finish(self):
        for c in self.stores:
            c.wait()
        for c in self.away:
            c.wait()


def leave_sems(m):
    return [DMA((m, 4)), DMA((m, 4)), DMA((m, 4))]


def experts_b_kernel(n, m, early, *refs):
    x_ref, cot_ref, gates_ref = refs[:3]
    own, w, (gin_a, mix_a, xa_ref, cota_ref, acts_a) = refs[3:6], refs[6:24], refs[24:29]
    dots_ref, acts_ref, gin_ref, mix_ref, grad_ref, sum_ref = refs[29:35]
    refs = refs[35:]
    if early:
        (same, got), refs = refs[:2], refs[2:]
    scratch, rest = refs[:13], refs[13:]
    gate_v, up_v, down_v, g_sem, d_sem, x, cot, acts = scratch[:8]
    weights = [
        weights_of(
            e, m,
            [
                (own[i].at[e],) + tuple(w[9 * e + 3 * i : 9 * e + 3 * i + 3]) for i in range(3)
            ],
            gate_v, up_v, down_v, g_sem, d_sem,
        )
        for e in range(EXP_DEV)
    ]
    rings = [
        RingSum(n, gin_a, grad_ref, *rest[:6]),
        RingSum(n, mix_a, sum_ref, *rest[6:12]),
    ]

    def between(stage):
        if stage == 0:
            for ring in rings:
                ring.load()
            for key in [0, "down"] + list(range(1, m)):
                weights[1].start(key)
            f = lax.axis_index("fsdp")
            pair = [{"fsdp": (f // 2) * 2 + 1 - f % 2}] if early else []
            greet([{"head": head_at(1)}, {"head": head_at(-1)}] + pair)
            for ring in rings:
                ring.start()

    def poll(step):
        for ring in rings:
            ring.step(step)

    more = []
    if early:
        part = x.shape[0]
        leave = Leave(m, same, got, *rest[12:15])
        l_sem = rest[15]
        dgate, dup, ddown = gate_v.at[0], up_v.at[0], down_v.at[0]
        x_a, cot_a = down_v.at[1, pl.ds(0, part)], down_v.at[1, pl.ds(part, part)]
        kept = [gate_v.at[1, pl.ds(k * part, part)] for k in range(3)]
        loads = [
            pltpu.make_async_copy(xa_ref, x_a, l_sem.at[0]),
            pltpu.make_async_copy(cota_ref, cot_a, l_sem.at[1]),
        ] + [
            pltpu.make_async_copy(acts_a.at[0, k], kept[k], l_sem.at[2 + k]) for k in range(3)
        ]

        def begin():
            for c in loads:
                c.start()
            for c in loads:
                c.wait()

        more.append((0.5, begin))
        for b in range(x.shape[1] // 512):

            def run(b=b):
                at = pl.ds(b * 512, 512)
                turned, turned_a = x[:, at].T, x_a[:, at].T
                dgate[at, :] = (dot(turned, acts[0, 1]) + dot(turned_a, kept[1][...])).astype(BF)
                dup[at, :] = (dot(turned, acts[0, 2]) + dot(turned_a, kept[2][...])).astype(BF)

            more.append((2.4, run))
        more.append((0.0, lambda: (leave.wide(0, dgate), leave.wide(1, dup))))
        for t in range(gate_v.shape[2] // 256):

            def run(t=t):
                at = pl.ds(t * 256, 256)
                ddown[at, :] = (
                    dot(acts[0, 0, :, at].T, cot[...]) + dot(kept[0][:, at].T, cot_a[...])
                ).astype(BF)

            more.append((1.2, run))
        more.append((0.0, lambda: leave.tall(ddown)))
    experts_steps(
        m, x_ref, cot_ref, gates_ref, weights, *scratch[5:10], dots_ref, acts_ref, gin_ref, mix_ref,
        *scratch[10:13], [functools.partial(poll, s) for s in range(1, n // 2 + 1)], between, more,
    )
    for ring in rings:
        ring.finish()
    if early:
        leave.finish()


def experts_b(x, cot, gates, own_w, weights, gin_a, mix_a, x_a, cot_a, acts_a, n, m):
    seq, width = x.shape
    ff = own_w[0].shape[2]
    early = seq <= 512
    flat = [a for kept in weights for a in kept]
    rows = seq // n
    own = jax.ShapeDtypeStruct((rows, width), F32)
    parts = [a.reshape(n, rows, width) for a in (gin_a, mix_a)]
    grads = [jax.ShapeDtypeStruct((m // 2, 3, width // m, ff), BF)] * (2 * early)
    return pl.pallas_call(
        functools.partial(experts_b_kernel, n, m, early),
        out_shape=row_outputs(x, ff) + [own, own] + grads,
        in_specs=[ANY, ANY, WHOLE] + [ANY] * 26,
        out_specs=[WHOLE, ANY, ANY, ANY, WHOLE, WHOLE] + [ANY] * len(grads),
        scratch_shapes=experts_scratch(m, seq, width, ff)
        + ring_sum_scratch(n, rows, width)
        + ring_sum_scratch(n, rows, width)
        + (leave_sems(m) + [DMA((5,))]) * early,
        **big(60, 7),
    )(x, cot, gates, *own_w, *flat, *parts, x_a, cot_a, acts_a)


def experts_d_kernel(n, m, experts, kinds, *refs):
    xs, cots, all_acts = refs[0:6:3], refs[1:6:3], refs[2:6:3]
    gin_b, mix_b, extra = refs[6:9]
    (k, back), kk, g = carried(kinds), len(kinds), 2 * len(experts)
    outs, (grad_ref, sum_ref, extra_out) = refs[9 + k : 9 + k + g], refs[9 + k + g : 12 + k + g]
    carry = Carry(kinds, refs[9 : 9 + k], refs[12 + k + g : 12 + k + kk + g], *refs[-back:])
    (x, cot, acts, dgate, dup, ddown, x_sem, a_sem, copy, e_send, e_recv) = refs[
        12 + k + kk + g : 23 + k + kk + g
    ]
    rest = refs[23 + k + kk + g : -back]
    me = lax.axis_index("head")
    rows, width = x.shape
    part = rows // 2
    ff = acts.shape[2]
    rings = [
        RingSum(n, gin_b, grad_ref, *rest[:6]),
        RingSum(n, mix_b, sum_ref, *rest[6:12]),
    ]
    loads = [
        pltpu.make_async_copy(src[i], dst.at[pl.ds(i * part, part)], x_sem.at[k, i])
        for k, (src, dst) in enumerate(((xs, x), (cots, cot)))
        for i in range(2)
    ]

    def act_loads(e):
        return [
            pltpu.make_async_copy(
                all_acts[i].at[e], acts.at[:, pl.ds(i * part, part)], a_sem.at[i]
            )
            for i in range(2)
        ]

    carry.first()
    for ring in rings:
        ring.load()
    for c in loads + act_loads(experts[0]):
        c.start()
    greet(other_heads() + other_parts())
    carry.begin()
    for ring in rings:
        ring.start()
    direct = [pltpu.make_async_copy(extra.at[me], extra_out.at[me], copy.at[0])] + [
        remote(extra.at[dev["head"]], extra_out.at[me], e_send.at[d], e_recv.at[d], dev)
        for d, dev in enumerate(other_heads())
    ]
    for c in direct:
        c.start()
    chunks, leaves = [], []
    for j, e in enumerate(experts):
        leave = Leave(m, outs[2 * j], outs[2 * j + 1], *rest[12 + 3 * j : 15 + 3 * j])

        def begin(j=j, e=e):
            if j:
                leaves[j - 1].finish()
                for c in act_loads(e):
                    c.start()
            for c in (loads if j == 0 else []) + act_loads(e):
                c.wait()

        leaves.append(leave)
        chunks.append((0.1, begin))
        for b in range(width // 512):

            def run(b=b):
                at = pl.ds(b * 512, 512)
                turned = x[:, at].T
                dgate[at, :] = dot(turned, acts[1]).astype(BF)
                dup[at, :] = dot(turned, acts[2]).astype(BF)

            chunks.append((2.2, run))
        chunks.append(
            (0.0, lambda leave=leave: (leave.wide(0, dgate), leave.wide(1, dup)))
        )
        for t in range(ff // 256):

            def run(t=t):
                at = pl.ds(t * 256, 256)
                ddown[at, :] = dot(acts[0, :, at].T, cot[...]).astype(BF)

            chunks.append((1.1, run))
        chunks.append((0.0, lambda leave=leave: leave.tall(ddown)))

    def poll(step):
        for ring in rings:
            ring.step(step)

    weave(chunks, [functools.partial(poll, t) for t in range(1, n // 2 + 1)])
    for ring in rings:
        ring.finish()
    for c in direct:
        c.wait()
    leaves[-1].finish()
    carry.end()


def experts_d(first, second, gin_b, mix_b, dots, n, m, experts, kinds, arrays):
    seq = first[2].shape[2]
    ff = first[2].shape[3]
    rows, width = first[0].shape[1:]
    grads = jax.ShapeDtypeStruct((m // 2, 3, width // m, ff), BF)
    own = jax.ShapeDtypeStruct((rows, width), F32)
    (k, shapes, scratch), g = carry_plan(kinds, arrays, m), 2 * len(experts)

    def flat(parts):
        return [parts[0].reshape(seq, width), parts[1].reshape(seq, width), parts[2]]

    out = pl.pallas_call(
        functools.partial(experts_d_kernel, n, m, experts, kinds),
        out_shape=[grads] * g
        + [own, own, jax.ShapeDtypeStruct(dots.shape, F32)]
        + shapes,
        in_specs=[ANY] * 8 + [WHOLE] + [ANY] * k,
        out_specs=[ANY] * g + [WHOLE, WHOLE, ANY] + [ANY] * len(kinds),
        scratch_shapes=[
            pltpu.VMEM((2 * seq, width), BF),
            pltpu.VMEM((2 * seq, width), BF),
            pltpu.VMEM((3, 2 * seq, ff), BF),
            pltpu.VMEM((width, ff), BF),
            pltpu.VMEM((width, ff), BF),
            pltpu.VMEM((ff, width), BF),
            DMA((2, 2)), DMA((2,)), DMA((1,)), DMA((n - 1,)), DMA((n - 1,)),
        ]
        + ring_sum_scratch(n, rows, width)
        + ring_sum_scratch(n, rows, width)
        + leave_sems(m) * len(experts)
        + scratch,
        **big(45, 8),
    )(
        *flat(first), *flat(second), gin_b.reshape(n, rows, width), mix_b.reshape(n, rows, width),
        dots, *arrays,
    )
    return [tuple(out[2 * j : 2 * j + 2]) for j in range(g // 2)], *out[g : g + 3], out[g + 3 :]


class RingSumHere(RingSum):
    def __init__(self, n, parts, out_ref, sbuf, rbuf, send, recv):
        super().__init__(n, parts, out_ref, None, sbuf, rbuf, None, send, recv)

    def piece(self, o, c):
        return self.parts[head_at(o), pl.ds(c * self.rows, self.rows)].astype(F32)


def closing_kernel(n, m, kinds, early, *refs):
    (k, back), kk = carried(kinds), len(kinds)
    (len_ref, gatt_ref, gao_ref, q_ref, k_ref, v_ref, att_ref, proj_ref, sums_ref, gains_ref,
     cos_ref, sin_ref, ain_ref, qkv_ref) = refs[:14]
    (gin_ref, dqkv_ref, dout_ref, dgains_ref) = refs[14 + k : 18 + k]
    (gheads, gao, ain, qkv, gin, dproj, scaled, dk, dv, own, buf,
     dqkv, gq, xs, xr, fin, dout, go, xso, xro, sbuf, rbuf,
     l_sem, a_send, a_recv, s_send, s_recv, p_send, p_recv, x_send, x_recv, t_send, t_recv, t_sem,
     g_send, g_recv, r_send, r_recv) = refs[18 + k + kk : -back]
    carry = Carry(kinds, refs[14 : 14 + k], refs[18 + k : 18 + k + kk], *refs[-back:])
    me = lax.axis_index("head")
    f = lax.axis_index("fsdp")
    nx = m // 2
    x, core = f // 2, f % 2
    rows, width = gao_ref.shape
    half_rows = rows // 2
    seq, dh = q_ref.shape
    qb = query_block(seq)
    scale = 1.0 / math.sqrt(HD)
    order = source_order(m)
    carry.first()
    loads = [
        pltpu.make_async_copy(ain_ref, ain, l_sem.at[0]),
        pltpu.make_async_copy(qkv_ref, qkv, l_sem.at[1]),
    ]
    for c in loads:
        c.start()
    greet(other_heads() + other_parts())

    here = gheads.at[pl.ds(pl.multiple_of(me * rows, rows), rows)]
    sends = [
        remote(
            gatt_ref.at[:, pl.ds(pl.multiple_of(dev["head"] * dh, 128), dh)], here,
            a_send.at[d], a_recv.at[d], dev,
        )
        for d, dev in enumerate(other_heads())
    ]
    for c in sends:
        c.start()
    gring = Ring(
        lambda c: gao_ref.at[pl.ds(c * half_rows, half_rows)],
        lambda h, c: gao.at[h, pl.ds(c * half_rows, half_rows)],
        g_send, g_recv, n,
    )
    gring.start()
    carry.begin(range(early))
    here[...] = gatt_ref[:, pl.ds(pl.multiple_of(me * dh, 128), dh)]
    gao[me] = gao_ref[...]
    for c in sends:
        c.wait_recv()

    for head in range(dh // HD):
        lanes = pl.ds(head * HD, HD)
        for j in range(seq // qb):
            at = pl.ds(j * qb, qb)
            probs = probs_of(len_ref, q_ref[at, lanes], k_ref[:, lanes])
            grad_probs = dot(gheads[at, lanes], v_ref[:, lanes], NT)
            inner = jnp.sum(probs * grad_probs, axis=-1, keepdims=True)
            grad_scores = (probs * (grad_probs - inner)).astype(BF)
            dproj[at, lanes] = (dot(grad_scores, k_ref[:, lanes]) * scale).astype(BF)
            add_k = dot(grad_scores, q_ref[at, lanes], TN)
            add_v = dot(probs.astype(BF), gheads[at, lanes], TN)
            if j == 0:
                dk[...] = add_k
                dv[...] = add_v
            else:
                dk[...] += add_k
                dv[...] += add_v
        dproj[:, pl.ds(dh + head * HD, HD)] = (dk[...] * scale).astype(BF)
        dproj[:, pl.ds(2 * dh + head * HD, HD)] = dv[...].astype(BF)
        gring.step(head + 1)
    for step in range(dh // HD + 1, 3):
        gring.step(step)

    inv_all = lax.rsqrt(sums_ref[...] / width + EPS)
    dgains = [jnp.zeros((1, HD), F32) for _ in range(2 * dh // HD)]
    for i in range(n):
        at = pl.ds(i * rows, rows)
        cosine = cos_ref[at, :]
        sine = -sin_ref[at, :]
        for kind in range(2):
            inv = as_column(inv_all[kind * n + i : kind * n + i + 1])
            sums = jnp.zeros((rows, 1), F32)
            for head in range(dh // HD):
                spot = kind * (dh // HD) + head
                lanes = pl.ds(kind * dh + head * HD, HD)
                turned = turn(dproj[at, lanes].astype(F32), cosine, sine)
                unit = proj_ref[at, lanes] * inv
                dgains[spot] = dgains[spot] + jnp.sum(turned * unit, axis=0, keepdims=True)
                grad = turned * gains_ref[kind : kind + 1, head * HD : (head + 1) * HD]
                scaled[at, lanes] = grad
                sums = sums + jnp.sum(grad * unit, axis=1, keepdims=True)
            own[pl.ds(kind * n + i, 1), :] = as_row(sums)
    for spot, value in enumerate(dgains):
        dgains_ref[pl.ds(spot, 1), :] = value
    moves = [
        remote(own, buf.at[me], s_send.at[d], s_recv.at[d], dev)
        for d, dev in enumerate(other_heads())
    ]
    for c in moves:
        c.start()
    buf[me] = own[...]
    for c in moves:
        c.wait()
    total_of = buf[0]
    for i in range(1, n):
        total_of = total_of + buf[i]
    means = total_of / width
    for i in range(n):
        at = pl.ds(i * rows, rows)
        for kind in range(2):
            inv = as_column(inv_all[kind * n + i : kind * n + i + 1])
            mean = as_column(means[kind * n + i : kind * n + i + 1])
            for head in range(dh // HD):
                lanes = pl.ds(kind * dh + head * HD, HD)
                unit = proj_ref[at, lanes] * inv
                dproj[at, lanes] = (inv * (scaled[at, lanes] - unit * mean)).astype(BF)

    for c in loads:
        c.wait()
    weight = qkv.reshape(width, 3 * dh)
    for g in range(n // 2):
        part = dot(dproj[pl.ds(g * 2 * rows, 2 * rows), :], weight[...], NT).astype(BF)
        gin[2 * g : 2 * g + 2] = part.reshape(2, rows, width)
    gring.step(3)
    ring = RingSumHere(n, gin, gin_ref, sbuf, rbuf, r_send, r_recv)
    ring.start()

    flat = dqkv.reshape(width, 3 * dh)
    for b in range(width // 512):
        at = pl.ds(b * 512, 512)
        turned = ain.reshape(seq, width)[:, at].T
        flat[at, :] = dot(turned, dproj[...]).astype(BF)
    pair = {"fsdp": x * 2 + 1 - core}
    pairs = [
        remote(dqkv.at[:, order[nx + i]], gq.at[i], p_send.at[i], p_recv.at[i], pair)
        for i in range(nx)
    ]
    for c in pairs:
        c.start()
    for step in range(4, n // 2 + 1):
        gring.step(step)
    for b in range(width // 512):
        at = pl.ds(b * 512, 512)
        value = dot(att_ref[...], gao.reshape(seq, width)[:, at], TN)
        dout[:, :, at] = value.astype(BF).reshape(dout.shape[:2] + (512,))
    pairs_out = [
        remote(dout.at[order[nx + i]], go.at[i], p_send.at[nx + i], p_recv.at[nx + i], pair)
        for i in range(nx)
    ]
    for c in pairs_out:
        c.start()
    ring.step(1)
    for c in pairs + pairs_out:
        c.wait_recv()
    across = []
    for i in range(1, nx):
        there = {"fsdp": ((x + i) % nx) * 2 + core}
        xs[i - 1] = (dqkv[:, order[i]].astype(F32) + gq[i].astype(F32)).astype(BF)
        xso[i - 1] = (dout[order[i]].astype(F32) + go[i].astype(F32)).astype(BF)
        across.append(remote(xs.at[i - 1], xr.at[i - 1], x_send.at[0, i - 1], x_recv.at[0, i - 1], there))
        across.append(remote(xso.at[i - 1], xro.at[i - 1], x_send.at[1, i - 1], x_recv.at[1, i - 1], there))
    for c in across:
        c.start()
    carry.begin(range(early, len(carry.jobs)))
    for step in range(2, n // 2):
        ring.step(step)
    for c in across:
        c.wait_recv()
    value = dqkv[:, order[0]].astype(F32) + gq[0].astype(F32)
    value_out = dout[order[0]].astype(F32) + go[0].astype(F32)
    for i in range(1, nx):
        value = value + xr[i - 1].astype(F32)
        value_out = value_out + xro[i - 1].astype(F32)
    fin[...] = value.astype(BF)
    dout_ref[...] = value_out
    to = [
        dqkv_ref.at[:, pl.ds(pl.multiple_of(j * width + me * dh, 128), dh)] for j in range(3)
    ]
    last = [
        remote(
            fin.at[dev["head"], :, pl.ds(j * dh, dh)], to[j], t_send.at[d, j], t_recv.at[d, j], dev
        )
        for d, dev in enumerate(other_heads())
        for j in range(3)
    ] + [
        pltpu.make_async_copy(fin.at[me, :, pl.ds(j * dh, dh)], to[j], t_sem.at[j])
        for j in range(3)
    ]
    for c in last:
        c.start()
    ring.step(n // 2)
    for c in last:
        c.wait()
    for c in sends + pairs + pairs_out + across:
        c.wait_send()
    gring.finish()
    ring.finish()
    carry.end()


def closing(lengths, gatt, gao, q, k, v, att, proj, sums, gains, cosine, sine, ain, qkv, n, m, kinds,
            arrays, early):
    rows, width = gao.shape
    seq, dh = q.shape
    nx = m // 2
    shard = qkv.shape[2]
    count, shapes, scratch = carry_plan(kinds, arrays, m)

    def vm(*shape, dtype=BF):
        return pltpu.VMEM(shape, dtype)

    return pl.pallas_call(
        functools.partial(closing_kernel, n, m, kinds, early),
        out_shape=[
            jax.ShapeDtypeStruct((rows, width), F32),
            jax.ShapeDtypeStruct((shard, 3 * width), BF),
            jax.ShapeDtypeStruct((shard, width), F32),
            jax.ShapeDtypeStruct((2 * dh // HD, HD), F32),
        ]
        + shapes,
        in_specs=[pl.BlockSpec(memory_space=pltpu.SMEM)] + [WHOLE] * 11 + [ANY] * (2 + count),
        out_specs=[WHOLE, ANY, WHOLE, WHOLE] + [ANY] * len(kinds),
        scratch_shapes=[
            vm(seq, dh), vm(n, rows, width), vm(n, rows, width), vm(n, m, shard, 3 * dh),
            vm(n, rows, width), vm(seq, 3 * dh), vm(seq, 2 * dh, dtype=F32),
            vm(seq, HD, dtype=F32), vm(seq, HD, dtype=F32),
            vm(2 * n, rows, dtype=F32), vm(n, 2 * n, rows, dtype=F32),
            vm(n, m, shard, 3 * dh), vm(nx, n, shard, 3 * dh),
            vm(nx - 1, n, shard, 3 * dh), vm(nx - 1, n, shard, 3 * dh), vm(n, shard, 3 * dh),
            vm(m, shard, width), vm(nx, shard, width),
            vm(nx - 1, shard, width), vm(nx - 1, shard, width),
            vm(2, 2, rows // 2, width), vm(2, n // 2, 2, rows // 2, width),
            DMA((2,)), DMA((n - 1,)), DMA((n - 1,)), DMA((n - 1,)), DMA((n - 1,)),
            DMA((m,)), DMA((m,)), DMA((2, nx - 1)), DMA((2, nx - 1)),
            DMA((n - 1, 3)), DMA((n - 1, 3)), DMA((3,)),
        ]
        + ring_sems(n)
        + ring_sems(n)
        + scratch,
        **big(110, 5),
    )(lengths, gatt, gao, q, k, v, att, proj, sums, gains, cosine, sine, ain, qkv, *arrays)


def settle_kernel(jobs, *refs):
    count = sum(len(sources) for sources, _ in jobs)
    outs = refs[count : count + 3]
    ins, result, l_sem, o_sem = refs[count + 3 :]
    steps, k = [], 0
    for sources, (which, e, columns) in jobs:
        arrays = refs[k : k + len(sources)]
        k += len(sources)
        rows = sources[0][1]
        for part in range(1 if columns else 2):
            size = rows if columns else rows // 2
            steps.append((arrays, sources, part * size, size, which, e, columns))

    def loads(i):
        arrays, sources, start, size = steps[i][:4]
        return [
            pltpu.make_async_copy(
                ref.at[index + (pl.ds(base + start, size),)], ins.at[i % 2, j, pl.ds(0, size)],
                l_sem.at[i % 2, j],
            )
            for j, (ref, (index, _, base)) in enumerate(zip(arrays, sources))
        ]

    def store(i):
        _, _, start, size, which, e, columns = steps[i]
        wide = result.shape[2]
        to = outs[which].at[e]
        to = to.at[:, pl.ds(columns[0], wide)] if columns else to.at[pl.ds(start, size)]
        return pltpu.make_async_copy(result.at[i % 2, pl.ds(0, size)], to, o_sem.at[i % 2])

    for c in loads(0):
        c.start()
    for i, (arrays, _, _, size, *_) in enumerate(steps):
        if i + 1 < len(steps):
            for c in loads(i + 1):
                c.start()
        for c in loads(i):
            c.wait()
        if i >= 2:
            store(i - 2).wait()
        value = ins[i % 2, 0, :size].astype(F32)
        for j in range(1, len(arrays)):
            value = value + ins[i % 2, j, :size].astype(F32)
        result[i % 2, :size] = value
        store(i).start()
    for i in range(max(len(steps) - 2, 0), len(steps)):
        store(i).wait()


def settle(grads, sums, m):
    block, ff = grads[0][0].shape[2:]
    tile = block // 2
    jobs, arrays = [], []
    for e, (same, got) in enumerate(grads):
        for which in range(3):
            k, holder = which, None
            for part in sums[e]:
                if k < part.shape[1]:
                    holder = part
                    break
                k -= part.shape[1]
            for half in range(1 if which < 2 else 2):
                rows, base = (block, 0) if which < 2 else (tile, half * tile)
                sources = [((0, which), rows, base)] * 2
                sources += [((i, k), rows, base) for i in range(m // 2 - 1)]
                arrays += [same, got] + [holder] * (m // 2 - 1)
                columns = None if which < 2 else (half * ff,)
                jobs.append((tuple(sources), (which, e, columns)))
    return pl.pallas_call(
        functools.partial(settle_kernel, tuple(jobs)),
        out_shape=[jax.ShapeDtypeStruct((EXP_DEV, block, ff), F32)] * 2
        + [jax.ShapeDtypeStruct((EXP_DEV, tile, 2 * ff), F32)],
        in_specs=[ANY] * len(arrays),
        out_specs=[ANY] * 3,
        scratch_shapes=[
            pltpu.VMEM((2, m // 2 + 1, tile, ff), BF),
            pltpu.VMEM((2, tile, ff), F32),
            DMA((2, m // 2 + 1)), DMA((2,)),
        ],
        compiler_params=pltpu.CompilerParams(vmem_limit_bytes=60 << 20),
        cost_estimate=cost(10),
    )(*arrays)


def joined(same, got):
    return same.astype(F32) + got.astype(F32)


def body(
    hidden,
    w_qkv,
    w_out,
    w_router,
    g_attn,
    g_ffn,
    g_q,
    g_k,
    w_gate,
    w_up,
    w_down,
    lengths,
    routes,
    route_codes,
    cotangent,
):
    n = lax.axis_size("head")
    m = lax.axis_size("fsdp")
    me = lax.axis_index("head")
    rows = hidden.shape[1]
    width = hidden.shape[2]
    seq = rows * n
    lh = HEADS // n
    dh = lh * HD
    experts = EXP_DEV * n
    shard = w_qkv.shape[0]
    both = ("head", "fsdp")

    sides = 128 // shard
    lane = jnp.arange(128, dtype=jnp.int32) // shard == lax.axis_index("fsdp") % sides
    small = jnp.tile(jnp.stack([g_attn, g_ffn, g_q, g_k]), (2, sides)).astype(F32)
    small = jnp.concatenate(
        [jnp.where(lane[None, :], small, 0.0), w_router.astype(F32).reshape(-1, 128)]
    )
    def inverse_rms(values):
        return lax.rsqrt(jnp.mean(values * values, axis=-1, keepdims=True) + EPS)

    angles = np.arange(seq)[:, None] * ROPE_BASE ** (-2.0 * np.arange(HD // 2) / HD)
    cosine = np.tile(np.cos(angles), (1, 2)).astype(np.float32)
    sine = np.concatenate([-np.sin(angles), np.sin(angles)], axis=1).astype(np.float32)
    (attn_input, qkv, proj, sums, queries, keys, values, attended, attended_tok, full_out, small,
     gains_wide, gains_heads, gate0x, up0x, down0x) = opening(
        lengths, hidden[0], w_qkv, w_out, small, cosine, sine, n, m, (("share", 0),) * 3,
        (w_gate, w_up, w_down),
    )
    router = small[:, :, 8:].reshape(width, experts).astype(BF)
    gain_attn, gain_ffn = gains_wide
    full_out = full_out.reshape(width, width)
    half = rows // 2
    own_w = (w_gate, w_up, w_down)
    over_x = (gate0x, up0x, down0x)
    residual, own_input, spread, x_a, cot_a, mine, gate1x, up1x, *got = routing(
        hidden[0], attended_tok, full_out, gains_wide[1:], jnp.pad(router, ((0, 0), (0, 128 - experts))),
        routes[0], route_codes[0], cotangent[0], n, m, experts,
        (("share", 1),) * 2 + (("pair", 0),) * 3 + ("pair",) * 3 + (("pair", 1),) * 3,
        (w_gate, w_up, *own_w, *over_x, *own_w),
    )
    spread = spread[:, :experts]
    weights0 = [(over_x[i], got[i], got[3 + i]) for i in range(3)]
    mine = mine.transpose(0, 2, 1)
    span = n * half

    def rows_of(part):
        return part.reshape(span, width)

    gates_a = mine[:, :half].reshape(span, EXP_DEV)
    gates_b = mine[:, half:].reshape(span, EXP_DEV)
    fresh = [gate1x, got[6], up1x, got[7], got[8]]
    dots_a, acts_a, gin_a, mix_a, x_b, cot_b, down1x, gate1c, up1c, down1c = experts_a(
        rows_of(x_a), rows_of(cot_a), gates_a, own_w, weights0, fresh, own_input[half:],
        cotangent[0, half:], n, m,
    )
    weights1 = [(gate1x, got[6], gate1c), (up1x, got[7], up1c), (down1x, got[8], down1c)]
    dots_b, acts_b, gin_b, mix_b, grad_ffn_a, summed_a, *grads0 = experts_b(
        rows_of(x_b), rows_of(cot_b), gates_b, own_w, weights0 + weights1, gin_a, mix_a,
        rows_of(x_a), rows_of(cot_a), acts_a, n, m,
    )
    dots = jnp.concatenate(
        [d.reshape(n, half, EXP_DEV).transpose(0, 2, 1) for d in (dots_a, dots_b)], axis=2
    )

    early = len(grads0) > 0
    grads, grad_ffn_b, summed_b, dots, sums0 = experts_d(
        (x_a, cot_a, acts_a), (x_b, cot_b, acts_b), gin_b, mix_b, dots, n, m,
        (1,) if early else (0, 1), (("join", 0, 2),) * early, tuple(grads0),
    )
    grads = [tuple(grads0)] * early + grads
    grad_ffn = jnp.concatenate([grad_ffn_a, grad_ffn_b], axis=0)
    summed = jnp.concatenate([summed_a, summed_b], axis=0)
    dots = dots.reshape(experts, rows).T
    grad_rows = cotangent[0].astype(F32)
    grad_logits = spread * (dots - jnp.sum(spread * dots, axis=1, keepdims=True))
    high = lax.Precision.HIGHEST
    grad_ffn = grad_ffn + jnp.dot(grad_logits, router.astype(F32).T, precision=high)
    grad_router = jnp.dot(own_input.astype(F32).T, grad_logits, precision=high)

    def norm_back(values, gain, grad):
        inv = inverse_rms(values)
        unit = values * inv
        scaled = grad * gain
        back = inv * (scaled - unit * jnp.mean(scaled * unit, axis=-1, keepdims=True))
        return back, jnp.sum(grad * unit, axis=0)

    back, grad_gain_ffn = norm_back(residual, gain_ffn, grad_ffn)
    grad_residual = grad_rows + back
    grad_attn_out = grad_residual.astype(BF)
    grad_attended = dot(grad_attn_out, full_out, NT).astype(BF)
    spans = [(span, 0) for span in (((2, 3),) if early else ((0, 2), (2, 3)))]
    spans += [(span, 1) for span in ((0, 1), (1, 2), (2, 3))]
    if early:
        kinds = tuple(("join",) + span for span, _ in spans)
        riders = [a for _, e in spans for a in grads[e]]
    else:
        kinds = ("across",) * len(spans)
        riders = [
            joined(*(part[1:, a:b] for part in grads[e])).astype(BF) for (a, b), e in spans
        ]
    grad_attn_in, grad_qkv, grad_out_w, grad_gains, *arrived = closing(
        lengths, grad_attended, grad_attn_out, queries, keys, values, attended, proj, sums,
        gains_heads, cosine, sine, attn_input, qkv, n, m,
        kinds, riders, 3,
    )
    sums0 = list(sums0) + arrived[:-3]
    sums1 = arrived[-3:]
    grad_gain_q, grad_gain_k = grad_gains.reshape(2, dh)
    out_rows = residual + summed

    grad_w_gate, grad_w_up, grad_w_down = settle(grads, (sums0, sums1), m)
    grad_qkv = grad_qkv.astype(F32)

    back, grad_gain_attn = norm_back(hidden[0].astype(F32), gain_attn, grad_attn_in)
    grad_hidden = grad_residual + back

    def at_mine(piece):
        return lax.dynamic_update_slice_in_dim(jnp.zeros((width,), F32), piece, me * dh, 0)

    pack = jnp.concatenate(
        [grad_router.reshape(n * m, shard * experts)]
        + [
            g.reshape(n * m, shard)
            for g in (grad_gain_attn, grad_gain_ffn, at_mine(grad_gain_q), at_mine(grad_gain_k))
        ],
        axis=1,
    )
    pack = lax.all_to_all(pack, both, split_axis=0, concat_axis=0, tiled=True)
    pack = jnp.sum(pack, axis=0)
    small_grads = pack[shard * experts :].reshape(4, shard)
    return (
        out_rows.astype(BF)[None],
        grad_hidden[None],
        grad_qkv,
        grad_out_w,
        pack[: shard * experts].reshape(shard, experts),
        small_grads[0],
        small_grads[1],
        small_grads[2],
        small_grads[3],
        grad_w_gate,
        grad_w_up,
        grad_w_down,
    )


def solution(mesh):
    both = ("head", "fsdp")
    return jax.shard_map(
        body,
        mesh=mesh,
        in_specs=(
            P("fsdp", "head", None),
            P(both, None),
            P(both, None),
            P(both, None),
            P(both),
            P(both),
            P(both),
            P(both),
            P("head", "fsdp", None),
            P("head", "fsdp", None),
            P("head", "fsdp", None),
            P("fsdp"),
            P("fsdp", "head", None),
            P("fsdp", "head", None),
            P("fsdp", "head", None),
        ),
        out_specs=(
            P("fsdp", "head", None),
            P("fsdp", "head", None),
            P(both, None),
            P(both, None),
            P(both, None),
            P(both),
            P(both),
            P(both),
            P(both),
            P("head", "fsdp", None),
            P("head", "fsdp", None),
            P("head", "fsdp", None),
        ),
        check_vma=False,
    )
```

```python
import functools
import math

import jax
import jax.numpy as jnp
import numpy as np
from jax import lax
from jax.experimental import pallas as pl
from jax.experimental.pallas import tpu as pltpu
from jax.sharding import PartitionSpec as P

HEADS = 16
HD = 128
FF = 1024
TOP = 8
EXP_DEV = 2

EPS = 1e-06
ROPE_BASE = 10000.0
NEGATIVE = -1e30
BF = jnp.bfloat16
F32 = jnp.float32
NN = ((1,), (0,))
NT = ((1,), (1,))
TN = ((0,), (0,))
ANY = pl.BlockSpec(memory_space=pl.ANY)
WHOLE = pl.BlockSpec(memory_space=pltpu.VMEM)
DMA = pltpu.SemaphoreType.DMA


def dot(a, b, dims=NN):
    return lax.dot_general(a, b, (dims, ((), ())), preferred_element_type=F32)


def cost(us):
    return pl.CostEstimate(flops=0, bytes_accessed=int(us * 3.6e6), transcendentals=0)


def ring_place():
    n = lax.axis_size("head")
    me = lax.axis_index("head")
    odd = me % 2
    return (1 - odd) * (me // 2) + odd * (n - 1 - me // 2)


def head_at(offset):
    n = lax.axis_size("head")
    k = (ring_place() + (offset + n)) % n
    down = k // (n // 2)
    return (1 - down) * 2 * k + down * (2 * n - 1 - 2 * k)


def remote(src, dst, send, recv, device):
    return pltpu.make_async_remote_copy(
        src_ref=src,
        dst_ref=dst,
        send_sem=send,
        recv_sem=recv,
        device_id=device,
        device_id_type=pl.DeviceIdType.MESH,
    )


def greet(devices):
    barrier = pltpu.get_barrier_semaphore()
    for device in devices:
        pl.semaphore_signal(
            barrier, inc=1, device_id=device, device_id_type=pl.DeviceIdType.MESH
        )
    pl.semaphore_wait(barrier, len(devices))


def other_heads():
    n = lax.axis_size("head")
    me = lax.axis_index("head")
    return [{"head": (me + d) % n} for d in range(1, n)]


def other_parts():
    m = lax.axis_size("fsdp")
    f = lax.axis_index("fsdp")
    return [{"fsdp": (f + d) % m} for d in range(1, m)]


class Ring:
    def __init__(self, own, place, send, recv, n):
        self.own, self.place, self.send, self.recv = own, place, send, recv
        self.half = n // 2

    def exists(self, way, step, c):
        return step < self.half or c == way

    def message(self, way, step, c):
        owner = head_at((1 - step) if way == 0 else (step - 1))
        return remote(
            self.own(c) if step == 1 else self.place(owner, c),
            self.place(owner, c),
            self.send.at[way, step - 1, c],
            self.recv.at[way, step - 1, c],
            {"head": head_at(1 if way == 0 else -1)},
        )

    def start(self):
        for c in range(2):
            for way in range(2):
                if self.exists(way, 1, c):
                    self.message(way, 1, c).start()

    def step(self, step):
        for c in range(2):
            for way in range(2):
                if self.exists(way, step, c):
                    self.message(way, step, c).wait_recv()
                    if step < self.half and self.exists(way, step + 1, c):
                        self.message(way, step + 1, c).start()

    def finish(self):
        for step in range(1, self.half + 1):
            for c in range(2):
                for way in range(2):
                    if self.exists(way, step, c):
                        self.message(way, step, c).wait_send()


def ring_sems(n):
    return [DMA((2, n // 2, 2)), DMA((2, n // 2, 2))]


class Carry:
    def __init__(self, kinds, ins, outs, send, recv, *joins):
        self.jobs, k = [], 0
        stages = list(joins)
        for kind, dst in zip(kinds, outs):
            name = kind if isinstance(kind, str) else kind[0]
            if name == "join":
                self.jobs.append((name, stages.pop(0), dst, kind[1:], ins[k : k + 2]))
                k += 2
                continue
            src = ins[k] if isinstance(kind, str) else ins[k].at[kind[1]]
            self.jobs.append((name, src, dst, None, None))
            k += 1
        self.tmp, self.j_sem = stages if stages else (None, None)
        self.fetched = None
        self.send, self.recv = send, recv

    def copies(self, j):
        m = lax.axis_size("fsdp")
        f = lax.axis_index("fsdp")
        nx = m // 2
        x, core = f // 2, f % 2
        name, src, dst = self.jobs[j][:3]
        if name == "pair":
            other = {"fsdp": x * 2 + 1 - core}
            return [remote(src, dst, self.send.at[j, 0], self.recv.at[j, 0], other)]
        return [
            remote(
                src if name == "share" else src.at[i - 1], dst.at[i - 1],
                self.send.at[j, i - 1], self.recv.at[j, i - 1],
                {"fsdp": ((x + i) % nx) * 2 + core},
            )
            for i in range(1, nx)
        ]

    def fetch(self, j):
        _, stage, _, (a, b), arrays = self.jobs[j]
        tmp = self.tmp.at[:, pl.ds(0, b - a)]
        self.fetched = [
            pltpu.make_async_copy(
                arrays[i].at[pl.ds(1, stage.shape[0]), pl.ds(a, b - a)], (stage, tmp)[i],
                self.j_sem.at[i],
            )
            for i in range(2)
        ]
        for c in self.fetched:
            c.start()

    def first(self):
        if self.jobs and self.jobs[0][0] == "join":
            self.fetch(0)

    def join(self, j):
        _, stage, _, (a, b), _ = self.jobs[j]
        if self.fetched is None:
            self.fetch(j)
        for c in self.fetched:
            c.wait()
        self.fetched = None
        for i in range(stage.shape[0]):
            for k in range(b - a):

                @pl.loop(0, stage.shape[2] // 64)
                def _(r, i=i, k=k):
                    at = pl.ds(pl.multiple_of(r * 64, 64), 64)
                    stage[i, k, at] = (
                        stage[i, k, at].astype(F32) + self.tmp[i, k, at].astype(F32)
                    ).astype(BF)

    def begin(self, some=None):
        for j in range(len(self.jobs)) if some is None else some:
            if self.jobs[j][0] == "join":
                self.join(j)
            for c in self.copies(j):
                c.start()

    def arrived(self, j):
        for c in self.copies(j):
            c.wait_recv()

    def end(self, seen=()):
        for j in range(len(self.jobs)):
            for c in self.copies(j):
                if j not in seen:
                    c.wait_recv()
                c.wait_send()


def carry_plan(kinds, arrays, m):
    shapes, stages, k = [], [], 0
    for kind in kinds:
        if kind[0] == "join":
            a, b = kind[1:]
            shape = (m // 2 - 1, b - a) + arrays[k].shape[2:]
            stages.append(shape)
            k += 2
        else:
            name = kind if isinstance(kind, str) else kind[0]
            shape = arrays[k].shape if isinstance(kind, str) else arrays[k].shape[1:]
            shape = (m // 2 - 1,) * (name == "share") + shape
            k += 1
        shapes.append(jax.ShapeDtypeStruct(shape, BF))
    sems = (max(len(kinds), 1), max(m // 2 - 1, 1))
    scratch = [DMA(sems), DMA(sems)] + [pltpu.VMEM(shape, BF) for shape in stages]
    if stages:
        widest = max(stages, key=lambda shape: shape[1])
        scratch += [pltpu.VMEM(widest, BF), DMA((2,))]
    return k, shapes, scratch


def carried(kinds):
    joins = sum(kind[0] == "join" for kind in kinds)
    return len(kinds) + joins, 2 + joins + 2 * (joins > 0)


def routing_kernel(n, m, experts, kinds, *refs):
    k, back = carried(kinds)
    (hid_ref, tok_ref, wout_ref, gain_ref, router_ref, routes_ref, codes_ref, cot_ref) = refs[:8]
    res_ref, own_ref, spread_ref, xa_ref, cota_ref, mine_ref = refs[8 + k : 14 + k]
    (wout, sets, w_sem, copies, x_send, x_recv, t_send, t_recv, e_send, e_recv) = refs[
        14 + k + len(kinds) : -back
    ]
    carry = Carry(kinds, refs[8 : 8 + k], refs[14 + k : 14 + k + len(kinds)], *refs[-back:])
    me = lax.axis_index("head")
    rows, width = hid_ref.shape
    half = rows // 2
    part = half // 2
    lanes = width // 4
    loads = [
        pltpu.make_async_copy(
            wout_ref.at[:, pl.ds(i * lanes, lanes)], wout.at[:, pl.ds(i * lanes, lanes)],
            w_sem.at[i],
        )
        for i in range(4)
    ]
    for c in loads:
        c.start()
    greet(other_heads() + other_parts())

    def ring_of(own, out, send, recv):
        return Ring(
            lambda c: own.at[pl.ds(c * part, part)],
            lambda h, c: out.at[h, pl.ds(c * part, part)],
            send, recv, n,
        )

    ring_cot = ring_of(cot_ref, cota_ref, t_send, t_recv)
    ring_x = ring_of(own_ref, xa_ref, x_send, x_recv)
    ring_cot.start()
    carry.begin()
    moves = [pltpu.make_async_copy(cot_ref.at[pl.ds(0, half)], cota_ref.at[me], copies.at[0])]
    moves[0].start()
    for i in range(4):
        at = pl.ds(i * lanes, lanes)
        loads[i].wait()
        res_ref[:, at] = hid_ref[:, at].astype(F32) + dot(tok_ref[...], wout[:, at])
    residual = res_ref[...]
    inv = lax.rsqrt(jnp.mean(residual * residual, axis=-1, keepdims=True) + EPS)
    own_ref[...] = (residual * inv * gain_ref[...]).astype(BF)
    ring_cot.step(1)
    ring_x.start()
    moves.append(pltpu.make_async_copy(own_ref.at[pl.ds(0, half)], xa_ref.at[me], copies.at[1]))
    moves[1].start()

    logits = dot(own_ref[...], router_ref[...])
    expert = lax.broadcasted_iota(jnp.int32, logits.shape, 1)
    matches, chosen = [], []
    for j in range(TOP):
        matches.append(expert == routes_ref[:, j : j + 1])
        picked = jnp.sum(jnp.where(matches[j], logits, 0.0), axis=1, keepdims=True)
        chosen.append(picked + codes_ref[:, j : j + 1].astype(F32) / 1024.0)
    peak = functools.reduce(jnp.maximum, chosen)
    chosen = [jnp.exp(c - peak) for c in chosen]
    whole = functools.reduce(lambda a, b: a + b, chosen)
    spread = jnp.zeros_like(logits)
    for j in range(TOP):
        spread = spread + jnp.where(matches[j], chosen[j] / whole, 0.0)
    spread_ref[...] = spread
    turned = spread.T
    for h in range(n):
        sets[h] = turned[h * EXP_DEV : (h + 1) * EXP_DEV]
    moves.append(pltpu.make_async_copy(sets.at[me], mine_ref.at[me], copies.at[2]))
    moves += [
        remote(sets.at[dev["head"]], mine_ref.at[me], e_send.at[d], e_recv.at[d], dev)
        for d, dev in enumerate(other_heads())
    ]
    for c in moves[2:]:
        c.start()
    for step in range(2, n // 2 + 1):
        ring_cot.step(step)
        ring_x.step(step - 1)
    ring_x.step(n // 2)
    for c in moves:
        c.wait()
    ring_cot.finish()
    ring_x.finish()
    carry.end()


def routing(hid, tok, w_out, gain, router, routes, codes, cot, n, m, experts, kinds, arrays):
    rows, width = hid.shape
    count, shapes, scratch = carry_plan(kinds, arrays, m)
    halves = jax.ShapeDtypeStruct((n, rows // 2, width), BF)
    return pl.pallas_call(
        functools.partial(routing_kernel, n, m, experts, kinds),
        out_shape=[
            jax.ShapeDtypeStruct((rows, width), F32),
            jax.ShapeDtypeStruct((rows, width), BF),
            jax.ShapeDtypeStruct((rows, 128), F32),
            halves, halves,
            jax.ShapeDtypeStruct((n, EXP_DEV, rows), F32),
        ]
        + shapes,
        in_specs=[WHOLE, WHOLE, ANY] + [WHOLE] * 5 + [ANY] * count,
        out_specs=[WHOLE] * 3 + [ANY] * (3 + len(kinds)),
        scratch_shapes=[
            pltpu.VMEM((width, width), BF),
            pltpu.VMEM((n, EXP_DEV, rows), F32),
            DMA((4,)), DMA((3,)),
        ]
        + ring_sems(n)
        + ring_sems(n)
        + [DMA((n - 1,)), DMA((n - 1,))]
        + scratch,
        compiler_params=pltpu.CompilerParams(
            collective_id=1, has_side_effects=True, vmem_limit_bytes=60 << 20
        ),
        cost_estimate=cost(55),
    )(hid, tok, w_out, gain, router, routes, codes, cot, *arrays)


class RingSum:
    def __init__(self, n, parts, out_ref, own, sbuf, rbuf, loads, send, recv):
        self.n, self.half, self.parts, self.out_ref = n, n // 2, parts, out_ref
        self.own, self.sbuf, self.rbuf, self.loads = own, sbuf, rbuf, loads
        self.send, self.recv = send, recv
        self.rows = out_ref.shape[0] // 2
        self.order = (
            [self.half] + [s * w for s in range(self.half - 1, 0, -1) for w in (1, -1)] + [0]
        )
        self.ready, self.started = set(), []

    def fetch(self, o):
        i = self.order.index(o)
        return pltpu.make_async_copy(self.parts.at[head_at(o)], self.own.at[i], self.loads.at[i])

    def load(self):
        for o in self.order:
            self.fetch(o).start()

    def piece(self, o, c):
        if o not in self.ready:
            self.fetch(o).wait()
            self.ready.add(o)
        return self.own[self.order.index(o), pl.ds(c * self.rows, self.rows)].astype(F32)

    def buffer(self, way, t, c):
        first = 1 if c == way else 2
        return self.sbuf.at[way, t - 1] if t == first else self.rbuf.at[way, t - 2, c]

    def message(self, way, t, c):
        return remote(
            self.buffer(way, t, c), self.rbuf.at[way, t - 1, c],
            self.send.at[way, t - 1, c], self.recv.at[way, t - 1, c],
            {"head": head_at(1 if way == 0 else -1)},
        )

    def offset(self, way, o):
        return o if way == 0 or o == self.half else -o

    def ship(self, way, t, c, value):
        self.buffer(way, t, c)[...] = value.astype(BF)
        self.message(way, t, c).start()
        self.started.append((way, t, c))

    def start(self):
        for way in range(2):
            self.ship(way, 1, way, self.piece(self.half, way))
        for way in range(2):
            self.ship(way, 2, 1 - way, self.piece(self.offset(way, self.half - 1), 1 - way))

    def step(self, t):
        if t < self.half:
            for c in range(2):
                for way in range(2):
                    if t == 1 and c != way:
                        continue
                    self.message(way, t, c).wait_recv()
                    self.ship(
                        way, t + 1, c,
                        self.piece(self.offset(way, self.half - t), c)
                        + self.rbuf[way, t - 1, c].astype(F32),
                    )
            return
        last = self.half - 1
        for c in range(2):
            for way in range(2):
                self.message(way, self.half, c).wait_recv()
            self.out_ref[pl.ds(c * self.rows, self.rows)] = (
                self.piece(0, c)
                + self.rbuf[0, last, c].astype(F32)
                + self.rbuf[1, last, c].astype(F32)
            )

    def finish(self):
        for way, t, c in self.started:
            self.message(way, t, c).wait_send()


def ring_sum_scratch(n, rows, width):
    return [
        pltpu.VMEM((n, rows, width), BF),
        pltpu.VMEM((2, 2, rows // 2, width), BF),
        pltpu.VMEM((2, n // 2, 2, rows // 2, width), BF),
        DMA((n,)),
    ] + ring_sems(n)


def probs_of(len_ref, q, k):
    scores = dot(q, k, NT) * (1.0 / math.sqrt(HD))
    at = lax.broadcasted_iota(jnp.int32, scores.shape, 1)
    scores = jnp.where(at < len_ref[0], scores, NEGATIVE)
    exponent = jnp.exp(scores - jnp.max(scores, axis=-1, keepdims=True))
    return exponent / jnp.sum(exponent, axis=-1, keepdims=True)


def query_block(seq):
    return 256 if seq <= 1024 else 128


def as_column(row):
    return jnp.broadcast_to(row, (row.shape[1], row.shape[1])).T


def as_row(column):
    return jnp.broadcast_to(column, (column.shape[0], column.shape[0])).T[:1]


def turn(values, cosine, sine):
    return values * cosine + pltpu.roll(values, HD // 2, 1) * sine


def opening_kernel(n, m, kinds, *refs):
    k, _ = carried(kinds)
    len_ref, x_ref, w_ref, wo_ref, gain_ref, cos_ref, sin_ref = refs[:7]
    (ain_ref, qkv_ref, proj_ref, sums_ref, q_ref, k_ref, v_ref, att_ref, tok_ref, wout_ref,
     gall_ref, wide_ref, narrow_ref) = refs[7 + k : 20 + k]
    (hid, qkv, wpair, gall, ain, buf, own, out_sem, copies, s_send, s_recv,
     w_send, w_recv, f_send, f_recv, g_send, g_recv, a_send, a_recv, o_send, o_recv,
     c_send, c_recv, t_send, t_recv, t_sem, h_send, h_recv, r_send, r_recv) = refs[20 + 2 * k : -2]
    carry = Carry(kinds, refs[7 : 7 + k], refs[20 + k : 20 + 2 * k], *refs[-2:])
    me = lax.axis_index("head")
    f = lax.axis_index("fsdp")
    nx = m // 2
    x, core = f // 2, f % 2
    rows, width = x_ref.shape
    dh = q_ref.shape[1]
    seq = n * rows
    qb = query_block(seq)
    part_rows = rows // 2

    def part(i, side):
        return ((x + i) % nx) * 2 + side

    pair = {"fsdp": part(0, 1 - core)}
    greet(other_heads() + other_parts())

    ring = Ring(
        lambda c: x_ref.at[pl.ds(c * part_rows, part_rows)],
        lambda h, c: hid.at[h, pl.ds(c * part_rows, part_rows)],
        h_send, h_recv, n,
    )
    to_parts = [
        remote(gain_ref, gall.at[me, f], g_send.at[d], g_recv.at[d], dev)
        for d, dev in enumerate(other_parts())
    ]
    outs = [
        remote(
            wo_ref, wpair.at[x], o_send.at[i - 1], o_recv.at[i - 1], {"fsdp": part(nx - i, core)}
        )
        for i in range(1, nx)
    ]
    columns = [
        remote(
            w_ref.at[:, pl.ds(pl.multiple_of(j * width + dev["head"] * dh, 128), dh)],
            qkv.at[me, f, :, pl.ds(j * dh, dh)],
            w_send.at[d, j],
            w_recv.at[d, j],
            dev,
        )
        for d, dev in enumerate(other_heads())
        for j in range(3)
    ]
    for c in to_parts + outs:
        c.start()
    carry.begin([0])
    ring.start()
    for c in columns:
        c.start()
    gall[me, f] = gain_ref[...]
    wpair[x] = wo_ref[...]
    hid[me] = x_ref[...]
    for j in range(3):
        qkv[me, f, :, pl.ds(j * dh, dh)] = w_ref[
            :, pl.ds(pl.multiple_of(j * width + me * dh, 128), dh)
        ]
    for c in to_parts:
        c.wait_recv()
    gains = [
        remote(gall.at[me], gall.at[me], a_send.at[d], a_recv.at[d], dev)
        for d, dev in enumerate(other_heads())
    ]
    for c in gains:
        c.start()
    for c in gains:
        c.wait_recv()

    def gain_row(k):
        return jnp.concatenate(
            [
                sum(gall[h, i * fs + j, k : k + 1, :] for j in range(fs))
                for h in range(n)
                for i in range(m // fs)
            ],
            axis=1,
        )

    fs = 128 // w_ref.shape[0]
    gain_attn = gain_row(0)
    stores = []

    def store(src, dst, sem):
        stores.append(pltpu.make_async_copy(src, dst, sem))
        stores[-1].start()

    def normalise(i, slot):
        wide = hid[i].astype(F32)
        inv = lax.rsqrt(jnp.mean(wide * wide, axis=-1, keepdims=True) + EPS)
        ain[i] = (wide * inv * gain_attn).astype(BF)
        store(ain.at[i], ain_ref.at[i], out_sem.at[slot])

    normalise(me, 0)
    for c in columns:
        c.wait_recv()
    across = [
        remote(qkv.at[:, f], qkv.at[:, f], f_send.at[i], f_recv.at[i], {"fsdp": part(nx - i, core)})
        for i in range(1, nx)
    ]
    for c in across:
        c.start()
    carry.begin(range(1, len(carry.jobs)))

    def beside(i):
        there = qkv.at[:, part(i, core)]
        return remote(there, there, f_send.at[nx + i], f_recv.at[nx + i], pair)

    beside(0).start()

    def receive(step):
        ring.step(step)
        normalise(head_at(step), 2 * step - 1)
        normalise(head_at(-step), 2 * step)

    for step in range(1, n // 2 - 1):
        receive(step)

    halves = nx // 2
    for c in outs:
        c.wait_recv()
    wring = Ring(
        lambda c: wpair.at[pl.ds(c * halves, halves)],
        lambda h, c: wout_ref.at[h, pl.ds(c * halves, halves), core],
        r_send, r_recv, n,
    )
    wring.start()
    mine = pltpu.make_async_copy(wpair, wout_ref.at[me, :, core], copies.at[0])
    mine.start()

    def over(offset, slot):
        there = wout_ref.at[head_at(offset), :, core]
        return remote(there, there, c_send.at[slot], c_recv.at[slot], pair)

    def advance(step):
        wring.step(step)
        if step < n // 2:
            over(step, 2 * step - 1).start()
            over(-step, 2 * step).start()
        else:
            over(step, n - 1).start()

    receive(n // 2 - 1)
    ring.step(n // 2)
    normalise(head_at(n // 2), n - 1)
    for i, c in enumerate(across):
        c.wait_recv()
        beside(i + 1).start()
    mine.wait()
    over(0, 0).start()
    advance(1)
    for i in range(nx):
        beside(i).wait_recv()
    store(qkv, qkv_ref, copies.at[1])
    weight = qkv.reshape(width, 3 * dh)
    for g in range(n // 2):
        at = pl.ds(g * 2 * rows, 2 * rows)
        projected = dot(ain[2 * g : 2 * g + 2].reshape(2 * rows, width), weight[...])
        proj_ref[at, :] = projected[:, : 2 * dh]
        v_ref[at, :] = projected[:, 2 * dh :].astype(BF)
        for k in range(2):
            squares = projected[:, k * dh : (k + 1) * dh]
            squares = jnp.sum(squares * squares, axis=1, keepdims=True)
            for j in range(2):
                own[pl.ds(k * n + 2 * g + j, 1), :] = as_row(squares[j * rows : (j + 1) * rows])
    moves = [
        remote(own, buf.at[me], s_send.at[d], s_recv.at[d], dev)
        for d, dev in enumerate(other_heads())
    ]
    for c in moves:
        c.start()
    buf[me] = own[...]
    gain_q, gain_k = (
        jnp.concatenate(
            [
                sum(gall[me, i * fs + j, k : k + 1, :] for j in range(fs))
                for i in range(m // fs)
            ],
            axis=1,
        )
        for k in (2, 3)
    )
    gall_ref[...] = gall[...]
    wide_ref[0:1] = gain_attn
    wide_ref[1:2] = gain_row(1)
    narrow_ref[0:1] = gain_q
    narrow_ref[1:2] = gain_k
    for c in moves:
        c.wait()
    total_of = buf[0]
    for i in range(1, n):
        total_of = total_of + buf[i]
    sums_ref[...] = total_of
    inv_all = lax.rsqrt(total_of / width + EPS)
    advance(2)
    for i in range(n):
        at = pl.ds(i * rows, rows)
        inv_q = as_column(inv_all[i : i + 1])
        inv_k = as_column(inv_all[n + i : n + i + 1])
        cosine = cos_ref[at, :]
        sine = sin_ref[at, :]
        for head in range(dh // HD):
            lanes = pl.ds(head * HD, HD)
            k_lanes = pl.ds(dh + head * HD, HD)
            span = slice(head * HD, (head + 1) * HD)
            q_ref[at, lanes] = turn(
                proj_ref[at, lanes] * inv_q * gain_q[:, span], cosine, sine
            ).astype(BF)
            k_ref[at, lanes] = turn(
                proj_ref[at, k_lanes] * inv_k * gain_k[:, span], cosine, sine
            ).astype(BF)
    to = tok_ref.at[:, pl.ds(pl.multiple_of(me * dh, 128), dh)]

    def leave(h):
        return remote(att_ref.at[pl.ds(h * rows, rows)], to, t_send.at[h], t_recv.at[me], {"head": h})

    def arrive(h):
        return remote(
            att_ref.at[pl.ds(h * rows, rows)], tok_ref.at[:, pl.ds(h * dh, dh)],
            t_send.at[h], t_recv.at[h], {"head": h},
        )

    def stay(h):
        return pltpu.make_async_copy(att_ref.at[pl.ds(h * rows, rows)], to, t_sem.at[h])

    for j in range(seq // qb):
        at = pl.ds(j * qb, qb)
        for head in range(dh // HD):
            lanes = pl.ds(head * HD, HD)
            probs = probs_of(len_ref, q_ref[at, lanes], k_ref[:, lanes])
            att_ref[at, lanes] = dot(probs.astype(BF), v_ref[:, lanes]).astype(BF)
        for h in range(j * qb // rows, (j + 1) * qb // rows):

            @pl.when(me != h)
            def _(h=h):
                leave(h).start()

            @pl.when(me == h)
            def _(h=h):
                stay(h).start()

        if j == 1:
            advance(3)
    for step in range(4, n // 2 + 1):
        advance(step)
    for h in range(n):

        @pl.when(me != h)
        def _(h=h):
            leave(h).wait_send()
            arrive(h).wait_recv()

        @pl.when(me == h)
        def _(h=h):
            stay(h).wait()

    for c in stores:
        c.wait()
    for slot in range(n):
        over(0, slot).wait_recv()
    over(0, 0).wait_send()
    for step in range(1, n // 2):
        over(step, 2 * step - 1).wait_send()
        over(-step, 2 * step).wait_send()
    over(n // 2, n - 1).wait_send()
    for c in to_parts + outs + columns + gains + across:
        c.wait_send()
    for i in range(nx):
        beside(i).wait_send()
    ring.finish()
    wring.finish()
    carry.end()


def opening(lengths, x, w, w_out, gains, cosine, sine, n, m, kinds, arrays):
    rows, width = x.shape
    seq = n * rows
    shard = w.shape[0]
    dh = w.shape[1] // 3 // n
    heads = jax.ShapeDtypeStruct((seq, dh), BF)
    count, shapes, scratch = carry_plan(kinds, arrays, m)
    return pl.pallas_call(
        functools.partial(opening_kernel, n, m, kinds),
        out_shape=[
            jax.ShapeDtypeStruct((n, rows, width), BF),
            jax.ShapeDtypeStruct((n, m, shard, 3 * dh), BF),
            jax.ShapeDtypeStruct((seq, 2 * dh), F32),
            jax.ShapeDtypeStruct((2 * n, rows), F32),
            heads, heads, heads, heads,
            jax.ShapeDtypeStruct((rows, width), BF),
            jax.ShapeDtypeStruct((n, m // 2, 2, shard, width), BF),
            jax.ShapeDtypeStruct((n, m) + gains.shape, F32),
            jax.ShapeDtypeStruct((2, width), F32),
            jax.ShapeDtypeStruct((2, dh), F32),
        ]
        + shapes,
        in_specs=[pl.BlockSpec(memory_space=pltpu.SMEM)] + [WHOLE] * 6 + [ANY] * count,
        out_specs=[ANY] * 2 + [WHOLE] * 6 + [ANY] * 2 + [WHOLE] * 3 + [ANY] * count,
        scratch_shapes=[
            pltpu.VMEM((n, rows, width), BF),
            pltpu.VMEM((n, m, shard, 3 * dh), BF),
            pltpu.VMEM((m // 2, shard, width), BF),
            pltpu.VMEM((n, m) + gains.shape, F32),
            pltpu.VMEM((n, rows, width), BF),
            pltpu.VMEM((n, 2 * n, rows), F32),
            pltpu.VMEM((2 * n, rows), F32),
            DMA((n,)), DMA((2,)), DMA((n - 1,)), DMA((n - 1,)),
            DMA((n - 1, 3)), DMA((n - 1, 3)), DMA((m,)), DMA((m,)), DMA((m - 1,)), DMA((m - 1,)),
            DMA((n - 1,)), DMA((n - 1,)), DMA((m // 2,)), DMA((m // 2,)),
            DMA((n,)), DMA((n,)), DMA((n,)), DMA((n,)), DMA((n,)),
        ]
        + ring_sems(n)
        + ring_sems(n)
        + scratch,
        compiler_params=pltpu.CompilerParams(
            collective_id=0, has_side_effects=True, vmem_limit_bytes=60 << 20
        ),
        cost_estimate=cost(100),
    )(lengths, x, w, w_out, gains, cosine, sine, *arrays)


def weave(chunks, polls):
    whole = sum(w for w, _ in chunks)
    done, k = 0.0, 0
    for weight, run in chunks:
        run()
        done += weight
        while k < len(polls) - 1 and done * len(polls) >= (k + 1) * whole:
            polls[k]()
            k += 1
    for poll in polls[k:]:
        poll()


def span_of(seq):
    return seq if seq <= 512 else 256


def source_order(m):
    f = lax.axis_index("fsdp")
    nx = m // 2
    x, core = f // 2, f % 2
    return [((x + i) % nx) * 2 + (core + side) % 2 for side in range(2) for i in range(nx)]


def piece_of(kept, r, nx):
    side, i = divmod(r, nx)
    return kept[2 * side] if i == 0 else kept[2 * side + 1].at[nx - 1 - i]


class Weights:
    def __init__(self, m, kept, bufs, sems):
        self.m, self.kept, self.bufs, self.sems = m, kept, bufs, sems

    def copies(self, key):
        m, nx = self.m, self.m // 2
        order = source_order(m)
        gate, up, down = self.bufs
        g_sem, d_sem = self.sems
        block, tile = gate.shape[0] // m, down.shape[0] // m
        rows = lambda r, size: pl.ds(pl.multiple_of(order[r] * size, size), size)
        if key == "down":
            return [
                pltpu.make_async_copy(
                    piece_of(self.kept[2], r, nx), down.at[rows(r, tile)], d_sem.at[r]
                )
                for r in range(m)
            ]
        cols = pl.ds(key * tile, tile)
        return [
            pltpu.make_async_copy(
                piece_of(self.kept[i], r, nx).at[:, cols], v.at[rows(r, block), cols],
                g_sem.at[i, r, key],
            )
            for i, v in enumerate((gate, up))
            for r in range(m)
        ]

    def start(self, key):
        for c in self.copies(key):
            c.start()

    def wait(self, key):
        for c in self.copies(key):
            c.wait()


def front_chunk(t, x, weights, pre):
    gate_v, up_v, down_v = weights.bufs
    tile = down_v.shape[0] // weights.m
    cols = pl.ds(t * tile, tile)
    weights.wait(t)
    pre[0, :, cols] = dot(x[...], gate_v[:, cols])
    pre[1, :, cols] = dot(x[...], up_v[:, cols])


def forward_chunk(e, t, x, cot, gates_ref, at, weights, acts, dots_ref, first, pre=None):
    gate_v, up_v, down_v = weights.bufs
    tile = down_v.shape[0] // weights.m
    cols = pl.ds(t * tile, tile)
    if t == 0:
        weights.wait("down")
    if pre is None:
        weights.wait(t)
        gate_pre = dot(x[...], gate_v[:, cols])
        up_pre = dot(x[...], up_v[:, cols])
    else:
        gate_pre = pre[0, :, cols]
        up_pre = pre[1, :, cols]
    back = dot(cot[...], down_v[cols, :], NT)
    gate = gates_ref[at, e : e + 1]
    sig = 1.0 / (1.0 + jnp.exp(-gate_pre))
    silu = gate_pre * sig
    value = silu * up_pre
    dots = jnp.sum(value * back, axis=1, keepdims=True)
    if first:
        dots_ref[at, e : e + 1] = dots
    else:
        dots_ref[at, e : e + 1] += dots
    grad_act = gate * back
    acts[e, 0, :, cols] = (gate * value).astype(BF)
    acts[e, 1, :, cols] = (grad_act * up_pre * sig * (1.0 + gate_pre * (1.0 - sig))).astype(BF)
    acts[e, 2, :, cols] = (grad_act * silu).astype(BF)


def experts_steps(m, x_ref, cot_ref, gates_ref, weights, x, cot, acts, stage, pre,
                  dots_ref, acts_ref, gin_ref, mix_ref, in_sem, a_sem, o_sem, polls, between, more=()):
    seq, width = x_ref.shape
    span = x.shape[0]
    spans = seq // span
    chunks = []
    stores = []

    def copy(store):
        store.start()
        stores.append(store)

    for q in range(spans):
        at = pl.ds(q * span, span)
        load_x = pltpu.make_async_copy(x_ref.at[at], x, in_sem.at[0])
        load_cot = pltpu.make_async_copy(cot_ref.at[at], cot, in_sem.at[1])

        def load(q=q, load_x=load_x, load_cot=load_cot):
            if q:
                while stores:
                    stores.pop().wait()
                load_x.start()
                load_cot.start()
            load_x.wait()
            load_cot.wait()

        if q == 0:
            load_x.start()
            for w in weights:
                if w is weights[0]:
                    w.start(0)
                    load_cot.start()
                    w.start("down")
                    for t in range(1, m):
                        w.start(t)
            between(0)
        chunks.append((0.1, load))
        for e in range(EXP_DEV):
            late = e == EXP_DEV - 1

            def front(t, e=e, q=q):
                if q == 0 and t == m - 1:
                    between(2)
                if q:
                    weights[e].wait = lambda key: None
                front_chunk(t, x, weights[e], pre)

            if late:
                for t in range(m):
                    chunks.append((1.1 * 4 / m, functools.partial(front, t)))
            for t in range(m):

                def run(e=e, t=t, q=q, at=at, late=late):
                    if q == 0 and not late and t == m // 2:
                        between(1)
                    if q == 0 and late and t == 0:
                        between(3)
                    if q:
                        weights[e].wait = lambda key: None
                    forward_chunk(
                        e, t, x, cot, gates_ref, at, weights[e], acts, dots_ref, t == 0,
                        pre if late else None,
                    )

                chunks.append(((0.6 if late else 1.6) * 4 / m, run))

            def keep(e=e, at=at):
                copy(pltpu.make_async_copy(acts.at[e], acts_ref.at[e, :, at], a_sem.at[e]))

            chunks.append((0.0, keep))
        for r in range(width // 512):

            def run(r=r, at=at):
                lanes = pl.ds(r * 512, 512)
                mixed, grads = None, None
                for e in range(EXP_DEV):
                    gate_v, up_v, down_v = weights[e].bufs
                    a = dot(acts[e, 0], down_v[:, lanes])
                    b = dot(acts[e, 1], gate_v[lanes, :], NT) + dot(acts[e, 2], up_v[lanes, :], NT)
                    mixed = a if mixed is None else mixed + a
                    grads = b if grads is None else grads + b
                stage[0, :, lanes] = grads.astype(BF)
                stage[1, :, lanes] = mixed.astype(BF)
                for i, to in enumerate((gin_ref, mix_ref)):
                    copy(
                        pltpu.make_async_copy(
                            stage.at[i, :, lanes], to.at[at, lanes], o_sem.at[i, r]
                        )
                    )

            chunks.append((3.2, run))
    weave(chunks + list(more), polls)
    for c in stores:
        c.wait()


def experts_scratch(m, seq, width, ff):
    span = span_of(seq)
    return [
        pltpu.VMEM((EXP_DEV, width, ff), BF),
        pltpu.VMEM((EXP_DEV, width, ff), BF),
        pltpu.VMEM((EXP_DEV, ff, width), BF),
        DMA((EXP_DEV, 2, m, m)),
        DMA((EXP_DEV, m)),
        pltpu.VMEM((span, width), BF),
        pltpu.VMEM((span, width), BF),
        pltpu.VMEM((EXP_DEV, 3, span, ff), BF),
        pltpu.VMEM((2, span, width), BF),
        pltpu.VMEM((2, span, ff), F32),
        DMA((2,)), DMA((EXP_DEV,)), DMA((2, width // 512)),
    ]


def weights_of(e, m, kept, gate_v, up_v, down_v, g_sem, d_sem):
    return Weights(
        m, kept, (gate_v.at[e], up_v.at[e], down_v.at[e]), (g_sem.at[e], d_sem.at[e])
    )


LATE = (("share", 1), "pair", "pair", "pair")


def experts_a_kernel(n, m, *refs):
    x_ref, cot_ref, gates_ref = refs[:3]
    wg, wu, wd = refs[3:6]
    w0, fresh, (xb_own, cotb_own) = refs[6:15], refs[15:20], refs[20:22]
    dots_ref, acts_ref, gin_ref, mix_ref, xb_ref, cotb_ref, down1x, gate1c, up1c, down1c = refs[22:32]
    scratch, rest = refs[32:45], refs[45:]
    gate_v, up_v, down_v, g_sem, d_sem = scratch[:5]
    send0, recv0, send1, recv1, l_sem, c_send, c_recv = rest
    half = xb_own.shape[0] // 4
    me = lax.axis_index("head")
    gate1x, gate1o, up1x, up1o, down1o = fresh
    g1 = (wg.at[1], gate1x, gate1o, gate1c)
    u1 = (wu.at[1], up1x, up1o, up1c)
    d1 = (wd.at[1], down1x, down1o, down1c)
    kept0 = [(w.at[0],) + tuple(w0[3 * i : 3 * i + 3]) for i, w in enumerate((wg, wu, wd))]
    weights = [
        weights_of(0, m, kept0, gate_v, up_v, down_v, g_sem, d_sem),
        weights_of(1, m, (g1, u1, d1), gate_v, up_v, down_v, g_sem, d_sem),
    ]
    carry = Carry(
        LATE, (wd, gate1x, up1x, down1x), (down1x, gate1c, up1c, down1c), c_send, c_recv
    )

    def ring_of(own, out, send, recv):
        return Ring(
            lambda c: own.at[pl.ds((2 + c) * half, half)],
            lambda h, c: out.at[h, pl.ds(c * half, half)],
            send, recv, n,
        )

    rings = [ring_of(xb_own, xb_ref, send0, recv0), ring_of(cotb_own, cotb_ref, send1, recv1)]
    mine = [
        pltpu.make_async_copy(xb_own.at[pl.ds(2 * half, 2 * half)], xb_ref.at[me], l_sem.at[0]),
        pltpu.make_async_copy(cotb_own.at[pl.ds(2 * half, 2 * half)], cotb_ref.at[me], l_sem.at[1]),
    ]

    def between(stage):
        if stage == 0:
            greet([{"head": head_at(1)}, {"head": head_at(-1)}] + other_parts())
            for ring in rings:
                ring.start()
            carry.begin(range(3))
            for c in mine:
                c.start()
        elif stage == 1:
            for j in (1, 2):
                carry.arrived(j)
            for key in range(m):
                weights[1].start(key)
        elif stage == 2:
            carry.arrived(0)
            carry.begin([3])
        else:
            carry.arrived(3)
            weights[1].start("down")

    def poll(step):
        for ring in rings:
            ring.step(step)

    experts_steps(
        m, x_ref, cot_ref, gates_ref, weights, *scratch[5:10], dots_ref, acts_ref, gin_ref, mix_ref,
        *scratch[10:13], [functools.partial(poll, s) for s in range(1, n // 2 + 1)], between,
    )
    for c in mine:
        c.wait()
    for ring in rings:
        ring.finish()
    carry.end(seen=range(4))


def row_outputs(x, ff):
    seq, width = x.shape
    return [
        jax.ShapeDtypeStruct((seq, EXP_DEV), F32),
        jax.ShapeDtypeStruct((EXP_DEV, 3, seq, ff), BF),
        jax.ShapeDtypeStruct((seq, width), BF),
        jax.ShapeDtypeStruct((seq, width), BF),
    ]


def big(us, identity):
    return dict(
        compiler_params=pltpu.CompilerParams(
            collective_id=identity, has_side_effects=True, vmem_limit_bytes=60 << 20
        ),
        cost_estimate=cost(us),
    )


def experts_a(x, cot, gates, weights, weights0, fresh, x_b, cot_b, n, m):
    seq, width = x.shape
    ff = fresh[0].shape[-1]
    w0 = [a for kept in weights0 for a in kept]
    out = jax.ShapeDtypeStruct((n, x_b.shape[0] // 2, width), BF)
    gate1x, up1x = fresh[0], fresh[2]
    moved = (weights[2], gate1x, up1x)
    late = [jax.ShapeDtypeStruct((m // 2 - 1,) + weights[2].shape[1:], BF)]
    late += [jax.ShapeDtypeStruct(a.shape, BF) for a in moved[1:]] + late
    return pl.pallas_call(
        functools.partial(experts_a_kernel, n, m),
        out_shape=row_outputs(x, ff) + [out, out] + late,
        in_specs=[ANY, ANY, WHOLE] + [ANY] * 17 + [WHOLE] * 2,
        out_specs=[WHOLE] + [ANY] * 9,
        scratch_shapes=experts_scratch(m, seq, width, ff)
        + ring_sems(n)
        + ring_sems(n)
        + [DMA((2,))]
        + [DMA((4, max(m // 2 - 1, 1)))] * 2,
        **big(45, 4),
    )(x, cot, gates, *weights, *w0, *fresh, x_b, cot_b)


class Leave:
    def __init__(self, m, same, got, local, send, recv):
        self.m, self.same, self.got = m, same, got
        self.local, self.send, self.recv = local, send, recv
        self.stores, self.away = [], []

    def put(self, r, src, index, spot):
        nx = self.m // 2
        f = lax.axis_index("fsdp")
        if r < nx:
            self.stores.append(
                pltpu.make_async_copy(src, self.same.at[(r,) + index], self.local.at[r, spot])
            )
            self.stores[-1].start()
        else:
            self.away.append(
                remote(
                    src, self.got.at[(r - nx,) + index], self.send.at[r, spot],
                    self.recv.at[r, spot], {"fsdp": (f // 2) * 2 + 1 - f % 2},
                )
            )
            self.away[-1].start()

    def wide(self, i, v):
        order = source_order(self.m)
        block = v.shape[0] // self.m
        for r in range(self.m):
            at = pl.ds(pl.multiple_of(order[r] * block, block), block)
            self.put(r, v.at[at], (i,), i)

    def tall(self, v):
        order = source_order(self.m)
        tile, ff = v.shape[0] // self.m, v.shape[0]
        for r in range(self.m):
            at = pl.ds(pl.multiple_of(order[r] * tile, tile), tile)
            for side in range(2):
                self.put(
                    r, v.at[at, pl.ds(side * ff, ff)], (2, pl.ds(side * tile, tile)), 2 + side
                )

    def finish(self):
        for c in self.stores:
            c.wait()
        for c in self.away:
            c.wait()


def leave_sems(m):
    return [DMA((m, 4)), DMA((m, 4)), DMA((m, 4))]


def experts_b_kernel(n, m, early, *refs):
    x_ref, cot_ref, gates_ref = refs[:3]
    own, w, (gin_a, mix_a, xa_ref, cota_ref, acts_a) = refs[3:6], refs[6:24], refs[24:29]
    dots_ref, acts_ref, gin_ref, mix_ref, grad_ref, sum_ref = refs[29:35]
    refs = refs[35:]
    if early:
        (same, got), refs = refs[:2], refs[2:]
    scratch, rest = refs[:13], refs[13:]
    gate_v, up_v, down_v, g_sem, d_sem, x, cot, acts = scratch[:8]
    weights = [
        weights_of(
            e, m,
            [
                (own[i].at[e],) + tuple(w[9 * e + 3 * i : 9 * e + 3 * i + 3]) for i in range(3)
            ],
            gate_v, up_v, down_v, g_sem, d_sem,
        )
        for e in range(EXP_DEV)
    ]
    rings = [
        RingSum(n, gin_a, grad_ref, *rest[:6]),
        RingSum(n, mix_a, sum_ref, *rest[6:12]),
    ]

    def between(stage):
        if stage == 0:
            for ring in rings:
                ring.load()
            for key in [0, "down"] + list(range(1, m)):
                weights[1].start(key)
            f = lax.axis_index("fsdp")
            pair = [{"fsdp": (f // 2) * 2 + 1 - f % 2}] if early else []
            greet([{"head": head_at(1)}, {"head": head_at(-1)}] + pair)
            for ring in rings:
                ring.start()

    def poll(step):
        for ring in rings:
            ring.step(step)

    more = []
    if early:
        part = x.shape[0]
        leave = Leave(m, same, got, *rest[12:15])
        l_sem = rest[15]
        dgate, dup, ddown = gate_v.at[0], up_v.at[0], down_v.at[0]
        x_a, cot_a = down_v.at[1, pl.ds(0, part)], down_v.at[1, pl.ds(part, part)]
        kept = [gate_v.at[1, pl.ds(k * part, part)] for k in range(3)]
        loads = [
            pltpu.make_async_copy(xa_ref, x_a, l_sem.at[0]),
            pltpu.make_async_copy(cota_ref, cot_a, l_sem.at[1]),
        ] + [
            pltpu.make_async_copy(acts_a.at[0, k], kept[k], l_sem.at[2 + k]) for k in range(3)
        ]

        def begin():
            for c in loads:
                c.start()
            for c in loads:
                c.wait()

        more.append((0.5, begin))
        for b in range(x.shape[1] // 512):

            def run(b=b):
                at = pl.ds(b * 512, 512)
                turned, turned_a = x[:, at].T, x_a[:, at].T
                dgate[at, :] = (dot(turned, acts[0, 1]) + dot(turned_a, kept[1][...])).astype(BF)
                dup[at, :] = (dot(turned, acts[0, 2]) + dot(turned_a, kept[2][...])).astype(BF)

            more.append((2.4, run))
        more.append((0.0, lambda: (leave.wide(0, dgate), leave.wide(1, dup))))
        for t in range(gate_v.shape[2] // 256):

            def run(t=t):
                at = pl.ds(t * 256, 256)
                ddown[at, :] = (
                    dot(acts[0, 0, :, at].T, cot[...]) + dot(kept[0][:, at].T, cot_a[...])
                ).astype(BF)

            more.append((1.2, run))
        more.append((0.0, lambda: leave.tall(ddown)))
    experts_steps(
        m, x_ref, cot_ref, gates_ref, weights, *scratch[5:10], dots_ref, acts_ref, gin_ref, mix_ref,
        *scratch[10:13], [functools.partial(poll, s) for s in range(1, n // 2 + 1)], between, more,
    )
    for ring in rings:
        ring.finish()
    if early:
        leave.finish()


def experts_b(x, cot, gates, own_w, weights, gin_a, mix_a, x_a, cot_a, acts_a, n, m):
    seq, width = x.shape
    ff = own_w[0].shape[2]
    early = seq <= 512
    flat = [a for kept in weights for a in kept]
    rows = seq // n
    own = jax.ShapeDtypeStruct((rows, width), F32)
    parts = [a.reshape(n, rows, width) for a in (gin_a, mix_a)]
    grads = [jax.ShapeDtypeStruct((m // 2, 3, width // m, ff), BF)] * (2 * early)
    return pl.pallas_call(
        functools.partial(experts_b_kernel, n, m, early),
        out_shape=row_outputs(x, ff) + [own, own] + grads,
        in_specs=[ANY, ANY, WHOLE] + [ANY] * 26,
        out_specs=[WHOLE, ANY, ANY, ANY, WHOLE, WHOLE] + [ANY] * len(grads),
        scratch_shapes=experts_scratch(m, seq, width, ff)
        + ring_sum_scratch(n, rows, width)
        + ring_sum_scratch(n, rows, width)
        + (leave_sems(m) + [DMA((5,))]) * early,
        **big(60, 7),
    )(x, cot, gates, *own_w, *flat, *parts, x_a, cot_a, acts_a)


def experts_d_kernel(n, m, experts, kinds, *refs):
    xs, cots, all_acts = refs[0:6:3], refs[1:6:3], refs[2:6:3]
    gin_b, mix_b, extra = refs[6:9]
    (k, back), kk, g = carried(kinds), len(kinds), 2 * len(experts)
    outs, (grad_ref, sum_ref, extra_out) = refs[9 + k : 9 + k + g], refs[9 + k + g : 12 + k + g]
    carry = Carry(kinds, refs[9 : 9 + k], refs[12 + k + g : 12 + k + kk + g], *refs[-back:])
    (x, cot, acts, dgate, dup, ddown, x_sem, a_sem, copy, e_send, e_recv) = refs[
        12 + k + kk + g : 23 + k + kk + g
    ]
    rest = refs[23 + k + kk + g : -back]
    me = lax.axis_index("head")
    rows, width = x.shape
    part = rows // 2
    ff = acts.shape[2]
    rings = [
        RingSum(n, gin_b, grad_ref, *rest[:6]),
        RingSum(n, mix_b, sum_ref, *rest[6:12]),
    ]
    loads = [
        pltpu.make_async_copy(src[i], dst.at[pl.ds(i * part, part)], x_sem.at[k, i])
        for k, (src, dst) in enumerate(((xs, x), (cots, cot)))
        for i in range(2)
    ]

    def act_loads(e):
        return [
            pltpu.make_async_copy(
                all_acts[i].at[e], acts.at[:, pl.ds(i * part, part)], a_sem.at[i]
            )
            for i in range(2)
        ]

    carry.first()
    for ring in rings:
        ring.load()
    for c in loads + act_loads(experts[0]):
        c.start()
    greet(other_heads() + other_parts())
    carry.begin()
    for ring in rings:
        ring.start()
    direct = [pltpu.make_async_copy(extra.at[me], extra_out.at[me], copy.at[0])] + [
        remote(extra.at[dev["head"]], extra_out.at[me], e_send.at[d], e_recv.at[d], dev)
        for d, dev in enumerate(other_heads())
    ]
    for c in direct:
        c.start()
    chunks, leaves = [], []
    for j, e in enumerate(experts):
        leave = Leave(m, outs[2 * j], outs[2 * j + 1], *rest[12 + 3 * j : 15 + 3 * j])

        def begin(j=j, e=e):
            if j:
                leaves[j - 1].finish()
                for c in act_loads(e):
                    c.start()
            for c in (loads if j == 0 else []) + act_loads(e):
                c.wait()

        leaves.append(leave)
        chunks.append((0.1, begin))
        for b in range(width // 512):

            def run(b=b):
                at = pl.ds(b * 512, 512)
                turned = x[:, at].T
                dgate[at, :] = dot(turned, acts[1]).astype(BF)
                dup[at, :] = dot(turned, acts[2]).astype(BF)

            chunks.append((2.2, run))
        chunks.append(
            (0.0, lambda leave=leave: (leave.wide(0, dgate), leave.wide(1, dup)))
        )
        for t in range(ff // 256):

            def run(t=t):
                at = pl.ds(t * 256, 256)
                ddown[at, :] = dot(acts[0, :, at].T, cot[...]).astype(BF)

            chunks.append((1.1, run))
        chunks.append((0.0, lambda leave=leave: leave.tall(ddown)))

    def poll(step):
        for ring in rings:
            ring.step(step)

    weave(chunks, [functools.partial(poll, t) for t in range(1, n // 2 + 1)])
    for ring in rings:
        ring.finish()
    for c in direct:
        c.wait()
    leaves[-1].finish()
    carry.end()


def experts_d(first, second, gin_b, mix_b, dots, n, m, experts, kinds, arrays):
    seq = first[2].shape[2]
    ff = first[2].shape[3]
    rows, width = first[0].shape[1:]
    grads = jax.ShapeDtypeStruct((m // 2, 3, width // m, ff), BF)
    own = jax.ShapeDtypeStruct((rows, width), F32)
    (k, shapes, scratch), g = carry_plan(kinds, arrays, m), 2 * len(experts)

    def flat(parts):
        return [parts[0].reshape(seq, width), parts[1].reshape(seq, width), parts[2]]

    out = pl.pallas_call(
        functools.partial(experts_d_kernel, n, m, experts, kinds),
        out_shape=[grads] * g
        + [own, own, jax.ShapeDtypeStruct(dots.shape, F32)]
        + shapes,
        in_specs=[ANY] * 8 + [WHOLE] + [ANY] * k,
        out_specs=[ANY] * g + [WHOLE, WHOLE, ANY] + [ANY] * len(kinds),
        scratch_shapes=[
            pltpu.VMEM((2 * seq, width), BF),
            pltpu.VMEM((2 * seq, width), BF),
            pltpu.VMEM((3, 2 * seq, ff), BF),
            pltpu.VMEM((width, ff), BF),
            pltpu.VMEM((width, ff), BF),
            pltpu.VMEM((ff, width), BF),
            DMA((2, 2)), DMA((2,)), DMA((1,)), DMA((n - 1,)), DMA((n - 1,)),
        ]
        + ring_sum_scratch(n, rows, width)
        + ring_sum_scratch(n, rows, width)
        + leave_sems(m) * len(experts)
        + scratch,
        **big(45, 8),
    )(
        *flat(first), *flat(second), gin_b.reshape(n, rows, width), mix_b.reshape(n, rows, width),
        dots, *arrays,
    )
    return [tuple(out[2 * j : 2 * j + 2]) for j in range(g // 2)], *out[g : g + 3], out[g + 3 :]


class RingSumHere(RingSum):
    def __init__(self, n, parts, out_ref, sbuf, rbuf, send, recv):
        super().__init__(n, parts, out_ref, None, sbuf, rbuf, None, send, recv)

    def piece(self, o, c):
        return self.parts[head_at(o), pl.ds(c * self.rows, self.rows)].astype(F32)


def closing_kernel(n, m, kinds, early, *refs):
    (k, back), kk = carried(kinds), len(kinds)
    (len_ref, gatt_ref, gao_ref, q_ref, k_ref, v_ref, att_ref, proj_ref, sums_ref, gains_ref,
     cos_ref, sin_ref, ain_ref, qkv_ref) = refs[:14]
    (gin_ref, dqkv_ref, dout_ref, dgains_ref) = refs[14 + k : 18 + k]
    (gheads, gao, ain, qkv, gin, dproj, scaled, dk, dv, own, buf,
     dqkv, gq, xs, xr, fin, dout, go, xso, xro, sbuf, rbuf,
     l_sem, a_send, a_recv, s_send, s_recv, p_send, p_recv, x_send, x_recv, t_send, t_recv, t_sem,
     g_send, g_recv, r_send, r_recv) = refs[18 + k + kk : -back]
    carry = Carry(kinds, refs[14 : 14 + k], refs[18 + k : 18 + k + kk], *refs[-back:])
    me = lax.axis_index("head")
    f = lax.axis_index("fsdp")
    nx = m // 2
    x, core = f // 2, f % 2
    rows, width = gao_ref.shape
    half_rows = rows // 2
    seq, dh = q_ref.shape
    qb = query_block(seq)
    scale = 1.0 / math.sqrt(HD)
    order = source_order(m)
    carry.first()
    loads = [
        pltpu.make_async_copy(ain_ref, ain, l_sem.at[0]),
        pltpu.make_async_copy(qkv_ref, qkv, l_sem.at[1]),
    ]
    for c in loads:
        c.start()
    greet(other_heads() + other_parts())

    here = gheads.at[pl.ds(pl.multiple_of(me * rows, rows), rows)]
    sends = [
        remote(
            gatt_ref.at[:, pl.ds(pl.multiple_of(dev["head"] * dh, 128), dh)], here,
            a_send.at[d], a_recv.at[d], dev,
        )
        for d, dev in enumerate(other_heads())
    ]
    for c in sends:
        c.start()
    gring = Ring(
        lambda c: gao_ref.at[pl.ds(c * half_rows, half_rows)],
        lambda h, c: gao.at[h, pl.ds(c * half_rows, half_rows)],
        g_send, g_recv, n,
    )
    gring.start()
    carry.begin(range(early))
    here[...] = gatt_ref[:, pl.ds(pl.multiple_of(me * dh, 128), dh)]
    gao[me] = gao_ref[...]
    for c in sends:
        c.wait_recv()

    for head in range(dh // HD):
        lanes = pl.ds(head * HD, HD)
        for j in range(seq // qb):
            at = pl.ds(j * qb, qb)
            probs = probs_of(len_ref, q_ref[at, lanes], k_ref[:, lanes])
            grad_probs = dot(gheads[at, lanes], v_ref[:, lanes], NT)
            inner = jnp.sum(probs * grad_probs, axis=-1, keepdims=True)
            grad_scores = (probs * (grad_probs - inner)).astype(BF)
            dproj[at, lanes] = (dot(grad_scores, k_ref[:, lanes]) * scale).astype(BF)
            add_k = dot(grad_scores, q_ref[at, lanes], TN)
            add_v = dot(probs.astype(BF), gheads[at, lanes], TN)
            if j == 0:
                dk[...] = add_k
                dv[...] = add_v
            else:
                dk[...] += add_k
                dv[...] += add_v
        dproj[:, pl.ds(dh + head * HD, HD)] = (dk[...] * scale).astype(BF)
        dproj[:, pl.ds(2 * dh + head * HD, HD)] = dv[...].astype(BF)
        gring.step(head + 1)
    for step in range(dh // HD + 1, 3):
        gring.step(step)

    inv_all = lax.rsqrt(sums_ref[...] / width + EPS)
    dgains = [jnp.zeros((1, HD), F32) for _ in range(2 * dh // HD)]
    for i in range(n):
        at = pl.ds(i * rows, rows)
        cosine = cos_ref[at, :]
        sine = -sin_ref[at, :]
        for kind in range(2):
            inv = as_column(inv_all[kind * n + i : kind * n + i + 1])
            sums = jnp.zeros((rows, 1), F32)
            for head in range(dh // HD):
                spot = kind * (dh // HD) + head
                lanes = pl.ds(kind * dh + head * HD, HD)
                turned = turn(dproj[at, lanes].astype(F32), cosine, sine)
                unit = proj_ref[at, lanes] * inv
                dgains[spot] = dgains[spot] + jnp.sum(turned * unit, axis=0, keepdims=True)
                grad = turned * gains_ref[kind : kind + 1, head * HD : (head + 1) * HD]
                scaled[at, lanes] = grad
                sums = sums + jnp.sum(grad * unit, axis=1, keepdims=True)
            own[pl.ds(kind * n + i, 1), :] = as_row(sums)
    for spot, value in enumerate(dgains):
        dgains_ref[pl.ds(spot, 1), :] = value
    moves = [
        remote(own, buf.at[me], s_send.at[d], s_recv.at[d], dev)
        for d, dev in enumerate(other_heads())
    ]
    for c in moves:
        c.start()
    buf[me] = own[...]
    for c in moves:
        c.wait()
    total_of = buf[0]
    for i in range(1, n):
        total_of = total_of + buf[i]
    means = total_of / width
    for i in range(n):
        at = pl.ds(i * rows, rows)
        for kind in range(2):
            inv = as_column(inv_all[kind * n + i : kind * n + i + 1])
            mean = as_column(means[kind * n + i : kind * n + i + 1])
            for head in range(dh // HD):
                lanes = pl.ds(kind * dh + head * HD, HD)
                unit = proj_ref[at, lanes] * inv
                dproj[at, lanes] = (inv * (scaled[at, lanes] - unit * mean)).astype(BF)

    for c in loads:
        c.wait()
    weight = qkv.reshape(width, 3 * dh)
    for g in range(n // 2):
        part = dot(dproj[pl.ds(g * 2 * rows, 2 * rows), :], weight[...], NT).astype(BF)
        gin[2 * g : 2 * g + 2] = part.reshape(2, rows, width)
    gring.step(3)
    ring = RingSumHere(n, gin, gin_ref, sbuf, rbuf, r_send, r_recv)
    ring.start()

    flat = dqkv.reshape(width, 3 * dh)
    for b in range(width // 512):
        at = pl.ds(b * 512, 512)
        turned = ain.reshape(seq, width)[:, at].T
        flat[at, :] = dot(turned, dproj[...]).astype(BF)
    pair = {"fsdp": x * 2 + 1 - core}
    pairs = [
        remote(dqkv.at[:, order[nx + i]], gq.at[i], p_send.at[i], p_recv.at[i], pair)
        for i in range(nx)
    ]
    for c in pairs:
        c.start()
    for step in range(4, n // 2 + 1):
        gring.step(step)
    for b in range(width // 512):
        at = pl.ds(b * 512, 512)
        value = dot(att_ref[...], gao.reshape(seq, width)[:, at], TN)
        dout[:, :, at] = value.astype(BF).reshape(dout.shape[:2] + (512,))
    pairs_out = [
        remote(dout.at[order[nx + i]], go.at[i], p_send.at[nx + i], p_recv.at[nx + i], pair)
        for i in range(nx)
    ]
    for c in pairs_out:
        c.start()
    ring.step(1)
    for c in pairs + pairs_out:
        c.wait_recv()
    across = []
    for i in range(1, nx):
        there = {"fsdp": ((x + i) % nx) * 2 + core}
        xs[i - 1] = (dqkv[:, order[i]].astype(F32) + gq[i].astype(F32)).astype(BF)
        xso[i - 1] = (dout[order[i]].astype(F32) + go[i].astype(F32)).astype(BF)
        across.append(remote(xs.at[i - 1], xr.at[i - 1], x_send.at[0, i - 1], x_recv.at[0, i - 1], there))
        across.append(remote(xso.at[i - 1], xro.at[i - 1], x_send.at[1, i - 1], x_recv.at[1, i - 1], there))
    for c in across:
        c.start()
    carry.begin(range(early, len(carry.jobs)))
    for step in range(2, n // 2):
        ring.step(step)
    for c in across:
        c.wait_recv()
    value = dqkv[:, order[0]].astype(F32) + gq[0].astype(F32)
    value_out = dout[order[0]].astype(F32) + go[0].astype(F32)
    for i in range(1, nx):
        value = value + xr[i - 1].astype(F32)
        value_out = value_out + xro[i - 1].astype(F32)
    fin[...] = value.astype(BF)
    dout_ref[...] = value_out
    to = [
        dqkv_ref.at[:, pl.ds(pl.multiple_of(j * width + me * dh, 128), dh)] for j in range(3)
    ]
    last = [
        remote(
            fin.at[dev["head"], :, pl.ds(j * dh, dh)], to[j], t_send.at[d, j], t_recv.at[d, j], dev
        )
        for d, dev in enumerate(other_heads())
        for j in range(3)
    ] + [
        pltpu.make_async_copy(fin.at[me, :, pl.ds(j * dh, dh)], to[j], t_sem.at[j])
        for j in range(3)
    ]
    for c in last:
        c.start()
    ring.step(n // 2)
    for c in last:
        c.wait()
    for c in sends + pairs + pairs_out + across:
        c.wait_send()
    gring.finish()
    ring.finish()
    carry.end()


def closing(lengths, gatt, gao, q, k, v, att, proj, sums, gains, cosine, sine, ain, qkv, n, m, kinds,
            arrays, early):
    rows, width = gao.shape
    seq, dh = q.shape
    nx = m // 2
    shard = qkv.shape[2]
    count, shapes, scratch = carry_plan(kinds, arrays, m)

    def vm(*shape, dtype=BF):
        return pltpu.VMEM(shape, dtype)

    return pl.pallas_call(
        functools.partial(closing_kernel, n, m, kinds, early),
        out_shape=[
            jax.ShapeDtypeStruct((rows, width), F32),
            jax.ShapeDtypeStruct((shard, 3 * width), BF),
            jax.ShapeDtypeStruct((shard, width), F32),
            jax.ShapeDtypeStruct((2 * dh // HD, HD), F32),
        ]
        + shapes,
        in_specs=[pl.BlockSpec(memory_space=pltpu.SMEM)] + [WHOLE] * 11 + [ANY] * (2 + count),
        out_specs=[WHOLE, ANY, WHOLE, WHOLE] + [ANY] * len(kinds),
        scratch_shapes=[
            vm(seq, dh), vm(n, rows, width), vm(n, rows, width), vm(n, m, shard, 3 * dh),
            vm(n, rows, width), vm(seq, 3 * dh), vm(seq, 2 * dh, dtype=F32),
            vm(seq, HD, dtype=F32), vm(seq, HD, dtype=F32),
            vm(2 * n, rows, dtype=F32), vm(n, 2 * n, rows, dtype=F32),
            vm(n, m, shard, 3 * dh), vm(nx, n, shard, 3 * dh),
            vm(nx - 1, n, shard, 3 * dh), vm(nx - 1, n, shard, 3 * dh), vm(n, shard, 3 * dh),
            vm(m, shard, width), vm(nx, shard, width),
            vm(nx - 1, shard, width), vm(nx - 1, shard, width),
            vm(2, 2, rows // 2, width), vm(2, n // 2, 2, rows // 2, width),
            DMA((2,)), DMA((n - 1,)), DMA((n - 1,)), DMA((n - 1,)), DMA((n - 1,)),
            DMA((m,)), DMA((m,)), DMA((2, nx - 1)), DMA((2, nx - 1)),
            DMA((n - 1, 3)), DMA((n - 1, 3)), DMA((3,)),
        ]
        + ring_sems(n)
        + ring_sems(n)
        + scratch,
        **big(110, 5),
    )(lengths, gatt, gao, q, k, v, att, proj, sums, gains, cosine, sine, ain, qkv, *arrays)


DEPTH = 4


def settle_kernel(jobs, *refs):
    count = sum(len(sources) for sources, _ in jobs)
    outs = refs[count : count + 3]
    ins, result, l_sem, o_sem = refs[count + 3 :]
    steps, k = [], 0
    for sources, (which, e, columns) in jobs:
        arrays = refs[k : k + len(sources)]
        k += len(sources)
        rows = sources[0][1]
        for part in range(1 if columns else 2):
            size = rows if columns else rows // 2
            steps.append((arrays, sources, part * size, size, which, e, columns))

    def loads(i):
        arrays, sources, start, size = steps[i][:4]
        return [
            pltpu.make_async_copy(
                ref.at[index + (pl.ds(base + start, size),)], ins.at[i % DEPTH, j, pl.ds(0, size)],
                l_sem.at[i % DEPTH, j],
            )
            for j, (ref, (index, _, base)) in enumerate(zip(arrays, sources))
        ]

    def store(i):
        _, _, start, size, which, e, columns = steps[i]
        wide = result.shape[2]
        to = outs[which].at[e]
        to = to.at[:, pl.ds(columns[0], wide)] if columns else to.at[pl.ds(start, size)]
        return pltpu.make_async_copy(result.at[i % DEPTH, pl.ds(0, size)], to, o_sem.at[i % DEPTH])

    for i in range(min(DEPTH - 1, len(steps))):
        for c in loads(i):
            c.start()
    for i, (arrays, _, _, size, *_) in enumerate(steps):
        if i + DEPTH - 1 < len(steps):
            for c in loads(i + DEPTH - 1):
                c.start()
        for c in loads(i):
            c.wait()
        if i >= DEPTH:
            store(i - DEPTH).wait()
        value = ins[i % DEPTH, 0, :size].astype(F32)
        for j in range(1, len(arrays)):
            value = value + ins[i % DEPTH, j, :size].astype(F32)
        result[i % DEPTH, :size] = value
        store(i).start()
    for i in range(max(len(steps) - DEPTH, 0), len(steps)):
        store(i).wait()


def settle(grads, sums, m):
    block, ff = grads[0][0].shape[2:]
    tile = block // 2
    jobs, arrays = [], []
    for e, (same, got) in enumerate(grads):
        for which in range(3):
            k, holder = which, None
            for part in sums[e]:
                if k < part.shape[1]:
                    holder = part
                    break
                k -= part.shape[1]
            for half in range(1 if which < 2 else 2):
                rows, base = (block, 0) if which < 2 else (tile, half * tile)
                sources = [((0, which), rows, base)] * 2
                sources += [((i, k), rows, base) for i in range(m // 2 - 1)]
                arrays += [same, got] + [holder] * (m // 2 - 1)
                columns = None if which < 2 else (half * ff,)
                jobs.append((tuple(sources), (which, e, columns)))
    return pl.pallas_call(
        functools.partial(settle_kernel, tuple(jobs)),
        out_shape=[jax.ShapeDtypeStruct((EXP_DEV, block, ff), F32)] * 2
        + [jax.ShapeDtypeStruct((EXP_DEV, tile, 2 * ff), F32)],
        in_specs=[ANY] * len(arrays),
        out_specs=[ANY] * 3,
        scratch_shapes=[
            pltpu.VMEM((DEPTH, m // 2 + 1, tile, ff), BF),
            pltpu.VMEM((DEPTH, tile, ff), F32),
            DMA((DEPTH, m // 2 + 1)), DMA((DEPTH,)),
        ],
        compiler_params=pltpu.CompilerParams(vmem_limit_bytes=60 << 20),
        cost_estimate=cost(10),
    )(*arrays)


def joined(same, got):
    return same.astype(F32) + got.astype(F32)


def body(
    hidden,
    w_qkv,
    w_out,
    w_router,
    g_attn,
    g_ffn,
    g_q,
    g_k,
    w_gate,
    w_up,
    w_down,
    lengths,
    routes,
    route_codes,
    cotangent,
):
    n = lax.axis_size("head")
    m = lax.axis_size("fsdp")
    me = lax.axis_index("head")
    rows = hidden.shape[1]
    width = hidden.shape[2]
    seq = rows * n
    lh = HEADS // n
    dh = lh * HD
    experts = EXP_DEV * n
    shard = w_qkv.shape[0]
    both = ("head", "fsdp")

    sides = 128 // shard
    lane = jnp.arange(128, dtype=jnp.int32) // shard == lax.axis_index("fsdp") % sides
    small = jnp.tile(jnp.stack([g_attn, g_ffn, g_q, g_k]), (2, sides)).astype(F32)
    small = jnp.concatenate(
        [jnp.where(lane[None, :], small, 0.0), w_router.astype(F32).reshape(-1, 128)]
    )
    def inverse_rms(values):
        return lax.rsqrt(jnp.mean(values * values, axis=-1, keepdims=True) + EPS)

    angles = np.arange(seq)[:, None] * ROPE_BASE ** (-2.0 * np.arange(HD // 2) / HD)
    cosine = np.tile(np.cos(angles), (1, 2)).astype(np.float32)
    sine = np.concatenate([-np.sin(angles), np.sin(angles)], axis=1).astype(np.float32)
    (attn_input, qkv, proj, sums, queries, keys, values, attended, attended_tok, full_out, small,
     gains_wide, gains_heads, gate0x, up0x, down0x) = opening(
        lengths, hidden[0], w_qkv, w_out, small, cosine, sine, n, m, (("share", 0),) * 3,
        (w_gate, w_up, w_down),
    )
    router = small[:, :, 8:].reshape(width, experts).astype(BF)
    gain_attn, gain_ffn = gains_wide
    full_out = full_out.reshape(width, width)
    half = rows // 2
    own_w = (w_gate, w_up, w_down)
    over_x = (gate0x, up0x, down0x)
    residual, own_input, spread, x_a, cot_a, mine, gate1x, up1x, *got = routing(
        hidden[0], attended_tok, full_out, gains_wide[1:], jnp.pad(router, ((0, 0), (0, 128 - experts))),
        routes[0], route_codes[0], cotangent[0], n, m, experts,
        (("share", 1),) * 2 + (("pair", 0),) * 3 + ("pair",) * 3 + (("pair", 1),) * 3,
        (w_gate, w_up, *own_w, *over_x, *own_w),
    )
    spread = spread[:, :experts]
    weights0 = [(over_x[i], got[i], got[3 + i]) for i in range(3)]
    mine = mine.transpose(0, 2, 1)
    span = n * half

    def rows_of(part):
        return part.reshape(span, width)

    gates_a = mine[:, :half].reshape(span, EXP_DEV)
    gates_b = mine[:, half:].reshape(span, EXP_DEV)
    fresh = [gate1x, got[6], up1x, got[7], got[8]]
    dots_a, acts_a, gin_a, mix_a, x_b, cot_b, down1x, gate1c, up1c, down1c = experts_a(
        rows_of(x_a), rows_of(cot_a), gates_a, own_w, weights0, fresh, own_input,
        cotangent[0], n, m,
    )
    weights1 = [(gate1x, got[6], gate1c), (up1x, got[7], up1c), (down1x, got[8], down1c)]
    dots_b, acts_b, gin_b, mix_b, grad_ffn_a, summed_a, *grads0 = experts_b(
        rows_of(x_b), rows_of(cot_b), gates_b, own_w, weights0 + weights1, gin_a, mix_a,
        rows_of(x_a), rows_of(cot_a), acts_a, n, m,
    )
    dots = jnp.concatenate(
        [d.reshape(n, half, EXP_DEV).transpose(0, 2, 1) for d in (dots_a, dots_b)], axis=2
    )

    early = len(grads0) > 0
    grads, grad_ffn_b, summed_b, dots, sums0 = experts_d(
        (x_a, cot_a, acts_a), (x_b, cot_b, acts_b), gin_b, mix_b, dots, n, m,
        (1,) if early else (0, 1), (("join", 0, 2),) * early, tuple(grads0),
    )
    grads = [tuple(grads0)] * early + grads
    grad_ffn = jnp.concatenate([grad_ffn_a, grad_ffn_b], axis=0)
    summed = jnp.concatenate([summed_a, summed_b], axis=0)
    dots = dots.reshape(experts, rows).T
    grad_rows = cotangent[0].astype(F32)
    grad_logits = spread * (dots - jnp.sum(spread * dots, axis=1, keepdims=True))
    high = lax.Precision.HIGHEST
    grad_ffn = grad_ffn + jnp.dot(grad_logits, router.astype(F32).T, precision=high)
    grad_router = jnp.dot(own_input.astype(F32).T, grad_logits, precision=high)

    def norm_back(values, gain, grad):
        inv = inverse_rms(values)
        unit = values * inv
        scaled = grad * gain
        back = inv * (scaled - unit * jnp.mean(scaled * unit, axis=-1, keepdims=True))
        return back, jnp.sum(grad * unit, axis=0)

    back, grad_gain_ffn = norm_back(residual, gain_ffn, grad_ffn)
    grad_residual = grad_rows + back
    grad_attn_out = grad_residual.astype(BF)
    grad_attended = dot(grad_attn_out, full_out, NT).astype(BF)
    spans = [(span, 0) for span in (((2, 3),) if early else ((0, 2), (2, 3)))]
    spans += [(span, 1) for span in ((0, 1), (1, 2), (2, 3))]
    if early:
        kinds = tuple(("join",) + span for span, _ in spans)
        riders = [a for _, e in spans for a in grads[e]]
    else:
        kinds = ("across",) * len(spans)
        riders = [
            joined(*(part[1:, a:b] for part in grads[e])).astype(BF) for (a, b), e in spans
        ]
    grad_attn_in, grad_qkv, grad_out_w, grad_gains, *arrived = closing(
        lengths, grad_attended, grad_attn_out, queries, keys, values, attended, proj, sums,
        gains_heads, cosine, sine, attn_input, qkv, n, m,
        kinds, riders, 3,
    )
    sums0 = list(sums0) + arrived[:-3]
    sums1 = arrived[-3:]
    grad_gain_q, grad_gain_k = grad_gains.reshape(2, dh)
    out_rows = residual + summed

    grad_w_gate, grad_w_up, grad_w_down = settle(grads, (sums0, sums1), m)
    grad_qkv = grad_qkv.astype(F32)

    back, grad_gain_attn = norm_back(hidden[0].astype(F32), gain_attn, grad_attn_in)
    grad_hidden = grad_residual + back

    def at_mine(piece):
        return lax.dynamic_update_slice_in_dim(jnp.zeros((width,), F32), piece, me * dh, 0)

    pack = jnp.concatenate(
        [grad_router.reshape(n * m, shard * experts)]
        + [
            g.reshape(n * m, shard)
            for g in (grad_gain_attn, grad_gain_ffn, at_mine(grad_gain_q), at_mine(grad_gain_k))
        ],
        axis=1,
    )
    pack = lax.all_to_all(pack, both, split_axis=0, concat_axis=0, tiled=True)
    pack = jnp.sum(pack, axis=0)
    small_grads = pack[shard * experts :].reshape(4, shard)
    return (
        out_rows.astype(BF)[None],
        grad_hidden[None],
        grad_qkv,
        grad_out_w,
        pack[: shard * experts].reshape(shard, experts),
        small_grads[0],
        small_grads[1],
        small_grads[2],
        small_grads[3],
        grad_w_gate,
        grad_w_up,
        grad_w_down,
    )


def solution(mesh):
    both = ("head", "fsdp")
    return jax.shard_map(
        body,
        mesh=mesh,
        in_specs=(
            P("fsdp", "head", None),
            P(both, None),
            P(both, None),
            P(both, None),
            P(both),
            P(both),
            P(both),
            P(both),
            P("head", "fsdp", None),
            P("head", "fsdp", None),
            P("head", "fsdp", None),
            P("fsdp"),
            P("fsdp", "head", None),
            P("fsdp", "head", None),
            P("fsdp", "head", None),
        ),
        out_specs=(
            P("fsdp", "head", None),
            P("fsdp", "head", None),
            P(both, None),
            P(both, None),
            P(both, None),
            P(both),
            P(both),
            P(both),
            P(both),
            P("head", "fsdp", None),
            P("head", "fsdp", None),
            P("head", "fsdp", None),
        ),
        check_vma=False,
    )
```

```python
import functools
import math

import jax
import jax.numpy as jnp
import numpy as np
from jax import lax
from jax.experimental import pallas as pl
from jax.experimental.pallas import tpu as pltpu
from jax.sharding import PartitionSpec as P

HEADS = 16
HD = 128
FF = 1024
TOP = 8
EXP_DEV = 2

EPS = 1e-06
ROPE_BASE = 10000.0
NEGATIVE = -1e30
BF = jnp.bfloat16
F32 = jnp.float32
NN = ((1,), (0,))
NT = ((1,), (1,))
TN = ((0,), (0,))
ANY = pl.BlockSpec(memory_space=pl.ANY)
WHOLE = pl.BlockSpec(memory_space=pltpu.VMEM)
DMA = pltpu.SemaphoreType.DMA


def dot(a, b, dims=NN):
    return lax.dot_general(a, b, (dims, ((), ())), preferred_element_type=F32)


def cost(us):
    return pl.CostEstimate(flops=0, bytes_accessed=int(us * 3.6e6), transcendentals=0)


def ring_place():
    n = lax.axis_size("head")
    me = lax.axis_index("head")
    odd = me % 2
    return (1 - odd) * (me // 2) + odd * (n - 1 - me // 2)


def head_at(offset):
    n = lax.axis_size("head")
    k = (ring_place() + (offset + n)) % n
    down = k // (n // 2)
    return (1 - down) * 2 * k + down * (2 * n - 1 - 2 * k)


def remote(src, dst, send, recv, device):
    return pltpu.make_async_remote_copy(
        src_ref=src,
        dst_ref=dst,
        send_sem=send,
        recv_sem=recv,
        device_id=device,
        device_id_type=pl.DeviceIdType.MESH,
    )


def greet(devices):
    barrier = pltpu.get_barrier_semaphore()
    for device in devices:
        pl.semaphore_signal(
            barrier, inc=1, device_id=device, device_id_type=pl.DeviceIdType.MESH
        )
    pl.semaphore_wait(barrier, len(devices))


def other_heads():
    n = lax.axis_size("head")
    me = lax.axis_index("head")
    return [{"head": (me + d) % n} for d in range(1, n)]


def other_parts():
    m = lax.axis_size("fsdp")
    f = lax.axis_index("fsdp")
    return [{"fsdp": (f + d) % m} for d in range(1, m)]


class Ring:
    def __init__(self, own, place, send, recv, n):
        self.own, self.place, self.send, self.recv = own, place, send, recv
        self.half = n // 2

    def exists(self, way, step, c):
        return step < self.half or c == way

    def message(self, way, step, c):
        owner = head_at((1 - step) if way == 0 else (step - 1))
        return remote(
            self.own(c) if step == 1 else self.place(owner, c),
            self.place(owner, c),
            self.send.at[way, step - 1, c],
            self.recv.at[way, step - 1, c],
            {"head": head_at(1 if way == 0 else -1)},
        )

    def start(self):
        for c in range(2):
            for way in range(2):
                if self.exists(way, 1, c):
                    self.message(way, 1, c).start()

    def step(self, step):
        for c in range(2):
            for way in range(2):
                if self.exists(way, step, c):
                    self.message(way, step, c).wait_recv()
                    if step < self.half and self.exists(way, step + 1, c):
                        self.message(way, step + 1, c).start()

    def finish(self):
        for step in range(1, self.half + 1):
            for c in range(2):
                for way in range(2):
                    if self.exists(way, step, c):
                        self.message(way, step, c).wait_send()


def ring_sems(n):
    return [DMA((2, n // 2, 2)), DMA((2, n // 2, 2))]


class Carry:
    def __init__(self, kinds, ins, outs, send, recv, *joins):
        self.jobs, k = [], 0
        stages = list(joins)
        for kind, dst in zip(kinds, outs):
            name = kind if isinstance(kind, str) else kind[0]
            if name == "join":
                self.jobs.append((name, stages.pop(0), dst, kind[1:], ins[k : k + 2]))
                k += 2
                continue
            src = ins[k] if isinstance(kind, str) else ins[k].at[kind[1]]
            self.jobs.append((name, src, dst, None, None))
            k += 1
        self.tmp, self.j_sem = stages if stages else (None, None)
        self.fetched = None
        self.send, self.recv = send, recv

    def copies(self, j):
        m = lax.axis_size("fsdp")
        f = lax.axis_index("fsdp")
        nx = m // 2
        x, core = f // 2, f % 2
        name, src, dst = self.jobs[j][:3]
        if name == "pair":
            other = {"fsdp": x * 2 + 1 - core}
            return [remote(src, dst, self.send.at[j, 0], self.recv.at[j, 0], other)]
        return [
            remote(
                src if name == "share" else src.at[i - 1], dst.at[i - 1],
                self.send.at[j, i - 1], self.recv.at[j, i - 1],
                {"fsdp": ((x + i) % nx) * 2 + core},
            )
            for i in range(1, nx)
        ]

    def fetch(self, j):
        _, stage, _, (a, b), arrays = self.jobs[j]
        tmp = self.tmp.at[:, pl.ds(0, b - a)]
        self.fetched = [
            pltpu.make_async_copy(
                arrays[i].at[pl.ds(1, stage.shape[0]), pl.ds(a, b - a)], (stage, tmp)[i],
                self.j_sem.at[i],
            )
            for i in range(2)
        ]
        for c in self.fetched:
            c.start()

    def first(self):
        if self.jobs and self.jobs[0][0] == "join":
            self.fetch(0)

    def join(self, j):
        _, stage, _, (a, b), _ = self.jobs[j]
        if self.fetched is None:
            self.fetch(j)
        for c in self.fetched:
            c.wait()
        self.fetched = None
        for i in range(stage.shape[0]):
            for k in range(b - a):

                @pl.loop(0, stage.shape[2] // 64)
                def _(r, i=i, k=k):
                    at = pl.ds(pl.multiple_of(r * 64, 64), 64)
                    stage[i, k, at] = (
                        stage[i, k, at].astype(F32) + self.tmp[i, k, at].astype(F32)
                    ).astype(BF)

    def begin(self, some=None):
        for j in range(len(self.jobs)) if some is None else some:
            if self.jobs[j][0] == "join":
                self.join(j)
            for c in self.copies(j):
                c.start()

    def arrived(self, j):
        for c in self.copies(j):
            c.wait_recv()

    def end(self, seen=()):
        for j in range(len(self.jobs)):
            for c in self.copies(j):
                if j not in seen:
                    c.wait_recv()
                c.wait_send()


def carry_plan(kinds, arrays, m):
    shapes, stages, k = [], [], 0
    for kind in kinds:
        if kind[0] == "join":
            a, b = kind[1:]
            shape = (m // 2 - 1, b - a) + arrays[k].shape[2:]
            stages.append(shape)
            k += 2
        else:
            name = kind if isinstance(kind, str) else kind[0]
            shape = arrays[k].shape if isinstance(kind, str) else arrays[k].shape[1:]
            shape = (m // 2 - 1,) * (name == "share") + shape
            k += 1
        shapes.append(jax.ShapeDtypeStruct(shape, BF))
    sems = (max(len(kinds), 1), max(m // 2 - 1, 1))
    scratch = [DMA(sems), DMA(sems)] + [pltpu.VMEM(shape, BF) for shape in stages]
    if stages:
        widest = max(stages, key=lambda shape: shape[1])
        scratch += [pltpu.VMEM(widest, BF), DMA((2,))]
    return k, shapes, scratch


def carried(kinds):
    joins = sum(kind[0] == "join" for kind in kinds)
    return len(kinds) + joins, 2 + joins + 2 * (joins > 0)


def routing_kernel(n, m, experts, kinds, *refs):
    k, back = carried(kinds)
    (hid_ref, tok_ref, wout_ref, gain_ref, router_ref, routes_ref, codes_ref, cot_ref) = refs[:8]
    res_ref, own_ref, spread_ref, xa_ref, cota_ref, mine_ref = refs[8 + k : 14 + k]
    (wout, sets, w_sem, copies, x_send, x_recv, t_send, t_recv, e_send, e_recv) = refs[
        14 + k + len(kinds) : -back
    ]
    carry = Carry(kinds, refs[8 : 8 + k], refs[14 + k : 14 + k + len(kinds)], *refs[-back:])
    me = lax.axis_index("head")
    rows, width = hid_ref.shape
    half = rows // 2
    part = half // 2
    lanes = width // 4
    loads = [
        pltpu.make_async_copy(
            wout_ref.at[:, pl.ds(i * lanes, lanes)], wout.at[:, pl.ds(i * lanes, lanes)],
            w_sem.at[i],
        )
        for i in range(4)
    ]
    for c in loads:
        c.start()
    greet(other_heads() + other_parts())

    def ring_of(own, out, send, recv):
        return Ring(
            lambda c: own.at[pl.ds(c * part, part)],
            lambda h, c: out.at[h, pl.ds(c * part, part)],
            send, recv, n,
        )

    ring_cot = ring_of(cot_ref, cota_ref, t_send, t_recv)
    ring_x = ring_of(own_ref, xa_ref, x_send, x_recv)
    ring_cot.start()
    carry.begin()
    moves = [pltpu.make_async_copy(cot_ref.at[pl.ds(0, half)], cota_ref.at[me], copies.at[0])]
    moves[0].start()
    for i in range(4):
        at = pl.ds(i * lanes, lanes)
        loads[i].wait()
        res_ref[:, at] = hid_ref[:, at].astype(F32) + dot(tok_ref[...], wout[:, at])
    residual = res_ref[...]
    inv = lax.rsqrt(jnp.mean(residual * residual, axis=-1, keepdims=True) + EPS)
    own_ref[...] = (residual * inv * gain_ref[...]).astype(BF)
    ring_cot.step(1)
    ring_x.start()
    moves.append(pltpu.make_async_copy(own_ref.at[pl.ds(0, half)], xa_ref.at[me], copies.at[1]))
    moves[1].start()

    logits = dot(own_ref[...], router_ref[...])
    expert = lax.broadcasted_iota(jnp.int32, logits.shape, 1)
    matches, chosen = [], []
    for j in range(TOP):
        matches.append(expert == routes_ref[:, j : j + 1])
        picked = jnp.sum(jnp.where(matches[j], logits, 0.0), axis=1, keepdims=True)
        chosen.append(picked + codes_ref[:, j : j + 1].astype(F32) / 1024.0)
    peak = functools.reduce(jnp.maximum, chosen)
    chosen = [jnp.exp(c - peak) for c in chosen]
    whole = functools.reduce(lambda a, b: a + b, chosen)
    spread = jnp.zeros_like(logits)
    for j in range(TOP):
        spread = spread + jnp.where(matches[j], chosen[j] / whole, 0.0)
    spread_ref[...] = spread
    turned = spread.T
    for h in range(n):
        sets[h] = turned[h * EXP_DEV : (h + 1) * EXP_DEV]
    moves.append(pltpu.make_async_copy(sets.at[me], mine_ref.at[me], copies.at[2]))
    moves += [
        remote(sets.at[dev["head"]], mine_ref.at[me], e_send.at[d], e_recv.at[d], dev)
        for d, dev in enumerate(other_heads())
    ]
    for c in moves[2:]:
        c.start()
    for step in range(2, n // 2 + 1):
        ring_cot.step(step)
        ring_x.step(step - 1)
    ring_x.step(n // 2)
    for c in moves:
        c.wait()
    ring_cot.finish()
    ring_x.finish()
    carry.end()


def routing(hid, tok, w_out, gain, router, routes, codes, cot, n, m, experts, kinds, arrays):
    rows, width = hid.shape
    count, shapes, scratch = carry_plan(kinds, arrays, m)
    halves = jax.ShapeDtypeStruct((n, rows // 2, width), BF)
    return pl.pallas_call(
        functools.partial(routing_kernel, n, m, experts, kinds),
        out_shape=[
            jax.ShapeDtypeStruct((rows, width), F32),
            jax.ShapeDtypeStruct((rows, width), BF),
            jax.ShapeDtypeStruct((rows, 128), F32),
            halves, halves,
            jax.ShapeDtypeStruct((n, EXP_DEV, rows), F32),
        ]
        + shapes,
        in_specs=[WHOLE, WHOLE, ANY] + [WHOLE] * 5 + [ANY] * count,
        out_specs=[WHOLE] * 3 + [ANY] * (3 + len(kinds)),
        scratch_shapes=[
            pltpu.VMEM((width, width), BF),
            pltpu.VMEM((n, EXP_DEV, rows), F32),
            DMA((4,)), DMA((3,)),
        ]
        + ring_sems(n)
        + ring_sems(n)
        + [DMA((n - 1,)), DMA((n - 1,))]
        + scratch,
        compiler_params=pltpu.CompilerParams(
            collective_id=1, has_side_effects=True, vmem_limit_bytes=60 << 20
        ),
        cost_estimate=cost(55),
    )(hid, tok, w_out, gain, router, routes, codes, cot, *arrays)


class RingSum:
    def __init__(self, n, parts, out_ref, own, sbuf, rbuf, loads, send, recv):
        self.n, self.half, self.parts, self.out_ref = n, n // 2, parts, out_ref
        self.own, self.sbuf, self.rbuf, self.loads = own, sbuf, rbuf, loads
        self.send, self.recv = send, recv
        self.rows = out_ref.shape[0] // 2
        self.order = (
            [self.half] + [s * w for s in range(self.half - 1, 0, -1) for w in (1, -1)] + [0]
        )
        self.ready, self.started = set(), []

    def fetch(self, o):
        i = self.order.index(o)
        return pltpu.make_async_copy(self.parts.at[head_at(o)], self.own.at[i], self.loads.at[i])

    def load(self):
        for o in self.order:
            self.fetch(o).start()

    def piece(self, o, c):
        if o not in self.ready:
            self.fetch(o).wait()
            self.ready.add(o)
        return self.own[self.order.index(o), pl.ds(c * self.rows, self.rows)].astype(F32)

    def buffer(self, way, t, c):
        first = 1 if c == way else 2
        return self.sbuf.at[way, t - 1] if t == first else self.rbuf.at[way, t - 2, c]

    def message(self, way, t, c):
        return remote(
            self.buffer(way, t, c), self.rbuf.at[way, t - 1, c],
            self.send.at[way, t - 1, c], self.recv.at[way, t - 1, c],
            {"head": head_at(1 if way == 0 else -1)},
        )

    def offset(self, way, o):
        return o if way == 0 or o == self.half else -o

    def ship(self, way, t, c, value):
        self.buffer(way, t, c)[...] = value.astype(BF)
        self.message(way, t, c).start()
        self.started.append((way, t, c))

    def start(self):
        for way in range(2):
            self.ship(way, 1, way, self.piece(self.half, way))
        for way in range(2):
            self.ship(way, 2, 1 - way, self.piece(self.offset(way, self.half - 1), 1 - way))

    def step(self, t):
        if t < self.half:
            for c in range(2):
                for way in range(2):
                    if t == 1 and c != way:
                        continue
                    self.message(way, t, c).wait_recv()
                    self.ship(
                        way, t + 1, c,
                        self.piece(self.offset(way, self.half - t), c)
                        + self.rbuf[way, t - 1, c].astype(F32),
                    )
            return
        last = self.half - 1
        for c in range(2):
            for way in range(2):
                self.message(way, self.half, c).wait_recv()
            self.out_ref[pl.ds(c * self.rows, self.rows)] = (
                self.piece(0, c)
                + self.rbuf[0, last, c].astype(F32)
                + self.rbuf[1, last, c].astype(F32)
            )

    def finish(self):
        for way, t, c in self.started:
            self.message(way, t, c).wait_send()


def ring_sum_scratch(n, rows, width):
    return [
        pltpu.VMEM((n, rows, width), BF),
        pltpu.VMEM((2, 2, rows // 2, width), BF),
        pltpu.VMEM((2, n // 2, 2, rows // 2, width), BF),
        DMA((n,)),
    ] + ring_sems(n)


def probs_of(len_ref, q, k):
    scores = dot(q, k, NT) * (1.0 / math.sqrt(HD))
    at = lax.broadcasted_iota(jnp.int32, scores.shape, 1)
    scores = jnp.where(at < len_ref[0], scores, NEGATIVE)
    exponent = jnp.exp(scores - jnp.max(scores, axis=-1, keepdims=True))
    return exponent / jnp.sum(exponent, axis=-1, keepdims=True)


def query_block(seq):
    return 256 if seq <= 1024 else 128


def as_column(row):
    return jnp.broadcast_to(row, (row.shape[1], row.shape[1])).T


def as_row(column):
    return jnp.broadcast_to(column, (column.shape[0], column.shape[0])).T[:1]


def turn(values, cosine, sine):
    return values * cosine + pltpu.roll(values, HD // 2, 1) * sine


def opening_kernel(n, m, kinds, *refs):
    k, _ = carried(kinds)
    len_ref, x_ref, w_ref, wo_ref, gain_ref, cos_ref, sin_ref = refs[:7]
    (ain_ref, qkv_ref, proj_ref, sums_ref, q_ref, k_ref, v_ref, att_ref, tok_ref, wout_ref,
     gall_ref, wide_ref, narrow_ref) = refs[7 + k : 20 + k]
    (hid, qkv, wpair, gall, ain, buf, own, out_sem, copies, s_send, s_recv,
     w_send, w_recv, f_send, f_recv, g_send, g_recv, a_send, a_recv, o_send, o_recv,
     c_send, c_recv, t_send, t_recv, t_sem, h_send, h_recv, r_send, r_recv) = refs[20 + 2 * k : -2]
    carry = Carry(kinds, refs[7 : 7 + k], refs[20 + k : 20 + 2 * k], *refs[-2:])
    me = lax.axis_index("head")
    f = lax.axis_index("fsdp")
    nx = m // 2
    x, core = f // 2, f % 2
    rows, width = x_ref.shape
    dh = q_ref.shape[1]
    seq = n * rows
    qb = query_block(seq)
    part_rows = rows // 2

    def part(i, side):
        return ((x + i) % nx) * 2 + side

    pair = {"fsdp": part(0, 1 - core)}
    greet(other_heads() + other_parts())

    ring = Ring(
        lambda c: x_ref.at[pl.ds(c * part_rows, part_rows)],
        lambda h, c: hid.at[h, pl.ds(c * part_rows, part_rows)],
        h_send, h_recv, n,
    )
    to_parts = [
        remote(gain_ref, gall.at[me, f], g_send.at[d], g_recv.at[d], dev)
        for d, dev in enumerate(other_parts())
    ]
    outs = [
        remote(
            wo_ref, wpair.at[x], o_send.at[i - 1], o_recv.at[i - 1], {"fsdp": part(nx - i, core)}
        )
        for i in range(1, nx)
    ]
    columns = [
        remote(
            w_ref.at[:, pl.ds(pl.multiple_of(j * width + dev["head"] * dh, 128), dh)],
            qkv.at[me, f, :, pl.ds(j * dh, dh)],
            w_send.at[d, j],
            w_recv.at[d, j],
            dev,
        )
        for d, dev in enumerate(other_heads())
        for j in range(3)
    ]
    for c in to_parts + outs:
        c.start()
    carry.begin([0])
    ring.start()
    for c in columns:
        c.start()
    gall[me, f] = gain_ref[...]
    wpair[x] = wo_ref[...]
    hid[me] = x_ref[...]
    for j in range(3):
        qkv[me, f, :, pl.ds(j * dh, dh)] = w_ref[
            :, pl.ds(pl.multiple_of(j * width + me * dh, 128), dh)
        ]
    for c in to_parts:
        c.wait_recv()
    gains = [
        remote(gall.at[me], gall.at[me], a_send.at[d], a_recv.at[d], dev)
        for d, dev in enumerate(other_heads())
    ]
    for c in gains:
        c.start()
    for c in gains:
        c.wait_recv()

    def gain_row(k):
        return jnp.concatenate(
            [
                sum(gall[h, i * fs + j, k : k + 1, :] for j in range(fs))
                for h in range(n)
                for i in range(m // fs)
            ],
            axis=1,
        )

    fs = 128 // w_ref.shape[0]
    gain_attn = gain_row(0)
    stores = []

    def store(src, dst, sem):
        stores.append(pltpu.make_async_copy(src, dst, sem))
        stores[-1].start()

    def normalise(i, slot):
        wide = hid[i].astype(F32)
        inv = lax.rsqrt(jnp.mean(wide * wide, axis=-1, keepdims=True) + EPS)
        ain[i] = (wide * inv * gain_attn).astype(BF)
        store(ain.at[i], ain_ref.at[i], out_sem.at[slot])

    normalise(me, 0)
    for c in columns:
        c.wait_recv()
    across = [
        remote(qkv.at[:, f], qkv.at[:, f], f_send.at[i], f_recv.at[i], {"fsdp": part(nx - i, core)})
        for i in range(1, nx)
    ]
    for c in across:
        c.start()
    carry.begin(range(1, len(carry.jobs)))

    def beside(i):
        there = qkv.at[:, part(i, core)]
        return remote(there, there, f_send.at[nx + i], f_recv.at[nx + i], pair)

    beside(0).start()

    def receive(step):
        ring.step(step)
        normalise(head_at(step), 2 * step - 1)
        normalise(head_at(-step), 2 * step)

    for step in range(1, n // 2 - 1):
        receive(step)

    halves = nx // 2
    for c in outs:
        c.wait_recv()
    wring = Ring(
        lambda c: wpair.at[pl.ds(c * halves, halves)],
        lambda h, c: wout_ref.at[h, pl.ds(c * halves, halves), core],
        r_send, r_recv, n,
    )
    wring.start()
    mine = pltpu.make_async_copy(wpair, wout_ref.at[me, :, core], copies.at[0])
    mine.start()

    def over(offset, slot):
        there = wout_ref.at[head_at(offset), :, core]
        return remote(there, there, c_send.at[slot], c_recv.at[slot], pair)

    def advance(step):
        wring.step(step)
        if step < n // 2:
            over(step, 2 * step - 1).start()
            over(-step, 2 * step).start()
        else:
            over(step, n - 1).start()

    receive(n // 2 - 1)
    ring.step(n // 2)
    normalise(head_at(n // 2), n - 1)
    for i, c in enumerate(across):
        c.wait_recv()
        beside(i + 1).start()
    mine.wait()
    over(0, 0).start()
    advance(1)
    for i in range(nx):
        beside(i).wait_recv()
    store(qkv, qkv_ref, copies.at[1])
    weight = qkv.reshape(width, 3 * dh)
    for g in range(n // 2):
        at = pl.ds(g * 2 * rows, 2 * rows)
        projected = dot(ain[2 * g : 2 * g + 2].reshape(2 * rows, width), weight[...])
        proj_ref[at, :] = projected[:, : 2 * dh]
        v_ref[at, :] = projected[:, 2 * dh :].astype(BF)
        for k in range(2):
            squares = projected[:, k * dh : (k + 1) * dh]
            squares = jnp.sum(squares * squares, axis=1, keepdims=True)
            for j in range(2):
                own[pl.ds(k * n + 2 * g + j, 1), :] = as_row(squares[j * rows : (j + 1) * rows])
    moves = [
        remote(own, buf.at[me], s_send.at[d], s_recv.at[d], dev)
        for d, dev in enumerate(other_heads())
    ]
    for c in moves:
        c.start()
    buf[me] = own[...]
    gain_q, gain_k = (
        jnp.concatenate(
            [
                sum(gall[me, i * fs + j, k : k + 1, :] for j in range(fs))
                for i in range(m // fs)
            ],
            axis=1,
        )
        for k in (2, 3)
    )
    gall_ref[...] = gall[...]
    wide_ref[0:1] = gain_attn
    wide_ref[1:2] = gain_row(1)
    narrow_ref[0:1] = gain_q
    narrow_ref[1:2] = gain_k
    for c in moves:
        c.wait()
    total_of = buf[0]
    for i in range(1, n):
        total_of = total_of + buf[i]
    sums_ref[...] = total_of
    inv_all = lax.rsqrt(total_of / width + EPS)
    advance(2)
    for i in range(n):
        at = pl.ds(i * rows, rows)
        inv_q = as_column(inv_all[i : i + 1])
        inv_k = as_column(inv_all[n + i : n + i + 1])
        cosine = cos_ref[at, :]
        sine = sin_ref[at, :]
        for head in range(dh // HD):
            lanes = pl.ds(head * HD, HD)
            k_lanes = pl.ds(dh + head * HD, HD)
            span = slice(head * HD, (head + 1) * HD)
            q_ref[at, lanes] = turn(
                proj_ref[at, lanes] * inv_q * gain_q[:, span], cosine, sine
            ).astype(BF)
            k_ref[at, lanes] = turn(
                proj_ref[at, k_lanes] * inv_k * gain_k[:, span], cosine, sine
            ).astype(BF)
    to = tok_ref.at[:, pl.ds(pl.multiple_of(me * dh, 128), dh)]

    def leave(h):
        return remote(att_ref.at[pl.ds(h * rows, rows)], to, t_send.at[h], t_recv.at[me], {"head": h})

    def arrive(h):
        return remote(
            att_ref.at[pl.ds(h * rows, rows)], tok_ref.at[:, pl.ds(h * dh, dh)],
            t_send.at[h], t_recv.at[h], {"head": h},
        )

    def stay(h):
        return pltpu.make_async_copy(att_ref.at[pl.ds(h * rows, rows)], to, t_sem.at[h])

    for j in range(seq // qb):
        at = pl.ds(j * qb, qb)
        for head in range(dh // HD):
            lanes = pl.ds(head * HD, HD)
            probs = probs_of(len_ref, q_ref[at, lanes], k_ref[:, lanes])
            att_ref[at, lanes] = dot(probs.astype(BF), v_ref[:, lanes]).astype(BF)
        for h in range(j * qb // rows, (j + 1) * qb // rows):

            @pl.when(me != h)
            def _(h=h):
                leave(h).start()

            @pl.when(me == h)
            def _(h=h):
                stay(h).start()

        if j == 1:
            advance(3)
    for step in range(4, n // 2 + 1):
        advance(step)
    for h in range(n):

        @pl.when(me != h)
        def _(h=h):
            leave(h).wait_send()
            arrive(h).wait_recv()

        @pl.when(me == h)
        def _(h=h):
            stay(h).wait()

    for c in stores:
        c.wait()
    for slot in range(n):
        over(0, slot).wait_recv()
    over(0, 0).wait_send()
    for step in range(1, n // 2):
        over(step, 2 * step - 1).wait_send()
        over(-step, 2 * step).wait_send()
    over(n // 2, n - 1).wait_send()
    for c in to_parts + outs + columns + gains + across:
        c.wait_send()
    for i in range(nx):
        beside(i).wait_send()
    ring.finish()
    wring.finish()
    carry.end()


def opening(lengths, x, w, w_out, gains, cosine, sine, n, m, kinds, arrays):
    rows, width = x.shape
    seq = n * rows
    shard = w.shape[0]
    dh = w.shape[1] // 3 // n
    heads = jax.ShapeDtypeStruct((seq, dh), BF)
    count, shapes, scratch = carry_plan(kinds, arrays, m)
    return pl.pallas_call(
        functools.partial(opening_kernel, n, m, kinds),
        out_shape=[
            jax.ShapeDtypeStruct((n, rows, width), BF),
            jax.ShapeDtypeStruct((n, m, shard, 3 * dh), BF),
            jax.ShapeDtypeStruct((seq, 2 * dh), F32),
            jax.ShapeDtypeStruct((2 * n, rows), F32),
            heads, heads, heads, heads,
            jax.ShapeDtypeStruct((rows, width), BF),
            jax.ShapeDtypeStruct((n, m // 2, 2, shard, width), BF),
            jax.ShapeDtypeStruct((n, m) + gains.shape, F32),
            jax.ShapeDtypeStruct((2, width), F32),
            jax.ShapeDtypeStruct((2, dh), F32),
        ]
        + shapes,
        in_specs=[pl.BlockSpec(memory_space=pltpu.SMEM)] + [WHOLE] * 6 + [ANY] * count,
        out_specs=[ANY] * 2 + [WHOLE] * 6 + [ANY] * 2 + [WHOLE] * 3 + [ANY] * count,
        scratch_shapes=[
            pltpu.VMEM((n, rows, width), BF),
            pltpu.VMEM((n, m, shard, 3 * dh), BF),
            pltpu.VMEM((m // 2, shard, width), BF),
            pltpu.VMEM((n, m) + gains.shape, F32),
            pltpu.VMEM((n, rows, width), BF),
            pltpu.VMEM((n, 2 * n, rows), F32),
            pltpu.VMEM((2 * n, rows), F32),
            DMA((n,)), DMA((2,)), DMA((n - 1,)), DMA((n - 1,)),
            DMA((n - 1, 3)), DMA((n - 1, 3)), DMA((m,)), DMA((m,)), DMA((m - 1,)), DMA((m - 1,)),
            DMA((n - 1,)), DMA((n - 1,)), DMA((m // 2,)), DMA((m // 2,)),
            DMA((n,)), DMA((n,)), DMA((n,)), DMA((n,)), DMA((n,)),
        ]
        + ring_sems(n)
        + ring_sems(n)
        + scratch,
        compiler_params=pltpu.CompilerParams(
            collective_id=0, has_side_effects=True, vmem_limit_bytes=60 << 20
        ),
        cost_estimate=cost(100),
    )(lengths, x, w, w_out, gains, cosine, sine, *arrays)


def weave(chunks, polls):
    whole = sum(w for w, _ in chunks)
    done, k = 0.0, 0
    for weight, run in chunks:
        run()
        done += weight
        while k < len(polls) - 1 and done * len(polls) >= (k + 1) * whole:
            polls[k]()
            k += 1
    for poll in polls[k:]:
        poll()


def span_of(seq):
    return seq if seq <= 512 else 256


def source_order(m):
    f = lax.axis_index("fsdp")
    nx = m // 2
    x, core = f // 2, f % 2
    return [((x + i) % nx) * 2 + (core + side) % 2 for side in range(2) for i in range(nx)]


def piece_of(kept, r, nx):
    side, i = divmod(r, nx)
    return kept[2 * side] if i == 0 else kept[2 * side + 1].at[nx - 1 - i]


class Weights:
    def __init__(self, m, kept, bufs, sems):
        self.m, self.kept, self.bufs, self.sems = m, kept, bufs, sems

    def copies(self, key):
        m, nx = self.m, self.m // 2
        order = source_order(m)
        gate, up, down = self.bufs
        g_sem, d_sem = self.sems
        block, tile = gate.shape[0] // m, down.shape[0] // m
        rows = lambda r, size: pl.ds(pl.multiple_of(order[r] * size, size), size)
        if key == "down":
            return [
                pltpu.make_async_copy(
                    piece_of(self.kept[2], r, nx), down.at[rows(r, tile)], d_sem.at[r]
                )
                for r in range(m)
            ]
        cols = pl.ds(key * tile, tile)
        return [
            pltpu.make_async_copy(
                piece_of(self.kept[i], r, nx).at[:, cols], v.at[rows(r, block), cols],
                g_sem.at[i, r, key],
            )
            for i, v in enumerate((gate, up))
            for r in range(m)
        ]

    def start(self, key):
        for c in self.copies(key):
            c.start()

    def wait(self, key):
        for c in self.copies(key):
            c.wait()


def front_chunk(t, x, weights, pre):
    gate_v, up_v, down_v = weights.bufs
    tile = down_v.shape[0] // weights.m
    cols = pl.ds(t * tile, tile)
    weights.wait(t)
    pre[0, :, cols] = dot(x[...], gate_v[:, cols])
    pre[1, :, cols] = dot(x[...], up_v[:, cols])


def forward_chunk(e, t, x, cot, gates_ref, at, weights, acts, dots_ref, first, pre=None):
    gate_v, up_v, down_v = weights.bufs
    tile = down_v.shape[0] // weights.m
    cols = pl.ds(t * tile, tile)
    if t == 0:
        weights.wait("down")
    if pre is None:
        weights.wait(t)
        gate_pre = dot(x[...], gate_v[:, cols])
        up_pre = dot(x[...], up_v[:, cols])
    else:
        gate_pre = pre[0, :, cols]
        up_pre = pre[1, :, cols]
    back = dot(cot[...], down_v[cols, :], NT)
    gate = gates_ref[at, e : e + 1]
    sig = 1.0 / (1.0 + jnp.exp(-gate_pre))
    silu = gate_pre * sig
    value = silu * up_pre
    dots = jnp.sum(value * back, axis=1, keepdims=True)
    if first:
        dots_ref[at, e : e + 1] = dots
    else:
        dots_ref[at, e : e + 1] += dots
    grad_act = gate * back
    acts[e, 0, :, cols] = (gate * value).astype(BF)
    acts[e, 1, :, cols] = (grad_act * up_pre * sig * (1.0 + gate_pre * (1.0 - sig))).astype(BF)
    acts[e, 2, :, cols] = (grad_act * silu).astype(BF)


def experts_steps(m, x_ref, cot_ref, gates_ref, weights, x, cot, acts, stage, pre,
                  dots_ref, acts_ref, gin_ref, mix_ref, in_sem, a_sem, o_sem, polls, between, more=()):
    seq, width = x_ref.shape
    span = x.shape[0]
    spans = seq // span
    chunks = []
    stores = []

    def copy(store):
        store.start()
        stores.append(store)

    for q in range(spans):
        at = pl.ds(q * span, span)
        load_x = pltpu.make_async_copy(x_ref.at[at], x, in_sem.at[0])
        load_cot = pltpu.make_async_copy(cot_ref.at[at], cot, in_sem.at[1])

        def load(q=q, load_x=load_x, load_cot=load_cot):
            if q:
                while stores:
                    stores.pop().wait()
                load_x.start()
                load_cot.start()
            load_x.wait()
            load_cot.wait()

        if q == 0:
            load_x.start()
            for w in weights:
                if w is weights[0]:
                    w.start(0)
                    load_cot.start()
                    w.start("down")
                    for t in range(1, m):
                        w.start(t)
            between(0)
        chunks.append((0.1, load))
        for e in range(EXP_DEV):
            late = e == EXP_DEV - 1

            def front(t, e=e, q=q):
                if q == 0 and t == m - 1:
                    between(2)
                if q:
                    weights[e].wait = lambda key: None
                front_chunk(t, x, weights[e], pre)

            if late:
                for t in range(m):
                    chunks.append((1.1 * 4 / m, functools.partial(front, t)))
            for t in range(m):

                def run(e=e, t=t, q=q, at=at, late=late):
                    if q == 0 and not late and t == m // 2:
                        between(1)
                    if q == 0 and late and t == 0:
                        between(3)
                    if q:
                        weights[e].wait = lambda key: None
                    forward_chunk(
                        e, t, x, cot, gates_ref, at, weights[e], acts, dots_ref, t == 0,
                        pre if late else None,
                    )

                chunks.append(((0.6 if late else 1.6) * 4 / m, run))

            def keep(e=e, at=at):
                copy(pltpu.make_async_copy(acts.at[e], acts_ref.at[e, :, at], a_sem.at[e]))

            chunks.append((0.0, keep))
        for r in range(width // 512):

            def run(r=r, at=at):
                lanes = pl.ds(r * 512, 512)
                mixed, grads = None, None
                for e in range(EXP_DEV):
                    gate_v, up_v, down_v = weights[e].bufs
                    a = dot(acts[e, 0], down_v[:, lanes])
                    b = dot(acts[e, 1], gate_v[lanes, :], NT) + dot(acts[e, 2], up_v[lanes, :], NT)
                    mixed = a if mixed is None else mixed + a
                    grads = b if grads is None else grads + b
                stage[0, :, lanes] = grads.astype(BF)
                stage[1, :, lanes] = mixed.astype(BF)
                for i, to in enumerate((gin_ref, mix_ref)):
                    copy(
                        pltpu.make_async_copy(
                            stage.at[i, :, lanes], to.at[at, lanes], o_sem.at[i, r]
                        )
                    )

            chunks.append((3.2, run))
    weave(chunks + list(more), polls)
    for c in stores:
        c.wait()


def experts_scratch(m, seq, width, ff):
    span = span_of(seq)
    return [
        pltpu.VMEM((EXP_DEV, width, ff), BF),
        pltpu.VMEM((EXP_DEV, width, ff), BF),
        pltpu.VMEM((EXP_DEV, ff, width), BF),
        DMA((EXP_DEV, 2, m, m)),
        DMA((EXP_DEV, m)),
        pltpu.VMEM((span, width), BF),
        pltpu.VMEM((span, width), BF),
        pltpu.VMEM((EXP_DEV, 3, span, ff), BF),
        pltpu.VMEM((2, span, width), BF),
        pltpu.VMEM((2, span, ff), F32),
        DMA((2,)), DMA((EXP_DEV,)), DMA((2, width // 512)),
    ]


def weights_of(e, m, kept, gate_v, up_v, down_v, g_sem, d_sem):
    return Weights(
        m, kept, (gate_v.at[e], up_v.at[e], down_v.at[e]), (g_sem.at[e], d_sem.at[e])
    )


LATE = (("share", 1), "pair", "pair", "pair")


def experts_a_kernel(n, m, *refs):
    x_ref, cot_ref, gates_ref = refs[:3]
    wg, wu, wd = refs[3:6]
    w0, fresh, (xb_own, cotb_own) = refs[6:15], refs[15:20], refs[20:22]
    dots_ref, acts_ref, gin_ref, mix_ref, xb_ref, cotb_ref, down1x, gate1c, up1c, down1c = refs[22:32]
    scratch, rest = refs[32:45], refs[45:]
    gate_v, up_v, down_v, g_sem, d_sem = scratch[:5]
    send0, recv0, send1, recv1, l_sem, c_send, c_recv = rest
    half = xb_own.shape[0] // 4
    me = lax.axis_index("head")
    gate1x, gate1o, up1x, up1o, down1o = fresh
    g1 = (wg.at[1], gate1x, gate1o, gate1c)
    u1 = (wu.at[1], up1x, up1o, up1c)
    d1 = (wd.at[1], down1x, down1o, down1c)
    kept0 = [(w.at[0],) + tuple(w0[3 * i : 3 * i + 3]) for i, w in enumerate((wg, wu, wd))]
    weights = [
        weights_of(0, m, kept0, gate_v, up_v, down_v, g_sem, d_sem),
        weights_of(1, m, (g1, u1, d1), gate_v, up_v, down_v, g_sem, d_sem),
    ]
    carry = Carry(
        LATE, (wd, gate1x, up1x, down1x), (down1x, gate1c, up1c, down1c), c_send, c_recv
    )

    def ring_of(own, out, send, recv):
        return Ring(
            lambda c: own.at[pl.ds((2 + c) * half, half)],
            lambda h, c: out.at[h, pl.ds(c * half, half)],
            send, recv, n,
        )

    rings = [ring_of(xb_own, xb_ref, send0, recv0), ring_of(cotb_own, cotb_ref, send1, recv1)]
    mine = [
        pltpu.make_async_copy(xb_own.at[pl.ds(2 * half, 2 * half)], xb_ref.at[me], l_sem.at[0]),
        pltpu.make_async_copy(cotb_own.at[pl.ds(2 * half, 2 * half)], cotb_ref.at[me], l_sem.at[1]),
    ]

    def between(stage):
        if stage == 0:
            greet([{"head": head_at(1)}, {"head": head_at(-1)}] + other_parts())
            for ring in rings:
                ring.start()
            carry.begin(range(3))
            for c in mine:
                c.start()
        elif stage == 1:
            for j in (1, 2):
                carry.arrived(j)
            for key in range(m):
                weights[1].start(key)
        elif stage == 2:
            carry.arrived(0)
            carry.begin([3])
        else:
            carry.arrived(3)
            weights[1].start("down")

    def poll(step):
        for ring in rings:
            ring.step(step)

    experts_steps(
        m, x_ref, cot_ref, gates_ref, weights, *scratch[5:10], dots_ref, acts_ref, gin_ref, mix_ref,
        *scratch[10:13], [functools.partial(poll, s) for s in range(1, n // 2 + 1)], between,
    )
    for c in mine:
        c.wait()
    for ring in rings:
        ring.finish()
    carry.end(seen=range(4))


def row_outputs(x, ff):
    seq, width = x.shape
    return [
        jax.ShapeDtypeStruct((seq, EXP_DEV), F32),
        jax.ShapeDtypeStruct((EXP_DEV, 3, seq, ff), BF),
        jax.ShapeDtypeStruct((seq, width), BF),
        jax.ShapeDtypeStruct((seq, width), BF),
    ]


def big(us, identity):
    return dict(
        compiler_params=pltpu.CompilerParams(
            collective_id=identity, has_side_effects=True, vmem_limit_bytes=60 << 20
        ),
        cost_estimate=cost(us),
    )


def experts_a(x, cot, gates, weights, weights0, fresh, x_b, cot_b, n, m):
    seq, width = x.shape
    ff = fresh[0].shape[-1]
    w0 = [a for kept in weights0 for a in kept]
    out = jax.ShapeDtypeStruct((n, x_b.shape[0] // 2, width), BF)
    gate1x, up1x = fresh[0], fresh[2]
    moved = (weights[2], gate1x, up1x)
    late = [jax.ShapeDtypeStruct((m // 2 - 1,) + weights[2].shape[1:], BF)]
    late += [jax.ShapeDtypeStruct(a.shape, BF) for a in moved[1:]] + late
    return pl.pallas_call(
        functools.partial(experts_a_kernel, n, m),
        out_shape=row_outputs(x, ff) + [out, out] + late,
        in_specs=[ANY, ANY, WHOLE] + [ANY] * 17 + [WHOLE] * 2,
        out_specs=[WHOLE] + [ANY] * 9,
        scratch_shapes=experts_scratch(m, seq, width, ff)
        + ring_sems(n)
        + ring_sems(n)
        + [DMA((2,))]
        + [DMA((4, max(m // 2 - 1, 1)))] * 2,
        **big(45, 4),
    )(x, cot, gates, *weights, *w0, *fresh, x_b, cot_b)


class Leave:
    def __init__(self, m, same, got, local, send, recv):
        self.m, self.same, self.got = m, same, got
        self.local, self.send, self.recv = local, send, recv
        self.stores, self.away = [], []

    def put(self, r, src, index, spot):
        nx = self.m // 2
        f = lax.axis_index("fsdp")
        if r < nx:
            self.stores.append(
                pltpu.make_async_copy(src, self.same.at[(r,) + index], self.local.at[r, spot])
            )
            self.stores[-1].start()
        else:
            self.away.append(
                remote(
                    src, self.got.at[(r - nx,) + index], self.send.at[r, spot],
                    self.recv.at[r, spot], {"fsdp": (f // 2) * 2 + 1 - f % 2},
                )
            )
            self.away[-1].start()

    def wide(self, i, v):
        order = source_order(self.m)
        block = v.shape[0] // self.m
        for r in range(self.m):
            at = pl.ds(pl.multiple_of(order[r] * block, block), block)
            self.put(r, v.at[at], (i,), i)

    def tall(self, v):
        order = source_order(self.m)
        tile, ff = v.shape[0] // self.m, v.shape[0]
        for r in range(self.m):
            at = pl.ds(pl.multiple_of(order[r] * tile, tile), tile)
            for side in range(2):
                self.put(
                    r, v.at[at, pl.ds(side * ff, ff)], (2, pl.ds(side * tile, tile)), 2 + side
                )

    def finish(self):
        for c in self.stores:
            c.wait()
        for c in self.away:
            c.wait()


def leave_sems(m):
    return [DMA((m, 4)), DMA((m, 4)), DMA((m, 4))]


def experts_b_kernel(n, m, early, *refs):
    x_ref, cot_ref, gates_ref = refs[:3]
    own, w, (gin_a, mix_a, xa_ref, cota_ref, acts_a) = refs[3:6], refs[6:24], refs[24:29]
    dots_ref, acts_ref, gin_ref, mix_ref, grad_ref, sum_ref = refs[29:35]
    refs = refs[35:]
    if early:
        (same, got), refs = refs[:2], refs[2:]
    scratch, rest = refs[:13], refs[13:]
    gate_v, up_v, down_v, g_sem, d_sem, x, cot, acts = scratch[:8]
    weights = [
        weights_of(
            e, m,
            [
                (own[i].at[e],) + tuple(w[9 * e + 3 * i : 9 * e + 3 * i + 3]) for i in range(3)
            ],
            gate_v, up_v, down_v, g_sem, d_sem,
        )
        for e in range(EXP_DEV)
    ]
    rings = [
        RingSum(n, gin_a, grad_ref, *rest[:6]),
        RingSum(n, mix_a, sum_ref, *rest[6:12]),
    ]

    def between(stage):
        if stage == 0:
            for ring in rings:
                ring.load()
            for key in [0, "down"] + list(range(1, m)):
                weights[1].start(key)
            f = lax.axis_index("fsdp")
            pair = [{"fsdp": (f // 2) * 2 + 1 - f % 2}] if early else []
            greet([{"head": head_at(1)}, {"head": head_at(-1)}] + pair)
            for ring in rings:
                ring.start()

    def poll(step):
        for ring in rings:
            ring.step(step)

    more = []
    if early:
        part = x.shape[0]
        leave = Leave(m, same, got, *rest[12:15])
        l_sem = rest[15]
        dgate, dup, ddown = gate_v.at[0], up_v.at[0], down_v.at[0]
        x_a, cot_a = down_v.at[1, pl.ds(0, part)], down_v.at[1, pl.ds(part, part)]
        kept = [gate_v.at[1, pl.ds(k * part, part)] for k in range(3)]
        loads = [
            pltpu.make_async_copy(xa_ref, x_a, l_sem.at[0]),
            pltpu.make_async_copy(cota_ref, cot_a, l_sem.at[1]),
        ] + [
            pltpu.make_async_copy(acts_a.at[0, k], kept[k], l_sem.at[2 + k]) for k in range(3)
        ]

        def begin():
            for c in loads:
                c.start()
            for c in loads:
                c.wait()

        more.append((0.5, begin))
        for b in range(x.shape[1] // 512):

            def run(b=b):
                at = pl.ds(b * 512, 512)
                turned, turned_a = x[:, at].T, x_a[:, at].T
                dgate[at, :] = (dot(turned, acts[0, 1]) + dot(turned_a, kept[1][...])).astype(BF)
                dup[at, :] = (dot(turned, acts[0, 2]) + dot(turned_a, kept[2][...])).astype(BF)

            more.append((2.4, run))
        more.append((0.0, lambda: (leave.wide(0, dgate), leave.wide(1, dup))))
        for t in range(gate_v.shape[2] // 256):

            def run(t=t):
                at = pl.ds(t * 256, 256)
                ddown[at, :] = (
                    dot(acts[0, 0, :, at].T, cot[...]) + dot(kept[0][:, at].T, cot_a[...])
                ).astype(BF)

            more.append((1.2, run))
        more.append((0.0, lambda: leave.tall(ddown)))
    experts_steps(
        m, x_ref, cot_ref, gates_ref, weights, *scratch[5:10], dots_ref, acts_ref, gin_ref, mix_ref,
        *scratch[10:13], [functools.partial(poll, s) for s in range(1, n // 2 + 1)], between, more,
    )
    for ring in rings:
        ring.finish()
    if early:
        leave.finish()


def experts_b(x, cot, gates, own_w, weights, gin_a, mix_a, x_a, cot_a, acts_a, n, m):
    seq, width = x.shape
    ff = own_w[0].shape[2]
    early = seq <= 512
    flat = [a for kept in weights for a in kept]
    rows = seq // n
    own = jax.ShapeDtypeStruct((rows, width), F32)
    parts = [a.reshape(n, rows, width) for a in (gin_a, mix_a)]
    grads = [jax.ShapeDtypeStruct((m // 2, 3, width // m, ff), BF)] * (2 * early)
    return pl.pallas_call(
        functools.partial(experts_b_kernel, n, m, early),
        out_shape=row_outputs(x, ff) + [own, own] + grads,
        in_specs=[ANY, ANY, WHOLE] + [ANY] * 26,
        out_specs=[WHOLE, ANY, ANY, ANY, WHOLE, WHOLE] + [ANY] * len(grads),
        scratch_shapes=experts_scratch(m, seq, width, ff)
        + ring_sum_scratch(n, rows, width)
        + ring_sum_scratch(n, rows, width)
        + (leave_sems(m) + [DMA((5,))]) * early,
        **big(60, 7),
    )(x, cot, gates, *own_w, *flat, *parts, x_a, cot_a, acts_a)


def experts_d_kernel(n, m, experts, kinds, *refs):
    xs, cots, all_acts = refs[0:6:3], refs[1:6:3], refs[2:6:3]
    gin_b, mix_b, extra = refs[6:9]
    (k, back), kk, g = carried(kinds), len(kinds), 2 * len(experts)
    outs, (grad_ref, sum_ref, extra_out) = refs[9 + k : 9 + k + g], refs[9 + k + g : 12 + k + g]
    carry = Carry(kinds, refs[9 : 9 + k], refs[12 + k + g : 12 + k + kk + g], *refs[-back:])
    (x, cot, acts, dgate, dup, ddown, x_sem, a_sem, copy, e_send, e_recv) = refs[
        12 + k + kk + g : 23 + k + kk + g
    ]
    rest = refs[23 + k + kk + g : -back]
    me = lax.axis_index("head")
    rows, width = x.shape
    part = rows // 2
    ff = acts.shape[2]
    rings = [
        RingSum(n, gin_b, grad_ref, *rest[:6]),
        RingSum(n, mix_b, sum_ref, *rest[6:12]),
    ]
    loads = [
        pltpu.make_async_copy(src[i], dst.at[pl.ds(i * part, part)], x_sem.at[k, i])
        for k, (src, dst) in enumerate(((xs, x), (cots, cot)))
        for i in range(2)
    ]

    def act_loads(e):
        return [
            pltpu.make_async_copy(
                all_acts[i].at[e], acts.at[:, pl.ds(i * part, part)], a_sem.at[i]
            )
            for i in range(2)
        ]

    carry.first()
    for ring in rings:
        ring.load()
    for c in loads + act_loads(experts[0]):
        c.start()
    greet(other_heads() + other_parts())
    carry.begin()
    for ring in rings:
        ring.start()
    direct = [pltpu.make_async_copy(extra.at[me], extra_out.at[me], copy.at[0])] + [
        remote(extra.at[dev["head"]], extra_out.at[me], e_send.at[d], e_recv.at[d], dev)
        for d, dev in enumerate(other_heads())
    ]
    for c in direct:
        c.start()
    chunks, leaves = [], []
    for j, e in enumerate(experts):
        leave = Leave(m, outs[2 * j], outs[2 * j + 1], *rest[12 + 3 * j : 15 + 3 * j])

        def begin(j=j, e=e):
            if j:
                leaves[j - 1].finish()
                for c in act_loads(e):
                    c.start()
            for c in (loads if j == 0 else []) + act_loads(e):
                c.wait()

        leaves.append(leave)
        chunks.append((0.1, begin))
        for b in range(width // 512):

            def run(b=b):
                at = pl.ds(b * 512, 512)
                turned = x[:, at].T
                dgate[at, :] = dot(turned, acts[1]).astype(BF)
                dup[at, :] = dot(turned, acts[2]).astype(BF)

            chunks.append((2.2, run))
        chunks.append(
            (0.0, lambda leave=leave: (leave.wide(0, dgate), leave.wide(1, dup)))
        )
        for t in range(ff // 256):

            def run(t=t):
                at = pl.ds(t * 256, 256)
                ddown[at, :] = dot(acts[0, :, at].T, cot[...]).astype(BF)

            chunks.append((1.1, run))
        chunks.append((0.0, lambda leave=leave: leave.tall(ddown)))

    def poll(step):
        for ring in rings:
            ring.step(step)

    weave(chunks, [functools.partial(poll, t) for t in range(1, n // 2 + 1)])
    for ring in rings:
        ring.finish()
    for c in direct:
        c.wait()
    leaves[-1].finish()
    carry.end()


def experts_d(first, second, gin_b, mix_b, dots, n, m, experts, kinds, arrays):
    seq = first[2].shape[2]
    ff = first[2].shape[3]
    rows, width = first[0].shape[1:]
    grads = jax.ShapeDtypeStruct((m // 2, 3, width // m, ff), BF)
    own = jax.ShapeDtypeStruct((rows, width), F32)
    (k, shapes, scratch), g = carry_plan(kinds, arrays, m), 2 * len(experts)

    def flat(parts):
        return [parts[0].reshape(seq, width), parts[1].reshape(seq, width), parts[2]]

    out = pl.pallas_call(
        functools.partial(experts_d_kernel, n, m, experts, kinds),
        out_shape=[grads] * g
        + [own, own, jax.ShapeDtypeStruct(dots.shape, F32)]
        + shapes,
        in_specs=[ANY] * 8 + [WHOLE] + [ANY] * k,
        out_specs=[ANY] * g + [WHOLE, WHOLE, ANY] + [ANY] * len(kinds),
        scratch_shapes=[
            pltpu.VMEM((2 * seq, width), BF),
            pltpu.VMEM((2 * seq, width), BF),
            pltpu.VMEM((3, 2 * seq, ff), BF),
            pltpu.VMEM((width, ff), BF),
            pltpu.VMEM((width, ff), BF),
            pltpu.VMEM((ff, width), BF),
            DMA((2, 2)), DMA((2,)), DMA((1,)), DMA((n - 1,)), DMA((n - 1,)),
        ]
        + ring_sum_scratch(n, rows, width)
        + ring_sum_scratch(n, rows, width)
        + leave_sems(m) * len(experts)
        + scratch,
        **big(45, 8),
    )(
        *flat(first), *flat(second), gin_b.reshape(n, rows, width), mix_b.reshape(n, rows, width),
        dots, *arrays,
    )
    return [tuple(out[2 * j : 2 * j + 2]) for j in range(g // 2)], *out[g : g + 3], out[g + 3 :]


class RingSumHere(RingSum):
    def __init__(self, n, parts, out_ref, sbuf, rbuf, send, recv):
        super().__init__(n, parts, out_ref, None, sbuf, rbuf, None, send, recv)

    def piece(self, o, c):
        return self.parts[head_at(o), pl.ds(c * self.rows, self.rows)].astype(F32)


def closing_kernel(n, m, kinds, early, *refs):
    (k, back), kk = carried(kinds), len(kinds)
    (len_ref, gatt_ref, gao_ref, q_ref, k_ref, v_ref, att_ref, proj_ref, sums_ref, gains_ref,
     cos_ref, sin_ref, ain_ref, qkv_ref) = refs[:14]
    (gin_ref, dqkv_ref, dout_ref, dgains_ref) = refs[14 + k : 18 + k]
    (gheads, gao, ain, qkv, gin, dproj, scaled, dk, dv, own, buf,
     dqkv, gq, xs, xr, fin, dout, go, xso, xro, sbuf, rbuf,
     l_sem, a_send, a_recv, s_send, s_recv, p_send, p_recv, x_send, x_recv, t_send, t_recv, t_sem,
     g_send, g_recv, r_send, r_recv) = refs[18 + k + kk : -back]
    carry = Carry(kinds, refs[14 : 14 + k], refs[18 + k : 18 + k + kk], *refs[-back:])
    me = lax.axis_index("head")
    f = lax.axis_index("fsdp")
    nx = m // 2
    x, core = f // 2, f % 2
    rows, width = gao_ref.shape
    half_rows = rows // 2
    seq, dh = q_ref.shape
    qb = query_block(seq)
    scale = 1.0 / math.sqrt(HD)
    order = source_order(m)
    carry.first()
    loads = [
        pltpu.make_async_copy(ain_ref, ain, l_sem.at[0]),
        pltpu.make_async_copy(qkv_ref, qkv, l_sem.at[1]),
    ]
    for c in loads:
        c.start()
    greet(other_heads() + other_parts())

    here = gheads.at[pl.ds(pl.multiple_of(me * rows, rows), rows)]
    sends = [
        remote(
            gatt_ref.at[:, pl.ds(pl.multiple_of(dev["head"] * dh, 128), dh)], here,
            a_send.at[d], a_recv.at[d], dev,
        )
        for d, dev in enumerate(other_heads())
    ]
    for c in sends:
        c.start()
    gring = Ring(
        lambda c: gao_ref.at[pl.ds(c * half_rows, half_rows)],
        lambda h, c: gao.at[h, pl.ds(c * half_rows, half_rows)],
        g_send, g_recv, n,
    )
    gring.start()
    carry.begin(range(early))
    here[...] = gatt_ref[:, pl.ds(pl.multiple_of(me * dh, 128), dh)]
    gao[me] = gao_ref[...]
    for c in sends:
        c.wait_recv()

    for head in range(dh // HD):
        lanes = pl.ds(head * HD, HD)
        for j in range(seq // qb):
            at = pl.ds(j * qb, qb)
            probs = probs_of(len_ref, q_ref[at, lanes], k_ref[:, lanes])
            grad_probs = dot(gheads[at, lanes], v_ref[:, lanes], NT)
            inner = jnp.sum(probs * grad_probs, axis=-1, keepdims=True)
            grad_scores = (probs * (grad_probs - inner)).astype(BF)
            dproj[at, lanes] = (dot(grad_scores, k_ref[:, lanes]) * scale).astype(BF)
            add_k = dot(grad_scores, q_ref[at, lanes], TN)
            add_v = dot(probs.astype(BF), gheads[at, lanes], TN)
            if j == 0:
                dk[...] = add_k
                dv[...] = add_v
            else:
                dk[...] += add_k
                dv[...] += add_v
        dproj[:, pl.ds(dh + head * HD, HD)] = (dk[...] * scale).astype(BF)
        dproj[:, pl.ds(2 * dh + head * HD, HD)] = dv[...].astype(BF)
        gring.step(head + 1)
    for step in range(dh // HD + 1, 3):
        gring.step(step)

    inv_all = lax.rsqrt(sums_ref[...] / width + EPS)
    dgains = [jnp.zeros((1, HD), F32) for _ in range(2 * dh // HD)]
    for i in range(n):
        at = pl.ds(i * rows, rows)
        cosine = cos_ref[at, :]
        sine = -sin_ref[at, :]
        for kind in range(2):
            inv = as_column(inv_all[kind * n + i : kind * n + i + 1])
            sums = jnp.zeros((rows, 1), F32)
            for head in range(dh // HD):
                spot = kind * (dh // HD) + head
                lanes = pl.ds(kind * dh + head * HD, HD)
                turned = turn(dproj[at, lanes].astype(F32), cosine, sine)
                unit = proj_ref[at, lanes] * inv
                dgains[spot] = dgains[spot] + jnp.sum(turned * unit, axis=0, keepdims=True)
                grad = turned * gains_ref[kind : kind + 1, head * HD : (head + 1) * HD]
                scaled[at, lanes] = grad
                sums = sums + jnp.sum(grad * unit, axis=1, keepdims=True)
            own[pl.ds(kind * n + i, 1), :] = as_row(sums)
    for spot, value in enumerate(dgains):
        dgains_ref[pl.ds(spot, 1), :] = value
    moves = [
        remote(own, buf.at[me], s_send.at[d], s_recv.at[d], dev)
        for d, dev in enumerate(other_heads())
    ]
    for c in moves:
        c.start()
    buf[me] = own[...]
    for c in moves:
        c.wait()
    total_of = buf[0]
    for i in range(1, n):
        total_of = total_of + buf[i]
    means = total_of / width
    for i in range(n):
        at = pl.ds(i * rows, rows)
        for kind in range(2):
            inv = as_column(inv_all[kind * n + i : kind * n + i + 1])
            mean = as_column(means[kind * n + i : kind * n + i + 1])
            for head in range(dh // HD):
                lanes = pl.ds(kind * dh + head * HD, HD)
                unit = proj_ref[at, lanes] * inv
                dproj[at, lanes] = (inv * (scaled[at, lanes] - unit * mean)).astype(BF)

    for c in loads:
        c.wait()
    weight = qkv.reshape(width, 3 * dh)
    for g in range(n // 2):
        part = dot(dproj[pl.ds(g * 2 * rows, 2 * rows), :], weight[...], NT).astype(BF)
        gin[2 * g : 2 * g + 2] = part.reshape(2, rows, width)
    gring.step(3)
    ring = RingSumHere(n, gin, gin_ref, sbuf, rbuf, r_send, r_recv)
    ring.start()

    flat = dqkv.reshape(width, 3 * dh)
    for b in range(width // 512):
        at = pl.ds(b * 512, 512)
        turned = ain.reshape(seq, width)[:, at].T
        flat[at, :] = dot(turned, dproj[...]).astype(BF)
    pair = {"fsdp": x * 2 + 1 - core}
    pairs = [
        remote(dqkv.at[:, order[nx + i]], gq.at[i], p_send.at[i], p_recv.at[i], pair)
        for i in range(nx)
    ]
    for c in pairs:
        c.start()
    for step in range(4, n // 2 + 1):
        gring.step(step)
    for b in range(width // 512):
        at = pl.ds(b * 512, 512)
        value = dot(att_ref[...], gao.reshape(seq, width)[:, at], TN)
        dout[:, :, at] = value.astype(BF).reshape(dout.shape[:2] + (512,))
    pairs_out = [
        remote(dout.at[order[nx + i]], go.at[i], p_send.at[nx + i], p_recv.at[nx + i], pair)
        for i in range(nx)
    ]
    for c in pairs_out:
        c.start()
    ring.step(1)
    for c in pairs + pairs_out:
        c.wait_recv()
    across = []
    for i in range(1, nx):
        there = {"fsdp": ((x + i) % nx) * 2 + core}
        xs[i - 1] = (dqkv[:, order[i]].astype(F32) + gq[i].astype(F32)).astype(BF)
        xso[i - 1] = (dout[order[i]].astype(F32) + go[i].astype(F32)).astype(BF)
        across.append(remote(xs.at[i - 1], xr.at[i - 1], x_send.at[0, i - 1], x_recv.at[0, i - 1], there))
        across.append(remote(xso.at[i - 1], xro.at[i - 1], x_send.at[1, i - 1], x_recv.at[1, i - 1], there))
    for c in across:
        c.start()
    carry.begin(range(early, len(carry.jobs)))
    for step in range(2, n // 2):
        ring.step(step)
    for c in across:
        c.wait_recv()
    value = dqkv[:, order[0]].astype(F32) + gq[0].astype(F32)
    value_out = dout[order[0]].astype(F32) + go[0].astype(F32)
    for i in range(1, nx):
        value = value + xr[i - 1].astype(F32)
        value_out = value_out + xro[i - 1].astype(F32)
    fin[...] = value.astype(BF)
    dout_ref[...] = value_out
    to = [
        dqkv_ref.at[:, pl.ds(pl.multiple_of(j * width + me * dh, 128), dh)] for j in range(3)
    ]
    last = [
        remote(
            fin.at[dev["head"], :, pl.ds(j * dh, dh)], to[j], t_send.at[d, j], t_recv.at[d, j], dev
        )
        for d, dev in enumerate(other_heads())
        for j in range(3)
    ] + [
        pltpu.make_async_copy(fin.at[me, :, pl.ds(j * dh, dh)], to[j], t_sem.at[j])
        for j in range(3)
    ]
    for c in last:
        c.start()
    ring.step(n // 2)
    for c in last:
        c.wait()
    for c in sends + pairs + pairs_out + across:
        c.wait_send()
    gring.finish()
    ring.finish()
    carry.end()


def closing(lengths, gatt, gao, q, k, v, att, proj, sums, gains, cosine, sine, ain, qkv, n, m, kinds,
            arrays, early):
    rows, width = gao.shape
    seq, dh = q.shape
    nx = m // 2
    shard = qkv.shape[2]
    count, shapes, scratch = carry_plan(kinds, arrays, m)

    def vm(*shape, dtype=BF):
        return pltpu.VMEM(shape, dtype)

    return pl.pallas_call(
        functools.partial(closing_kernel, n, m, kinds, early),
        out_shape=[
            jax.ShapeDtypeStruct((rows, width), F32),
            jax.ShapeDtypeStruct((shard, 3 * width), BF),
            jax.ShapeDtypeStruct((shard, width), F32),
            jax.ShapeDtypeStruct((2 * dh // HD, HD), F32),
        ]
        + shapes,
        in_specs=[pl.BlockSpec(memory_space=pltpu.SMEM)] + [WHOLE] * 11 + [ANY] * (2 + count),
        out_specs=[WHOLE, ANY, WHOLE, WHOLE] + [ANY] * len(kinds),
        scratch_shapes=[
            vm(seq, dh), vm(n, rows, width), vm(n, rows, width), vm(n, m, shard, 3 * dh),
            vm(n, rows, width), vm(seq, 3 * dh), vm(seq, 2 * dh, dtype=F32),
            vm(seq, HD, dtype=F32), vm(seq, HD, dtype=F32),
            vm(2 * n, rows, dtype=F32), vm(n, 2 * n, rows, dtype=F32),
            vm(n, m, shard, 3 * dh), vm(nx, n, shard, 3 * dh),
            vm(nx - 1, n, shard, 3 * dh), vm(nx - 1, n, shard, 3 * dh), vm(n, shard, 3 * dh),
            vm(m, shard, width), vm(nx, shard, width),
            vm(nx - 1, shard, width), vm(nx - 1, shard, width),
            vm(2, 2, rows // 2, width), vm(2, n // 2, 2, rows // 2, width),
            DMA((2,)), DMA((n - 1,)), DMA((n - 1,)), DMA((n - 1,)), DMA((n - 1,)),
            DMA((m,)), DMA((m,)), DMA((2, nx - 1)), DMA((2, nx - 1)),
            DMA((n - 1, 3)), DMA((n - 1, 3)), DMA((3,)),
        ]
        + ring_sems(n)
        + ring_sems(n)
        + scratch,
        **big(110, 5),
    )(lengths, gatt, gao, q, k, v, att, proj, sums, gains, cosine, sine, ain, qkv, *arrays)


DEPTH = 4


def settle_kernel(jobs, *refs):
    count = sum(len(sources) for sources, _ in jobs)
    qkv_ref, out_ref = refs[count : count + 2]
    outs = refs[count + 2 : count + 5]
    qkv_out, out_out, ins, result, l_sem, o_sem = refs[count + 5 :]
    steps, k = [], 0
    for sources, (which, e, columns) in jobs:
        arrays = refs[k : k + len(sources)]
        k += len(sources)
        rows = sources[0][1]
        for part in range(1 if columns else 2):
            size = rows if columns else rows // 2
            steps.append((arrays, sources, part * size, size, which, e, columns))

    def loads(i):
        arrays, sources, start, size = steps[i][:4]
        return [
            pltpu.make_async_copy(
                ref.at[index + (pl.ds(base + start, size),)], ins.at[i % DEPTH, j, pl.ds(0, size)],
                l_sem.at[i % DEPTH, j],
            )
            for j, (ref, (index, _, base)) in enumerate(zip(arrays, sources))
        ]

    def store(i):
        _, _, start, size, which, e, columns = steps[i]
        wide = result.shape[2]
        to = outs[which].at[e]
        to = to.at[:, pl.ds(columns[0], wide)] if columns else to.at[pl.ds(start, size)]
        return pltpu.make_async_copy(result.at[i % DEPTH, pl.ds(0, size)], to, o_sem.at[i % DEPTH])

    for i in range(min(DEPTH - 1, len(steps))):
        for c in loads(i):
            c.start()
    qkv_out[...] = qkv_ref[...].astype(F32)
    out_out[...] = out_ref[...]
    for i, (arrays, _, _, size, *_) in enumerate(steps):
        if i + DEPTH - 1 < len(steps):
            for c in loads(i + DEPTH - 1):
                c.start()
        for c in loads(i):
            c.wait()
        if i >= DEPTH:
            store(i - DEPTH).wait()
        value = ins[i % DEPTH, 0, :size].astype(F32)
        for j in range(1, len(arrays)):
            value = value + ins[i % DEPTH, j, :size].astype(F32)
        result[i % DEPTH, :size] = value
        store(i).start()
    for i in range(max(len(steps) - DEPTH, 0), len(steps)):
        store(i).wait()


def settle(grads, sums, qkv, out, m):
    block, ff = grads[0][0].shape[2:]
    tile = block // 2
    jobs, arrays = [], []
    for e, (same, got) in enumerate(grads):
        for which in range(3):
            k, holder = which, None
            for part in sums[e]:
                if k < part.shape[1]:
                    holder = part
                    break
                k -= part.shape[1]
            for half in range(1 if which < 2 else 2):
                rows, base = (block, 0) if which < 2 else (tile, half * tile)
                sources = [((0, which), rows, base)] * 2
                sources += [((i, k), rows, base) for i in range(m // 2 - 1)]
                arrays += [same, got] + [holder] * (m // 2 - 1)
                columns = None if which < 2 else (half * ff,)
                jobs.append((tuple(sources), (which, e, columns)))
    return pl.pallas_call(
        functools.partial(settle_kernel, tuple(jobs)),
        out_shape=[jax.ShapeDtypeStruct((EXP_DEV, block, ff), F32)] * 2
        + [jax.ShapeDtypeStruct((EXP_DEV, tile, 2 * ff), F32)]
        + [jax.ShapeDtypeStruct(a.shape, F32) for a in (qkv, out)],
        in_specs=[ANY] * len(arrays) + [WHOLE] * 2,
        out_specs=[ANY] * 3 + [WHOLE] * 2,
        scratch_shapes=[
            pltpu.VMEM((DEPTH, m // 2 + 1, tile, ff), BF),
            pltpu.VMEM((DEPTH, tile, ff), F32),
            DMA((DEPTH, m // 2 + 1)), DMA((DEPTH,)),
        ],
        compiler_params=pltpu.CompilerParams(vmem_limit_bytes=60 << 20),
        cost_estimate=cost(10),
    )(*arrays, qkv, out)


def joined(same, got):
    return same.astype(F32) + got.astype(F32)


def body(
    hidden,
    w_qkv,
    w_out,
    w_router,
    g_attn,
    g_ffn,
    g_q,
    g_k,
    w_gate,
    w_up,
    w_down,
    lengths,
    routes,
    route_codes,
    cotangent,
):
    n = lax.axis_size("head")
    m = lax.axis_size("fsdp")
    me = lax.axis_index("head")
    rows = hidden.shape[1]
    width = hidden.shape[2]
    seq = rows * n
    lh = HEADS // n
    dh = lh * HD
    experts = EXP_DEV * n
    shard = w_qkv.shape[0]
    both = ("head", "fsdp")

    sides = 128 // shard
    lane = jnp.arange(128, dtype=jnp.int32) // shard == lax.axis_index("fsdp") % sides
    small = jnp.tile(jnp.stack([g_attn, g_ffn, g_q, g_k]), (2, sides)).astype(F32)
    small = jnp.concatenate(
        [jnp.where(lane[None, :], small, 0.0), w_router.astype(F32).reshape(-1, 128)]
    )
    def inverse_rms(values):
        return lax.rsqrt(jnp.mean(values * values, axis=-1, keepdims=True) + EPS)

    angles = np.arange(seq)[:, None] * ROPE_BASE ** (-2.0 * np.arange(HD // 2) / HD)
    cosine = np.tile(np.cos(angles), (1, 2)).astype(np.float32)
    sine = np.concatenate([-np.sin(angles), np.sin(angles)], axis=1).astype(np.float32)
    (attn_input, qkv, proj, sums, queries, keys, values, attended, attended_tok, full_out, small,
     gains_wide, gains_heads, gate0x, up0x, down0x) = opening(
        lengths, hidden[0], w_qkv, w_out, small, cosine, sine, n, m, (("share", 0),) * 3,
        (w_gate, w_up, w_down),
    )
    router = small[:, :, 8:].reshape(width, experts).astype(BF)
    gain_attn, gain_ffn = gains_wide
    full_out = full_out.reshape(width, width)
    half = rows // 2
    own_w = (w_gate, w_up, w_down)
    over_x = (gate0x, up0x, down0x)
    residual, own_input, spread, x_a, cot_a, mine, gate1x, up1x, *got = routing(
        hidden[0], attended_tok, full_out, gains_wide[1:], jnp.pad(router, ((0, 0), (0, 128 - experts))),
        routes[0], route_codes[0], cotangent[0], n, m, experts,
        (("share", 1),) * 2 + (("pair", 0),) * 3 + ("pair",) * 3 + (("pair", 1),) * 3,
        (w_gate, w_up, *own_w, *over_x, *own_w),
    )
    spread = spread[:, :experts]
    weights0 = [(over_x[i], got[i], got[3 + i]) for i in range(3)]
    mine = mine.transpose(0, 2, 1)
    span = n * half

    def rows_of(part):
        return part.reshape(span, width)

    gates_a = mine[:, :half].reshape(span, EXP_DEV)
    gates_b = mine[:, half:].reshape(span, EXP_DEV)
    fresh = [gate1x, got[6], up1x, got[7], got[8]]
    dots_a, acts_a, gin_a, mix_a, x_b, cot_b, down1x, gate1c, up1c, down1c = experts_a(
        rows_of(x_a), rows_of(cot_a), gates_a, own_w, weights0, fresh, own_input,
        cotangent[0], n, m,
    )
    weights1 = [(gate1x, got[6], gate1c), (up1x, got[7], up1c), (down1x, got[8], down1c)]
    dots_b, acts_b, gin_b, mix_b, grad_ffn_a, summed_a, *grads0 = experts_b(
        rows_of(x_b), rows_of(cot_b), gates_b, own_w, weights0 + weights1, gin_a, mix_a,
        rows_of(x_a), rows_of(cot_a), acts_a, n, m,
    )
    dots = jnp.concatenate(
        [d.reshape(n, half, EXP_DEV).transpose(0, 2, 1) for d in (dots_a, dots_b)], axis=2
    )

    early = len(grads0) > 0
    grads, grad_ffn_b, summed_b, dots, sums0 = experts_d(
        (x_a, cot_a, acts_a), (x_b, cot_b, acts_b), gin_b, mix_b, dots, n, m,
        (1,) if early else (0, 1), (("join", 0, 2),) * early, tuple(grads0),
    )
    grads = [tuple(grads0)] * early + grads
    grad_ffn = jnp.concatenate([grad_ffn_a, grad_ffn_b], axis=0)
    summed = jnp.concatenate([summed_a, summed_b], axis=0)
    dots = dots.reshape(experts, rows).T
    grad_rows = cotangent[0].astype(F32)
    grad_logits = spread * (dots - jnp.sum(spread * dots, axis=1, keepdims=True))
    high = lax.Precision.HIGHEST
    grad_ffn = grad_ffn + jnp.dot(grad_logits, router.astype(F32).T, precision=high)
    grad_router = jnp.dot(own_input.astype(F32).T, grad_logits, precision=high)

    def norm_back(values, gain, grad):
        inv = inverse_rms(values)
        unit = values * inv
        scaled = grad * gain
        back = inv * (scaled - unit * jnp.mean(scaled * unit, axis=-1, keepdims=True))
        return back, jnp.sum(grad * unit, axis=0)

    back, grad_gain_ffn = norm_back(residual, gain_ffn, grad_ffn)
    grad_residual = grad_rows + back
    grad_attn_out = grad_residual.astype(BF)
    grad_attended = dot(grad_attn_out, full_out, NT).astype(BF)
    spans = [(span, 0) for span in (((2, 3),) if early else ((0, 2), (2, 3)))]
    spans += [(span, 1) for span in ((0, 1), (1, 2), (2, 3))]
    if early:
        kinds = tuple(("join",) + span for span, _ in spans)
        riders = [a for _, e in spans for a in grads[e]]
    else:
        kinds = ("across",) * len(spans)
        riders = [
            joined(*(part[1:, a:b] for part in grads[e])).astype(BF) for (a, b), e in spans
        ]
    grad_attn_in, grad_qkv, grad_out_w, grad_gains, *arrived = closing(
        lengths, grad_attended, grad_attn_out, queries, keys, values, attended, proj, sums,
        gains_heads, cosine, sine, attn_input, qkv, n, m,
        kinds, riders, 3,
    )
    sums0 = list(sums0) + arrived[:-3]
    sums1 = arrived[-3:]
    grad_gain_q, grad_gain_k = grad_gains.reshape(2, dh)
    out_rows = residual + summed

    grad_w_gate, grad_w_up, grad_w_down, grad_qkv, grad_out_w = settle(
        grads, (sums0, sums1), grad_qkv, grad_out_w, m
    )

    back, grad_gain_attn = norm_back(hidden[0].astype(F32), gain_attn, grad_attn_in)
    grad_hidden = grad_residual + back

    def at_mine(piece):
        return lax.dynamic_update_slice_in_dim(jnp.zeros((width,), F32), piece, me * dh, 0)

    pack = jnp.concatenate(
        [grad_router.reshape(n * m, shard * experts)]
        + [
            g.reshape(n * m, shard)
            for g in (grad_gain_attn, grad_gain_ffn, at_mine(grad_gain_q), at_mine(grad_gain_k))
        ],
        axis=1,
    )
    pack = lax.all_to_all(pack, both, split_axis=0, concat_axis=0, tiled=True)
    pack = jnp.sum(pack, axis=0)
    small_grads = pack[shard * experts :].reshape(4, shard)
    return (
        out_rows.astype(BF)[None],
        grad_hidden[None],
        grad_qkv,
        grad_out_w,
        pack[: shard * experts].reshape(shard, experts),
        small_grads[0],
        small_grads[1],
        small_grads[2],
        small_grads[3],
        grad_w_gate,
        grad_w_up,
        grad_w_down,
    )


def solution(mesh):
    both = ("head", "fsdp")
    return jax.shard_map(
        body,
        mesh=mesh,
        in_specs=(
            P("fsdp", "head", None),
            P(both, None),
            P(both, None),
            P(both, None),
            P(both),
            P(both),
            P(both),
            P(both),
            P("head", "fsdp", None),
            P("head", "fsdp", None),
            P("head", "fsdp", None),
            P("fsdp"),
            P("fsdp", "head", None),
            P("fsdp", "head", None),
            P("fsdp", "head", None),
        ),
        out_specs=(
            P("fsdp", "head", None),
            P("fsdp", "head", None),
            P(both, None),
            P(both, None),
            P(both, None),
            P(both),
            P(both),
            P(both),
            P(both),
            P("head", "fsdp", None),
            P("head", "fsdp", None),
            P("head", "fsdp", None),
        ),
        check_vma=False,
    )
```
